32 devices in a mesh: seq: 2 (over y), dp: 16 (over z, x, core).
Axes of the slice: x: 2, y: 2, z: 4, core: 2. Of those that a mesh axis runs over, the one named last changes fastest.
Arguments:
- tokens: bfloat16 [16, 512, 1024], P('dp', 'seq'), may hold values from -6 to 6
- starts: int32 [16, 512], P('dp', 'seq'), may hold values 0 or 1
- routes: int32 [16, 512, 8], P('dp', 'seq'), may hold values from 0 to 15, all different within a row; in each aligned block of 256 rows (0 to 255, 256 to 511, ..., all dimensions but the last counted through in order) at most 224 rows name the same one
- gain_one: bfloat16 [1024], P('dp'), may hold values from 0.5 to 1.5
- query_key_value_weight: bfloat16 [1024, 2048], P('dp'), may hold values from -0.1875 to 0.1875
- w_out: bfloat16 [1024, 1024], P('dp'), may hold values from -1.5 to 1.5
- gain_two: bfloat16 [1024], P('dp'), may hold values from 0.5 to 1.5
- w_router: bfloat16 [1024, 16], P('dp'), may hold values from -0.09375 to 0.09375
- w_gate_up: bfloat16 [1024, 16, 1024], P('dp'), may hold values from -0.1875 to 0.1875
- w_down: bfloat16 [512, 16, 1024], P('dp'), may hold values from -1 to 1
- cotangent: bfloat16 [16, 512, 1024], P('dp', 'seq'), may hold values from -6 to 6
Outputs:
- output: bfloat16 [16, 512, 1024], P('dp', 'seq')
- input_grad: bfloat16 [16, 512, 1024], P('dp', 'seq')
- grad_gain_one: float32 [1024], P('dp')
- grad_w_qkv: float32 [1024, 2048], P('dp')
- grad_w_out: float32 [1024, 1024], P('dp')
- grad_gain_two: float32 [1024], P('dp')
- grad_w_router: float32 [1024, 16], P('dp')
- grad_w_gate_up: float32 [1024, 16, 1024], P('dp')
- grad_w_down: float32 [512, 16, 1024], P('dp')
- stream_rms: float32 [16, 2], P('dp')
The draws below stay inside these ranges and needn't reach their ends.
Inputs may be any that keep to these rules, and one draw needn't show every extreme that they name: `starts`: 1 marks a token that begins a document; a stream's first token begins one whatever its entry. `routes`: each row names 8 different experts; within the 256 rows of one device no expert is named more than 224 times, and in every draw some expert is named exactly 224 times on some device.
All inputs are finite; a program needn't handle non-finite values. No bound on the sum of `starts` on one device may be relied on, other than what follows from the above.
Results may differ from the reference program's by a relative error of at most 0.015.
Values may be sent and summed in bfloat16 or wider, within the bound.
A program may use at most 384 MiB of HBM per device.

```python
import math
import jax
import jax.numpy as jnp
import numpy as np
from jax import lax

MODEL_WIDTH = 1024
QUERY_HEADS = 16
KEY_VALUE_HEADS = 8
HEAD_SIZE = 64
F = 512
EXPERTS = 16
TOPK = 8
TOK_DEV = 256
CAP = 224
STREAM = 512
N_SEQ = 2
N_DP = 16


def plant(values, key, least, largest):
    place = [jax.random.randint(jax.random.fold_in(key, axis), (), 0, length) for axis, length in enumerate(values.shape)]
    widest = values.shape.index(max(values.shape))
    neighbour = place[:widest] + [(place[widest] + 1) % values.shape[widest]] + place[widest + 1:]
    return values.at[tuple(place)].set(least).at[tuple(neighbour)].set(largest)


def shard_levels(own_key, extent, split, smallest, largest):
    def one(position, blocks):
        steps = jax.random.uniform(jax.random.fold_in(jax.random.fold_in(own_key, 6), position), (blocks,), jnp.float32, smallest / len(split), largest / len(split))
        return jnp.repeat(jnp.exp(steps), extent[position] // blocks).reshape((-1,) + (1,) * (len(extent) - position - 1))

    loudness = one(*split[0])
    for cut in split[1:]:
        loudness = loudness * one(*cut)
    return loudness


def deal_out(rng, own, number, rows, count, top, reach, skew):
    order = jax.random.permutation(rng, count)
    crowded, common = shares(count, rows * top, reach, skew, True), shares(count, rows * top, reach, skew, False)
    places = jnp.arange(count)

    def named(tallies, offset_by):
        used = int((tallies > 0).sum())
        fixed = max(1, used // 4)
        moved = fixed + (places - fixed + offset_by * (used - fixed)) % max(1, count - fixed)
        return jnp.zeros((count,), jnp.int32).at[order[jnp.where(places < fixed, places, moved)]].set(jnp.asarray(tallies, jnp.int32))

    tallies = jnp.where(number % 4 == 0, named(crowded, number // 4), named(common, number - number // 4 - 1))
    mixed = jax.random.permutation(jax.random.fold_in(own, 3), count)
    giver, taker = mixed[0:count // 2 * 2:2], mixed[1:count // 2 * 2:2]
    margin = jnp.minimum(tallies[giver] - 1, reach - tallies[taker]) // 2
    margin = jnp.where((giver == order[0]) | (taker == order[0]) | (tallies[taker] == 0), 0, jnp.maximum(margin, 0))
    moved = jax.random.randint(jax.random.fold_in(own, 4), (count // 2,), 0, 1 << 20) % (margin + 1)
    tallies = tallies.at[giver].add(-moved).at[taker].add(moved)
    items = jnp.searchsorted(jnp.cumsum(tallies), jnp.arange(rows * top), side="right").astype(jnp.int32)
    listing = items.reshape(top, rows).T
    listing = listing[jax.random.permutation(jax.random.fold_in(own, 1), rows)]
    offset_by = jax.random.randint(jax.random.fold_in(own, 2), (rows, 1), 0, top)
    return jnp.take_along_axis(listing, (jnp.arange(top)[None, :] + offset_by) % top, axis=1)


def shares(number_of, total, limit, skew, full):
    weights = [(1 << 20) // math.isqrt(rank ** skew) + 1 for rank in range(1, number_of + 1)]
    largest = limit if full else min(limit, max(-(-total // number_of), total * weights[0] // sum(weights)))
    least = 1 if total - largest >= number_of - 1 else 0
    holding, surplus = [largest] + [least] * (number_of - 1), total - largest - least * (number_of - 1)
    while surplus > 0:
        movable = [i for i in range(1, number_of) if holding[i] < largest] or [i for i in range(1, number_of) if holding[i] < limit]
        whole, left = sum([weights[i] for i in movable]), surplus
        for i in movable:
            extra = min(limit - holding[i], max(1, left * weights[i] // whole), surplus)
            holding[i] = holding[i] + extra
            surplus = surplus - extra
    return np.array(holding)


def centred(stream_key, shape, scale, limit, pieces=(), kind=jnp.bfloat16):
    array = scale * jax.random.normal(stream_key, shape, jnp.float32)
    if pieces:
        array = array * shard_levels(stream_key, shape, pieces, -0.22, 0.18)
    return jnp.clip(array, -limit, limit).astype(kind)


def setup_inputs(seed: int = 0) -> dict:
    key_of = jax.random.split(jax.random.key(seed), 12)
    tokens = centred(key_of[0], (N_DP, STREAM, MODEL_WIDTH), 1.0, 6.0, ((0, 16), (1, 2)))
    starts = plant((jax.random.randint(key_of[1], (N_DP, STREAM), 0, STREAM) < 4).astype(jnp.int32), jax.random.fold_in(key_of[1], 1), 0, 1)
    routes_keys = jax.random.split(jax.random.fold_in(key_of[2], 1), N_DP * STREAM // TOK_DEV)
    routes_turns = jax.random.permutation(jax.random.fold_in(key_of[2], 3), N_DP * STREAM // TOK_DEV)
    routes = jax.vmap(lambda own, number: deal_out(jax.random.fold_in(key_of[2], 2), own, number, TOK_DEV, EXPERTS, TOPK, CAP, 1))(routes_keys, routes_turns).reshape((N_DP, STREAM, TOPK))
    gain_one = jnp.clip(1.0 + 0.1 * jax.random.normal(key_of[3], (MODEL_WIDTH,), jnp.float32), 0.5, 1.5).astype(jnp.bfloat16)
    query_key_value_weight = centred(key_of[4], (MODEL_WIDTH, (QUERY_HEADS + 2 * KEY_VALUE_HEADS) * HEAD_SIZE), MODEL_WIDTH ** -0.5, 0.1875, ((0, 16),))
    w_out = centred(key_of[5], (QUERY_HEADS * HEAD_SIZE, MODEL_WIDTH), (QUERY_HEADS * HEAD_SIZE // 64) ** -0.5, 1.5, ((0, 16),))
    gain_two = jnp.clip(1.0 + 0.1 * jax.random.normal(key_of[6], (MODEL_WIDTH,), jnp.float32), 0.5, 1.5).astype(jnp.bfloat16)
    w_router = centred(key_of[7], (MODEL_WIDTH, EXPERTS), (4 * MODEL_WIDTH) ** -0.5, 0.09375, ((0, 16),))
    w_gate_up = centred(key_of[8], (MODEL_WIDTH, EXPERTS, 2 * F), MODEL_WIDTH ** -0.5, 0.1875, ((0, 16),))
    w_down = centred(key_of[9], (F, EXPERTS, MODEL_WIDTH), (F // 16) ** -0.5, 1.0, ((0, 16),))
    cotangent = centred(key_of[10], (N_DP, STREAM, MODEL_WIDTH), 1.0, 6.0, ((0, 16), (1, 2)))
    return dict(tokens=tokens, starts=starts, routes=routes, gain_one=gain_one, query_key_value_weight=query_key_value_weight, w_out=w_out, gain_two=gain_two, w_router=w_router, w_gate_up=w_gate_up, w_down=w_down, cotangent=cotangent)


@jax.custom_vjp
def low(v):
    return lax.optimization_barrier(v.astype(jnp.bfloat16)).astype(jnp.float32)

@jax.custom_vjp
def low_back(v):
    return v

def low_keep(v):
    return (low(v), None)

def low_pass(kept, grad):
    return (grad,)

def back_keep(v):
    return (v, None)

def back_low(kept, grad):
    return (low(grad),)
low.defvjp(low_keep, low_pass)
low_back.defvjp(back_keep, back_low)
epsilon = 1e-06
rope_base = 10000.0
highest = lax.Precision.HIGHEST
masked_score = -1e+30

def rms_normed(token_rows, gain_row):
    inverse = lax.rsqrt(lax.optimization_barrier(jnp.mean(token_rows * token_rows, axis=-1, keepdims=True)) + epsilon)
    return token_rows * inverse * gain_row

def rope_tables(positions, head_dim):
    half_dim = head_dim // 2
    frequency = rope_base ** (-(jnp.arange(half_dim, dtype=jnp.float32) * 2.0) / head_dim)
    angles = positions.astype(jnp.float32)[:, None] * frequency[None, :]
    cosine_table = jnp.cos(angles)
    sine_values = jnp.sin(angles)
    return (jnp.concatenate([cosine_table, cosine_table], 1), jnp.concatenate([sine_values, sine_values], 1))

def rotary_apply(head_rows, cosine_table, sine_values):
    half_dim = head_rows.shape[-1] // 2
    turned = jnp.concatenate([-head_rows[..., half_dim:], head_rows[..., :half_dim]], -1)
    return head_rows * cosine_table[:, None, :] + turned * sine_values[:, None, :]

def doc_layout(flag_row):
    index_all = jnp.arange(flag_row.shape[0], dtype=jnp.int32)
    begins = jnp.where(index_all == 0, 1, flag_row).astype(jnp.int32)
    segment_ids = jnp.cumsum(begins).astype(jnp.int32)
    last_begin = lax.cummax(jnp.where(begins > 0, index_all, -1).astype(jnp.int32), axis=0)
    return ((index_all - last_begin).astype(jnp.int32), segment_ids)

def slot_tables(route_rows):
    pair_count = route_rows.shape[0] * route_rows.shape[1]
    flat_routes = route_rows.reshape(-1)
    one_hot = (flat_routes[:, None] == jnp.arange(EXPERTS, dtype=jnp.int32)[None, :]).astype(jnp.int32)
    earlier = jnp.cumsum(one_hot, axis=0) - one_hot
    within = lax.optimization_barrier(jnp.sum(earlier * one_hot, axis=1))
    slot_flat = (flat_routes * CAP + within).astype(jnp.int32)
    pair_of_slot = jnp.full((EXPERTS * CAP,), pair_count, jnp.int32).at[slot_flat].set(jnp.arange(pair_count, dtype=jnp.int32))
    return (slot_flat.reshape(route_rows.shape), pair_of_slot)

def attend_stream(token_rows, positions, segment_ids, gain_row, qkv_weight, out_weight):
    sequence_length = token_rows.shape[0]
    query_columns = QUERY_HEADS * HEAD_SIZE
    key_value_columns = KEY_VALUE_HEADS * HEAD_SIZE
    normed = low(rms_normed(token_rows, gain_row))
    projected_rows = low_back(jnp.dot(normed, qkv_weight, precision=highest))
    cosine_table, sine_values = rope_tables(positions, HEAD_SIZE)
    queries = rotary_apply(projected_rows[:, :query_columns].reshape(sequence_length, QUERY_HEADS, HEAD_SIZE), cosine_table, sine_values)
    every_key_row = rotary_apply(projected_rows[:, query_columns:query_columns + key_value_columns].reshape(sequence_length, KEY_VALUE_HEADS, HEAD_SIZE), cosine_table, sine_values)
    every_value_row = projected_rows[:, query_columns + key_value_columns:].reshape(sequence_length, KEY_VALUE_HEADS, HEAD_SIZE)
    queries = low_back(low(queries))
    every_key_row = low_back(low(every_key_row))
    every_value_row = low_back(low(every_value_row))
    repeated_keys = jnp.repeat(every_key_row, QUERY_HEADS // KEY_VALUE_HEADS, axis=1)
    repeated_values = jnp.repeat(every_value_row, QUERY_HEADS // KEY_VALUE_HEADS, axis=1)
    scores = jnp.einsum('qhd,khd->hqk', queries, repeated_keys, precision=highest) * HEAD_SIZE ** (-0.5)
    scores = low_back(scores)
    index_all = jnp.arange(sequence_length, dtype=jnp.int32)
    allowed = (segment_ids[:, None] == segment_ids[None, :]) & (index_all[None, :] <= index_all[:, None])
    scores = jnp.where(allowed[None], scores, masked_score)
    probs = jax.nn.softmax(scores, axis=-1)
    attended = jnp.einsum('hqk,khd->qhd', low(probs), repeated_values, precision=highest).reshape(sequence_length, query_columns)
    attended = low_back(low(attended))
    return low_back(jnp.dot(attended, out_weight, precision=highest))

def expert_block(hidden_rows, route_rows, gain_row, router_weight, gate_up_weight, down_weight):
    normed = low(rms_normed(hidden_rows, gain_row))
    logits = jnp.dot(normed, router_weight, precision=highest)
    chosen = jnp.take_along_axis(logits, route_rows, axis=1)
    gate_weights = jax.nn.softmax(chosen, axis=-1)
    slot_index, pair_of_slot = slot_tables(route_rows)
    token_of_slot = pair_of_slot // TOPK
    padded = jnp.concatenate([normed, jnp.zeros((1, MODEL_WIDTH), jnp.float32)], 0)
    dispatched = padded[token_of_slot].reshape(EXPERTS, CAP, MODEL_WIDTH)
    gate_up = low_back(jnp.einsum('ecd,def->ecf', dispatched, gate_up_weight, precision=highest))
    act = low(jax.nn.silu(gate_up[..., :F]) * gate_up[..., F:])
    expert_out = low_back(jnp.einsum('ecf,fed->ecd', act, down_weight, precision=highest)).reshape(EXPERTS * CAP, MODEL_WIDTH)
    picked = expert_out[slot_index]
    return lax.optimization_barrier(jnp.sum(gate_weights[:, :, None] * picked, axis=1))

def reference(tokens, starts, routes, gain_one, query_key_value_weight, w_out, gain_two, w_router, w_gate_up, w_down, cotangent):
    positions, segment_ids = jax.vmap(doc_layout)(starts)
    route_blocks = routes.reshape(N_DP * N_SEQ, TOK_DEV, TOPK)

    def forward(token_rows, gain_a, qkv_weight, out_weight, gain_b, router_weight, gate_up_weight, down_weight):

        def one_stream(packed):
            return attend_stream(packed[0], packed[1], packed[2], gain_a, qkv_weight, out_weight)
        attended = lax.map(jax.checkpoint(one_stream), (token_rows, positions, segment_ids))
        hidden = token_rows + attended

        def one_block(packed):
            return expert_block(packed[0], packed[1], gain_b, router_weight, gate_up_weight, down_weight)
        mixed = lax.map(jax.checkpoint(one_block), (hidden.reshape(N_DP * N_SEQ, TOK_DEV, MODEL_WIDTH), route_blocks))
        mixed = mixed.reshape(N_DP, STREAM, MODEL_WIDTH)
        return (hidden + mixed, (hidden, mixed))
    output, pullback, kept_values = jax.vjp(forward, tokens.astype(jnp.float32), gain_one.astype(jnp.float32), query_key_value_weight.astype(jnp.float32), w_out.astype(jnp.float32), gain_two.astype(jnp.float32), w_router.astype(jnp.float32), w_gate_up.astype(jnp.float32), w_down.astype(jnp.float32), has_aux=True)
    hidden, mixed = kept_values
    gradients = pullback(cotangent.astype(jnp.float32))
    stream_rms = jnp.stack([jnp.sqrt(lax.optimization_barrier(jnp.mean(hidden * hidden, axis=(1, 2)))), jnp.sqrt(lax.optimization_barrier(jnp.mean(mixed * mixed, axis=(1, 2))))], axis=1)
    return (output.astype(jnp.bfloat16), gradients[0].astype(jnp.bfloat16), gradients[1], gradients[2], gradients[3], gradients[4], gradients[5], gradients[6], gradients[7], stream_rms)
```

```python
import jax
import jax.numpy as jnp
from jax import lax
from jax.sharding import PartitionSpec as P

MODEL_WIDTH = 1024
QUERY_HEADS = 16
KEY_VALUE_HEADS = 8
HEAD_SIZE = 64
F = 512
EXPERTS = 16
TOPK = 8

epsilon = 1e-06
rope_base = 10000.0
highest = lax.Precision.HIGHEST
masked_score = -1e30
f32 = jnp.float32
bf16 = jnp.bfloat16


def inverse_rms(rows):
    return lax.rsqrt(jnp.mean(rows * rows, axis=-1, keepdims=True) + epsilon)


def norm_back(rows, gain_row, upstream):
    inverse = inverse_rms(rows)
    gain_grad = jnp.sum(upstream * rows * inverse, axis=0)
    scaled = upstream * gain_row
    rows_grad = inverse * scaled - rows * inverse**3 * jnp.mean(scaled * rows, axis=-1, keepdims=True)
    return rows_grad, gain_grad


def rope_tables(positions):
    half = HEAD_SIZE // 2
    frequency = rope_base ** (-(jnp.arange(half, dtype=f32) * 2.0) / HEAD_SIZE)
    angles = positions.astype(f32)[:, None] * frequency[None, :]
    cosine, sine = jnp.cos(angles), jnp.sin(angles)
    return jnp.concatenate([cosine, cosine], 1), jnp.concatenate([sine, sine], 1)


def rotary_apply(rows, cosine, sine):
    half = HEAD_SIZE // 2
    turned = jnp.concatenate([-rows[..., half:], rows[..., :half]], -1)
    return rows * cosine[:, None, :] + turned * sine[:, None, :]


def unrotate(rows, cosine, sine):
    half = HEAD_SIZE // 2
    scaled = rows * sine[:, None, :]
    back = jnp.concatenate([scaled[..., half:], -scaled[..., :half]], -1)
    return rows * cosine[:, None, :] + back


def make_body(n_dp):
    groups_count = n_dp // EXPERTS
    token_groups = (
        None
        if groups_count == 1
        else [[g * EXPERTS + j for j in range(EXPERTS)] for g in range(groups_count)]
    )
    expert_groups = [[g * EXPERTS + j for g in range(groups_count)] for j in range(EXPERTS)]

    def token_gather(rows):
        return lax.all_gather(rows, "dp", axis=0, tiled=True, axis_index_groups=token_groups)

    def token_scatter(rows):
        return lax.psum_scatter(
            rows, "dp", scatter_dimension=0, tiled=True, axis_index_groups=token_groups
        )

    def exchange(rows, split, concat):
        return lax.all_to_all(
            rows, "dp", split_axis=split, concat_axis=concat, tiled=True, axis_index_groups=token_groups
        )

    def expert_weight(shard):
        whole = exchange(shard, 1, 0)
        if groups_count > 1:
            whole = lax.all_gather(whole, "dp", axis=0, tiled=True, axis_index_groups=expert_groups)
        return whole[:, 0]

    def expert_weight_grad(grad):
        if groups_count > 1:
            grad = lax.psum_scatter(
                grad, "dp", scatter_dimension=0, tiled=True, axis_index_groups=expert_groups
            )
        return exchange(grad.astype(bf16)[:, None, :], 0, 1)

    def body(
        tokens, starts, routes, gain_one, query_key_value_weight, w_out,
        gain_two, w_router, w_gate_up, w_down, cotangent,
    ):
        count = tokens.shape[1]
        seq_rank = lax.axis_index("seq")
        expert_rank = lax.axis_index("dp") % EXPERTS
        query_columns = QUERY_HEADS * HEAD_SIZE
        key_columns = KEY_VALUE_HEADS * HEAD_SIZE
        group = QUERY_HEADS // KEY_VALUE_HEADS
        forward_pair, back_pair = [(0, 1)], [(1, 0)]

        tokens_before = lax.ppermute(tokens[0], "seq", forward_pair)
        starts_before = lax.ppermute(starts, "seq", forward_pair)
        gather = lambda value: lax.all_gather(value, "dp", axis=0, tiled=True)
        qkv_weight = gather(query_key_value_weight)
        out_weight = gather(w_out)
        router_weight = gather(w_router)
        gain_a = gather(gain_one).astype(f32)
        gain_b = gather(gain_two).astype(f32)
        gate_up_weight = expert_weight(w_gate_up)
        down_weight = expert_weight(w_down)
        grad_all = token_gather(cotangent[0])

        token_rows = tokens[0].astype(f32)
        grad_output = cotangent[0].astype(f32)
        both = 2 * count
        index = jnp.arange(both, dtype=jnp.int32)
        flags = jnp.concatenate([starts_before[0], starts[0]])
        begins = (flags > 0) | (index == jnp.where(seq_rank == 0, count, 0))
        last_begin = jnp.max(
            jnp.where(begins[None, :] & (index[None, :] <= index[:, None]), index[None, :], 0), axis=1
        )
        cosine_all, sine_all = rope_tables(index - last_begin)
        cosine, sine = cosine_all[count:], sine_all[count:]

        rows_all = jnp.concatenate([tokens_before.astype(f32), token_rows], 0)
        normed_all = (rows_all * inverse_rms(rows_all) * gain_a).astype(bf16)
        normed_one = normed_all[count:]
        projected_q = jnp.dot(normed_one, qkv_weight[:, :query_columns], preferred_element_type=f32)
        projected_kv = jnp.dot(normed_all, qkv_weight[:, query_columns:], preferred_element_type=f32)
        queries = rotary_apply(
            projected_q.reshape(count, QUERY_HEADS, HEAD_SIZE), cosine, sine
        ).astype(bf16).reshape(count, KEY_VALUE_HEADS, group, HEAD_SIZE)
        keys = rotary_apply(
            projected_kv[:, :key_columns].reshape(both, KEY_VALUE_HEADS, HEAD_SIZE), cosine_all, sine_all
        ).astype(bf16)
        values = projected_kv[:, key_columns:].astype(bf16).reshape(both, KEY_VALUE_HEADS, HEAD_SIZE)

        scale = HEAD_SIZE ** (-0.5)
        allowed = (index[None, :] <= index[count:, None]) & (index[None, :] >= last_begin[count:, None])
        scores = jnp.einsum("qgrd,kgd->grqk", queries, keys, preferred_element_type=f32) * scale
        scores = jnp.where(allowed[None, None], scores, masked_score)
        top = jnp.max(scores, axis=-1, keepdims=True)
        exps = jnp.exp(scores - top)
        probs = exps / jnp.sum(exps, axis=-1, keepdims=True)
        probs_low = probs.astype(bf16)
        attended = jnp.einsum(
            "grqk,kgd->qgrd", probs_low, values, preferred_element_type=f32
        ).reshape(count, query_columns).astype(bf16)
        hidden = token_rows + jnp.dot(attended, out_weight, preferred_element_type=f32)
        normed_two = (hidden * inverse_rms(hidden) * gain_b).astype(bf16)
        logits = jnp.dot(normed_two, router_weight, preferred_element_type=f32)
        expert_ids = jnp.arange(EXPERTS, dtype=jnp.int32)
        chosen = jnp.any(routes[0][:, :, None] == expert_ids[None, None, :], axis=1)
        gates = jax.nn.softmax(jnp.where(chosen, logits, -jnp.inf), axis=-1)

        rows_in = token_gather(normed_two)
        gates_all = token_gather(gates)
        gate = lax.dynamic_slice_in_dim(gates_all, expert_rank, 1, axis=1)
        gate_up = jnp.dot(rows_in, gate_up_weight, preferred_element_type=f32)
        gate_part, up_part = gate_up[:, :F], gate_up[:, F:]
        sigmoid = jax.nn.sigmoid(gate_part)
        silu = gate_part * sigmoid
        act = (silu * up_part).astype(bf16)
        expert_out = jnp.dot(act, down_weight, preferred_element_type=f32)
        grad_all_wide = grad_all.astype(f32)
        gate_grad_part = jnp.sum(expert_out * grad_all_wide, axis=-1, keepdims=True)
        mixed_part = (gate * expert_out).astype(bf16)
        expert_grad = (gate * grad_all_wide).astype(bf16)
        act_grad = lax.dot_general(
            expert_grad, down_weight, (((1,), (1,)), ((), ())), preferred_element_type=f32
        )
        gate_up_grad = jnp.concatenate(
            [act_grad * up_part * (sigmoid * (1.0 + gate_part * (1.0 - sigmoid))), act_grad * silu], -1
        ).astype(bf16)
        normed_part = lax.dot_general(
            gate_up_grad, gate_up_weight, (((1,), (1,)), ((), ())), preferred_element_type=f32
        ).astype(bf16)
        over_rows = (((0,), (0,)), ((), ()))
        down_wgrad = lax.dot_general(act, expert_grad, over_rows, preferred_element_type=f32)
        gate_up_wgrad = lax.dot_general(rows_in, gate_up_grad, over_rows, preferred_element_type=f32)
        normed_grad = token_scatter(normed_part).astype(f32)
        gate_grad = exchange(gate_grad_part, 0, 1)
        mixed = token_scatter(mixed_part).astype(f32)

        output = (hidden + mixed).astype(bf16)[None]
        stat_sums = jnp.stack([jnp.sum(hidden * hidden), jnp.sum(mixed * mixed)])
        weighted = jnp.where(chosen, gates * gate_grad, 0.0)
        logits_grad = weighted - gates * jnp.sum(weighted, axis=-1, keepdims=True)
        router_wide = router_weight.astype(f32)
        normed_grad = normed_grad + jnp.dot(logits_grad, router_wide.T, precision=highest)
        router_wgrad = jnp.dot(normed_two.astype(f32).T, logits_grad, precision=highest)
        hidden_branch, gain_two_grad = norm_back(hidden, gain_b, normed_grad)
        hidden_grad = grad_output + hidden_branch
        branch_low = hidden_grad.astype(bf16)
        out_wgrad = lax.dot_general(attended, branch_low, over_rows, preferred_element_type=f32)
        attended_grad = lax.dot_general(
            branch_low, out_weight, (((1,), (1,)), ((), ())), preferred_element_type=f32
        ).astype(bf16).reshape(count, KEY_VALUE_HEADS, group, HEAD_SIZE)

        prob_grad = jnp.einsum("qgrd,kgd->grqk", attended_grad, values, preferred_element_type=f32)
        delta = jnp.sum(probs * prob_grad, axis=-1, keepdims=True)
        score_grad = (probs * (prob_grad - delta)).astype(bf16)
        query_grad = (
            jnp.einsum("grqk,kgd->qgrd", score_grad, keys, preferred_element_type=f32) * scale
        ).reshape(count, QUERY_HEADS, HEAD_SIZE)
        key_grad = (
            jnp.einsum("grqk,qgrd->kgd", score_grad, queries, preferred_element_type=f32) * scale
        ).reshape(both, key_columns)
        value_grad = jnp.einsum(
            "grqk,qgrd->kgd", probs_low, attended_grad, preferred_element_type=f32
        ).reshape(both, key_columns)
        kv_grad = jnp.concatenate([key_grad, value_grad], 1)
        kv_back = lax.ppermute(kv_grad[:count].astype(bf16), "seq", back_pair)
        kv_grad = (kv_grad[count:] + kv_back.astype(f32)).astype(bf16).astype(f32)
        query_grad = query_grad.astype(bf16).astype(f32)
        query_back = unrotate(query_grad, cosine, sine).reshape(count, query_columns)
        key_back = unrotate(
            kv_grad[:, :key_columns].reshape(count, KEY_VALUE_HEADS, HEAD_SIZE), cosine, sine
        ).reshape(count, key_columns)
        projected_grad = jnp.concatenate([query_back, key_back, kv_grad[:, key_columns:]], 1).astype(bf16)
        qkv_wgrad = lax.dot_general(normed_one, projected_grad, over_rows, preferred_element_type=f32)
        normed_one_grad = lax.dot_general(
            projected_grad, qkv_weight, (((1,), (1,)), ((), ())), preferred_element_type=f32
        )
        rows_branch, gain_one_grad = norm_back(token_rows, gain_a, normed_one_grad)
        input_grad = (hidden_grad + rows_branch).astype(bf16)[None]

        scatter = lambda value: lax.psum_scatter(value, "dp", scatter_dimension=0, tiled=True)
        shards = (
            scatter(gain_one_grad),
            scatter(qkv_wgrad.astype(bf16)),
            scatter(out_wgrad.astype(bf16)),
            scatter(gain_two_grad),
            scatter(router_wgrad),
            expert_weight_grad(gate_up_wgrad),
            expert_weight_grad(down_wgrad),
            stat_sums,
        )
        summed = [lax.psum(part.astype(bf16), "seq").astype(f32) for part in shards]
        stream_rms = jnp.sqrt(summed[7] / (both * MODEL_WIDTH)).reshape(1, 2)
        return (output, input_grad, *summed[:7], stream_rms)

    return body


def solution(mesh):
    placed = (
        P("dp", "seq", None),
        P("dp", "seq"),
        P("dp", "seq", None),
        P("dp"),
        P("dp", None),
        P("dp", None),
        P("dp"),
        P("dp", None),
        P("dp", None, None),
        P("dp", None, None),
        P("dp", "seq", None),
    )
    return jax.shard_map(
        make_body(mesh.shape["dp"]),
        mesh=mesh,
        in_specs=placed,
        out_specs=(
            P("dp", "seq", None),
            P("dp", "seq", None),
            P("dp"),
            P("dp", None),
            P("dp", None),
            P("dp"),
            P("dp", None),
            P("dp", None, None),
            P("dp", None, None),
            P("dp", None),
        ),
        check_vma=False,
    )
```

```python
import functools

import jax
import jax.numpy as jnp
from jax import lax
from jax.experimental import pallas as pl
from jax.experimental.pallas import tpu as pltpu
from jax.sharding import PartitionSpec as P

MODEL_WIDTH = 1024
QUERY_HEADS = 16
KEY_VALUE_HEADS = 8
HEAD_SIZE = 64
F = 512
EXPERTS = 16
TOPK = 8
RANKS = 8
GROUP = 16

epsilon = 1e-06
rope_base = 10000.0
highest = lax.Precision.HIGHEST
masked_score = -1e30
f32 = jnp.float32
bf16 = jnp.bfloat16
MESH = pl.DeviceIdType.MESH

LINKS = ((8, 4, 2), (4, 2, 8), (2, 8, 4))


def flip(value, bit):
    return value + bit * (1 - 2 * ((value // bit) % 2))


def flip_mask(value, mask):
    for bit in (1, 2, 4, 8):
        if mask & bit:
            value = flip(value, bit)
    return value


def subsets(bits):
    out = [0]
    for bit in bits:
        out = out + [m | bit for m in out]
    return out


def row_parts(rows):
    first = (rows // 3 + 15) // 16 * 16
    second = (rows - first) // 2 // 16 * 16
    return ((0, first), (first, second), (first + second, rows - first - second))


def my_place():
    seq = lax.axis_index("seq")
    dp = lax.axis_index("dp")
    rank = seq * RANKS + dp % RANKS

    def peer(bit):
        if bit == 8:
            return {"seq": 1 - seq, "dp": dp}
        return {"seq": seq, "dp": flip(dp, bit)}

    return rank, peer


def meet(peer):
    barrier = pltpu.get_barrier_semaphore()
    for bit in (1, 2, 4, 8):
        pl.semaphore_signal(barrier, inc=1, device_id=peer(bit), device_id_type=MESH)
    pl.semaphore_wait(barrier, 4)


def gather_kernel(count, *refs):
    ins, outs = refs[:count], refs[count : 2 * count]
    send, recv, send_core, recv_core, local = refs[2 * count :]
    rank, peer = my_place()
    own = [
        pltpu.make_async_copy(ins[a], outs[a].at[rank], local.at[a]) for a in range(count)
    ]
    for copy in own:
        copy.start()
    meet(peer)
    parts = [row_parts(ref.shape[0]) for ref in ins]

    def remote(a, p, mask, bit, sems, index):
        start, size = parts[a][p]
        rows = pl.ds(start, size)
        shard = flip_mask(rank, mask)
        src = ins[a].at[rows] if mask == 0 else outs[a].at[shard, rows]
        return pltpu.make_async_remote_copy(
            src_ref=src,
            dst_ref=outs[a].at[shard, rows],
            send_sem=sems[0].at[a, p, index],
            recv_sem=sems[1].at[a, p, index],
            device_id=peer(bit),
            device_id_type=MESH,
        )

    started = []
    live = {}
    for step in range(4):
        for p in range(3):
            for a in range(count):
                if parts[a][p][1] == 0:
                    continue
                order = LINKS[p]
                if step > 0:
                    for copy in live.pop((a, p)):
                        copy.wait_recv()
                if step < 3:
                    now = []
                    for index, mask in enumerate(subsets(order[:step])):
                        copy = remote(a, p, mask, order[step], (send, recv), 2**step - 1 + index)
                        copy.start()
                        now.append(copy)
                        started.append(copy)
                    live[(a, p)] = now
                fresh = [0] if step == 0 else [m | order[step - 1] for m in subsets(order[: step - 1])]
                base = 0 if step == 0 else 2 ** (step - 1)
                for index, mask in enumerate(fresh):
                    copy = remote(a, p, mask, 1, (send_core, recv_core), base + index)
                    copy.start()
                    live.setdefault("core", []).append(copy)
    for copy in live["core"]:
        copy.wait()
    for copy in started:
        copy.wait_send()
    for copy in own:
        copy.wait()


def group_gather(collective_id, *arrays):
    count = len(arrays)
    return pl.pallas_call(
        functools.partial(gather_kernel, count),
        out_shape=[jax.ShapeDtypeStruct((GROUP,) + a.shape, a.dtype) for a in arrays],
        in_specs=[pl.BlockSpec(memory_space=pltpu.VMEM)] * count,
        out_specs=[pl.BlockSpec(memory_space=pl.ANY)] * count,
        scratch_shapes=[
            pltpu.SemaphoreType.DMA((count, 3, 7)),
            pltpu.SemaphoreType.DMA((count, 3, 7)),
            pltpu.SemaphoreType.DMA((count, 3, 8)),
            pltpu.SemaphoreType.DMA((count, 3, 8)),
            pltpu.SemaphoreType.DMA((count,)),
        ],
        compiler_params=pltpu.CompilerParams(collective_id=collective_id, has_side_effects=True),
        name="group_gather",
    )(*arrays)


def add_rows(target, source, start, size):
    def step(i, carry):
        rows = pl.ds(pl.multiple_of(start + i * 16, 16), 16)
        target[rows] = (target[rows].astype(f32) + source[rows].astype(f32)).astype(target.dtype)
        return carry

    lax.fori_loop(0, size // 16, step, 0)


def reduce_kernel(
    mixed_ref, normed_ref, gate_ref, mixed_out, normed_out, gate_out,
    total, got0, got1, got2, got3, sems, gate_sems, local, own_gate,
):
    rank, peer = my_place()
    chip = rank // 2
    core = rank % 2
    parts = row_parts(mixed_ref.shape[1])
    ins = (mixed_ref, normed_ref)
    outs = (mixed_out, normed_out)
    loads = []
    for t in range(2):
        for c in range(8):
            copy = pltpu.make_async_copy(ins[t].at[2 * c + core], total.at[t, c], local.at[t, c])
            copy.start()
            loads.append(copy)
    barrier = pltpu.get_barrier_semaphore()
    seq = lax.axis_index("seq")
    dp = lax.axis_index("dp")
    everyone = [
        {"seq": 1 - seq if mask & 8 else seq, "dp": flip_mask(dp, mask & 7)} for mask in range(1, 16)
    ]
    for there in everyone:
        pl.semaphore_signal(barrier, inc=1, device_id=there, device_id_type=MESH)
    pl.semaphore_wait(barrier, 15)
    gates = []
    keep = pltpu.make_async_copy(gate_ref.at[rank], gate_out.at[rank], own_gate)
    keep.start()
    for mask, there in zip(range(1, 16), everyone):
        copy = pltpu.make_async_remote_copy(
            src_ref=gate_ref.at[flip_mask(rank, mask)],
            dst_ref=gate_out.at[rank],
            send_sem=gate_sems.at[0, mask],
            recv_sem=gate_sems.at[1, mask],
            device_id=there,
            device_id_type=MESH,
        )
        copy.start()
        gates.append(copy)

    started = []
    live = {}

    def send(t, p, stage, index, src, dst, bit):
        copy = pltpu.make_async_remote_copy(
            src_ref=src,
            dst_ref=dst,
            send_sem=sems.at[0, t, p, stage, index],
            recv_sem=sems.at[1, t, p, stage, index],
            device_id=peer(bit),
            device_id_type=MESH,
        )
        copy.start()
        started.append(copy)
        live.setdefault((t, p), []).append(copy)

    def chip_of(mask):
        return flip_mask(rank, mask) // 2

    for p in range(3):
        for t in range(2):
            rows = pl.ds(*parts[p])
            for c in range(8):
                send(
                    t, p, 0, c, ins[t].at[2 * c + 1 - core, rows], got0.at[t, c, rows], 1
                )
    for copy in loads:
        copy.wait()
    got = (got1, got2, got3)
    for stage in range(4):
        for p in range(3):
            for t in range(2):
                order = LINKS[p]
                rows = pl.ds(*parts[p])
                for copy in live.pop((t, p)):
                    copy.wait_recv()
                if stage == 0:

                    def over_chips(c, carry, t=t, p=p):
                        add_rows(total.at[t, c], got0.at[t, c], *parts[p])
                        return carry

                    lax.fori_loop(0, 8, over_chips, 0)
                else:
                    for index, mask in enumerate(subsets(order[stage:])):
                        if stage == 3:
                            outs[t][rows] = total[t, chip, rows].astype(f32) + got3[t, 0, rows].astype(f32)
                        else:
                            add_rows(
                                total.at[t, chip_of(mask)], got[stage - 1].at[t, index], *parts[p]
                            )
                if stage < 3:
                    for index, mask in enumerate(subsets(order[stage + 1 :])):
                        send(
                            t, p, stage + 1, index,
                            total.at[t, chip_of(mask | order[stage]), rows],
                            got[stage].at[t, index, rows],
                            order[stage],
                        )
    for copy in started:
        copy.wait_send()
    for copy in gates:
        copy.wait()
    keep.wait()


def group_reduce(collective_id, mixed, normed, gate_grad):
    rows, width = mixed.shape[1:]
    return pl.pallas_call(
        reduce_kernel,
        out_shape=[
            jax.ShapeDtypeStruct((rows, width), f32),
            jax.ShapeDtypeStruct((rows, width), f32),
            jax.ShapeDtypeStruct(gate_grad.shape, gate_grad.dtype),
        ],
        in_specs=[pl.BlockSpec(memory_space=pl.ANY)] * 3,
        out_specs=[
            pl.BlockSpec(memory_space=pltpu.VMEM),
            pl.BlockSpec(memory_space=pltpu.VMEM),
            pl.BlockSpec(memory_space=pl.ANY),
        ],
        scratch_shapes=[
            pltpu.VMEM((2, 8, rows, width), bf16),
            pltpu.VMEM((2, 8, rows, width), bf16),
            pltpu.VMEM((2, 4, rows, width), bf16),
            pltpu.VMEM((2, 2, rows, width), bf16),
            pltpu.VMEM((2, 1, rows, width), bf16),
            pltpu.SemaphoreType.DMA((2, 2, 3, 4, 8)),
            pltpu.SemaphoreType.DMA((2, 16)),
            pltpu.SemaphoreType.DMA((2, 8)),
            pltpu.SemaphoreType.DMA(()),
        ],
        compiler_params=pltpu.CompilerParams(
            collective_id=collective_id, has_side_effects=True, vmem_limit_bytes=48 * 2**20
        ),
        name="group_reduce",
    )(mixed, normed, gate_grad)


def expert_kernel(
    rows_ref, grad_ref, gate_ref, gate_up_ref, down_ref,
    mixed_ref, normed_ref, gate_grad_ref, gate_up_out, down_out,
    gate_up_sum, down_sum,
):
    step = pl.program_id(0)
    shards, each, width = rows_ref.shape
    count = shards * each
    rows = rows_ref[...].reshape(count, width)
    grad = grad_ref[...].reshape(count, width).astype(f32)
    gate = jnp.concatenate(
        [jnp.broadcast_to(gate_ref[i], (128, each)).T[:, :1] for i in range(shards)], 0
    )
    down = down_ref[...]
    gate_up_weight = gate_up_ref[...]
    gate_up = jnp.dot(rows, gate_up_weight, preferred_element_type=f32)
    gate_part, up_part = gate_up[:, :F], gate_up[:, F:]
    sigmoid = 1.0 / (1.0 + jnp.exp(-gate_part))
    silu = gate_part * sigmoid
    act = (silu * up_part).astype(bf16)
    out = jnp.dot(act, down, preferred_element_type=f32)
    inner = jnp.sum(out * grad, axis=-1, keepdims=True)
    for i in range(shards):
        line = jnp.broadcast_to(inner[i * each : (i + 1) * each], (each, 128)).T
        gate_grad_ref[i] = line[:8]
    mixed_ref[...] = (gate * out).astype(bf16).reshape(shards, each, width)
    expert_grad = (gate * grad).astype(bf16)
    across = (((1,), (1,)), ((), ()))
    over_rows = (((0,), (0,)), ((), ()))
    act_grad = lax.dot_general(expert_grad, down, across, preferred_element_type=f32)
    gate_up_grad = jnp.concatenate(
        [act_grad * up_part * (sigmoid * (1.0 + gate_part * (1.0 - sigmoid))), act_grad * silu], -1
    ).astype(bf16)
    normed_ref[...] = (
        lax.dot_general(gate_up_grad, gate_up_weight, across, preferred_element_type=f32)
        .astype(bf16)
        .reshape(shards, each, width)
    )

    @pl.when(step == 0)
    def _():
        gate_up_sum[...] = jnp.zeros_like(gate_up_sum)
        down_sum[...] = jnp.zeros_like(down_sum)

    down_sum[...] += lax.dot_general(act, expert_grad, over_rows, preferred_element_type=f32)
    gate_up_sum[...] += lax.dot_general(rows, gate_up_grad, over_rows, preferred_element_type=f32)

    @pl.when(step == pl.num_programs(0) - 1)
    def _():
        gate_up_out[...] = gate_up_sum[...].astype(bf16)
        down_out[...] = down_sum[...].astype(bf16)


def expert_layer(rows, grad, gate, gate_up_weight, down_weight):
    each, width = rows.shape[1:]
    shards = 2
    tile = pl.BlockSpec((shards, each, width), lambda i: (i, 0, 0))
    whole = lambda shape: pl.BlockSpec(shape, lambda i: (0, 0))
    return pl.pallas_call(
        expert_kernel,
        grid=(GROUP // shards,),
        out_shape=[
            jax.ShapeDtypeStruct(rows.shape, bf16),
            jax.ShapeDtypeStruct(rows.shape, bf16),
            jax.ShapeDtypeStruct((GROUP, 8, each), f32),
            jax.ShapeDtypeStruct(gate_up_weight.shape, bf16),
            jax.ShapeDtypeStruct(down_weight.shape, bf16),
        ],
        in_specs=[
            tile,
            tile,
            pl.BlockSpec((shards, 1, each), lambda i: (i, 0, 0)),
            whole(gate_up_weight.shape),
            whole(down_weight.shape),
        ],
        out_specs=[
            tile,
            tile,
            pl.BlockSpec((shards, 8, each), lambda i: (i, 0, 0)),
            whole(gate_up_weight.shape),
            whole(down_weight.shape),
        ],
        scratch_shapes=[
            pltpu.VMEM(gate_up_weight.shape, f32),
            pltpu.VMEM(down_weight.shape, f32),
        ],
        compiler_params=pltpu.CompilerParams(vmem_limit_bytes=56 * 2**20),
        name="expert_layer",
    )(rows, grad, gate, gate_up_weight, down_weight)


def inverse_rms(rows):
    return lax.rsqrt(jnp.mean(rows * rows, axis=-1, keepdims=True) + epsilon)


def norm_back(rows, gain_row, upstream):
    inverse = inverse_rms(rows)
    gain_grad = jnp.sum(upstream * rows * inverse, axis=0)
    scaled = upstream * gain_row
    rows_grad = inverse * scaled - rows * inverse**3 * jnp.mean(scaled * rows, axis=-1, keepdims=True)
    return rows_grad, gain_grad


def rope_tables(positions):
    half = HEAD_SIZE // 2
    frequency = rope_base ** (-(jnp.arange(half, dtype=f32) * 2.0) / HEAD_SIZE)
    angles = positions.astype(f32)[:, None] * frequency[None, :]
    cosine, sine = jnp.cos(angles), jnp.sin(angles)
    return jnp.concatenate([cosine, cosine], 1), jnp.concatenate([sine, sine], 1)


def rotary_apply(rows, cosine, sine):
    half = HEAD_SIZE // 2
    turned = jnp.concatenate([-rows[..., half:], rows[..., :half]], -1)
    return rows * cosine[:, None, :] + turned * sine[:, None, :]


def unrotate(rows, cosine, sine):
    half = HEAD_SIZE // 2
    scaled = rows * sine[:, None, :]
    back = jnp.concatenate([scaled[..., half:], -scaled[..., :half]], -1)
    return rows * cosine[:, None, :] + back


def make_body(n_dp):
    groups_count = n_dp // RANKS
    inside = [[g * RANKS + j for j in range(RANKS)] for g in range(groups_count)]
    between = [[g * RANKS + j for g in range(groups_count)] for j in range(RANKS)]
    half_experts = EXPERTS // 2

    def expert_weight(shard, seq_rank):
        mine = lax.dynamic_slice_in_dim(shard, seq_rank * half_experts, half_experts, axis=1)
        mine = jnp.swapaxes(mine, 0, 1)
        mine = lax.all_to_all(
            mine, "dp", split_axis=0, concat_axis=0, tiled=True, axis_index_groups=inside
        )
        mine = mine.reshape(-1, shard.shape[2])
        return lax.all_gather(mine, "dp", axis=0, tiled=True, axis_index_groups=between)

    def expert_weight_grad(grad):
        grad = lax.psum_scatter(
            grad, "dp", scatter_dimension=0, tiled=True, axis_index_groups=between
        )
        grad = grad.reshape(RANKS, -1, grad.shape[1])
        grad = lax.all_to_all(
            grad, "dp", split_axis=0, concat_axis=0, tiled=True, axis_index_groups=inside
        )
        grad = lax.all_gather(grad, "seq", axis=0, tiled=True)
        return jnp.swapaxes(grad, 0, 1).astype(f32)

    def body(
        tokens, starts, routes, gain_one, query_key_value_weight, w_out,
        gain_two, w_router, w_gate_up, w_down, cotangent,
    ):
        count = tokens.shape[1]
        seq_rank = lax.axis_index("seq")
        expert = seq_rank * RANKS + lax.axis_index("dp") % RANKS
        query_columns = QUERY_HEADS * HEAD_SIZE
        key_columns = KEY_VALUE_HEADS * HEAD_SIZE
        group = QUERY_HEADS // KEY_VALUE_HEADS
        forward_pair, back_pair = [(0, 1)], [(1, 0)]

        tokens_before = lax.ppermute(tokens[0], "seq", forward_pair)
        starts_before = lax.ppermute(starts, "seq", forward_pair)
        gather = lambda value: lax.all_gather(value, "dp", axis=0, tiled=True)
        qkv_weight = gather(query_key_value_weight)
        out_weight = gather(w_out)
        small = gather(jnp.concatenate([w_router, gain_one[:, None], gain_two[:, None]], 1))
        router_weight = small[:, :EXPERTS]
        gain_a = small[:, EXPERTS].astype(f32)
        gain_b = small[:, EXPERTS + 1].astype(f32)
        gate_up_weight = expert_weight(w_gate_up, seq_rank)
        down_weight = expert_weight(w_down, seq_rank)
        (grad_all,) = group_gather(0, cotangent[0])

        token_rows = tokens[0].astype(f32)
        grad_output = cotangent[0].astype(f32)
        both = 2 * count
        index = jnp.arange(both, dtype=jnp.int32)
        flags = jnp.concatenate([starts_before[0], starts[0]])
        begins = (flags > 0) | (index == jnp.where(seq_rank == 0, count, 0))
        last_begin = jnp.max(
            jnp.where(begins[None, :] & (index[None, :] <= index[:, None]), index[None, :], 0), axis=1
        )
        cosine_all, sine_all = rope_tables(index - last_begin)
        cosine, sine = cosine_all[count:], sine_all[count:]

        rows_all = jnp.concatenate([tokens_before.astype(f32), token_rows], 0)
        normed_all = (rows_all * inverse_rms(rows_all) * gain_a).astype(bf16)
        normed_one = normed_all[count:]
        projected_q = jnp.dot(normed_one, qkv_weight[:, :query_columns], preferred_element_type=f32)
        projected_kv = jnp.dot(normed_all, qkv_weight[:, query_columns:], preferred_element_type=f32)
        queries = rotary_apply(
            projected_q.reshape(count, QUERY_HEADS, HEAD_SIZE), cosine, sine
        ).astype(bf16).reshape(count, KEY_VALUE_HEADS, group, HEAD_SIZE)
        keys = rotary_apply(
            projected_kv[:, :key_columns].reshape(both, KEY_VALUE_HEADS, HEAD_SIZE), cosine_all, sine_all
        ).astype(bf16)
        values = projected_kv[:, key_columns:].astype(bf16).reshape(both, KEY_VALUE_HEADS, HEAD_SIZE)

        scale = HEAD_SIZE ** (-0.5)
        allowed = (index[None, :] <= index[count:, None]) & (index[None, :] >= last_begin[count:, None])
        scores = jnp.einsum("qgrd,kgd->grqk", queries, keys, preferred_element_type=f32) * scale
        scores = jnp.where(allowed[None, None], scores, masked_score)
        top = jnp.max(scores, axis=-1, keepdims=True)
        exps = jnp.exp(scores - top)
        probs = exps / jnp.sum(exps, axis=-1, keepdims=True)
        probs_low = probs.astype(bf16)
        attended = jnp.einsum(
            "grqk,kgd->qgrd", probs_low, values, preferred_element_type=f32
        ).reshape(count, query_columns).astype(bf16)
        hidden = token_rows + jnp.dot(attended, out_weight, preferred_element_type=f32)
        normed_two = (hidden * inverse_rms(hidden) * gain_b).astype(bf16)
        logits = jnp.dot(normed_two, router_weight, preferred_element_type=f32)
        expert_ids = jnp.arange(EXPERTS, dtype=jnp.int32)
        chosen = jnp.any(routes[0][:, :, None] == expert_ids[None, None, :], axis=1)
        gates = jax.nn.softmax(jnp.where(chosen, logits, -jnp.inf), axis=-1)

        rows_in, gates_all = group_gather(1, normed_two, gates.T)
        gate = lax.dynamic_slice_in_dim(gates_all, expert, 1, axis=1)
        mixed_part, normed_part, gate_grad_part, gate_up_wgrad, down_wgrad = expert_layer(
            rows_in, grad_all, gate, gate_up_weight, down_weight
        )
        mixed, normed_grad, gate_grad = group_reduce(2, mixed_part, normed_part, gate_grad_part)
        gate_grad = gate_grad[:, 0].T

        over_rows = (((0,), (0,)), ((), ()))
        output = (hidden + mixed).astype(bf16)[None]
        stat_sums = jnp.stack([jnp.sum(hidden * hidden), jnp.sum(mixed * mixed)])
        weighted = jnp.where(chosen, gates * gate_grad, 0.0)
        logits_grad = weighted - gates * jnp.sum(weighted, axis=-1, keepdims=True)
        router_wide = router_weight.astype(f32)
        normed_grad = normed_grad + jnp.dot(logits_grad, router_wide.T, precision=highest)
        router_wgrad = jnp.dot(normed_two.astype(f32).T, logits_grad, precision=highest)
        hidden_branch, gain_two_grad = norm_back(hidden, gain_b, normed_grad)
        hidden_grad = grad_output + hidden_branch
        branch_low = hidden_grad.astype(bf16)
        out_wgrad = lax.dot_general(attended, branch_low, over_rows, preferred_element_type=f32)
        attended_grad = lax.dot_general(
            branch_low, out_weight, (((1,), (1,)), ((), ())), preferred_element_type=f32
        ).astype(bf16).reshape(count, KEY_VALUE_HEADS, group, HEAD_SIZE)

        prob_grad = jnp.einsum("qgrd,kgd->grqk", attended_grad, values, preferred_element_type=f32)
        delta = jnp.sum(probs * prob_grad, axis=-1, keepdims=True)
        score_grad = (probs * (prob_grad - delta)).astype(bf16)
        query_grad = (
            jnp.einsum("grqk,kgd->qgrd", score_grad, keys, preferred_element_type=f32) * scale
        ).reshape(count, QUERY_HEADS, HEAD_SIZE)
        key_grad = (
            jnp.einsum("grqk,qgrd->kgd", score_grad, queries, preferred_element_type=f32) * scale
        ).reshape(both, key_columns)
        value_grad = jnp.einsum(
            "grqk,qgrd->kgd", probs_low, attended_grad, preferred_element_type=f32
        ).reshape(both, key_columns)
        kv_grad = jnp.concatenate([key_grad, value_grad], 1)
        kv_back = lax.ppermute(kv_grad[:count].astype(bf16), "seq", back_pair)
        kv_grad = (kv_grad[count:] + kv_back.astype(f32)).astype(bf16).astype(f32)
        query_grad = query_grad.astype(bf16).astype(f32)
        query_back = unrotate(query_grad, cosine, sine).reshape(count, query_columns)
        key_back = unrotate(
            kv_grad[:, :key_columns].reshape(count, KEY_VALUE_HEADS, HEAD_SIZE), cosine, sine
        ).reshape(count, key_columns)
        projected_grad = jnp.concatenate([query_back, key_back, kv_grad[:, key_columns:]], 1).astype(bf16)
        qkv_wgrad = lax.dot_general(normed_one, projected_grad, over_rows, preferred_element_type=f32)
        normed_one_grad = lax.dot_general(
            projected_grad, qkv_weight, (((1,), (1,)), ((), ())), preferred_element_type=f32
        )
        rows_branch, gain_one_grad = norm_back(token_rows, gain_a, normed_one_grad)
        input_grad = (hidden_grad + rows_branch).astype(bf16)[None]

        scatter = lambda value: lax.psum_scatter(value, "dp", scatter_dimension=0, tiled=True)
        little = jnp.concatenate([router_wgrad, gain_one_grad[:, None], gain_two_grad[:, None]], 1)
        shards = (scatter(qkv_wgrad.astype(bf16)), scatter(out_wgrad.astype(bf16)), scatter(little), stat_sums)
        summed = [lax.psum(part.astype(bf16), "seq").astype(f32) for part in shards]
        stream_rms = jnp.sqrt(summed[3] / (both * MODEL_WIDTH)).reshape(1, 2)
        return (
            output,
            input_grad,
            summed[2][:, EXPERTS],
            summed[0],
            summed[1],
            summed[2][:, EXPERTS + 1],
            summed[2][:, :EXPERTS],
            expert_weight_grad(gate_up_wgrad),
            expert_weight_grad(down_wgrad),
            stream_rms,
        )

    return body


def solution(mesh):
    placed = (
        P("dp", "seq", None),
        P("dp", "seq"),
        P("dp", "seq", None),
        P("dp"),
        P("dp", None),
        P("dp", None),
        P("dp"),
        P("dp", None),
        P("dp", None, None),
        P("dp", None, None),
        P("dp", "seq", None),
    )
    return jax.shard_map(
        make_body(mesh.shape["dp"]),
        mesh=mesh,
        in_specs=placed,
        out_specs=(
            P("dp", "seq", None),
            P("dp", "seq", None),
            P("dp"),
            P("dp", None),
            P("dp", None),
            P("dp"),
            P("dp", None),
            P("dp", None, None),
            P("dp", None, None),
            P("dp", None),
        ),
        check_vma=False,
    )
```

```python
import functools

import jax
import jax.numpy as jnp
from jax import lax
from jax.experimental import pallas as pl
from jax.experimental.pallas import tpu as pltpu
from jax.sharding import PartitionSpec as P

MODEL_WIDTH = 1024
QUERY_HEADS = 16
KEY_VALUE_HEADS = 8
HEAD_SIZE = 64
F = 512
EXPERTS = 16
TOPK = 8
RANKS = 8
GROUP = 16

epsilon = 1e-06
rope_base = 10000.0
highest = lax.Precision.HIGHEST
masked_score = -1e30
f32 = jnp.float32
bf16 = jnp.bfloat16
MESH = pl.DeviceIdType.MESH

LINKS = ((8, 4, 2), (4, 2, 8), (2, 8, 4))


def flip(value, bit):
    return value + bit * (1 - 2 * ((value // bit) % 2))


def flip_mask(value, mask):
    for bit in (1, 2, 4, 8):
        if mask & bit:
            value = flip(value, bit)
    return value


def subsets(bits):
    out = [0]
    for bit in bits:
        out = out + [m | bit for m in out]
    return out


def row_parts(rows):
    first = (rows // 3 + 15) // 16 * 16
    second = (rows - first) // 2 // 16 * 16
    return ((0, first), (first, second), (first + second, rows - first - second))


def my_place():
    seq = lax.axis_index("seq")
    dp = lax.axis_index("dp")
    rank = seq * RANKS + dp % RANKS

    def peer(bit):
        if bit == 8:
            return {"seq": 1 - seq, "dp": dp}
        return {"seq": seq, "dp": flip(dp, bit)}

    return rank, peer


def meet(peer):
    barrier = pltpu.get_barrier_semaphore()
    for bit in (1, 2, 4, 8):
        pl.semaphore_signal(barrier, inc=1, device_id=peer(bit), device_id_type=MESH)
    pl.semaphore_wait(barrier, 4)


def gather_kernel(count, *refs):
    ins, outs = refs[:count], refs[count : 2 * count]
    send, recv, send_core, recv_core, local = refs[2 * count :]
    rank, peer = my_place()
    own = [
        pltpu.make_async_copy(ins[a], outs[a].at[rank], local.at[a]) for a in range(count)
    ]
    for copy in own:
        copy.start()
    meet(peer)
    parts = [row_parts(ref.shape[0]) for ref in ins]

    def remote(a, p, mask, bit, sems, index):
        start, size = parts[a][p]
        rows = pl.ds(start, size)
        shard = flip_mask(rank, mask)
        src = ins[a].at[rows] if mask == 0 else outs[a].at[shard, rows]
        return pltpu.make_async_remote_copy(
            src_ref=src,
            dst_ref=outs[a].at[shard, rows],
            send_sem=sems[0].at[a, p, index],
            recv_sem=sems[1].at[a, p, index],
            device_id=peer(bit),
            device_id_type=MESH,
        )

    started = []
    live = {}
    for step in range(4):
        for p in range(3):
            for a in range(count):
                if parts[a][p][1] == 0:
                    continue
                order = LINKS[p]
                if step > 0:
                    for copy in live.pop((a, p)):
                        copy.wait_recv()
                if step < 3:
                    now = []
                    for index, mask in enumerate(subsets(order[:step])):
                        copy = remote(a, p, mask, order[step], (send, recv), 2**step - 1 + index)
                        copy.start()
                        now.append(copy)
                        started.append(copy)
                    live[(a, p)] = now
                fresh = [0] if step == 0 else [m | order[step - 1] for m in subsets(order[: step - 1])]
                base = 0 if step == 0 else 2 ** (step - 1)
                for index, mask in enumerate(fresh):
                    copy = remote(a, p, mask, 1, (send_core, recv_core), base + index)
                    copy.start()
                    live.setdefault("core", []).append(copy)
    for copy in live["core"]:
        copy.wait()
    for copy in started:
        copy.wait_send()
    for copy in own:
        copy.wait()


def group_gather(collective_id, *arrays):
    count = len(arrays)
    return pl.pallas_call(
        functools.partial(gather_kernel, count),
        out_shape=[jax.ShapeDtypeStruct((GROUP,) + a.shape, a.dtype) for a in arrays],
        in_specs=[pl.BlockSpec(memory_space=pltpu.VMEM)] * count,
        out_specs=[pl.BlockSpec(memory_space=pl.ANY)] * count,
        scratch_shapes=[
            pltpu.SemaphoreType.DMA((count, 3, 7)),
            pltpu.SemaphoreType.DMA((count, 3, 7)),
            pltpu.SemaphoreType.DMA((count, 3, 8)),
            pltpu.SemaphoreType.DMA((count, 3, 8)),
            pltpu.SemaphoreType.DMA((count,)),
        ],
        compiler_params=pltpu.CompilerParams(collective_id=collective_id, has_side_effects=True),
        name="group_gather",
    )(*arrays)


def add_rows(target, source, start, size):
    def step(i, carry):
        rows = pl.ds(pl.multiple_of(start + i * 16, 16), 16)
        target[rows] = (target[rows].astype(f32) + source[rows].astype(f32)).astype(target.dtype)
        return carry

    lax.fori_loop(0, size // 16, step, 0)


def reduce_kernel(
    mixed_ref, normed_ref, gate_ref, mixed_out, normed_out, gate_out,
    total, got0, got1, got2, got3, sems, gate_sems, local, own_gate,
):
    rank, peer = my_place()
    chip = rank // 2
    core = rank % 2
    parts = row_parts(mixed_ref.shape[1])
    ins = (mixed_ref, normed_ref)
    outs = (mixed_out, normed_out)
    loads = []
    for t in range(2):
        for c in range(8):
            copy = pltpu.make_async_copy(ins[t].at[2 * c + core], total.at[t, c], local.at[t, c])
            copy.start()
            loads.append(copy)
    barrier = pltpu.get_barrier_semaphore()
    seq = lax.axis_index("seq")
    dp = lax.axis_index("dp")
    everyone = [
        {"seq": 1 - seq if mask & 8 else seq, "dp": flip_mask(dp, mask & 7)} for mask in range(1, 16)
    ]
    for there in everyone:
        pl.semaphore_signal(barrier, inc=1, device_id=there, device_id_type=MESH)
    pl.semaphore_wait(barrier, 15)
    gates = []
    keep = pltpu.make_async_copy(gate_ref.at[rank], gate_out.at[rank], own_gate)
    keep.start()
    for mask, there in zip(range(1, 16), everyone):
        copy = pltpu.make_async_remote_copy(
            src_ref=gate_ref.at[flip_mask(rank, mask)],
            dst_ref=gate_out.at[rank],
            send_sem=gate_sems.at[0, mask],
            recv_sem=gate_sems.at[1, mask],
            device_id=there,
            device_id_type=MESH,
        )
        copy.start()
        gates.append(copy)

    started = []
    live = {}

    def send(t, p, stage, index, src, dst, bit):
        copy = pltpu.make_async_remote_copy(
            src_ref=src,
            dst_ref=dst,
            send_sem=sems.at[0, t, p, stage, index],
            recv_sem=sems.at[1, t, p, stage, index],
            device_id=peer(bit),
            device_id_type=MESH,
        )
        copy.start()
        started.append(copy)
        live.setdefault((t, p), []).append(copy)

    def chip_of(mask):
        return flip_mask(rank, mask) // 2

    for p in range(3):
        for t in range(2):
            rows = pl.ds(*parts[p])
            for c in range(8):
                send(
                    t, p, 0, c, ins[t].at[2 * c + 1 - core, rows], got0.at[t, c, rows], 1
                )
    for copy in loads:
        copy.wait()
    got = (got1, got2, got3)
    for stage in range(4):
        for p in range(3):
            for t in range(2):
                order = LINKS[p]
                rows = pl.ds(*parts[p])
                for copy in live.pop((t, p)):
                    copy.wait_recv()
                if stage == 0:

                    def over_chips(c, carry, t=t, p=p):
                        add_rows(total.at[t, c], got0.at[t, c], *parts[p])
                        return carry

                    lax.fori_loop(0, 8, over_chips, 0)
                else:
                    for index, mask in enumerate(subsets(order[stage:])):
                        if stage == 3:
                            outs[t][rows] = total[t, chip, rows].astype(f32) + got3[t, 0, rows].astype(f32)
                        else:
                            add_rows(
                                total.at[t, chip_of(mask)], got[stage - 1].at[t, index], *parts[p]
                            )
                if stage < 3:
                    for index, mask in enumerate(subsets(order[stage + 1 :])):
                        send(
                            t, p, stage + 1, index,
                            total.at[t, chip_of(mask | order[stage]), rows],
                            got[stage].at[t, index, rows],
                            order[stage],
                        )
    for copy in started:
        copy.wait_send()
    for copy in gates:
        copy.wait()
    keep.wait()


def group_reduce(collective_id, mixed, normed, gate_grad):
    rows, width = mixed.shape[1:]
    return pl.pallas_call(
        reduce_kernel,
        out_shape=[
            jax.ShapeDtypeStruct((rows, width), f32),
            jax.ShapeDtypeStruct((rows, width), f32),
            jax.ShapeDtypeStruct(gate_grad.shape, gate_grad.dtype),
        ],
        in_specs=[pl.BlockSpec(memory_space=pl.ANY)] * 3,
        out_specs=[
            pl.BlockSpec(memory_space=pltpu.VMEM),
            pl.BlockSpec(memory_space=pltpu.VMEM),
            pl.BlockSpec(memory_space=pl.ANY),
        ],
        scratch_shapes=[
            pltpu.VMEM((2, 8, rows, width), bf16),
            pltpu.VMEM((2, 8, rows, width), bf16),
            pltpu.VMEM((2, 4, rows, width), bf16),
            pltpu.VMEM((2, 2, rows, width), bf16),
            pltpu.VMEM((2, 1, rows, width), bf16),
            pltpu.SemaphoreType.DMA((2, 2, 3, 4, 8)),
            pltpu.SemaphoreType.DMA((2, 16)),
            pltpu.SemaphoreType.DMA((2, 8)),
            pltpu.SemaphoreType.DMA(()),
        ],
        compiler_params=pltpu.CompilerParams(
            collective_id=collective_id, has_side_effects=True, vmem_limit_bytes=48 * 2**20
        ),
        name="group_reduce",
    )(mixed, normed, gate_grad)


def column_parts(half, which):
    tiles = half // 128
    if tiles == 1:
        sizes = (1, 0, 0)
    elif which % 2 == 0:
        big = -(-tiles // 3)
        sizes = (big, big, tiles - 2 * big)
    else:
        small = tiles // 3
        sizes = (small, small, tiles - 2 * small)
    out, start = [], 0
    for size in sizes:
        out.append((start * 128, size * 128))
        start += size
    return out


def shard_view(ref, halves, a, p, rank_value):
    start, size = column_parts(halves[a], a)[p]
    offset = pl.multiple_of((rank_value // RANKS) * halves[a] + start, 128)
    return ref.at[:, rank_value % RANKS, :, pl.ds(offset, size)]


def other_groups(groups_count):
    dp = lax.axis_index("dp")
    seq = lax.axis_index("seq")
    place, home = dp % RANKS, dp // RANKS
    return home, [
        {"seq": seq, "dp": ((home + k) % groups_count) * RANKS + place} for k in range(1, groups_count)
    ]


def weights_gather_kernel(count, groups_count, *refs):
    ins, outs = refs[:count], refs[count : 2 * count]
    send, recv, far_send, far_recv, local = refs[2 * count :]
    rank, peer = my_place()
    home, far = other_groups(groups_count)
    seq = lax.axis_index("seq")
    halves = [ref.shape[1] // 2 for ref in ins]

    def half(ref, a):
        return ref.at[:, pl.ds(pl.multiple_of(seq * halves[a], 128), halves[a])]

    def own_slot(a):
        columns = pl.ds(pl.multiple_of(seq * halves[a], 128), halves[a])
        return outs[a].at[home, rank % RANKS, :, columns]

    own = [pltpu.make_async_copy(half(ins[a], a), own_slot(a), local.at[a]) for a in range(count)]
    for copy in own:
        copy.start()
    barrier = pltpu.get_barrier_semaphore()
    for there in [peer(bit) for bit in (1, 2, 4, 8)] + far:
        pl.semaphore_signal(barrier, inc=1, device_id=there, device_id_type=MESH)
    pl.semaphore_wait(barrier, 4 + len(far))
    started, waiting = [], []
    for k, there in enumerate(far):
        for a in range(count):
            copy = pltpu.make_async_remote_copy(
                src_ref=half(ins[a], a),
                dst_ref=own_slot(a),
                send_sem=far_send.at[k, a],
                recv_sem=far_recv.at[k, a],
                device_id=there,
                device_id_type=MESH,
            )
            copy.start()
            started.append(copy)
            waiting.append(copy)
    for copy in own:
        copy.wait()
    for copy in waiting:
        copy.wait_recv()

    def remote(a, p, mask, bit, index):
        view = shard_view(outs[a], halves, a, p, flip_mask(rank, mask))
        copy = pltpu.make_async_remote_copy(
            src_ref=view,
            dst_ref=view,
            send_sem=send.at[a, p, index],
            recv_sem=recv.at[a, p, index],
            device_id=peer(bit),
            device_id_type=MESH,
        )
        copy.start()
        started.append(copy)
        return copy

    live = {}
    last = []
    for step in range(4):
        for p in range(3):
            for a in range(count):
                if column_parts(halves[a], a)[p][1] == 0:
                    continue
                order = LINKS[p]
                if step > 0:
                    for copy in live.pop((a, p)):
                        copy.wait_recv()
                if step < 3:
                    live[(a, p)] = [
                        remote(a, p, mask, order[step], 2**step - 1 + index)
                        for index, mask in enumerate(subsets(order[:step]))
                    ]
                fresh = [0] if step == 0 else [m | order[step - 1] for m in subsets(order[: step - 1])]
                base = 0 if step == 0 else 2 ** (step - 1)
                for index, mask in enumerate(fresh):
                    last.append(remote(a, p, mask, 1, 7 + base + index))
    for copy in last:
        copy.wait_recv()
    for copy in started:
        copy.wait_send()


def weights_gather(collective_id, groups_count, *arrays):
    count = len(arrays)
    whole = pl.pallas_call(
        functools.partial(weights_gather_kernel, count, groups_count),
        out_shape=[
            jax.ShapeDtypeStruct((groups_count, RANKS) + a.shape, a.dtype) for a in arrays
        ],
        in_specs=[pl.BlockSpec(memory_space=pltpu.VMEM)] * count,
        out_specs=[pl.BlockSpec(memory_space=pl.ANY)] * count,
        scratch_shapes=[
            pltpu.SemaphoreType.DMA((count, 3, 15)),
            pltpu.SemaphoreType.DMA((count, 3, 15)),
            pltpu.SemaphoreType.DMA((max(groups_count - 1, 1), count)),
            pltpu.SemaphoreType.DMA((max(groups_count - 1, 1), count)),
            pltpu.SemaphoreType.DMA((count,)),
        ],
        compiler_params=pltpu.CompilerParams(collective_id=collective_id, has_side_effects=True),
        name="weights_gather",
    )(*arrays)
    return [w.reshape(-1, w.shape[3]) for w in whole]


def add_block(target, source, at, start, size):
    groups, rows = source.shape[0], source.shape[1]
    columns = pl.ds(start, size)
    pieces = rows // 16

    def step(i, carry):
        lines = pl.ds(pl.multiple_of((i % pieces) * 16, 16), 16)
        index = (i // pieces, lines, columns)
        new = target[(at,) + index].astype(f32) + source[index].astype(f32)
        target[(at,) + index] = new.astype(target.dtype)
        return carry

    lax.fori_loop(0, groups * pieces, step, 0)


def weights_reduce_kernel(count, groups_count, *refs):
    ins = refs[:count]
    pieces = refs[count : count + 2]
    outs = refs[count + 2 : 2 * count + 2]
    whole = refs[2 * count + 2 : 2 * count + 4]
    rest = refs[2 * count + 4 :]
    total, got0, got1, got2, got3, far_got = [rest[i * count : (i + 1) * count] for i in range(6)]
    sems, far_sems, seq_sems, piece_sems, local, own_sems = rest[6 * count :]
    rank, peer = my_place()
    chip, core = rank // 2, rank % 2
    home, far = other_groups(groups_count)
    seq = lax.axis_index("seq")
    dp = lax.axis_index("dp")
    halves = [ref.shape[3] // 2 for ref in ins]
    parts = [column_parts(halves[a], a) for a in range(count)]

    def half_view(ref, a, rank_value):
        offset = pl.multiple_of((rank_value // RANKS) * halves[a], 128)
        return ref.at[:, rank_value % RANKS, :, pl.ds(offset, halves[a])]

    loads = []
    for a in range(count):
        for c in range(8):
            copy = pltpu.make_async_copy(
                half_view(ins[a], a, 2 * c + core), total[a].at[c], local.at[a, c]
            )
            copy.start()
            loads.append(copy)
    keeps = [
        pltpu.make_async_copy(pieces[i].at[rank % RANKS], whole[i].at[rank], own_sems.at[i])
        for i in range(2)
    ]
    for copy in keeps:
        copy.start()
    barrier = pltpu.get_barrier_semaphore()
    everyone = [
        {"seq": 1 - seq if mask & 8 else seq, "dp": flip_mask(dp, mask & 7)} for mask in range(1, 16)
    ]
    for there in everyone + far:
        pl.semaphore_signal(barrier, inc=1, device_id=there, device_id_type=MESH)
    pl.semaphore_wait(barrier, 15 + len(far))

    started = []
    live = {}

    def send(a, p, stage, index, src, dst, bit):
        copy = pltpu.make_async_remote_copy(
            src_ref=src,
            dst_ref=dst,
            send_sem=sems.at[0, a, p, stage, index],
            recv_sem=sems.at[1, a, p, stage, index],
            device_id=peer(bit),
            device_id_type=MESH,
        )
        copy.start()
        started.append(copy)
        live.setdefault((a, p), []).append(copy)

    def chip_of(mask):
        return flip_mask(rank, mask) // 2

    for p in range(3):
        for a in range(count):
            columns = pl.ds(*parts[a][p])
            if parts[a][p][1]:
                for c in range(8):
                    send(
                        a, p, 0, c,
                        shard_view(ins[a], halves, a, p, 2 * c + 1 - core),
                        got0[a].at[c, :, :, columns],
                        1,
                    )
    arrivals = []
    for mask, there in zip(range(1, 16), everyone):
        for i in range(2):
            copy = pltpu.make_async_remote_copy(
                src_ref=pieces[i].at[flip_mask(rank, mask) % RANKS],
                dst_ref=whole[i].at[rank],
                send_sem=piece_sems.at[0, i, mask],
                recv_sem=piece_sems.at[1, i, mask],
                device_id=there,
                device_id_type=MESH,
            )
            copy.start()
            arrivals.append(copy)
    for copy in loads:
        copy.wait()
    got = (got1, got2, got3)
    for stage in range(4):
        for p in range(3):
            for a in range(count):
                start, size = parts[a][p]
                if size == 0:
                    continue
                order = LINKS[p]
                columns = pl.ds(start, size)
                for copy in live.pop((a, p)):
                    copy.wait_recv()
                if stage == 0:

                    def over_chips(c, carry, a=a, start=start, size=size):
                        add_block(total[a], got0[a].at[c], c, start, size)
                        return carry

                    lax.fori_loop(0, 8, over_chips, 0)
                else:
                    for index, mask in enumerate(subsets(order[stage:])):
                        add_block(total[a], got[stage - 1][a].at[index], chip_of(mask), start, size)
                if stage < 3:
                    for index, mask in enumerate(subsets(order[stage + 1 :])):
                        send(
                            a, p, stage + 1, index,
                            total[a].at[chip_of(mask | order[stage]), :, :, columns],
                            got[stage][a].at[index, :, :, columns],
                            order[stage],
                        )
    waiting = []
    for k, there in enumerate(far):
        for a in range(count):
            copy = pltpu.make_async_remote_copy(
                src_ref=total[a].at[chip, there["dp"] // RANKS],
                dst_ref=far_got[a].at[k],
                send_sem=far_sems.at[0, k, a],
                recv_sem=far_sems.at[1, k, a],
                device_id=there,
                device_id_type=MESH,
            )
            copy.start()
            waiting.append(copy)
    for copy in waiting:
        copy.wait()
    last = []
    for a in range(count):
        columns = pl.ds(pl.multiple_of(seq * halves[a], 128), halves[a])
        value = total[a][chip, home].astype(f32)
        for k in range(len(far)):
            value = value + far_got[a][k].astype(f32)
        outs[a][:, columns] = value.astype(outs[a].dtype)
        copy = pltpu.make_async_remote_copy(
            src_ref=outs[a].at[:, columns],
            dst_ref=outs[a].at[:, columns],
            send_sem=seq_sems.at[0, a],
            recv_sem=seq_sems.at[1, a],
            device_id=peer(8),
            device_id_type=MESH,
        )
        copy.start()
        last.append(copy)
    for copy in last + arrivals:
        copy.wait()
    for copy in started:
        copy.wait_send()
    for copy in keeps:
        copy.wait()


def weights_reduce(collective_id, groups_count, arrays, pieces):
    count = len(arrays)
    views = [a.reshape(groups_count, RANKS, -1, a.shape[1]) for a in arrays]
    rows = views[0].shape[2]
    halves = [a.shape[1] // 2 for a in arrays]

    def buffers(*lead):
        return [
            pltpu.VMEM(lead + (groups_count, rows, h), a.dtype) for h, a in zip(halves, arrays)
        ]

    far_buffers = [
        pltpu.VMEM((max(groups_count - 1, 1), rows, h), a.dtype) for h, a in zip(halves, arrays)
    ]
    dma = pltpu.SemaphoreType.DMA
    vmem = pl.BlockSpec(memory_space=pltpu.VMEM)
    any_space = pl.BlockSpec(memory_space=pl.ANY)
    return pl.pallas_call(
        functools.partial(weights_reduce_kernel, count, groups_count),
        out_shape=[jax.ShapeDtypeStruct((rows, a.shape[1]), a.dtype) for a in arrays]
        + [jax.ShapeDtypeStruct((EXPERTS,) + p.shape[1:], p.dtype) for p in pieces],
        in_specs=[any_space] * count + [vmem] * 2,
        out_specs=[vmem] * count + [any_space] * 2,
        scratch_shapes=buffers(8) + buffers(8) + buffers(4) + buffers(2) + buffers(1) + far_buffers
        + [
            dma((2, count, 3, 4, 8)),
            dma((2, max(groups_count - 1, 1), count)),
            dma((2, count)),
            dma((2, 2, 16)),
            dma((count, 8)),
            dma((2,)),
        ],
        compiler_params=pltpu.CompilerParams(
            collective_id=collective_id, has_side_effects=True, vmem_limit_bytes=48 * 2**20
        ),
        name="weights_reduce",
    )(*views, *pieces)


def expert_kernel(
    rows_ref, grad_ref, gate_ref, gate_up_ref, down_ref,
    mixed_ref, normed_ref, gate_grad_ref, gate_up_out, down_out,
    gate_up_sum, down_sum,
):
    step = pl.program_id(0)
    shards, each, width = rows_ref.shape
    count = shards * each
    rows = rows_ref[...].reshape(count, width)
    grad = grad_ref[...].reshape(count, width).astype(f32)
    gate = jnp.concatenate(
        [jnp.broadcast_to(gate_ref[i], (128, each)).T[:, :1] for i in range(shards)], 0
    )
    down = down_ref[...]
    gate_up_weight = gate_up_ref[...]
    gate_up = jnp.dot(rows, gate_up_weight, preferred_element_type=f32)
    gate_part, up_part = gate_up[:, :F], gate_up[:, F:]
    sigmoid = 1.0 / (1.0 + jnp.exp(-gate_part))
    silu = gate_part * sigmoid
    act = (silu * up_part).astype(bf16)
    out = jnp.dot(act, down, preferred_element_type=f32)
    inner = jnp.sum(out * grad, axis=-1, keepdims=True)
    for i in range(shards):
        line = jnp.broadcast_to(inner[i * each : (i + 1) * each], (each, 128)).T
        gate_grad_ref[i] = line[:8]
    mixed_ref[...] = (gate * out).astype(bf16).reshape(shards, each, width)
    expert_grad = (gate * grad).astype(bf16)
    across = (((1,), (1,)), ((), ()))
    over_rows = (((0,), (0,)), ((), ()))
    act_grad = lax.dot_general(expert_grad, down, across, preferred_element_type=f32)
    gate_up_grad = jnp.concatenate(
        [act_grad * up_part * (sigmoid * (1.0 + gate_part * (1.0 - sigmoid))), act_grad * silu], -1
    ).astype(bf16)
    normed_ref[...] = (
        lax.dot_general(gate_up_grad, gate_up_weight, across, preferred_element_type=f32)
        .astype(bf16)
        .reshape(shards, each, width)
    )

    @pl.when(step == 0)
    def _():
        gate_up_sum[...] = jnp.zeros_like(gate_up_sum)
        down_sum[...] = jnp.zeros_like(down_sum)

    down_sum[...] += lax.dot_general(act, expert_grad, over_rows, preferred_element_type=f32)
    gate_up_sum[...] += lax.dot_general(rows, gate_up_grad, over_rows, preferred_element_type=f32)

    @pl.when(step == pl.num_programs(0) - 1)
    def _():
        gate_up_out[...] = gate_up_sum[...].astype(bf16)
        down_out[...] = down_sum[...].astype(bf16)


def expert_layer(rows, grad, gate, gate_up_weight, down_weight):
    each, width = rows.shape[1:]
    shards = 2
    tile = pl.BlockSpec((shards, each, width), lambda i: (i, 0, 0))
    whole = lambda shape: pl.BlockSpec(shape, lambda i: (0, 0))
    return pl.pallas_call(
        expert_kernel,
        grid=(GROUP // shards,),
        out_shape=[
            jax.ShapeDtypeStruct(rows.shape, bf16),
            jax.ShapeDtypeStruct(rows.shape, bf16),
            jax.ShapeDtypeStruct((GROUP, 8, each), f32),
            jax.ShapeDtypeStruct(gate_up_weight.shape, bf16),
            jax.ShapeDtypeStruct(down_weight.shape, bf16),
        ],
        in_specs=[
            tile,
            tile,
            pl.BlockSpec((shards, 1, each), lambda i: (i, 0, 0)),
            whole(gate_up_weight.shape),
            whole(down_weight.shape),
        ],
        out_specs=[
            tile,
            tile,
            pl.BlockSpec((shards, 8, each), lambda i: (i, 0, 0)),
            whole(gate_up_weight.shape),
            whole(down_weight.shape),
        ],
        scratch_shapes=[
            pltpu.VMEM(gate_up_weight.shape, f32),
            pltpu.VMEM(down_weight.shape, f32),
        ],
        compiler_params=pltpu.CompilerParams(vmem_limit_bytes=56 * 2**20),
        name="expert_layer",
    )(rows, grad, gate, gate_up_weight, down_weight)


def inverse_rms(rows):
    return lax.rsqrt(jnp.mean(rows * rows, axis=-1, keepdims=True) + epsilon)


def norm_back(rows, gain_row, upstream):
    inverse = inverse_rms(rows)
    gain_grad = jnp.sum(upstream * rows * inverse, axis=0)
    scaled = upstream * gain_row
    rows_grad = inverse * scaled - rows * inverse**3 * jnp.mean(scaled * rows, axis=-1, keepdims=True)
    return rows_grad, gain_grad


def rope_tables(positions):
    half = HEAD_SIZE // 2
    frequency = rope_base ** (-(jnp.arange(half, dtype=f32) * 2.0) / HEAD_SIZE)
    angles = positions.astype(f32)[:, None] * frequency[None, :]
    cosine, sine = jnp.cos(angles), jnp.sin(angles)
    return jnp.concatenate([cosine, cosine], 1), jnp.concatenate([sine, sine], 1)


def rotary_apply(rows, cosine, sine):
    half = HEAD_SIZE // 2
    turned = jnp.concatenate([-rows[..., half:], rows[..., :half]], -1)
    return rows * cosine[:, None, :] + turned * sine[:, None, :]


def unrotate(rows, cosine, sine):
    half = HEAD_SIZE // 2
    scaled = rows * sine[:, None, :]
    back = jnp.concatenate([scaled[..., half:], -scaled[..., :half]], -1)
    return rows * cosine[:, None, :] + back


def make_body(n_dp):
    groups_count = n_dp // RANKS
    inside = [[g * RANKS + j for j in range(RANKS)] for g in range(groups_count)]
    between = [[g * RANKS + j for g in range(groups_count)] for j in range(RANKS)]
    half_experts = EXPERTS // 2

    def expert_weight(shard, seq_rank):
        mine = lax.dynamic_slice_in_dim(shard, seq_rank * half_experts, half_experts, axis=1)
        mine = jnp.swapaxes(mine, 0, 1)
        mine = lax.all_to_all(
            mine, "dp", split_axis=0, concat_axis=0, tiled=True, axis_index_groups=inside
        )
        mine = mine.reshape(-1, shard.shape[2])
        return lax.all_gather(mine, "dp", axis=0, tiled=True, axis_index_groups=between)

    def expert_weight_grad(grad):
        grad = lax.psum_scatter(
            grad, "dp", scatter_dimension=0, tiled=True, axis_index_groups=between
        )
        return grad.reshape(RANKS, -1, grad.shape[1])

    def body(
        tokens, starts, routes, gain_one, query_key_value_weight, w_out,
        gain_two, w_router, w_gate_up, w_down, cotangent,
    ):
        count = tokens.shape[1]
        seq_rank = lax.axis_index("seq")
        expert = seq_rank * RANKS + lax.axis_index("dp") % RANKS
        query_columns = QUERY_HEADS * HEAD_SIZE
        key_columns = KEY_VALUE_HEADS * HEAD_SIZE
        group = QUERY_HEADS // KEY_VALUE_HEADS
        forward_pair, back_pair = [(0, 1)], [(1, 0)]

        tokens_before = lax.ppermute(tokens[0], "seq", forward_pair)
        starts_before = lax.ppermute(starts, "seq", forward_pair)
        spare = lambda value: jnp.pad(value, ((0, 0), (0, 128 - value.shape[1])))
        qkv_weight, out_weight, small = weights_gather(
            0,
            groups_count,
            query_key_value_weight,
            w_out,
            jnp.concatenate(
                [spare(w_router), spare(jnp.stack([gain_one, gain_two], 1))], 1
            ),
        )
        router_weight = small[:, :EXPERTS]
        gain_a = small[:, 128].astype(f32)
        gain_b = small[:, 129].astype(f32)
        gate_up_weight = expert_weight(w_gate_up, seq_rank)
        down_weight = expert_weight(w_down, seq_rank)

        token_rows = tokens[0].astype(f32)
        grad_output = cotangent[0].astype(f32)
        both = 2 * count
        index = jnp.arange(both, dtype=jnp.int32)
        flags = jnp.concatenate([starts_before[0], starts[0]])
        begins = (flags > 0) | (index == jnp.where(seq_rank == 0, count, 0))
        last_begin = jnp.max(
            jnp.where(begins[None, :] & (index[None, :] <= index[:, None]), index[None, :], 0), axis=1
        )
        cosine_all, sine_all = rope_tables(index - last_begin)
        cosine, sine = cosine_all[count:], sine_all[count:]

        rows_all = jnp.concatenate([tokens_before.astype(f32), token_rows], 0)
        normed_all = (rows_all * inverse_rms(rows_all) * gain_a).astype(bf16)
        normed_one = normed_all[count:]
        projected_q = jnp.dot(normed_one, qkv_weight[:, :query_columns], preferred_element_type=f32)
        projected_kv = jnp.dot(normed_all, qkv_weight[:, query_columns:], preferred_element_type=f32)
        queries = rotary_apply(
            projected_q.reshape(count, QUERY_HEADS, HEAD_SIZE), cosine, sine
        ).astype(bf16).reshape(count, KEY_VALUE_HEADS, group, HEAD_SIZE)
        keys = rotary_apply(
            projected_kv[:, :key_columns].reshape(both, KEY_VALUE_HEADS, HEAD_SIZE), cosine_all, sine_all
        ).astype(bf16)
        values = projected_kv[:, key_columns:].astype(bf16).reshape(both, KEY_VALUE_HEADS, HEAD_SIZE)

        scale = HEAD_SIZE ** (-0.5)
        allowed = (index[None, :] <= index[count:, None]) & (index[None, :] >= last_begin[count:, None])
        scores = jnp.einsum("qgrd,kgd->grqk", queries, keys, preferred_element_type=f32) * scale
        scores = jnp.where(allowed[None, None], scores, masked_score)
        top = jnp.max(scores, axis=-1, keepdims=True)
        exps = jnp.exp(scores - top)
        probs = exps / jnp.sum(exps, axis=-1, keepdims=True)
        probs_low = probs.astype(bf16)
        attended = jnp.einsum(
            "grqk,kgd->qgrd", probs_low, values, preferred_element_type=f32
        ).reshape(count, query_columns).astype(bf16)
        hidden = token_rows + jnp.dot(attended, out_weight, preferred_element_type=f32)
        normed_two = (hidden * inverse_rms(hidden) * gain_b).astype(bf16)
        logits = jnp.dot(normed_two, router_weight, preferred_element_type=f32)
        expert_ids = jnp.arange(EXPERTS, dtype=jnp.int32)
        chosen = jnp.any(routes[0][:, :, None] == expert_ids[None, None, :], axis=1)
        gates = jax.nn.softmax(jnp.where(chosen, logits, -jnp.inf), axis=-1)

        rows_in, gates_all, grad_all = group_gather(1, normed_two, gates.T, cotangent[0])
        gate = lax.dynamic_slice_in_dim(gates_all, expert, 1, axis=1)
        mixed_part, normed_part, gate_grad_part, gate_up_wgrad, down_wgrad = expert_layer(
            rows_in, grad_all, gate, gate_up_weight, down_weight
        )
        mixed, normed_grad, gate_grad = group_reduce(2, mixed_part, normed_part, gate_grad_part)
        gate_grad = gate_grad[:, 0].T

        over_rows = (((0,), (0,)), ((), ()))
        output = (hidden + mixed).astype(bf16)[None]
        stat_sums = jnp.stack([jnp.sum(hidden * hidden), jnp.sum(mixed * mixed)])
        weighted = jnp.where(chosen, gates * gate_grad, 0.0)
        logits_grad = weighted - gates * jnp.sum(weighted, axis=-1, keepdims=True)
        router_wide = router_weight.astype(f32)
        normed_grad = normed_grad + jnp.dot(logits_grad, router_wide.T, precision=highest)
        router_wgrad = jnp.dot(normed_two.astype(f32).T, logits_grad, precision=highest)
        hidden_branch, gain_two_grad = norm_back(hidden, gain_b, normed_grad)
        hidden_grad = grad_output + hidden_branch
        branch_low = hidden_grad.astype(bf16)
        out_wgrad = lax.dot_general(attended, branch_low, over_rows, preferred_element_type=f32)
        attended_grad = lax.dot_general(
            branch_low, out_weight, (((1,), (1,)), ((), ())), preferred_element_type=f32
        ).astype(bf16).reshape(count, KEY_VALUE_HEADS, group, HEAD_SIZE)

        prob_grad = jnp.einsum("qgrd,kgd->grqk", attended_grad, values, preferred_element_type=f32)
        delta = jnp.sum(probs * prob_grad, axis=-1, keepdims=True)
        score_grad = (probs * (prob_grad - delta)).astype(bf16)
        query_grad = (
            jnp.einsum("grqk,kgd->qgrd", score_grad, keys, preferred_element_type=f32) * scale
        ).reshape(count, QUERY_HEADS, HEAD_SIZE)
        key_grad = (
            jnp.einsum("grqk,qgrd->kgd", score_grad, queries, preferred_element_type=f32) * scale
        ).reshape(both, key_columns)
        value_grad = jnp.einsum(
            "grqk,qgrd->kgd", probs_low, attended_grad, preferred_element_type=f32
        ).reshape(both, key_columns)
        kv_grad = jnp.concatenate([key_grad, value_grad], 1)
        kv_back = lax.ppermute(kv_grad[:count].astype(bf16), "seq", back_pair)
        kv_grad = (kv_grad[count:] + kv_back.astype(f32)).astype(bf16).astype(f32)
        query_grad = query_grad.astype(bf16).astype(f32)
        query_back = unrotate(query_grad, cosine, sine).reshape(count, query_columns)
        key_back = unrotate(
            kv_grad[:, :key_columns].reshape(count, KEY_VALUE_HEADS, HEAD_SIZE), cosine, sine
        ).reshape(count, key_columns)
        projected_grad = jnp.concatenate([query_back, key_back, kv_grad[:, key_columns:]], 1).astype(bf16)
        qkv_wgrad = lax.dot_general(normed_one, projected_grad, over_rows, preferred_element_type=f32)
        normed_one_grad = lax.dot_general(
            projected_grad, qkv_weight, (((1,), (1,)), ((), ())), preferred_element_type=f32
        )
        rows_branch, gain_one_grad = norm_back(token_rows, gain_a, normed_one_grad)
        input_grad = (hidden_grad + rows_branch).astype(bf16)[None]

        little = jnp.concatenate(
            [spare(router_wgrad), spare(jnp.stack([gain_one_grad, gain_two_grad], 1))], 1
        )
        qkv_shard, out_shard, little, gate_up_all, down_all = weights_reduce(
            3,
            groups_count,
            (qkv_wgrad.astype(bf16), out_wgrad.astype(bf16), little),
            (expert_weight_grad(gate_up_wgrad), expert_weight_grad(down_wgrad)),
        )
        stat_sums = lax.psum(stat_sums, "seq")
        stream_rms = jnp.sqrt(stat_sums / (both * MODEL_WIDTH)).reshape(1, 2)
        return (
            output,
            input_grad,
            little[:, 128],
            qkv_shard.astype(f32),
            out_shard.astype(f32),
            little[:, 129],
            little[:, :EXPERTS],
            jnp.swapaxes(gate_up_all, 0, 1).astype(f32),
            jnp.swapaxes(down_all, 0, 1).astype(f32),
            stream_rms,
        )

    return body


def solution(mesh):
    placed = (
        P("dp", "seq", None),
        P("dp", "seq"),
        P("dp", "seq", None),
        P("dp"),
        P("dp", None),
        P("dp", None),
        P("dp"),
        P("dp", None),
        P("dp", None, None),
        P("dp", None, None),
        P("dp", "seq", None),
    )
    return jax.shard_map(
        make_body(mesh.shape["dp"]),
        mesh=mesh,
        in_specs=placed,
        out_specs=(
            P("dp", "seq", None),
            P("dp", "seq", None),
            P("dp"),
            P("dp", None),
            P("dp", None),
            P("dp"),
            P("dp", None),
            P("dp", None, None),
            P("dp", None, None),
            P("dp", None),
        ),
        check_vma=False,
    )
```

```python
import functools

import jax
import jax.numpy as jnp
from jax import lax
from jax.experimental import pallas as pl
from jax.experimental.pallas import tpu as pltpu
from jax.sharding import PartitionSpec as P

MODEL_WIDTH = 1024
QUERY_HEADS = 16
KEY_VALUE_HEADS = 8
HEAD_SIZE = 64
F = 512
EXPERTS = 16
TOPK = 8
RANKS = 8
GROUP = 16

epsilon = 1e-06
rope_base = 10000.0
highest = lax.Precision.HIGHEST
masked_score = -1e30
f32 = jnp.float32
bf16 = jnp.bfloat16
MESH = pl.DeviceIdType.MESH

LINKS = ((8, 4, 2), (4, 2, 8), (2, 8, 4))


def flip(value, bit):
    return value + bit * (1 - 2 * ((value // bit) % 2))


def flip_mask(value, mask):
    for bit in (1, 2, 4, 8):
        if mask & bit:
            value = flip(value, bit)
    return value


def subsets(bits):
    out = [0]
    for bit in bits:
        out = out + [m | bit for m in out]
    return out


def row_parts(rows):
    first = (rows // 3 + 15) // 16 * 16
    second = (rows - first) // 2 // 16 * 16
    return ((0, first), (first, second), (first + second, rows - first - second))


def my_place():
    seq = lax.axis_index("seq")
    dp = lax.axis_index("dp")
    rank = seq * RANKS + dp % RANKS

    def peer(bit):
        if bit == 8:
            return {"seq": 1 - seq, "dp": dp}
        return {"seq": seq, "dp": flip(dp, bit)}

    return rank, peer


def meet(peer):
    barrier = pltpu.get_barrier_semaphore()
    for bit in (1, 2, 4, 8):
        pl.semaphore_signal(barrier, inc=1, device_id=peer(bit), device_id_type=MESH)
    pl.semaphore_wait(barrier, 4)


def gather_kernel(count, *refs):
    ins, outs = refs[:count], refs[count : 2 * count]
    send, recv, send_core, recv_core, local = refs[2 * count :]
    rank, peer = my_place()
    own = [
        pltpu.make_async_copy(ins[a], outs[a].at[rank], local.at[a]) for a in range(count)
    ]
    for copy in own:
        copy.start()
    meet(peer)
    parts = [row_parts(ref.shape[0]) for ref in ins]

    def remote(a, p, mask, bit, sems, index):
        start, size = parts[a][p]
        rows = pl.ds(start, size)
        shard = flip_mask(rank, mask)
        src = ins[a].at[rows] if mask == 0 else outs[a].at[shard, rows]
        return pltpu.make_async_remote_copy(
            src_ref=src,
            dst_ref=outs[a].at[shard, rows],
            send_sem=sems[0].at[a, p, index],
            recv_sem=sems[1].at[a, p, index],
            device_id=peer(bit),
            device_id_type=MESH,
        )

    started = []
    live = {}
    for step in range(4):
        for p in range(3):
            for a in range(count):
                if parts[a][p][1] == 0:
                    continue
                order = LINKS[p]
                if step > 0:
                    for copy in live.pop((a, p)):
                        copy.wait_recv()
                if step < 3:
                    now = []
                    for index, mask in enumerate(subsets(order[:step])):
                        copy = remote(a, p, mask, order[step], (send, recv), 2**step - 1 + index)
                        copy.start()
                        now.append(copy)
                        started.append(copy)
                    live[(a, p)] = now
                fresh = [0] if step == 0 else [m | order[step - 1] for m in subsets(order[: step - 1])]
                base = 0 if step == 0 else 2 ** (step - 1)
                for index, mask in enumerate(fresh):
                    copy = remote(a, p, mask, 1, (send_core, recv_core), base + index)
                    copy.start()
                    live.setdefault("core", []).append(copy)
    for copy in live["core"]:
        copy.wait()
    for copy in started:
        copy.wait_send()
    for copy in own:
        copy.wait()


def group_gather(collective_id, *arrays):
    count = len(arrays)
    return pl.pallas_call(
        functools.partial(gather_kernel, count),
        out_shape=[jax.ShapeDtypeStruct((GROUP,) + a.shape, a.dtype) for a in arrays],
        in_specs=[pl.BlockSpec(memory_space=pltpu.VMEM)] * count,
        out_specs=[pl.BlockSpec(memory_space=pl.ANY)] * count,
        scratch_shapes=[
            pltpu.SemaphoreType.DMA((count, 3, 7)),
            pltpu.SemaphoreType.DMA((count, 3, 7)),
            pltpu.SemaphoreType.DMA((count, 3, 8)),
            pltpu.SemaphoreType.DMA((count, 3, 8)),
            pltpu.SemaphoreType.DMA((count,)),
        ],
        compiler_params=pltpu.CompilerParams(collective_id=collective_id, has_side_effects=True),
        cost_estimate=pl.CostEstimate(flops=60000000000, bytes_accessed=2**24, transcendentals=0),
        name="group_gather",
    )(*arrays)


def add_rows(target, source, start, size):
    def step(i, carry):
        rows = pl.ds(pl.multiple_of(start + i * 16, 16), 16)
        target[rows] = (target[rows].astype(f32) + source[rows].astype(f32)).astype(target.dtype)
        return carry

    lax.fori_loop(0, size // 16, step, 0)


def reduce_kernel(
    groups_count, mixed_ref, normed_ref, gate_ref, weights_ref, mixed_out, normed_out, gate_out, far_out,
    total, got0, got1, got2, got3, sems, gate_sems, local, own_gate, far_sems,
):
    rank, peer = my_place()
    chip = rank // 2
    core = rank % 2
    parts = row_parts(mixed_ref.shape[1])
    ins = (mixed_ref, normed_ref)
    outs = (mixed_out, normed_out)
    loads = []
    for t in range(2):
        for c in range(8):
            copy = pltpu.make_async_copy(ins[t].at[2 * c + core], total.at[t, c], local.at[t, c])
            copy.start()
            loads.append(copy)
    barrier = pltpu.get_barrier_semaphore()
    seq = lax.axis_index("seq")
    dp = lax.axis_index("dp")
    everyone = [
        {"seq": 1 - seq if mask & 8 else seq, "dp": flip_mask(dp, mask & 7)} for mask in range(1, 16)
    ]
    home, far = other_groups(groups_count)
    for there in everyone + far:
        pl.semaphore_signal(barrier, inc=1, device_id=there, device_id_type=MESH)
    pl.semaphore_wait(barrier, 15 + len(far))
    gates = []
    keep = pltpu.make_async_copy(gate_ref.at[rank], gate_out.at[rank], own_gate)
    keep.start()
    for mask, there in zip(range(1, 16), everyone):
        copy = pltpu.make_async_remote_copy(
            src_ref=gate_ref.at[flip_mask(rank, mask)],
            dst_ref=gate_out.at[rank],
            send_sem=gate_sems.at[0, mask],
            recv_sem=gate_sems.at[1, mask],
            device_id=there,
            device_id_type=MESH,
        )
        copy.start()
        gates.append(copy)

    started = []
    live = {}

    def send(t, p, stage, index, src, dst, bit):
        copy = pltpu.make_async_remote_copy(
            src_ref=src,
            dst_ref=dst,
            send_sem=sems.at[0, t, p, stage, index],
            recv_sem=sems.at[1, t, p, stage, index],
            device_id=peer(bit),
            device_id_type=MESH,
        )
        copy.start()
        started.append(copy)
        live.setdefault((t, p), []).append(copy)

    def chip_of(mask):
        return flip_mask(rank, mask) // 2

    for p in range(3):
        for t in range(2):
            rows = pl.ds(*parts[p])
            for c in range(8):
                send(
                    t, p, 0, c, ins[t].at[2 * c + 1 - core, rows], got0.at[t, c, rows], 1
                )
    for k, there in enumerate(far):
        copy = pltpu.make_async_remote_copy(
            src_ref=weights_ref.at[there["dp"] // RANKS],
            dst_ref=far_out.at[k],
            send_sem=far_sems.at[0, k],
            recv_sem=far_sems.at[1, k],
            device_id=there,
            device_id_type=MESH,
        )
        copy.start()
        gates.append(copy)
    for copy in loads:
        copy.wait()
    got = (got1, got2, got3)
    for stage in range(4):
        for p in range(3):
            for t in range(2):
                order = LINKS[p]
                rows = pl.ds(*parts[p])
                for copy in live.pop((t, p)):
                    copy.wait_recv()
                if stage == 0:

                    def over_chips(c, carry, t=t, p=p):
                        add_rows(total.at[t, c], got0.at[t, c], *parts[p])
                        return carry

                    lax.fori_loop(0, 8, over_chips, 0)
                else:
                    for index, mask in enumerate(subsets(order[stage:])):
                        if stage == 3:
                            outs[t][rows] = total[t, chip, rows].astype(f32) + got3[t, 0, rows].astype(f32)
                        else:
                            add_rows(
                                total.at[t, chip_of(mask)], got[stage - 1].at[t, index], *parts[p]
                            )
                if stage < 3:
                    for index, mask in enumerate(subsets(order[stage + 1 :])):
                        send(
                            t, p, stage + 1, index,
                            total.at[t, chip_of(mask | order[stage]), rows],
                            got[stage].at[t, index, rows],
                            order[stage],
                        )
    for copy in started:
        copy.wait_send()
    for copy in gates:
        copy.wait()
    keep.wait()


def group_reduce(collective_id, mixed, normed, gate_grad, weights):
    rows, width = mixed.shape[1:]
    groups_count = weights.shape[0]
    others = max(groups_count - 1, 1)
    return pl.pallas_call(
        functools.partial(reduce_kernel, groups_count),
        out_shape=[
            jax.ShapeDtypeStruct((rows, width), f32),
            jax.ShapeDtypeStruct((rows, width), f32),
            jax.ShapeDtypeStruct(gate_grad.shape, gate_grad.dtype),
            jax.ShapeDtypeStruct((others,) + weights.shape[1:], weights.dtype),
        ],
        in_specs=[pl.BlockSpec(memory_space=pl.ANY)] * 4,
        out_specs=[
            pl.BlockSpec(memory_space=pltpu.VMEM),
            pl.BlockSpec(memory_space=pltpu.VMEM),
            pl.BlockSpec(memory_space=pl.ANY),
            pl.BlockSpec(memory_space=pl.ANY),
        ],
        scratch_shapes=[
            pltpu.VMEM((2, 8, rows, width), bf16),
            pltpu.VMEM((2, 8, rows, width), bf16),
            pltpu.VMEM((2, 4, rows, width), bf16),
            pltpu.VMEM((2, 2, rows, width), bf16),
            pltpu.VMEM((2, 1, rows, width), bf16),
            pltpu.SemaphoreType.DMA((2, 2, 3, 4, 8)),
            pltpu.SemaphoreType.DMA((2, 16)),
            pltpu.SemaphoreType.DMA((2, 8)),
            pltpu.SemaphoreType.DMA(()),
            pltpu.SemaphoreType.DMA((2, others)),
        ],
        compiler_params=pltpu.CompilerParams(
            collective_id=collective_id, has_side_effects=True, vmem_limit_bytes=48 * 2**20
        ),
        cost_estimate=pl.CostEstimate(flops=70000000000, bytes_accessed=2**24, transcendentals=0),
        name="group_reduce",
    )(mixed, normed, gate_grad, weights)


def column_parts(half, which):
    tiles = half // 128
    if tiles == 1:
        sizes = (1, 0, 0)
    elif which % 2 == 0:
        big = -(-tiles // 3)
        sizes = (big, big, tiles - 2 * big)
    else:
        small = tiles // 3
        sizes = (small, small, tiles - 2 * small)
    out, start = [], 0
    for size in sizes:
        out.append((start * 128, size * 128))
        start += size
    return out


def shard_view(ref, halves, a, p, rank_value):
    start, size = column_parts(halves[a], a)[p]
    offset = pl.multiple_of((rank_value // RANKS) * halves[a] + start, 128)
    return ref.at[:, rank_value % RANKS, :, pl.ds(offset, size)]


def other_groups(groups_count):
    dp = lax.axis_index("dp")
    seq = lax.axis_index("seq")
    place, home = dp % RANKS, dp // RANKS
    return home, [
        {"seq": seq, "dp": ((home + k) % groups_count) * RANKS + place} for k in range(1, groups_count)
    ]


def weights_gather_kernel(count, groups_count, *refs):
    ins, outs = refs[:count], refs[count : 2 * count]
    send, recv, far_send, far_recv, local = refs[2 * count :]
    rank, peer = my_place()
    home, far = other_groups(groups_count)
    seq = lax.axis_index("seq")
    halves = [ref.shape[1] // 2 for ref in ins]

    def half(ref, a):
        return ref.at[:, pl.ds(pl.multiple_of(seq * halves[a], 128), halves[a])]

    def own_slot(a):
        columns = pl.ds(pl.multiple_of(seq * halves[a], 128), halves[a])
        return outs[a].at[home, rank % RANKS, :, columns]

    own = [pltpu.make_async_copy(half(ins[a], a), own_slot(a), local.at[a]) for a in range(count)]
    for copy in own:
        copy.start()
    barrier = pltpu.get_barrier_semaphore()
    for there in [peer(bit) for bit in (1, 2, 4, 8)] + far:
        pl.semaphore_signal(barrier, inc=1, device_id=there, device_id_type=MESH)
    pl.semaphore_wait(barrier, 4 + len(far))
    started, waiting = [], []
    for k, there in enumerate(far):
        for a in range(count):
            copy = pltpu.make_async_remote_copy(
                src_ref=half(ins[a], a),
                dst_ref=own_slot(a),
                send_sem=far_send.at[k, a],
                recv_sem=far_recv.at[k, a],
                device_id=there,
                device_id_type=MESH,
            )
            copy.start()
            started.append(copy)
            waiting.append(copy)
    for copy in own:
        copy.wait()
    for copy in waiting:
        copy.wait_recv()

    def remote(a, p, mask, bit, index):
        view = shard_view(outs[a], halves, a, p, flip_mask(rank, mask))
        copy = pltpu.make_async_remote_copy(
            src_ref=view,
            dst_ref=view,
            send_sem=send.at[a, p, index],
            recv_sem=recv.at[a, p, index],
            device_id=peer(bit),
            device_id_type=MESH,
        )
        copy.start()
        started.append(copy)
        return copy

    live = {}
    last = []
    for step in range(4):
        for p in range(3):
            for a in range(count):
                if column_parts(halves[a], a)[p][1] == 0:
                    continue
                order = LINKS[p]
                if step > 0:
                    for copy in live.pop((a, p)):
                        copy.wait_recv()
                if step < 3:
                    live[(a, p)] = [
                        remote(a, p, mask, order[step], 2**step - 1 + index)
                        for index, mask in enumerate(subsets(order[:step]))
                    ]
                fresh = [0] if step == 0 else [m | order[step - 1] for m in subsets(order[: step - 1])]
                base = 0 if step == 0 else 2 ** (step - 1)
                for index, mask in enumerate(fresh):
                    last.append(remote(a, p, mask, 1, 7 + base + index))
    for copy in last:
        copy.wait_recv()
    for copy in started:
        copy.wait_send()


def weights_gather(collective_id, groups_count, *arrays):
    count = len(arrays)
    whole = pl.pallas_call(
        functools.partial(weights_gather_kernel, count, groups_count),
        out_shape=[
            jax.ShapeDtypeStruct((groups_count, RANKS) + a.shape, a.dtype) for a in arrays
        ],
        in_specs=[pl.BlockSpec(memory_space=pltpu.VMEM)] * count,
        out_specs=[pl.BlockSpec(memory_space=pl.ANY)] * count,
        scratch_shapes=[
            pltpu.SemaphoreType.DMA((count, 3, 15)),
            pltpu.SemaphoreType.DMA((count, 3, 15)),
            pltpu.SemaphoreType.DMA((max(groups_count - 1, 1), count)),
            pltpu.SemaphoreType.DMA((max(groups_count - 1, 1), count)),
            pltpu.SemaphoreType.DMA((count,)),
        ],
        compiler_params=pltpu.CompilerParams(collective_id=collective_id, has_side_effects=True),
        cost_estimate=pl.CostEstimate(flops=45000000000, bytes_accessed=2**24, transcendentals=0),
        name="weights_gather",
    )(*arrays)
    return [w.reshape(-1, w.shape[3]) for w in whole]


def add_block(target, source, at, start, size):
    groups, rows = source.shape[0], source.shape[1]
    columns = pl.ds(start, size)
    pieces = rows // 16

    def step(i, carry):
        lines = pl.ds(pl.multiple_of((i % pieces) * 16, 16), 16)
        index = (i // pieces, lines, columns)
        new = target[(at,) + index].astype(f32) + source[index].astype(f32)
        target[(at,) + index] = new.astype(target.dtype)
        return carry

    lax.fori_loop(0, groups * pieces, step, 0)


def weights_reduce_kernel(count, groups_count, *refs):
    ins = refs[:count]
    pieces = refs[count]
    outs = refs[count + 1 : 2 * count + 1]
    whole = refs[2 * count + 1]
    rest = refs[2 * count + 2 :]
    total, got0, got1, got2, got3, far_got = [rest[i * count : (i + 1) * count] for i in range(6)]
    sems, far_sems, seq_sems, piece_sems, local, own_sems = rest[6 * count :]
    rank, peer = my_place()
    chip, core = rank // 2, rank % 2
    home, far = other_groups(groups_count)
    seq = lax.axis_index("seq")
    dp = lax.axis_index("dp")
    halves = [ref.shape[3] // 2 for ref in ins]
    parts = [column_parts(halves[a], a) for a in range(count)]

    def half_view(ref, a, rank_value):
        offset = pl.multiple_of((rank_value // RANKS) * halves[a], 128)
        return ref.at[:, rank_value % RANKS, :, pl.ds(offset, halves[a])]

    loads = []
    for a in range(count):
        for c in range(8):
            copy = pltpu.make_async_copy(
                half_view(ins[a], a, 2 * c + core), total[a].at[c], local.at[a, c]
            )
            copy.start()
            loads.append(copy)
    keep = pltpu.make_async_copy(pieces.at[rank % RANKS], whole.at[rank], own_sems)
    keep.start()
    barrier = pltpu.get_barrier_semaphore()
    everyone = [
        {"seq": 1 - seq if mask & 8 else seq, "dp": flip_mask(dp, mask & 7)} for mask in range(1, 16)
    ]
    for there in everyone + far:
        pl.semaphore_signal(barrier, inc=1, device_id=there, device_id_type=MESH)
    pl.semaphore_wait(barrier, 15 + len(far))

    started = []
    live = {}

    def send(a, p, stage, index, src, dst, bit):
        copy = pltpu.make_async_remote_copy(
            src_ref=src,
            dst_ref=dst,
            send_sem=sems.at[0, a, p, stage, index],
            recv_sem=sems.at[1, a, p, stage, index],
            device_id=peer(bit),
            device_id_type=MESH,
        )
        copy.start()
        started.append(copy)
        live.setdefault((a, p), []).append(copy)

    def chip_of(mask):
        return flip_mask(rank, mask) // 2

    for p in range(3):
        for a in range(count):
            columns = pl.ds(*parts[a][p])
            if parts[a][p][1]:
                for c in range(8):
                    send(
                        a, p, 0, c,
                        shard_view(ins[a], halves, a, p, 2 * c + 1 - core),
                        got0[a].at[c, :, :, columns],
                        1,
                    )
    arrivals = []
    for mask, there in zip(range(1, 16), everyone):
        copy = pltpu.make_async_remote_copy(
            src_ref=pieces.at[flip_mask(rank, mask) % RANKS],
            dst_ref=whole.at[rank],
            send_sem=piece_sems.at[0, mask],
            recv_sem=piece_sems.at[1, mask],
            device_id=there,
            device_id_type=MESH,
        )
        copy.start()
        arrivals.append(copy)
    for copy in loads:
        copy.wait()
    got = (got1, got2, got3)
    for stage in range(4):
        for p in range(3):
            for a in range(count):
                start, size = parts[a][p]
                if size == 0:
                    continue
                order = LINKS[p]
                columns = pl.ds(start, size)
                for copy in live.pop((a, p)):
                    copy.wait_recv()
                if stage == 0:

                    def over_chips(c, carry, a=a, start=start, size=size):
                        add_block(total[a], got0[a].at[c], c, start, size)
                        return carry

                    lax.fori_loop(0, 8, over_chips, 0)
                else:
                    for index, mask in enumerate(subsets(order[stage:])):
                        add_block(total[a], got[stage - 1][a].at[index], chip_of(mask), start, size)
                if stage < 3:
                    for index, mask in enumerate(subsets(order[stage + 1 :])):
                        send(
                            a, p, stage + 1, index,
                            total[a].at[chip_of(mask | order[stage]), :, :, columns],
                            got[stage][a].at[index, :, :, columns],
                            order[stage],
                        )
    waiting = []
    for k, there in enumerate(far):
        for a in range(count):
            copy = pltpu.make_async_remote_copy(
                src_ref=total[a].at[chip, there["dp"] // RANKS],
                dst_ref=far_got[a].at[k],
                send_sem=far_sems.at[0, k, a],
                recv_sem=far_sems.at[1, k, a],
                device_id=there,
                device_id_type=MESH,
            )
            copy.start()
            waiting.append(copy)
    for copy in waiting:
        copy.wait()
    last = []
    for a in range(count):
        columns = pl.ds(pl.multiple_of(seq * halves[a], 128), halves[a])
        value = total[a][chip, home].astype(f32)
        for k in range(len(far)):
            value = value + far_got[a][k].astype(f32)
        outs[a][:, columns] = value.astype(outs[a].dtype)
        copy = pltpu.make_async_remote_copy(
            src_ref=outs[a].at[:, columns],
            dst_ref=outs[a].at[:, columns],
            send_sem=seq_sems.at[0, a],
            recv_sem=seq_sems.at[1, a],
            device_id=peer(8),
            device_id_type=MESH,
        )
        copy.start()
        last.append(copy)
    for copy in last + arrivals:
        copy.wait()
    for copy in started:
        copy.wait_send()
    keep.wait()


def weights_reduce(collective_id, groups_count, arrays, pieces):
    count = len(arrays)
    views = [a.reshape(groups_count, RANKS, -1, a.shape[1]) for a in arrays]
    rows = views[0].shape[2]
    halves = [a.shape[1] // 2 for a in arrays]

    def buffers(*lead):
        return [
            pltpu.VMEM(lead + (groups_count, rows, h), a.dtype) for h, a in zip(halves, arrays)
        ]

    far_buffers = [
        pltpu.VMEM((max(groups_count - 1, 1), rows, h), a.dtype) for h, a in zip(halves, arrays)
    ]
    dma = pltpu.SemaphoreType.DMA
    vmem = pl.BlockSpec(memory_space=pltpu.VMEM)
    any_space = pl.BlockSpec(memory_space=pl.ANY)
    return pl.pallas_call(
        functools.partial(weights_reduce_kernel, count, groups_count),
        out_shape=[jax.ShapeDtypeStruct((rows, a.shape[1]), a.dtype) for a in arrays]
        + [jax.ShapeDtypeStruct((EXPERTS,) + pieces.shape[1:], pieces.dtype)],
        in_specs=[any_space] * count + [vmem],
        out_specs=[vmem] * count + [any_space],
        scratch_shapes=buffers(8) + buffers(8) + buffers(4) + buffers(2) + buffers(1) + far_buffers
        + [
            dma((2, count, 3, 4, 8)),
            dma((2, max(groups_count - 1, 1), count)),
            dma((2, count)),
            dma((2, 16)),
            dma((count, 8)),
            dma(()),
        ],
        compiler_params=pltpu.CompilerParams(
            collective_id=collective_id, has_side_effects=True, vmem_limit_bytes=48 * 2**20
        ),
        cost_estimate=pl.CostEstimate(flops=80000000000, bytes_accessed=2**24, transcendentals=0),
        name="weights_reduce",
    )(*views, pieces)


def expert_kernel(
    rows_ref, grad_ref, gate_ref, gate_up_ref, down_ref,
    mixed_ref, normed_ref, gate_grad_ref, weights_out,
    gate_up_sum, down_sum,
):
    step = pl.program_id(0)
    shards, each, width = rows_ref.shape
    count = shards * each
    rows = rows_ref[...].reshape(count, width)
    grad = grad_ref[...].reshape(count, width).astype(f32)
    gate = jnp.concatenate(
        [jnp.broadcast_to(gate_ref[i], (128, each)).T[:, :1] for i in range(shards)], 0
    )
    down = down_ref[...]
    gate_up_weight = gate_up_ref[...]
    gate_up = jnp.dot(rows, gate_up_weight, preferred_element_type=f32)
    gate_part, up_part = gate_up[:, :F], gate_up[:, F:]
    sigmoid = 1.0 / (1.0 + jnp.exp(-gate_part))
    silu = gate_part * sigmoid
    act = (silu * up_part).astype(bf16)
    out = jnp.dot(act, down, preferred_element_type=f32)
    inner = jnp.sum(out * grad, axis=-1, keepdims=True)
    for i in range(shards):
        line = jnp.broadcast_to(inner[i * each : (i + 1) * each], (each, 128)).T
        gate_grad_ref[i] = line[:8]
    mixed_ref[...] = (gate * out).astype(bf16).reshape(shards, each, width)
    expert_grad = (gate * grad).astype(bf16)
    across = (((1,), (1,)), ((), ()))
    over_rows = (((0,), (0,)), ((), ()))
    act_grad = lax.dot_general(expert_grad, down, across, preferred_element_type=f32)
    gate_up_grad = jnp.concatenate(
        [act_grad * up_part * (sigmoid * (1.0 + gate_part * (1.0 - sigmoid))), act_grad * silu], -1
    ).astype(bf16)
    normed_ref[...] = (
        lax.dot_general(gate_up_grad, gate_up_weight, across, preferred_element_type=f32)
        .astype(bf16)
        .reshape(shards, each, width)
    )

    @pl.when(step == 0)
    def _():
        gate_up_sum[...] = jnp.zeros_like(gate_up_sum)
        down_sum[...] = jnp.zeros_like(down_sum)

    down_sum[...] += lax.dot_general(act, expert_grad, over_rows, preferred_element_type=f32)
    gate_up_sum[...] += lax.dot_general(rows, gate_up_grad, over_rows, preferred_element_type=f32)

    @pl.when(step == pl.num_programs(0) - 1)
    def _():
        owners, _, columns = weights_out.shape
        first = gate_up_sum.shape[0] // owners
        weights_out[:, :first] = gate_up_sum[...].astype(bf16).reshape(owners, first, columns)
        weights_out[:, first:] = down_sum[...].astype(bf16).reshape(owners, -1, columns)


def expert_layer(n_dp, rows, grad, gate, gate_up_weight, down_weight):
    packed = (n_dp, (gate_up_weight.shape[0] + down_weight.shape[0]) // n_dp, rows.shape[2])
    each, width = rows.shape[1:]
    shards = 2
    tile = pl.BlockSpec((shards, each, width), lambda i: (i, 0, 0))
    whole = lambda shape: pl.BlockSpec(shape, lambda i: (0, 0))
    return pl.pallas_call(
        expert_kernel,
        grid=(GROUP // shards,),
        out_shape=[
            jax.ShapeDtypeStruct(rows.shape, bf16),
            jax.ShapeDtypeStruct(rows.shape, bf16),
            jax.ShapeDtypeStruct((GROUP, 8, each), f32),
            jax.ShapeDtypeStruct(packed, bf16),
        ],
        in_specs=[
            tile,
            tile,
            pl.BlockSpec((shards, 1, each), lambda i: (i, 0, 0)),
            whole(gate_up_weight.shape),
            whole(down_weight.shape),
        ],
        out_specs=[
            tile,
            tile,
            pl.BlockSpec((shards, 8, each), lambda i: (i, 0, 0)),
            pl.BlockSpec(packed, lambda i: (0, 0, 0)),
        ],
        scratch_shapes=[
            pltpu.VMEM(gate_up_weight.shape, f32),
            pltpu.VMEM(down_weight.shape, f32),
        ],
        compiler_params=pltpu.CompilerParams(vmem_limit_bytes=56 * 2**20),
        cost_estimate=pl.CostEstimate(flops=45000000000, bytes_accessed=2**24, transcendentals=0),
        name="expert_layer",
    )(rows, grad, gate, gate_up_weight, down_weight)


def inverse_rms(rows):
    return lax.rsqrt(jnp.mean(rows * rows, axis=-1, keepdims=True) + epsilon)


def norm_back(rows, gain_row, upstream):
    inverse = inverse_rms(rows)
    gain_grad = jnp.sum(upstream * rows * inverse, axis=0)
    scaled = upstream * gain_row
    rows_grad = inverse * scaled - rows * inverse**3 * jnp.mean(scaled * rows, axis=-1, keepdims=True)
    return rows_grad, gain_grad


def rope_tables(positions):
    half = HEAD_SIZE // 2
    frequency = rope_base ** (-(jnp.arange(half, dtype=f32) * 2.0) / HEAD_SIZE)
    angles = positions.astype(f32)[:, None] * frequency[None, :]
    cosine, sine = jnp.cos(angles), jnp.sin(angles)
    return jnp.concatenate([cosine, cosine], 1), jnp.concatenate([sine, sine], 1)


def rotary_apply(rows, cosine, sine):
    half = HEAD_SIZE // 2
    turned = jnp.concatenate([-rows[..., half:], rows[..., :half]], -1)
    return rows * cosine[:, None, :] + turned * sine[:, None, :]


def unrotate(rows, cosine, sine):
    half = HEAD_SIZE // 2
    scaled = rows * sine[:, None, :]
    back = jnp.concatenate([scaled[..., half:], -scaled[..., :half]], -1)
    return rows * cosine[:, None, :] + back


def make_body(n_dp):
    groups_count = n_dp // RANKS
    inside = [[g * RANKS + j for j in range(RANKS)] for g in range(groups_count)]
    half_experts = EXPERTS // 2

    def to_group(value, k):
        turn = [(d, (d + k * RANKS) % n_dp) for d in range(n_dp)]
        return lax.ppermute(value, "dp", turn)

    def expert_pieces(gate_up_shard, down_shard, seq_rank):
        mine = [
            jnp.swapaxes(lax.dynamic_slice_in_dim(w, seq_rank * half_experts, half_experts, axis=1), 0, 1)
            for w in (gate_up_shard, down_shard)
        ]
        return lax.all_to_all(
            jnp.concatenate(mine, 1), "dp", split_axis=0, concat_axis=0, tiled=True, axis_index_groups=inside
        )

    def expert_weights(mine, first):
        home = lax.axis_index("dp") // RANKS
        parts = [to_group(mine, k) for k in range(groups_count - 1, 0, -1)] + [mine]
        ring = jnp.stack(parts + parts)
        start = (2 * groups_count - 1 - home) % groups_count
        whole = lax.dynamic_slice_in_dim(ring, start, groups_count, axis=0)
        width = whole.shape[-1]
        return whole[:, :, :first].reshape(-1, width), whole[:, :, first:].reshape(-1, width)

    def body(
        tokens, starts, routes, gain_one, query_key_value_weight, w_out,
        gain_two, w_router, w_gate_up, w_down, cotangent,
    ):
        count = tokens.shape[1]
        seq_rank = lax.axis_index("seq")
        expert = seq_rank * RANKS + lax.axis_index("dp") % RANKS
        query_columns = QUERY_HEADS * HEAD_SIZE
        key_columns = KEY_VALUE_HEADS * HEAD_SIZE
        group = QUERY_HEADS // KEY_VALUE_HEADS
        forward_pair, back_pair = [(0, 1)], [(1, 0)]

        tokens_before = lax.ppermute(tokens[0], "seq", forward_pair)
        starts_before = lax.ppermute(starts, "seq", forward_pair)
        spare = lambda value: jnp.pad(value, ((0, 0), (0, 128 - value.shape[1])))
        qkv_weight, out_weight, small = weights_gather(
            0,
            groups_count,
            query_key_value_weight,
            w_out,
            jnp.concatenate(
                [spare(w_router), spare(jnp.stack([gain_one, gain_two], 1))], 1
            ),
        )
        mine, qkv_weight, out_weight, small = lax.optimization_barrier(
            (expert_pieces(w_gate_up, w_down, seq_rank), qkv_weight, out_weight, small)
        )
        gate_up_weight, down_weight = expert_weights(mine, w_gate_up.shape[0])
        router_weight = small[:, :EXPERTS]
        gain_a = small[:, 128].astype(f32)
        gain_b = small[:, 129].astype(f32)

        token_rows = tokens[0].astype(f32)
        grad_output = cotangent[0].astype(f32)
        both = 2 * count
        index = jnp.arange(both, dtype=jnp.int32)
        flags = jnp.concatenate([starts_before[0], starts[0]])
        begins = (flags > 0) | (index == jnp.where(seq_rank == 0, count, 0))
        last_begin = jnp.max(
            jnp.where(begins[None, :] & (index[None, :] <= index[:, None]), index[None, :], 0), axis=1
        )
        cosine_all, sine_all = rope_tables(index - last_begin)
        cosine, sine = cosine_all[count:], sine_all[count:]

        rows_all = jnp.concatenate([tokens_before.astype(f32), token_rows], 0)
        normed_all = (rows_all * inverse_rms(rows_all) * gain_a).astype(bf16)
        normed_one = normed_all[count:]
        projected_q = jnp.dot(normed_one, qkv_weight[:, :query_columns], preferred_element_type=f32)
        projected_kv = jnp.dot(normed_all, qkv_weight[:, query_columns:], preferred_element_type=f32)
        queries = rotary_apply(
            projected_q.reshape(count, QUERY_HEADS, HEAD_SIZE), cosine, sine
        ).astype(bf16).reshape(count, KEY_VALUE_HEADS, group, HEAD_SIZE)
        keys = rotary_apply(
            projected_kv[:, :key_columns].reshape(both, KEY_VALUE_HEADS, HEAD_SIZE), cosine_all, sine_all
        ).astype(bf16)
        values = projected_kv[:, key_columns:].astype(bf16).reshape(both, KEY_VALUE_HEADS, HEAD_SIZE)

        scale = HEAD_SIZE ** (-0.5)
        allowed = (index[None, :] <= index[count:, None]) & (index[None, :] >= last_begin[count:, None])
        scores = jnp.einsum("qgrd,kgd->grqk", queries, keys, preferred_element_type=f32) * scale
        scores = jnp.where(allowed[None, None], scores, masked_score)
        top = jnp.max(scores, axis=-1, keepdims=True)
        exps = jnp.exp(scores - top)
        probs = exps / jnp.sum(exps, axis=-1, keepdims=True)
        probs_low = probs.astype(bf16)
        attended = jnp.einsum(
            "grqk,kgd->qgrd", probs_low, values, preferred_element_type=f32
        ).reshape(count, query_columns).astype(bf16)
        hidden = token_rows + jnp.dot(attended, out_weight, preferred_element_type=f32)
        normed_two = (hidden * inverse_rms(hidden) * gain_b).astype(bf16)
        logits = jnp.dot(normed_two, router_weight, preferred_element_type=f32)
        expert_ids = jnp.arange(EXPERTS, dtype=jnp.int32)
        chosen = jnp.any(routes[0][:, :, None] == expert_ids[None, None, :], axis=1)
        gates = jax.nn.softmax(jnp.where(chosen, logits, -jnp.inf), axis=-1)

        normed_two, gate_up_weight, down_weight = lax.optimization_barrier(
            (normed_two, gate_up_weight, down_weight)
        )
        rows_in, gates_all, grad_all = group_gather(1, normed_two, gates.T, cotangent[0])
        gate = lax.dynamic_slice_in_dim(gates_all, expert, 1, axis=1)
        mixed_part, normed_part, gate_grad_part, expert_wgrads = expert_layer(
            n_dp, rows_in, grad_all, gate, gate_up_weight, down_weight
        )
        expert_wgrads = expert_wgrads.reshape((groups_count, RANKS) + expert_wgrads.shape[1:])
        mixed, normed_grad, gate_grad, expert_far = group_reduce(
            2, mixed_part, normed_part, gate_grad_part, expert_wgrads
        )
        expert_grads = lax.dynamic_index_in_dim(
            expert_wgrads, lax.axis_index("dp") // RANKS, 0, keepdims=False
        ).astype(f32)
        for k in range(groups_count - 1):
            expert_grads = expert_grads + expert_far[k].astype(f32)
        expert_grads = expert_grads.astype(bf16)
        gate_grad = gate_grad[:, 0].T

        over_rows = (((0,), (0,)), ((), ()))
        output = (hidden + mixed).astype(bf16)[None]
        stat_sums = jnp.stack([jnp.sum(hidden * hidden), jnp.sum(mixed * mixed)])
        weighted = jnp.where(chosen, gates * gate_grad, 0.0)
        logits_grad = weighted - gates * jnp.sum(weighted, axis=-1, keepdims=True)
        router_wide = router_weight.astype(f32)
        normed_grad = normed_grad + jnp.dot(logits_grad, router_wide.T, precision=highest)
        router_wgrad = jnp.dot(normed_two.astype(f32).T, logits_grad, precision=highest)
        hidden_branch, gain_two_grad = norm_back(hidden, gain_b, normed_grad)
        hidden_grad = grad_output + hidden_branch
        branch_low = hidden_grad.astype(bf16)
        out_wgrad = lax.dot_general(attended, branch_low, over_rows, preferred_element_type=f32)
        attended_grad = lax.dot_general(
            branch_low, out_weight, (((1,), (1,)), ((), ())), preferred_element_type=f32
        ).astype(bf16).reshape(count, KEY_VALUE_HEADS, group, HEAD_SIZE)

        prob_grad = jnp.einsum("qgrd,kgd->grqk", attended_grad, values, preferred_element_type=f32)
        delta = jnp.sum(probs * prob_grad, axis=-1, keepdims=True)
        score_grad = (probs * (prob_grad - delta)).astype(bf16)
        query_grad = (
            jnp.einsum("grqk,kgd->qgrd", score_grad, keys, preferred_element_type=f32) * scale
        ).reshape(count, QUERY_HEADS, HEAD_SIZE)
        key_grad = (
            jnp.einsum("grqk,qgrd->kgd", score_grad, queries, preferred_element_type=f32) * scale
        ).reshape(both, key_columns)
        value_grad = jnp.einsum(
            "grqk,qgrd->kgd", probs_low, attended_grad, preferred_element_type=f32
        ).reshape(both, key_columns)
        kv_grad = jnp.concatenate([key_grad, value_grad], 1)
        kv_back = lax.ppermute(kv_grad[:count].astype(bf16), "seq", back_pair)
        kv_grad = (kv_grad[count:] + kv_back.astype(f32)).astype(bf16).astype(f32)
        query_grad = query_grad.astype(bf16).astype(f32)
        query_back = unrotate(query_grad, cosine, sine).reshape(count, query_columns)
        key_back = unrotate(
            kv_grad[:, :key_columns].reshape(count, KEY_VALUE_HEADS, HEAD_SIZE), cosine, sine
        ).reshape(count, key_columns)
        projected_grad = jnp.concatenate([query_back, key_back, kv_grad[:, key_columns:]], 1).astype(bf16)
        qkv_wgrad = lax.dot_general(normed_one, projected_grad, over_rows, preferred_element_type=f32)
        normed_one_grad = lax.dot_general(
            projected_grad, qkv_weight, (((1,), (1,)), ((), ())), preferred_element_type=f32
        )
        rows_branch, gain_one_grad = norm_back(token_rows, gain_a, normed_one_grad)
        input_grad = (hidden_grad + rows_branch).astype(bf16)[None]

        little = jnp.concatenate(
            [spare(router_wgrad), spare(jnp.stack([gain_one_grad, gain_two_grad], 1))], 1
        )
        qkv_shard, out_shard, little, experts_all = weights_reduce(
            3,
            groups_count,
            (qkv_wgrad.astype(bf16), out_wgrad.astype(bf16), little),
            expert_grads,
        )
        stat_sums = stat_sums + lax.ppermute(stat_sums, "seq", [(0, 1), (1, 0)])
        first = w_gate_up.shape[0]
        stream_rms = jnp.sqrt(stat_sums / (both * MODEL_WIDTH)).reshape(1, 2)
        return (
            output,
            input_grad,
            little[:, 128],
            qkv_shard.astype(f32),
            out_shard.astype(f32),
            little[:, 129],
            little[:, :EXPERTS],
            jnp.swapaxes(experts_all[:, :first], 0, 1).astype(f32),
            jnp.swapaxes(experts_all[:, first:], 0, 1).astype(f32),
            stream_rms,
        )

    return body


def solution(mesh):
    placed = (
        P("dp", "seq", None),
        P("dp", "seq"),
        P("dp", "seq", None),
        P("dp"),
        P("dp", None),
        P("dp", None),
        P("dp"),
        P("dp", None),
        P("dp", None, None),
        P("dp", None, None),
        P("dp", "seq", None),
    )
    return jax.shard_map(
        make_body(mesh.shape["dp"]),
        mesh=mesh,
        in_specs=placed,
        out_specs=(
            P("dp", "seq", None),
            P("dp", "seq", None),
            P("dp"),
            P("dp", None),
            P("dp", None),
            P("dp"),
            P("dp", None),
            P("dp", None, None),
            P("dp", None, None),
            P("dp", None),
        ),
        check_vma=False,
    )
```

```python
import functools

import jax
import jax.numpy as jnp
from jax import lax
from jax.experimental import pallas as pl
from jax.experimental.pallas import tpu as pltpu
from jax.sharding import PartitionSpec as P

MODEL_WIDTH = 1024
QUERY_HEADS = 16
KEY_VALUE_HEADS = 8
HEAD_SIZE = 64
F = 512
EXPERTS = 16
TOPK = 8
RANKS = 8
GROUP = 16

epsilon = 1e-06
rope_base = 10000.0
highest = lax.Precision.HIGHEST
masked_score = -1e30
f32 = jnp.float32
bf16 = jnp.bfloat16
MESH = pl.DeviceIdType.MESH

LINKS = ((8, 4, 2), (4, 2, 8), (2, 8, 4))
TOKEN_LINKS = ((4, 8, 2), (4, 2, 8))
TOKEN_SUMS = ((8, 2, 4), (2, 8, 4))


def flip(value, bit):
    return value + bit * (1 - 2 * ((value // bit) % 2))


def flip_mask(value, mask):
    for bit in (1, 2, 4, 8):
        if mask & bit:
            value = flip(value, bit)
    return value


def subsets(bits):
    out = [0]
    for bit in bits:
        out = out + [m | bit for m in out]
    return out


def row_parts(rows):
    first = (rows // 2 + 15) // 16 * 16
    return ((0, first), (first, rows - first))


def my_place():
    seq = lax.axis_index("seq")
    dp = lax.axis_index("dp")
    rank = seq * RANKS + dp % RANKS

    def peer(bit):
        if bit == 8:
            return {"seq": 1 - seq, "dp": dp}
        return {"seq": seq, "dp": flip(dp, bit)}

    return rank, peer


def meet(peer):
    barrier = pltpu.get_barrier_semaphore()
    for bit in (1, 2, 4, 8):
        pl.semaphore_signal(barrier, inc=1, device_id=peer(bit), device_id_type=MESH)
    pl.semaphore_wait(barrier, 4)


def gather_kernel(count, *refs):
    ins, outs = refs[:count], refs[count : 2 * count]
    send, recv, send_core, recv_core, local = refs[2 * count :]
    rank, peer = my_place()
    own = [
        pltpu.make_async_copy(ins[a], outs[a].at[rank], local.at[a]) for a in range(count)
    ]
    for copy in own:
        copy.start()
    meet(peer)
    parts = [row_parts(ref.shape[0]) for ref in ins]

    def remote(a, p, mask, bit, sems, index):
        start, size = parts[a][p]
        rows = pl.ds(start, size)
        shard = flip_mask(rank, mask)
        src = ins[a].at[rows] if mask == 0 else outs[a].at[shard, rows]
        return pltpu.make_async_remote_copy(
            src_ref=src,
            dst_ref=outs[a].at[shard, rows],
            send_sem=sems[0].at[a, p, index],
            recv_sem=sems[1].at[a, p, index],
            device_id=peer(bit),
            device_id_type=MESH,
        )

    started = []
    live = {}
    for step in range(4):
        for p in range(2):
            for a in range(count):
                if parts[a][p][1] == 0:
                    continue
                order = TOKEN_LINKS[p]
                if step > 0:
                    for copy in live.pop((a, p)):
                        copy.wait_recv()
                if step < 3:
                    now = []
                    for index, mask in enumerate(subsets(order[:step])):
                        copy = remote(a, p, mask, order[step], (send, recv), 2**step - 1 + index)
                        copy.start()
                        now.append(copy)
                        started.append(copy)
                    live[(a, p)] = now
                fresh = [0] if step == 0 else [m | order[step - 1] for m in subsets(order[: step - 1])]
                base = 0 if step == 0 else 2 ** (step - 1)
                for index, mask in enumerate(fresh):
                    copy = remote(a, p, mask, 1, (send_core, recv_core), base + index)
                    copy.start()
                    live.setdefault("core", []).append(copy)
    for copy in live["core"]:
        copy.wait()
    for copy in started:
        copy.wait_send()
    for copy in own:
        copy.wait()


def group_gather(collective_id, *arrays):
    count = len(arrays)
    return pl.pallas_call(
        functools.partial(gather_kernel, count),
        out_shape=[jax.ShapeDtypeStruct((GROUP,) + a.shape, a.dtype) for a in arrays],
        in_specs=[pl.BlockSpec(memory_space=pltpu.VMEM)] * count,
        out_specs=[pl.BlockSpec(memory_space=pl.ANY)] * count,
        scratch_shapes=[
            pltpu.SemaphoreType.DMA((count, 3, 7)),
            pltpu.SemaphoreType.DMA((count, 3, 7)),
            pltpu.SemaphoreType.DMA((count, 3, 8)),
            pltpu.SemaphoreType.DMA((count, 3, 8)),
            pltpu.SemaphoreType.DMA((count,)),
        ],
        compiler_params=pltpu.CompilerParams(collective_id=collective_id, has_side_effects=True),
        cost_estimate=pl.CostEstimate(flops=60000000000, bytes_accessed=2**24, transcendentals=0),
        name="group_gather",
    )(*arrays)


def add_rows(target, source, start, size):
    def step(i, carry):
        rows = pl.ds(pl.multiple_of(start + i * 16, 16), 16)
        target[rows] = (target[rows].astype(f32) + source[rows].astype(f32)).astype(target.dtype)
        return carry

    lax.fori_loop(0, size // 16, step, 0)


def reduce_kernel(
    groups_count, mixed_ref, normed_ref, gate_ref, weights_ref, mixed_out, normed_out, gate_out, far_out,
    total, got0, got1, got2, got3, sems, gate_sems, local, own_gate, far_sems,
):
    rank, peer = my_place()
    chip = rank // 2
    core = rank % 2
    parts = row_parts(mixed_ref.shape[1])
    ins = (mixed_ref, normed_ref)
    outs = (mixed_out, normed_out)
    loads = []
    for t in range(2):
        for c in range(8):
            copy = pltpu.make_async_copy(ins[t].at[2 * c + core], total.at[t, c], local.at[t, c])
            copy.start()
            loads.append(copy)
    barrier = pltpu.get_barrier_semaphore()
    seq = lax.axis_index("seq")
    dp = lax.axis_index("dp")
    everyone = [
        {"seq": 1 - seq if mask & 8 else seq, "dp": flip_mask(dp, mask & 7)} for mask in range(1, 16)
    ]
    home, far = other_groups(groups_count)
    for there in everyone + far:
        pl.semaphore_signal(barrier, inc=1, device_id=there, device_id_type=MESH)
    pl.semaphore_wait(barrier, 15 + len(far))
    gates = []
    keep = pltpu.make_async_copy(gate_ref.at[rank], gate_out.at[rank], own_gate)
    keep.start()
    for mask, there in zip(range(1, 16), everyone):
        copy = pltpu.make_async_remote_copy(
            src_ref=gate_ref.at[flip_mask(rank, mask)],
            dst_ref=gate_out.at[rank],
            send_sem=gate_sems.at[0, mask],
            recv_sem=gate_sems.at[1, mask],
            device_id=there,
            device_id_type=MESH,
        )
        copy.start()
        gates.append(copy)

    started = []
    live = {}

    def send(t, p, stage, index, src, dst, bit):
        copy = pltpu.make_async_remote_copy(
            src_ref=src,
            dst_ref=dst,
            send_sem=sems.at[0, t, p, stage, index],
            recv_sem=sems.at[1, t, p, stage, index],
            device_id=peer(bit),
            device_id_type=MESH,
        )
        copy.start()
        started.append(copy)
        live.setdefault((t, p), []).append(copy)

    def chip_of(mask):
        return flip_mask(rank, mask) // 2

    for p in range(2):
        for t in range(2):
            rows = pl.ds(*parts[p])
            for c in range(8):
                send(
                    t, p, 0, c, ins[t].at[2 * c + 1 - core, rows], got0.at[t, c, rows], 1
                )
    for k, there in enumerate(far):
        copy = pltpu.make_async_remote_copy(
            src_ref=weights_ref.at[there["dp"] // RANKS],
            dst_ref=far_out.at[k],
            send_sem=far_sems.at[0, k],
            recv_sem=far_sems.at[1, k],
            device_id=there,
            device_id_type=MESH,
        )
        copy.start()
        gates.append(copy)
    for copy in loads:
        copy.wait()
    got = (got1, got2, got3)
    for stage in range(4):
        for p in range(2):
            for t in range(2):
                order = TOKEN_SUMS[p]
                rows = pl.ds(*parts[p])
                for copy in live.pop((t, p)):
                    copy.wait_recv()
                if stage == 0:

                    def over_chips(c, carry, t=t, p=p):
                        add_rows(total.at[t, c], got0.at[t, c], *parts[p])
                        return carry

                    lax.fori_loop(0, 8, over_chips, 0)
                else:
                    for index, mask in enumerate(subsets(order[stage:])):
                        if stage == 3:
                            outs[t][rows] = total[t, chip, rows].astype(f32) + got3[t, 0, rows].astype(f32)
                        else:
                            add_rows(
                                total.at[t, chip_of(mask)], got[stage - 1].at[t, index], *parts[p]
                            )
                if stage < 3:
                    for index, mask in enumerate(subsets(order[stage + 1 :])):
                        send(
                            t, p, stage + 1, index,
                            total.at[t, chip_of(mask | order[stage]), rows],
                            got[stage].at[t, index, rows],
                            order[stage],
                        )
    for copy in started:
        copy.wait_send()
    for copy in gates:
        copy.wait()
    keep.wait()


def group_reduce(collective_id, mixed, normed, gate_grad, weights):
    rows, width = mixed.shape[1:]
    groups_count = weights.shape[0]
    others = max(groups_count - 1, 1)
    return pl.pallas_call(
        functools.partial(reduce_kernel, groups_count),
        out_shape=[
            jax.ShapeDtypeStruct((rows, width), f32),
            jax.ShapeDtypeStruct((rows, width), f32),
            jax.ShapeDtypeStruct(gate_grad.shape, gate_grad.dtype),
            jax.ShapeDtypeStruct((others,) + weights.shape[1:], weights.dtype),
        ],
        in_specs=[pl.BlockSpec(memory_space=pl.ANY)] * 4,
        out_specs=[
            pl.BlockSpec(memory_space=pltpu.VMEM),
            pl.BlockSpec(memory_space=pltpu.VMEM),
            pl.BlockSpec(memory_space=pl.ANY),
            pl.BlockSpec(memory_space=pl.ANY),
        ],
        scratch_shapes=[
            pltpu.VMEM((2, 8, rows, width), bf16),
            pltpu.VMEM((2, 8, rows, width), bf16),
            pltpu.VMEM((2, 4, rows, width), bf16),
            pltpu.VMEM((2, 2, rows, width), bf16),
            pltpu.VMEM((2, 1, rows, width), bf16),
            pltpu.SemaphoreType.DMA((2, 2, 3, 4, 8)),
            pltpu.SemaphoreType.DMA((2, 16)),
            pltpu.SemaphoreType.DMA((2, 8)),
            pltpu.SemaphoreType.DMA(()),
            pltpu.SemaphoreType.DMA((2, others)),
        ],
        compiler_params=pltpu.CompilerParams(
            collective_id=collective_id, has_side_effects=True, vmem_limit_bytes=48 * 2**20
        ),
        cost_estimate=pl.CostEstimate(flops=70000000000, bytes_accessed=2**24, transcendentals=0),
        name="group_reduce",
    )(mixed, normed, gate_grad, weights)


def column_parts(half, which):
    tiles = half // 128
    if tiles == 1:
        sizes = (1, 0, 0)
    elif which % 2 == 0:
        big = -(-tiles // 3)
        sizes = (big, big, tiles - 2 * big)
    else:
        small = tiles // 3
        sizes = (small, small, tiles - 2 * small)
    out, start = [], 0
    for size in sizes:
        out.append((start * 128, size * 128))
        start += size
    return out


def shard_view(ref, halves, a, p, rank_value):
    start, size = column_parts(halves[a], a)[p]
    offset = pl.multiple_of((rank_value // RANKS) * halves[a] + start, 128)
    return ref.at[:, rank_value % RANKS, :, pl.ds(offset, size)]


def other_groups(groups_count):
    dp = lax.axis_index("dp")
    seq = lax.axis_index("seq")
    place, home = dp % RANKS, dp // RANKS
    return home, [
        {"seq": seq, "dp": ((home + k) % groups_count) * RANKS + place} for k in range(1, groups_count)
    ]


def weights_gather_kernel(count, groups_count, *refs):
    ins, outs = refs[:count], refs[count : 2 * count]
    send, recv, far_send, far_recv, local = refs[2 * count :]
    rank, peer = my_place()
    home, far = other_groups(groups_count)
    seq = lax.axis_index("seq")
    halves = [ref.shape[1] // 2 for ref in ins]

    def half(ref, a):
        return ref.at[:, pl.ds(pl.multiple_of(seq * halves[a], 128), halves[a])]

    def own_slot(a):
        columns = pl.ds(pl.multiple_of(seq * halves[a], 128), halves[a])
        return outs[a].at[home, rank % RANKS, :, columns]

    own = [pltpu.make_async_copy(half(ins[a], a), own_slot(a), local.at[a]) for a in range(count)]
    for copy in own:
        copy.start()
    barrier = pltpu.get_barrier_semaphore()
    for there in [peer(bit) for bit in (1, 2, 4, 8)] + far:
        pl.semaphore_signal(barrier, inc=1, device_id=there, device_id_type=MESH)
    pl.semaphore_wait(barrier, 4 + len(far))
    started, waiting = [], []
    for k, there in enumerate(far):
        for a in range(count):
            copy = pltpu.make_async_remote_copy(
                src_ref=half(ins[a], a),
                dst_ref=own_slot(a),
                send_sem=far_send.at[k, a],
                recv_sem=far_recv.at[k, a],
                device_id=there,
                device_id_type=MESH,
            )
            copy.start()
            started.append(copy)
            waiting.append(copy)
    for copy in own:
        copy.wait()
    for copy in waiting:
        copy.wait_recv()

    def remote(a, p, mask, bit, index):
        view = shard_view(outs[a], halves, a, p, flip_mask(rank, mask))
        copy = pltpu.make_async_remote_copy(
            src_ref=view,
            dst_ref=view,
            send_sem=send.at[a, p, index],
            recv_sem=recv.at[a, p, index],
            device_id=peer(bit),
            device_id_type=MESH,
        )
        copy.start()
        started.append(copy)
        return copy

    live = {}
    last = []
    for step in range(4):
        for p in range(3):
            for a in range(count):
                if column_parts(halves[a], a)[p][1] == 0:
                    continue
                order = LINKS[p]
                if step > 0:
                    for copy in live.pop((a, p)):
                        copy.wait_recv()
                if step < 3:
                    live[(a, p)] = [
                        remote(a, p, mask, order[step], 2**step - 1 + index)
                        for index, mask in enumerate(subsets(order[:step]))
                    ]
                fresh = [0] if step == 0 else [m | order[step - 1] for m in subsets(order[: step - 1])]
                base = 0 if step == 0 else 2 ** (step - 1)
                for index, mask in enumerate(fresh):
                    last.append(remote(a, p, mask, 1, 7 + base + index))
    for copy in last:
        copy.wait_recv()
    for copy in started:
        copy.wait_send()


def weights_gather(collective_id, groups_count, *arrays):
    count = len(arrays)
    whole = pl.pallas_call(
        functools.partial(weights_gather_kernel, count, groups_count),
        out_shape=[
            jax.ShapeDtypeStruct((groups_count, RANKS) + a.shape, a.dtype) for a in arrays
        ],
        in_specs=[pl.BlockSpec(memory_space=pltpu.VMEM)] * count,
        out_specs=[pl.BlockSpec(memory_space=pl.ANY)] * count,
        scratch_shapes=[
            pltpu.SemaphoreType.DMA((count, 3, 15)),
            pltpu.SemaphoreType.DMA((count, 3, 15)),
            pltpu.SemaphoreType.DMA((max(groups_count - 1, 1), count)),
            pltpu.SemaphoreType.DMA((max(groups_count - 1, 1), count)),
            pltpu.SemaphoreType.DMA((count,)),
        ],
        compiler_params=pltpu.CompilerParams(collective_id=collective_id, has_side_effects=True),
        cost_estimate=pl.CostEstimate(flops=45000000000, bytes_accessed=2**24, transcendentals=0),
        name="weights_gather",
    )(*arrays)
    return [w.reshape(-1, w.shape[3]) for w in whole]


def add_block(target, source, at, start, size):
    groups, rows = source.shape[0], source.shape[1]
    columns = pl.ds(start, size)
    pieces = rows // 16

    def step(i, carry):
        lines = pl.ds(pl.multiple_of((i % pieces) * 16, 16), 16)
        index = (i // pieces, lines, columns)
        new = target[(at,) + index].astype(f32) + source[index].astype(f32)
        target[(at,) + index] = new.astype(target.dtype)
        return carry

    lax.fori_loop(0, groups * pieces, step, 0)


def weights_reduce_kernel(count, groups_count, *refs):
    ins = refs[:count]
    outs = refs[count : 2 * count]
    rest = refs[2 * count :]
    total, got0, got1, got2, got3, far_got = [rest[i * count : (i + 1) * count] for i in range(6)]
    sems, far_sems, seq_sems, local = rest[6 * count :]
    rank, peer = my_place()
    chip, core = rank // 2, rank % 2
    home, far = other_groups(groups_count)
    seq = lax.axis_index("seq")
    dp = lax.axis_index("dp")
    halves = [ref.shape[3] // 2 for ref in ins]
    parts = [column_parts(halves[a], a) for a in range(count)]

    def half_view(ref, a, rank_value):
        offset = pl.multiple_of((rank_value // RANKS) * halves[a], 128)
        return ref.at[:, rank_value % RANKS, :, pl.ds(offset, halves[a])]

    loads = []
    for a in range(count):
        for c in range(8):
            copy = pltpu.make_async_copy(
                half_view(ins[a], a, 2 * c + core), total[a].at[c], local.at[a, c]
            )
            copy.start()
            loads.append(copy)
    barrier = pltpu.get_barrier_semaphore()
    for there in [peer(bit) for bit in (1, 2, 4, 8)] + far:
        pl.semaphore_signal(barrier, inc=1, device_id=there, device_id_type=MESH)
    pl.semaphore_wait(barrier, 4 + len(far))

    started = []
    live = {}

    def send(a, p, stage, index, src, dst, bit):
        copy = pltpu.make_async_remote_copy(
            src_ref=src,
            dst_ref=dst,
            send_sem=sems.at[0, a, p, stage, index],
            recv_sem=sems.at[1, a, p, stage, index],
            device_id=peer(bit),
            device_id_type=MESH,
        )
        copy.start()
        started.append(copy)
        live.setdefault((a, p), []).append(copy)

    def chip_of(mask):
        return flip_mask(rank, mask) // 2

    for p in range(3):
        for a in range(count):
            columns = pl.ds(*parts[a][p])
            if parts[a][p][1]:
                for c in range(8):
                    send(
                        a, p, 0, c,
                        shard_view(ins[a], halves, a, p, 2 * c + 1 - core),
                        got0[a].at[c, :, :, columns],
                        1,
                    )
    for copy in loads:
        copy.wait()
    got = (got1, got2, got3)
    for stage in range(4):
        for p in range(3):
            for a in range(count):
                start, size = parts[a][p]
                if size == 0:
                    continue
                order = LINKS[p]
                columns = pl.ds(start, size)
                for copy in live.pop((a, p)):
                    copy.wait_recv()
                if stage == 0:

                    def over_chips(c, carry, a=a, start=start, size=size):
                        add_block(total[a], got0[a].at[c], c, start, size)
                        return carry

                    lax.fori_loop(0, 8, over_chips, 0)
                else:
                    for index, mask in enumerate(subsets(order[stage:])):
                        add_block(total[a], got[stage - 1][a].at[index], chip_of(mask), start, size)
                if stage < 3:
                    for index, mask in enumerate(subsets(order[stage + 1 :])):
                        send(
                            a, p, stage + 1, index,
                            total[a].at[chip_of(mask | order[stage]), :, :, columns],
                            got[stage][a].at[index, :, :, columns],
                            order[stage],
                        )
    waiting = []
    for k, there in enumerate(far):
        for a in range(count):
            copy = pltpu.make_async_remote_copy(
                src_ref=total[a].at[chip, there["dp"] // RANKS],
                dst_ref=far_got[a].at[k],
                send_sem=far_sems.at[0, k, a],
                recv_sem=far_sems.at[1, k, a],
                device_id=there,
                device_id_type=MESH,
            )
            copy.start()
            waiting.append(copy)
    for copy in waiting:
        copy.wait()
    last = []
    for a in range(count):
        columns = pl.ds(pl.multiple_of(seq * halves[a], 128), halves[a])
        value = total[a][chip, home].astype(f32)
        for k in range(len(far)):
            value = value + far_got[a][k].astype(f32)
        outs[a][:, columns] = value.astype(outs[a].dtype)
        copy = pltpu.make_async_remote_copy(
            src_ref=outs[a].at[:, columns],
            dst_ref=outs[a].at[:, columns],
            send_sem=seq_sems.at[0, a],
            recv_sem=seq_sems.at[1, a],
            device_id=peer(8),
            device_id_type=MESH,
        )
        copy.start()
        last.append(copy)
    for copy in last:
        copy.wait()
    for copy in started:
        copy.wait_send()


def weights_reduce(collective_id, groups_count, arrays):
    count = len(arrays)
    views = [a.reshape(groups_count, RANKS, -1, a.shape[1]) for a in arrays]
    rows = views[0].shape[2]
    halves = [a.shape[1] // 2 for a in arrays]

    def buffers(*lead):
        return [
            pltpu.VMEM(lead + (groups_count, rows, h), a.dtype) for h, a in zip(halves, arrays)
        ]

    far_buffers = [
        pltpu.VMEM((max(groups_count - 1, 1), rows, h), a.dtype) for h, a in zip(halves, arrays)
    ]
    dma = pltpu.SemaphoreType.DMA
    vmem = pl.BlockSpec(memory_space=pltpu.VMEM)
    any_space = pl.BlockSpec(memory_space=pl.ANY)
    return pl.pallas_call(
        functools.partial(weights_reduce_kernel, count, groups_count),
        out_shape=[jax.ShapeDtypeStruct((rows, a.shape[1]), a.dtype) for a in arrays],
        in_specs=[any_space] * count,
        out_specs=[vmem] * count,
        scratch_shapes=buffers(8) + buffers(8) + buffers(4) + buffers(2) + buffers(1) + far_buffers
        + [
            dma((2, count, 3, 4, 8)),
            dma((2, max(groups_count - 1, 1), count)),
            dma((2, count)),
            dma((count, 8)),
        ],
        compiler_params=pltpu.CompilerParams(
            collective_id=collective_id, has_side_effects=True, vmem_limit_bytes=48 * 2**20
        ),
        cost_estimate=pl.CostEstimate(flops=80000000000, bytes_accessed=2**24, transcendentals=0),
        name="weights_reduce",
    )(*views)


def expert_kernel(
    rows_ref, grad_ref, gate_ref, gate_up_ref, down_ref,
    mixed_ref, normed_ref, gate_grad_ref, weights_out,
    gate_up_sum, down_sum,
):
    step = pl.program_id(0)
    shards, each, width = rows_ref.shape
    count = shards * each
    rows = rows_ref[...].reshape(count, width)
    grad = grad_ref[...].reshape(count, width).astype(f32)
    gate = jnp.concatenate(
        [jnp.broadcast_to(gate_ref[i], (128, each)).T[:, :1] for i in range(shards)], 0
    )
    down = down_ref[...]
    gate_up_weight = gate_up_ref[...]
    gate_up = jnp.dot(rows, gate_up_weight, preferred_element_type=f32)
    gate_part, up_part = gate_up[:, :F], gate_up[:, F:]
    sigmoid = 1.0 / (1.0 + jnp.exp(-gate_part))
    silu = gate_part * sigmoid
    act = (silu * up_part).astype(bf16)
    out = jnp.dot(act, down, preferred_element_type=f32)
    inner = jnp.sum(out * grad, axis=-1, keepdims=True)
    for i in range(shards):
        line = jnp.broadcast_to(inner[i * each : (i + 1) * each], (each, 128)).T
        gate_grad_ref[i] = line[:8]
    mixed_ref[...] = (gate * out).astype(bf16).reshape(shards, each, width)
    expert_grad = (gate * grad).astype(bf16)
    across = (((1,), (1,)), ((), ()))
    over_rows = (((0,), (0,)), ((), ()))
    act_grad = lax.dot_general(expert_grad, down, across, preferred_element_type=f32)
    gate_up_grad = jnp.concatenate(
        [act_grad * up_part * (sigmoid * (1.0 + gate_part * (1.0 - sigmoid))), act_grad * silu], -1
    ).astype(bf16)
    normed_ref[...] = (
        lax.dot_general(gate_up_grad, gate_up_weight, across, preferred_element_type=f32)
        .astype(bf16)
        .reshape(shards, each, width)
    )

    @pl.when(step == 0)
    def _():
        gate_up_sum[...] = jnp.zeros_like(gate_up_sum)
        down_sum[...] = jnp.zeros_like(down_sum)

    down_sum[...] += lax.dot_general(act, expert_grad, over_rows, preferred_element_type=f32)
    gate_up_sum[...] += lax.dot_general(rows, gate_up_grad, over_rows, preferred_element_type=f32)

    @pl.when(step == pl.num_programs(0) - 1)
    def _():
        owners, _, columns = weights_out.shape
        first = gate_up_sum.shape[0] // owners
        weights_out[:, :first] = gate_up_sum[...].astype(bf16).reshape(owners, first, columns)
        weights_out[:, first:] = down_sum[...].astype(bf16).reshape(owners, -1, columns)


def expert_layer(n_dp, rows, grad, gate, gate_up_weight, down_weight):
    packed = (n_dp, (gate_up_weight.shape[0] + down_weight.shape[0]) // n_dp, rows.shape[2])
    each, width = rows.shape[1:]
    shards = 2
    tile = pl.BlockSpec((shards, each, width), lambda i: (i, 0, 0))
    whole = lambda shape: pl.BlockSpec(shape, lambda i: (0, 0))
    return pl.pallas_call(
        expert_kernel,
        grid=(GROUP // shards,),
        out_shape=[
            jax.ShapeDtypeStruct(rows.shape, bf16),
            jax.ShapeDtypeStruct(rows.shape, bf16),
            jax.ShapeDtypeStruct((GROUP, 8, each), f32),
            jax.ShapeDtypeStruct(packed, bf16),
        ],
        in_specs=[
            tile,
            tile,
            pl.BlockSpec((shards, 1, each), lambda i: (i, 0, 0)),
            whole(gate_up_weight.shape),
            whole(down_weight.shape),
        ],
        out_specs=[
            tile,
            tile,
            pl.BlockSpec((shards, 8, each), lambda i: (i, 0, 0)),
            pl.BlockSpec(packed, lambda i: (0, 0, 0)),
        ],
        scratch_shapes=[
            pltpu.VMEM(gate_up_weight.shape, f32),
            pltpu.VMEM(down_weight.shape, f32),
        ],
        compiler_params=pltpu.CompilerParams(vmem_limit_bytes=56 * 2**20),
        cost_estimate=pl.CostEstimate(flops=45000000000, bytes_accessed=2**24, transcendentals=0),
        name="expert_layer",
    )(rows, grad, gate, gate_up_weight, down_weight)


def inverse_rms(rows):
    return lax.rsqrt(jnp.mean(rows * rows, axis=-1, keepdims=True) + epsilon)


def norm_back(rows, gain_row, upstream):
    inverse = inverse_rms(rows)
    gain_grad = jnp.sum(upstream * rows * inverse, axis=0)
    scaled = upstream * gain_row
    rows_grad = inverse * scaled - rows * inverse**3 * jnp.mean(scaled * rows, axis=-1, keepdims=True)
    return rows_grad, gain_grad


def rope_tables(positions):
    half = HEAD_SIZE // 2
    frequency = rope_base ** (-(jnp.arange(half, dtype=f32) * 2.0) / HEAD_SIZE)
    angles = positions.astype(f32)[:, None] * frequency[None, :]
    cosine, sine = jnp.cos(angles), jnp.sin(angles)
    return jnp.concatenate([cosine, cosine], 1), jnp.concatenate([sine, sine], 1)


def rotary_apply(rows, cosine, sine):
    half = HEAD_SIZE // 2
    turned = jnp.concatenate([-rows[..., half:], rows[..., :half]], -1)
    return rows * cosine[:, None, :] + turned * sine[:, None, :]


def unrotate(rows, cosine, sine):
    half = HEAD_SIZE // 2
    scaled = rows * sine[:, None, :]
    back = jnp.concatenate([scaled[..., half:], -scaled[..., :half]], -1)
    return rows * cosine[:, None, :] + back


def make_body(n_dp):
    groups_count = n_dp // RANKS
    inside = [[g * RANKS + j for j in range(RANKS)] for g in range(groups_count)]
    half_experts = EXPERTS // 2

    def to_group(value, k):
        turn = [(d, (d + k * RANKS) % n_dp) for d in range(n_dp)]
        return lax.ppermute(value, "dp", turn)

    def expert_pieces(gate_up_shard, down_shard, seq_rank):
        mine = [
            jnp.swapaxes(lax.dynamic_slice_in_dim(w, seq_rank * half_experts, half_experts, axis=1), 0, 1)
            for w in (gate_up_shard, down_shard)
        ]
        return lax.all_to_all(
            jnp.concatenate(mine, 1), "dp", split_axis=0, concat_axis=0, tiled=True, axis_index_groups=inside
        )

    def from_groups(mine):
        home = lax.axis_index("dp") // RANKS
        parts = [to_group(mine, k) for k in range(groups_count - 1, 0, -1)] + [mine]
        ring = jnp.stack(parts + parts)
        start = (2 * groups_count - 1 - home) % groups_count
        whole = lax.dynamic_slice_in_dim(ring, start, groups_count, axis=0)
        return whole.reshape(-1, whole.shape[-1])

    def body(
        tokens, starts, routes, gain_one, query_key_value_weight, w_out,
        gain_two, w_router, w_gate_up, w_down, cotangent,
    ):
        count = tokens.shape[1]
        seq_rank = lax.axis_index("seq")
        expert = seq_rank * RANKS + lax.axis_index("dp") % RANKS
        query_columns = QUERY_HEADS * HEAD_SIZE
        key_columns = KEY_VALUE_HEADS * HEAD_SIZE
        group = QUERY_HEADS // KEY_VALUE_HEADS
        forward_pair, back_pair = [(0, 1)], [(1, 0)]

        tokens_before = lax.ppermute(tokens[0], "seq", forward_pair)
        starts_before = lax.ppermute(starts, "seq", forward_pair)
        spare = lambda value: jnp.pad(value, ((0, 0), (0, 128 - value.shape[1])))
        qkv_weight, out_weight, small = weights_gather(
            0,
            groups_count,
            query_key_value_weight,
            w_out,
            jnp.concatenate(
                [spare(w_router), spare(jnp.stack([gain_one, gain_two], 1))], 1
            ),
        )
        mine, qkv_weight, out_weight, small = lax.optimization_barrier(
            (expert_pieces(w_gate_up, w_down, seq_rank), qkv_weight, out_weight, small)
        )
        first = w_gate_up.shape[0]
        gate_up_mine = mine[:, :first]
        down_weight = from_groups(mine[:, first:])
        router_weight = small[:, :EXPERTS]
        gain_a = small[:, 128].astype(f32)
        gain_b = small[:, 129].astype(f32)

        token_rows = tokens[0].astype(f32)
        grad_output = cotangent[0].astype(f32)
        both = 2 * count
        index = jnp.arange(both, dtype=jnp.int32)
        flags = jnp.concatenate([starts_before[0], starts[0]])
        begins = (flags > 0) | (index == jnp.where(seq_rank == 0, count, 0))
        last_begin = jnp.max(
            jnp.where(begins[None, :] & (index[None, :] <= index[:, None]), index[None, :], 0), axis=1
        )
        cosine_all, sine_all = rope_tables(index - last_begin)
        cosine, sine = cosine_all[count:], sine_all[count:]

        rows_all = jnp.concatenate([tokens_before.astype(f32), token_rows], 0)
        normed_all = (rows_all * inverse_rms(rows_all) * gain_a).astype(bf16)
        normed_one = normed_all[count:]
        projected_q = jnp.dot(normed_one, qkv_weight[:, :query_columns], preferred_element_type=f32)
        projected_kv = jnp.dot(normed_all, qkv_weight[:, query_columns:], preferred_element_type=f32)
        queries = rotary_apply(
            projected_q.reshape(count, QUERY_HEADS, HEAD_SIZE), cosine, sine
        ).astype(bf16).reshape(count, KEY_VALUE_HEADS, group, HEAD_SIZE)
        keys = rotary_apply(
            projected_kv[:, :key_columns].reshape(both, KEY_VALUE_HEADS, HEAD_SIZE), cosine_all, sine_all
        ).astype(bf16)
        values = projected_kv[:, key_columns:].astype(bf16).reshape(both, KEY_VALUE_HEADS, HEAD_SIZE)

        scale = HEAD_SIZE ** (-0.5)
        allowed = (index[None, :] <= index[count:, None]) & (index[None, :] >= last_begin[count:, None])
        scores = jnp.einsum("qgrd,kgd->grqk", queries, keys, preferred_element_type=f32) * scale
        scores = jnp.where(allowed[None, None], scores, masked_score)
        top = jnp.max(scores, axis=-1, keepdims=True)
        exps = jnp.exp(scores - top)
        probs = exps / jnp.sum(exps, axis=-1, keepdims=True)
        probs_low = probs.astype(bf16)
        attended = jnp.einsum(
            "grqk,kgd->qgrd", probs_low, values, preferred_element_type=f32
        ).reshape(count, query_columns).astype(bf16)
        hidden = token_rows + jnp.dot(attended, out_weight, preferred_element_type=f32)
        normed_two = (hidden * inverse_rms(hidden) * gain_b).astype(bf16)
        logits = jnp.dot(normed_two, router_weight, preferred_element_type=f32)
        expert_ids = jnp.arange(EXPERTS, dtype=jnp.int32)
        chosen = jnp.any(routes[0][:, :, None] == expert_ids[None, None, :], axis=1)
        gates = jax.nn.softmax(jnp.where(chosen, logits, -jnp.inf), axis=-1)

        normed_two, gate_up_mine, down_weight = lax.optimization_barrier(
            (normed_two, gate_up_mine, down_weight)
        )
        gate_up_weight = from_groups(gate_up_mine)
        rows_in, gates_all, grad_all = group_gather(1, normed_two, gates.T, cotangent[0])
        gate = lax.dynamic_slice_in_dim(gates_all, expert, 1, axis=1)
        mixed_part, normed_part, gate_grad_part, expert_wgrads = expert_layer(
            n_dp, rows_in, grad_all, gate, gate_up_weight, down_weight
        )
        expert_wgrads = expert_wgrads.reshape((groups_count, RANKS) + expert_wgrads.shape[1:])
        mixed, normed_grad, gate_grad, expert_far = group_reduce(
            2, mixed_part, normed_part, gate_grad_part, expert_wgrads
        )
        expert_grads = lax.dynamic_index_in_dim(
            expert_wgrads, lax.axis_index("dp") // RANKS, 0, keepdims=False
        ).astype(f32)
        for k in range(groups_count - 1):
            expert_grads = expert_grads + expert_far[k].astype(f32)
        expert_grads = lax.all_to_all(
            expert_grads.astype(bf16), "dp", split_axis=0, concat_axis=0, tiled=True,
            axis_index_groups=inside,
        )
        gate_grad = gate_grad[:, 0].T

        over_rows = (((0,), (0,)), ((), ()))
        output = (hidden + mixed).astype(bf16)[None]
        stat_sums = jnp.stack([jnp.sum(hidden * hidden), jnp.sum(mixed * mixed)])
        weighted = jnp.where(chosen, gates * gate_grad, 0.0)
        logits_grad = weighted - gates * jnp.sum(weighted, axis=-1, keepdims=True)
        router_wide = router_weight.astype(f32)
        normed_grad = normed_grad + jnp.dot(logits_grad, router_wide.T, precision=highest)
        router_wgrad = jnp.dot(normed_two.astype(f32).T, logits_grad, precision=highest)
        hidden_branch, gain_two_grad = norm_back(hidden, gain_b, normed_grad)
        hidden_grad = grad_output + hidden_branch
        branch_low = hidden_grad.astype(bf16)
        out_wgrad = lax.dot_general(attended, branch_low, over_rows, preferred_element_type=f32)
        attended_grad = lax.dot_general(
            branch_low, out_weight, (((1,), (1,)), ((), ())), preferred_element_type=f32
        ).astype(bf16).reshape(count, KEY_VALUE_HEADS, group, HEAD_SIZE)

        prob_grad = jnp.einsum("qgrd,kgd->grqk", attended_grad, values, preferred_element_type=f32)
        delta = jnp.sum(probs * prob_grad, axis=-1, keepdims=True)
        score_grad = (probs * (prob_grad - delta)).astype(bf16)
        query_grad = (
            jnp.einsum("grqk,kgd->qgrd", score_grad, keys, preferred_element_type=f32) * scale
        ).reshape(count, QUERY_HEADS, HEAD_SIZE)
        key_grad = (
            jnp.einsum("grqk,qgrd->kgd", score_grad, queries, preferred_element_type=f32) * scale
        ).reshape(both, key_columns)
        value_grad = jnp.einsum(
            "grqk,qgrd->kgd", probs_low, attended_grad, preferred_element_type=f32
        ).reshape(both, key_columns)
        kv_grad = jnp.concatenate([key_grad, value_grad], 1)
        kv_back = lax.ppermute(kv_grad[:count].astype(bf16), "seq", back_pair)
        kv_grad = (kv_grad[count:] + kv_back.astype(f32)).astype(bf16).astype(f32)
        query_grad = query_grad.astype(bf16).astype(f32)
        query_back = unrotate(query_grad, cosine, sine).reshape(count, query_columns)
        key_back = unrotate(
            kv_grad[:, :key_columns].reshape(count, KEY_VALUE_HEADS, HEAD_SIZE), cosine, sine
        ).reshape(count, key_columns)
        projected_grad = jnp.concatenate([query_back, key_back, kv_grad[:, key_columns:]], 1).astype(bf16)
        qkv_wgrad = lax.dot_general(normed_one, projected_grad, over_rows, preferred_element_type=f32)
        normed_one_grad = lax.dot_general(
            projected_grad, qkv_weight, (((1,), (1,)), ((), ())), preferred_element_type=f32
        )
        rows_branch, gain_one_grad = norm_back(token_rows, gain_a, normed_one_grad)
        input_grad = (hidden_grad + rows_branch).astype(bf16)[None]

        little = jnp.concatenate(
            [spare(router_wgrad), spare(jnp.stack([gain_one_grad, gain_two_grad], 1))], 1
        )
        qkv_shard, out_shard, little = weights_reduce(
            3,
            groups_count,
            (qkv_wgrad.astype(bf16), out_wgrad.astype(bf16), little),
        )
        ours, theirs = expert_grads, lax.ppermute(expert_grads, "seq", [(0, 1), (1, 0)])
        experts_all = jnp.where(
            seq_rank == 0, jnp.stack([ours, theirs]), jnp.stack([theirs, ours])
        ).reshape((EXPERTS,) + ours.shape[1:])
        stat_sums = stat_sums + lax.ppermute(stat_sums, "seq", [(0, 1), (1, 0)])
        first = w_gate_up.shape[0]
        stream_rms = jnp.sqrt(stat_sums / (both * MODEL_WIDTH)).reshape(1, 2)
        return (
            output,
            input_grad,
            little[:, 128],
            qkv_shard.astype(f32),
            out_shard.astype(f32),
            little[:, 129],
            little[:, :EXPERTS],
            jnp.swapaxes(experts_all[:, :first], 0, 1).astype(f32),
            jnp.swapaxes(experts_all[:, first:], 0, 1).astype(f32),
            stream_rms,
        )

    return body


def solution(mesh):
    placed = (
        P("dp", "seq", None),
        P("dp", "seq"),
        P("dp", "seq", None),
        P("dp"),
        P("dp", None),
        P("dp", None),
        P("dp"),
        P("dp", None),
        P("dp", None, None),
        P("dp", None, None),
        P("dp", "seq", None),
    )
    return jax.shard_map(
        make_body(mesh.shape["dp"]),
        mesh=mesh,
        in_specs=placed,
        out_specs=(
            P("dp", "seq", None),
            P("dp", "seq", None),
            P("dp"),
            P("dp", None),
            P("dp", None),
            P("dp"),
            P("dp", None),
            P("dp", None, None),
            P("dp", None, None),
            P("dp", None),
        ),
        check_vma=False,
    )
```

```python
import functools

import jax
import jax.numpy as jnp
from jax import lax
from jax.experimental import pallas as pl
from jax.experimental.pallas import tpu as pltpu
from jax.sharding import PartitionSpec as P

MODEL_WIDTH = 1024
QUERY_HEADS = 16
KEY_VALUE_HEADS = 8
HEAD_SIZE = 64
F = 512
EXPERTS = 16
TOPK = 8
RANKS = 8
GROUP = 16

epsilon = 1e-06
rope_base = 10000.0
highest = lax.Precision.HIGHEST
masked_score = -1e30
f32 = jnp.float32
bf16 = jnp.bfloat16
MESH = pl.DeviceIdType.MESH

LINKS = ((8, 4, 2), (4, 2, 8), (2, 8, 4))


def flip(value, bit):
    return value + bit * (1 - 2 * ((value // bit) % 2))


def flip_mask(value, mask):
    for bit in (1, 2, 4, 8):
        if mask & bit:
            value = flip(value, bit)
    return value


def subsets(bits):
    out = [0]
    for bit in bits:
        out = out + [m | bit for m in out]
    return out


def row_parts(rows):
    first = (rows // 3 + 15) // 16 * 16
    second = (rows - first) // 2 // 16 * 16
    return ((0, first), (first, second), (first + second, rows - first - second))


def my_place():
    seq = lax.axis_index("seq")
    dp = lax.axis_index("dp")
    rank = seq * RANKS + dp % RANKS

    def peer(bit):
        if bit == 8:
            return {"seq": 1 - seq, "dp": dp}
        return {"seq": seq, "dp": flip(dp, bit)}

    return rank, peer


def meet(peer):
    barrier = pltpu.get_barrier_semaphore()
    for bit in (1, 2, 4, 8):
        pl.semaphore_signal(barrier, inc=1, device_id=peer(bit), device_id_type=MESH)
    pl.semaphore_wait(barrier, 4)


def gather_kernel(count, *refs):
    ins, outs = refs[:count], refs[count : 2 * count]
    send, recv, send_core, recv_core, local = refs[2 * count :]
    rank, peer = my_place()
    own = [
        pltpu.make_async_copy(ins[a], outs[a].at[rank], local.at[a]) for a in range(count)
    ]
    for copy in own:
        copy.start()
    meet(peer)
    parts = [row_parts(ref.shape[0]) for ref in ins]

    def remote(a, p, mask, bit, sems, index):
        start, size = parts[a][p]
        rows = pl.ds(start, size)
        shard = flip_mask(rank, mask)
        src = ins[a].at[rows] if mask == 0 else outs[a].at[shard, rows]
        return pltpu.make_async_remote_copy(
            src_ref=src,
            dst_ref=outs[a].at[shard, rows],
            send_sem=sems[0].at[a, p, index],
            recv_sem=sems[1].at[a, p, index],
            device_id=peer(bit),
            device_id_type=MESH,
        )

    started = []
    live = {}
    for step in range(4):
        for p in range(3):
            for a in range(count):
                if parts[a][p][1] == 0:
                    continue
                order = LINKS[p]
                if step > 0:
                    for copy in live.pop((a, p)):
                        copy.wait_recv()
                if step < 3:
                    now = []
                    for index, mask in enumerate(subsets(order[:step])):
                        copy = remote(a, p, mask, order[step], (send, recv), 2**step - 1 + index)
                        copy.start()
                        now.append(copy)
                        started.append(copy)
                    live[(a, p)] = now
                fresh = [0] if step == 0 else [m | order[step - 1] for m in subsets(order[: step - 1])]
                base = 0 if step == 0 else 2 ** (step - 1)
                for index, mask in enumerate(fresh):
                    copy = remote(a, p, mask, 1, (send_core, recv_core), base + index)
                    copy.start()
                    live.setdefault("core", []).append(copy)
    for copy in live["core"]:
        copy.wait()
    for copy in started:
        copy.wait_send()
    for copy in own:
        copy.wait()


def group_gather(collective_id, *arrays):
    count = len(arrays)
    return pl.pallas_call(
        functools.partial(gather_kernel, count),
        out_shape=[jax.ShapeDtypeStruct((GROUP,) + a.shape, a.dtype) for a in arrays],
        in_specs=[pl.BlockSpec(memory_space=pltpu.VMEM)] * count,
        out_specs=[pl.BlockSpec(memory_space=pl.ANY)] * count,
        scratch_shapes=[
            pltpu.SemaphoreType.DMA((count, 3, 7)),
            pltpu.SemaphoreType.DMA((count, 3, 7)),
            pltpu.SemaphoreType.DMA((count, 3, 8)),
            pltpu.SemaphoreType.DMA((count, 3, 8)),
            pltpu.SemaphoreType.DMA((count,)),
        ],
        compiler_params=pltpu.CompilerParams(collective_id=collective_id, has_side_effects=True),
        cost_estimate=pl.CostEstimate(flops=60000000000, bytes_accessed=2**24, transcendentals=0),
        name="group_gather",
    )(*arrays)


def add_rows(target, source, start, size):
    def step(i, carry):
        rows = pl.ds(pl.multiple_of(start + i * 16, 16), 16)
        target[rows] = (target[rows].astype(f32) + source[rows].astype(f32)).astype(target.dtype)
        return carry

    lax.fori_loop(0, size // 16, step, 0)


def reduce_kernel(
    mixed_ref, normed_ref, gate_ref, mixed_out, normed_out, gate_out,
    total, got0, got1, got2, got3, sems, gate_sems, local, own_gate,
):
    rank, peer = my_place()
    chip = rank // 2
    core = rank % 2
    parts = row_parts(mixed_ref.shape[1])
    ins = (mixed_ref, normed_ref)
    outs = (mixed_out, normed_out)
    loads = []
    for t in range(2):
        for c in range(8):
            copy = pltpu.make_async_copy(ins[t].at[2 * c + core], total.at[t, c], local.at[t, c])
            copy.start()
            loads.append(copy)
    barrier = pltpu.get_barrier_semaphore()
    seq = lax.axis_index("seq")
    dp = lax.axis_index("dp")
    everyone = [
        {"seq": 1 - seq if mask & 8 else seq, "dp": flip_mask(dp, mask & 7)} for mask in range(1, 16)
    ]
    for there in everyone:
        pl.semaphore_signal(barrier, inc=1, device_id=there, device_id_type=MESH)
    pl.semaphore_wait(barrier, 15)
    gates = []
    keep = pltpu.make_async_copy(gate_ref.at[rank], gate_out.at[rank], own_gate)
    keep.start()
    for mask, there in zip(range(1, 16), everyone):
        copy = pltpu.make_async_remote_copy(
            src_ref=gate_ref.at[flip_mask(rank, mask)],
            dst_ref=gate_out.at[rank],
            send_sem=gate_sems.at[0, mask],
            recv_sem=gate_sems.at[1, mask],
            device_id=there,
            device_id_type=MESH,
        )
        copy.start()
        gates.append(copy)

    started = []
    live = {}

    def send(t, p, stage, index, src, dst, bit):
        copy = pltpu.make_async_remote_copy(
            src_ref=src,
            dst_ref=dst,
            send_sem=sems.at[0, t, p, stage, index],
            recv_sem=sems.at[1, t, p, stage, index],
            device_id=peer(bit),
            device_id_type=MESH,
        )
        copy.start()
        started.append(copy)
        live.setdefault((t, p), []).append(copy)

    def chip_of(mask):
        return flip_mask(rank, mask) // 2

    for p in range(3):
        for t in range(2):
            rows = pl.ds(*parts[p])
            for c in range(8):
                send(
                    t, p, 0, c, ins[t].at[2 * c + 1 - core, rows], got0.at[t, c, rows], 1
                )
    for copy in loads:
        copy.wait()
    got = (got1, got2, got3)
    for stage in range(4):
        for p in range(3):
            for t in range(2):
                order = LINKS[p]
                rows = pl.ds(*parts[p])
                for copy in live.pop((t, p)):
                    copy.wait_recv()
                if stage == 0:

                    def over_chips(c, carry, t=t, p=p):
                        add_rows(total.at[t, c], got0.at[t, c], *parts[p])
                        return carry

                    lax.fori_loop(0, 8, over_chips, 0)
                else:
                    for index, mask in enumerate(subsets(order[stage:])):
                        if stage == 3:
                            outs[t][rows] = total[t, chip, rows].astype(f32) + got3[t, 0, rows].astype(f32)
                        else:
                            add_rows(
                                total.at[t, chip_of(mask)], got[stage - 1].at[t, index], *parts[p]
                            )
                if stage < 3:
                    for index, mask in enumerate(subsets(order[stage + 1 :])):
                        send(
                            t, p, stage + 1, index,
                            total.at[t, chip_of(mask | order[stage]), rows],
                            got[stage].at[t, index, rows],
                            order[stage],
                        )
    for copy in started:
        copy.wait_send()
    for copy in gates:
        copy.wait()
    keep.wait()


def group_reduce(collective_id, mixed, normed, gate_grad):
    rows, width = mixed.shape[1:]
    return pl.pallas_call(
        reduce_kernel,
        out_shape=[
            jax.ShapeDtypeStruct((rows, width), f32),
            jax.ShapeDtypeStruct((rows, width), f32),
            jax.ShapeDtypeStruct(gate_grad.shape, gate_grad.dtype),
        ],
        in_specs=[pl.BlockSpec(memory_space=pl.ANY)] * 3,
        out_specs=[
            pl.BlockSpec(memory_space=pltpu.VMEM),
            pl.BlockSpec(memory_space=pltpu.VMEM),
            pl.BlockSpec(memory_space=pl.ANY),
        ],
        scratch_shapes=[
            pltpu.VMEM((2, 8, rows, width), bf16),
            pltpu.VMEM((2, 8, rows, width), bf16),
            pltpu.VMEM((2, 4, rows, width), bf16),
            pltpu.VMEM((2, 2, rows, width), bf16),
            pltpu.VMEM((2, 1, rows, width), bf16),
            pltpu.SemaphoreType.DMA((2, 2, 3, 4, 8)),
            pltpu.SemaphoreType.DMA((2, 16)),
            pltpu.SemaphoreType.DMA((2, 8)),
            pltpu.SemaphoreType.DMA(()),
        ],
        compiler_params=pltpu.CompilerParams(
            collective_id=collective_id, has_side_effects=True, vmem_limit_bytes=48 * 2**20
        ),
        cost_estimate=pl.CostEstimate(flops=70000000000, bytes_accessed=2**24, transcendentals=0),
        name="group_reduce",
    )(mixed, normed, gate_grad)


def column_parts(half, which):
    tiles = half // 128
    if tiles == 1:
        sizes = (1, 0, 0)
    elif which % 2 == 0:
        big = -(-tiles // 3)
        sizes = (big, big, tiles - 2 * big)
    else:
        small = tiles // 3
        sizes = (small, small, tiles - 2 * small)
    out, start = [], 0
    for size in sizes:
        out.append((start * 128, size * 128))
        start += size
    return out


def shard_view(ref, halves, a, p, rank_value):
    start, size = column_parts(halves[a], a)[p]
    offset = pl.multiple_of((rank_value // RANKS) * halves[a] + start, 128)
    return ref.at[:, rank_value % RANKS, :, pl.ds(offset, size)]


def other_groups(groups_count):
    dp = lax.axis_index("dp")
    seq = lax.axis_index("seq")
    place, home = dp % RANKS, dp // RANKS
    return home, [
        {"seq": seq, "dp": ((home + k) % groups_count) * RANKS + place} for k in range(1, groups_count)
    ]


def weights_gather_kernel(count, groups_count, *refs):
    ins, outs = refs[:count], refs[count : 2 * count]
    send, recv, far_send, far_recv, local = refs[2 * count :]
    rank, peer = my_place()
    home, far = other_groups(groups_count)
    seq = lax.axis_index("seq")
    halves = [ref.shape[1] // 2 for ref in ins]

    def half(ref, a):
        return ref.at[:, pl.ds(pl.multiple_of(seq * halves[a], 128), halves[a])]

    def own_slot(a):
        columns = pl.ds(pl.multiple_of(seq * halves[a], 128), halves[a])
        return outs[a].at[home, rank % RANKS, :, columns]

    own = [pltpu.make_async_copy(half(ins[a], a), own_slot(a), local.at[a]) for a in range(count)]
    for copy in own:
        copy.start()
    barrier = pltpu.get_barrier_semaphore()
    for there in [peer(bit) for bit in (1, 2, 4, 8)] + far:
        pl.semaphore_signal(barrier, inc=1, device_id=there, device_id_type=MESH)
    pl.semaphore_wait(barrier, 4 + len(far))
    started, waiting = [], []
    for k, there in enumerate(far):
        for a in range(count):
            copy = pltpu.make_async_remote_copy(
                src_ref=half(ins[a], a),
                dst_ref=own_slot(a),
                send_sem=far_send.at[k, a],
                recv_sem=far_recv.at[k, a],
                device_id=there,
                device_id_type=MESH,
            )
            copy.start()
            started.append(copy)
            waiting.append(copy)
    for copy in own:
        copy.wait()
    for copy in waiting:
        copy.wait_recv()

    def remote(a, p, mask, bit, index):
        view = shard_view(outs[a], halves, a, p, flip_mask(rank, mask))
        copy = pltpu.make_async_remote_copy(
            src_ref=view,
            dst_ref=view,
            send_sem=send.at[a, p, index],
            recv_sem=recv.at[a, p, index],
            device_id=peer(bit),
            device_id_type=MESH,
        )
        copy.start()
        started.append(copy)
        return copy

    live = {}
    last = []
    for step in range(4):
        for p in range(3):
            for a in range(count):
                if column_parts(halves[a], a)[p][1] == 0:
                    continue
                order = LINKS[p]
                if step > 0:
                    for copy in live.pop((a, p)):
                        copy.wait_recv()
                if step < 3:
                    live[(a, p)] = [
                        remote(a, p, mask, order[step], 2**step - 1 + index)
                        for index, mask in enumerate(subsets(order[:step]))
                    ]
                fresh = [0] if step == 0 else [m | order[step - 1] for m in subsets(order[: step - 1])]
                base = 0 if step == 0 else 2 ** (step - 1)
                for index, mask in enumerate(fresh):
                    last.append(remote(a, p, mask, 1, 7 + base + index))
    for copy in last:
        copy.wait_recv()
    for copy in started:
        copy.wait_send()


def weights_gather(collective_id, groups_count, *arrays):
    count = len(arrays)
    whole = pl.pallas_call(
        functools.partial(weights_gather_kernel, count, groups_count),
        out_shape=[
            jax.ShapeDtypeStruct((groups_count, RANKS) + a.shape, a.dtype) for a in arrays
        ],
        in_specs=[pl.BlockSpec(memory_space=pltpu.VMEM)] * count,
        out_specs=[pl.BlockSpec(memory_space=pl.ANY)] * count,
        scratch_shapes=[
            pltpu.SemaphoreType.DMA((count, 3, 15)),
            pltpu.SemaphoreType.DMA((count, 3, 15)),
            pltpu.SemaphoreType.DMA((max(groups_count - 1, 1), count)),
            pltpu.SemaphoreType.DMA((max(groups_count - 1, 1), count)),
            pltpu.SemaphoreType.DMA((count,)),
        ],
        compiler_params=pltpu.CompilerParams(collective_id=collective_id, has_side_effects=True),
        cost_estimate=pl.CostEstimate(flops=45000000000, bytes_accessed=2**24, transcendentals=0),
        name="weights_gather",
    )(*arrays)
    return [w.reshape(-1, w.shape[3]) for w in whole]


def add_block(target, source, at, start, size):
    groups, rows = source.shape[0], source.shape[1]
    columns = pl.ds(start, size)
    pieces = rows // 16

    def step(i, carry):
        lines = pl.ds(pl.multiple_of((i % pieces) * 16, 16), 16)
        index = (i // pieces, lines, columns)
        new = target[(at,) + index].astype(f32) + source[index].astype(f32)
        target[(at,) + index] = new.astype(target.dtype)
        return carry

    lax.fori_loop(0, groups * pieces, step, 0)


def weights_reduce_kernel(count, groups_count, *refs):
    ins = refs[:count]
    pieces = refs[count]
    outs = refs[count + 1 : 2 * count + 1]
    whole = refs[2 * count + 1]
    rest = refs[2 * count + 2 :]
    total, got0, got1, got2, got3, far_got = [rest[i * count : (i + 1) * count] for i in range(6)]
    sems, far_sems, seq_sems, piece_sems, local, own_sems = rest[6 * count :]
    rank, peer = my_place()
    chip, core = rank // 2, rank % 2
    home, far = other_groups(groups_count)
    seq = lax.axis_index("seq")
    dp = lax.axis_index("dp")
    halves = [ref.shape[3] // 2 for ref in ins]
    parts = [column_parts(halves[a], a) for a in range(count)]

    def half_view(ref, a, rank_value):
        offset = pl.multiple_of((rank_value // RANKS) * halves[a], 128)
        return ref.at[:, rank_value % RANKS, :, pl.ds(offset, halves[a])]

    loads = []
    for a in range(count):
        for c in range(8):
            copy = pltpu.make_async_copy(
                half_view(ins[a], a, 2 * c + core), total[a].at[c], local.at[a, c]
            )
            copy.start()
            loads.append(copy)
    keep = pltpu.make_async_copy(pieces.at[rank % RANKS], whole.at[rank], own_sems)
    keep.start()
    barrier = pltpu.get_barrier_semaphore()
    everyone = [
        {"seq": 1 - seq if mask & 8 else seq, "dp": flip_mask(dp, mask & 7)} for mask in range(1, 16)
    ]
    for there in everyone + far:
        pl.semaphore_signal(barrier, inc=1, device_id=there, device_id_type=MESH)
    pl.semaphore_wait(barrier, 15 + len(far))

    started = []
    live = {}

    def send(a, p, stage, index, src, dst, bit):
        copy = pltpu.make_async_remote_copy(
            src_ref=src,
            dst_ref=dst,
            send_sem=sems.at[0, a, p, stage, index],
            recv_sem=sems.at[1, a, p, stage, index],
            device_id=peer(bit),
            device_id_type=MESH,
        )
        copy.start()
        started.append(copy)
        live.setdefault((a, p), []).append(copy)

    def chip_of(mask):
        return flip_mask(rank, mask) // 2

    for p in range(3):
        for a in range(count):
            columns = pl.ds(*parts[a][p])
            if parts[a][p][1]:
                for c in range(8):
                    send(
                        a, p, 0, c,
                        shard_view(ins[a], halves, a, p, 2 * c + 1 - core),
                        got0[a].at[c, :, :, columns],
                        1,
                    )
    arrivals = []

    def send_pieces(masks):
        for mask in masks:
            copy = pltpu.make_async_remote_copy(
                src_ref=pieces.at[flip_mask(rank, mask) % RANKS],
                dst_ref=whole.at[rank],
                send_sem=piece_sems.at[0, mask],
                recv_sem=piece_sems.at[1, mask],
                device_id=everyone[mask - 1],
                device_id_type=MESH,
            )
            copy.start()
            arrivals.append(copy)

    for copy in loads:
        copy.wait()
    got = (got1, got2, got3)
    for stage in range(4):
        for p in range(3):
            for a in range(count):
                start, size = parts[a][p]
                if size == 0:
                    continue
                order = LINKS[p]
                columns = pl.ds(start, size)
                for copy in live.pop((a, p)):
                    copy.wait_recv()
                if stage == 0:

                    def over_chips(c, carry, a=a, start=start, size=size):
                        add_block(total[a], got0[a].at[c], c, start, size)
                        return carry

                    lax.fori_loop(0, 8, over_chips, 0)
                else:
                    for index, mask in enumerate(subsets(order[stage:])):
                        add_block(total[a], got[stage - 1][a].at[index], chip_of(mask), start, size)
                if stage < 3:
                    for index, mask in enumerate(subsets(order[stage + 1 :])):
                        send(
                            a, p, stage + 1, index,
                            total[a].at[chip_of(mask | order[stage]), :, :, columns],
                            got[stage][a].at[index, :, :, columns],
                            order[stage],
                        )
        send_pieces(((1, 2, 4, 8), (3, 5, 9, 6), (10, 12, 7), ())[stage])
    waiting = []
    for k, there in enumerate(far):
        for a in range(count):
            copy = pltpu.make_async_remote_copy(
                src_ref=total[a].at[chip, there["dp"] // RANKS],
                dst_ref=far_got[a].at[k],
                send_sem=far_sems.at[0, k, a],
                recv_sem=far_sems.at[1, k, a],
                device_id=there,
                device_id_type=MESH,
            )
            copy.start()
            waiting.append(copy)
    send_pieces((14, 11, 13, 15))
    for copy in waiting:
        copy.wait()
    last = []
    for a in range(count):
        columns = pl.ds(pl.multiple_of(seq * halves[a], 128), halves[a])
        value = total[a][chip, home].astype(f32)
        for k in range(len(far)):
            value = value + far_got[a][k].astype(f32)
        outs[a][:, columns] = value.astype(outs[a].dtype)
        copy = pltpu.make_async_remote_copy(
            src_ref=outs[a].at[:, columns],
            dst_ref=outs[a].at[:, columns],
            send_sem=seq_sems.at[0, a],
            recv_sem=seq_sems.at[1, a],
            device_id=peer(8),
            device_id_type=MESH,
        )
        copy.start()
        last.append(copy)
    for copy in last + arrivals:
        copy.wait()
    for copy in started:
        copy.wait_send()
    keep.wait()


def weights_reduce(collective_id, groups_count, arrays, pieces):
    count = len(arrays)
    views = [a.reshape(groups_count, RANKS, -1, a.shape[1]) for a in arrays]
    rows = views[0].shape[2]
    halves = [a.shape[1] // 2 for a in arrays]

    def buffers(*lead):
        return [
            pltpu.VMEM(lead + (groups_count, rows, h), a.dtype) for h, a in zip(halves, arrays)
        ]

    far_buffers = [
        pltpu.VMEM((max(groups_count - 1, 1), rows, h), a.dtype) for h, a in zip(halves, arrays)
    ]
    dma = pltpu.SemaphoreType.DMA
    vmem = pl.BlockSpec(memory_space=pltpu.VMEM)
    any_space = pl.BlockSpec(memory_space=pl.ANY)
    return pl.pallas_call(
        functools.partial(weights_reduce_kernel, count, groups_count),
        out_shape=[jax.ShapeDtypeStruct((rows, a.shape[1]), a.dtype) for a in arrays]
        + [jax.ShapeDtypeStruct((EXPERTS,) + pieces.shape[1:], pieces.dtype)],
        in_specs=[any_space] * count + [vmem],
        out_specs=[vmem] * count + [any_space],
        scratch_shapes=buffers(8) + buffers(8) + buffers(4) + buffers(2) + buffers(1) + far_buffers
        + [
            dma((2, count, 3, 4, 8)),
            dma((2, max(groups_count - 1, 1), count)),
            dma((2, count)),
            dma((2, 16)),
            dma((count, 8)),
            dma(()),
        ],
        compiler_params=pltpu.CompilerParams(
            collective_id=collective_id, has_side_effects=True, vmem_limit_bytes=48 * 2**20
        ),
        cost_estimate=pl.CostEstimate(flops=80000000000, bytes_accessed=2**24, transcendentals=0),
        name="weights_reduce",
    )(*views, pieces)


def expert_kernel(
    rows_ref, grad_ref, gate_ref, gate_up_ref, down_ref,
    mixed_ref, normed_ref, gate_grad_ref, weights_out,
    gate_up_sum, down_sum,
):
    step = pl.program_id(0)
    shards, each, width = rows_ref.shape
    count = shards * each
    rows = rows_ref[...].reshape(count, width)
    grad = grad_ref[...].reshape(count, width).astype(f32)
    gate = jnp.concatenate(
        [jnp.broadcast_to(gate_ref[i], (128, each)).T[:, :1] for i in range(shards)], 0
    )
    down = down_ref[...]
    gate_up_weight = gate_up_ref[...]
    gate_up = jnp.dot(rows, gate_up_weight, preferred_element_type=f32)
    gate_part, up_part = gate_up[:, :F], gate_up[:, F:]
    sigmoid = 1.0 / (1.0 + jnp.exp(-gate_part))
    silu = gate_part * sigmoid
    act = (silu * up_part).astype(bf16)
    out = jnp.dot(act, down, preferred_element_type=f32)
    inner = jnp.sum(out * grad, axis=-1, keepdims=True)
    for i in range(shards):
        line = jnp.broadcast_to(inner[i * each : (i + 1) * each], (each, 128)).T
        gate_grad_ref[i] = line[:8]
    mixed_ref[...] = (gate * out).astype(bf16).reshape(shards, each, width)
    expert_grad = (gate * grad).astype(bf16)
    across = (((1,), (1,)), ((), ()))
    over_rows = (((0,), (0,)), ((), ()))
    act_grad = lax.dot_general(expert_grad, down, across, preferred_element_type=f32)
    gate_up_grad = jnp.concatenate(
        [act_grad * up_part * (sigmoid * (1.0 + gate_part * (1.0 - sigmoid))), act_grad * silu], -1
    ).astype(bf16)
    normed_ref[...] = (
        lax.dot_general(gate_up_grad, gate_up_weight, across, preferred_element_type=f32)
        .astype(bf16)
        .reshape(shards, each, width)
    )

    @pl.when(step == 0)
    def _():
        gate_up_sum[...] = jnp.zeros_like(gate_up_sum)
        down_sum[...] = jnp.zeros_like(down_sum)

    down_sum[...] += lax.dot_general(act, expert_grad, over_rows, preferred_element_type=f32)
    gate_up_sum[...] += lax.dot_general(rows, gate_up_grad, over_rows, preferred_element_type=f32)

    @pl.when(step == pl.num_programs(0) - 1)
    def _():
        owners, _, columns = weights_out.shape
        first = gate_up_sum.shape[0] // owners
        weights_out[:, :first] = gate_up_sum[...].astype(bf16).reshape(owners, first, columns)
        weights_out[:, first:] = down_sum[...].astype(bf16).reshape(owners, -1, columns)


def expert_layer(n_dp, rows, grad, gate, gate_up_weight, down_weight):
    packed = (n_dp, (gate_up_weight.shape[0] + down_weight.shape[0]) // n_dp, rows.shape[2])
    each, width = rows.shape[1:]
    shards = 2
    tile = pl.BlockSpec((shards, each, width), lambda i: (i, 0, 0))
    whole = lambda shape: pl.BlockSpec(shape, lambda i: (0, 0))
    return pl.pallas_call(
        expert_kernel,
        grid=(GROUP // shards,),
        out_shape=[
            jax.ShapeDtypeStruct(rows.shape, bf16),
            jax.ShapeDtypeStruct(rows.shape, bf16),
            jax.ShapeDtypeStruct((GROUP, 8, each), f32),
            jax.ShapeDtypeStruct(packed, bf16),
        ],
        in_specs=[
            tile,
            tile,
            pl.BlockSpec((shards, 1, each), lambda i: (i, 0, 0)),
            whole(gate_up_weight.shape),
            whole(down_weight.shape),
        ],
        out_specs=[
            tile,
            tile,
            pl.BlockSpec((shards, 8, each), lambda i: (i, 0, 0)),
            pl.BlockSpec(packed, lambda i: (0, 0, 0)),
        ],
        scratch_shapes=[
            pltpu.VMEM(gate_up_weight.shape, f32),
            pltpu.VMEM(down_weight.shape, f32),
        ],
        compiler_params=pltpu.CompilerParams(vmem_limit_bytes=56 * 2**20),
        cost_estimate=pl.CostEstimate(flops=45000000000, bytes_accessed=2**24, transcendentals=0),
        name="expert_layer",
    )(rows, grad, gate, gate_up_weight, down_weight)


def inverse_rms(rows):
    return lax.rsqrt(jnp.mean(rows * rows, axis=-1, keepdims=True) + epsilon)


def norm_back(rows, gain_row, upstream):
    inverse = inverse_rms(rows)
    gain_grad = jnp.sum(upstream * rows * inverse, axis=0)
    scaled = upstream * gain_row
    rows_grad = inverse * scaled - rows * inverse**3 * jnp.mean(scaled * rows, axis=-1, keepdims=True)
    return rows_grad, gain_grad


def rope_tables(positions):
    half = HEAD_SIZE // 2
    frequency = rope_base ** (-(jnp.arange(half, dtype=f32) * 2.0) / HEAD_SIZE)
    angles = positions.astype(f32)[:, None] * frequency[None, :]
    cosine, sine = jnp.cos(angles), jnp.sin(angles)
    return jnp.concatenate([cosine, cosine], 1), jnp.concatenate([sine, sine], 1)


def rotary_apply(rows, cosine, sine):
    half = HEAD_SIZE // 2
    turned = jnp.concatenate([-rows[..., half:], rows[..., :half]], -1)
    return rows * cosine[:, None, :] + turned * sine[:, None, :]


def unrotate(rows, cosine, sine):
    half = HEAD_SIZE // 2
    scaled = rows * sine[:, None, :]
    back = jnp.concatenate([scaled[..., half:], -scaled[..., :half]], -1)
    return rows * cosine[:, None, :] + back


def make_body(n_dp):
    groups_count = n_dp // RANKS
    inside = [[g * RANKS + j for j in range(RANKS)] for g in range(groups_count)]
    half_experts = EXPERTS // 2

    between = [[g * RANKS + j for g in range(groups_count)] for j in range(RANKS)]

    def expert_half(w, seq_rank):
        return lax.dynamic_slice_in_dim(w, seq_rank * half_experts, half_experts, axis=1)

    def expert_weights(halves, first):
        mine = halves.transpose(2, 0, 1, 3)
        mine = lax.all_to_all(
            mine, "dp", split_axis=0, concat_axis=0, tiled=True, axis_index_groups=inside
        )
        mine = jnp.swapaxes(mine, 0, 1)
        width = mine.shape[-1]
        return mine[:, :, :first].reshape(-1, width), mine[:, :, first:].reshape(-1, width)

    def body(
        tokens, starts, routes, gain_one, query_key_value_weight, w_out,
        gain_two, w_router, w_gate_up, w_down, cotangent,
    ):
        count = tokens.shape[1]
        seq_rank = lax.axis_index("seq")
        expert = seq_rank * RANKS + lax.axis_index("dp") % RANKS
        query_columns = QUERY_HEADS * HEAD_SIZE
        key_columns = KEY_VALUE_HEADS * HEAD_SIZE
        group = QUERY_HEADS // KEY_VALUE_HEADS
        forward_pair, back_pair = [(0, 1)], [(1, 0)]

        expert_halves = lax.all_gather(
            jnp.concatenate([expert_half(w_gate_up, seq_rank), expert_half(w_down, seq_rank)], 0),
            "dp", axis=0, axis_index_groups=between,
        )
        tokens_before = lax.ppermute(tokens[0], "seq", forward_pair)
        starts_before = lax.ppermute(starts, "seq", forward_pair)
        spare = lambda value: jnp.pad(value, ((0, 0), (0, 128 - value.shape[1])))
        qkv_weight, out_weight, small = weights_gather(
            0,
            groups_count,
            query_key_value_weight,
            w_out,
            jnp.concatenate(
                [spare(w_router), spare(jnp.stack([gain_one, gain_two], 1))], 1
            ),
        )
        router_weight = small[:, :EXPERTS]
        gain_a = small[:, 128].astype(f32)
        gain_b = small[:, 129].astype(f32)

        token_rows = tokens[0].astype(f32)
        grad_output = cotangent[0].astype(f32)
        both = 2 * count
        index = jnp.arange(both, dtype=jnp.int32)
        flags = jnp.concatenate([starts_before[0], starts[0]])
        begins = (flags > 0) | (index == jnp.where(seq_rank == 0, count, 0))
        last_begin = jnp.max(
            jnp.where(begins[None, :] & (index[None, :] <= index[:, None]), index[None, :], 0), axis=1
        )
        cosine_all, sine_all = rope_tables(index - last_begin)
        cosine, sine = cosine_all[count:], sine_all[count:]

        rows_all = jnp.concatenate([tokens_before.astype(f32), token_rows], 0)
        normed_all = (rows_all * inverse_rms(rows_all) * gain_a).astype(bf16)
        normed_one = normed_all[count:]
        projected_q = jnp.dot(normed_one, qkv_weight[:, :query_columns], preferred_element_type=f32)
        projected_kv = jnp.dot(normed_all, qkv_weight[:, query_columns:], preferred_element_type=f32)
        queries = rotary_apply(
            projected_q.reshape(count, QUERY_HEADS, HEAD_SIZE), cosine, sine
        ).astype(bf16).reshape(count, KEY_VALUE_HEADS, group, HEAD_SIZE)
        keys = rotary_apply(
            projected_kv[:, :key_columns].reshape(both, KEY_VALUE_HEADS, HEAD_SIZE), cosine_all, sine_all
        ).astype(bf16)
        values = projected_kv[:, key_columns:].astype(bf16).reshape(both, KEY_VALUE_HEADS, HEAD_SIZE)

        scale = HEAD_SIZE ** (-0.5)
        allowed = (index[None, :] <= index[count:, None]) & (index[None, :] >= last_begin[count:, None])
        scores = jnp.einsum("qgrd,kgd->grqk", queries, keys, preferred_element_type=f32) * scale
        scores = jnp.where(allowed[None, None], scores, masked_score)
        top = jnp.max(scores, axis=-1, keepdims=True)
        exps = jnp.exp(scores - top)
        probs = exps / jnp.sum(exps, axis=-1, keepdims=True)
        probs_low, expert_halves = lax.optimization_barrier((probs.astype(bf16), expert_halves))
        gate_up_weight, down_weight = expert_weights(expert_halves, w_gate_up.shape[0])
        attended = jnp.einsum(
            "grqk,kgd->qgrd", probs_low, values, preferred_element_type=f32
        ).reshape(count, query_columns).astype(bf16)
        hidden = token_rows + jnp.dot(attended, out_weight, preferred_element_type=f32)
        normed_two = (hidden * inverse_rms(hidden) * gain_b).astype(bf16)
        logits = jnp.dot(normed_two, router_weight, preferred_element_type=f32)
        expert_ids = jnp.arange(EXPERTS, dtype=jnp.int32)
        chosen = jnp.any(routes[0][:, :, None] == expert_ids[None, None, :], axis=1)
        gates = jax.nn.softmax(jnp.where(chosen, logits, -jnp.inf), axis=-1)

        normed_two, gate_up_weight, down_weight = lax.optimization_barrier(
            (normed_two, gate_up_weight, down_weight)
        )
        rows_in, gates_all, grad_all = group_gather(1, normed_two, gates.T, cotangent[0])
        gate = lax.dynamic_slice_in_dim(gates_all, expert, 1, axis=1)
        mixed_part, normed_part, gate_grad_part, expert_wgrads = expert_layer(
            n_dp, rows_in, grad_all, gate, gate_up_weight, down_weight
        )
        expert_grads = lax.psum_scatter(
            expert_wgrads, "dp", scatter_dimension=0, tiled=True, axis_index_groups=between
        )
        mixed, normed_grad, gate_grad = group_reduce(2, mixed_part, normed_part, gate_grad_part)
        gate_grad = gate_grad[:, 0].T

        over_rows = (((0,), (0,)), ((), ()))
        output = (hidden + mixed).astype(bf16)[None]
        stat_sums = jnp.stack([jnp.sum(hidden * hidden), jnp.sum(mixed * mixed)])
        weighted = jnp.where(chosen, gates * gate_grad, 0.0)
        logits_grad = weighted - gates * jnp.sum(weighted, axis=-1, keepdims=True)
        router_wide = router_weight.astype(f32)
        normed_grad = normed_grad + jnp.dot(logits_grad, router_wide.T, precision=highest)
        router_wgrad = jnp.dot(normed_two.astype(f32).T, logits_grad, precision=highest)
        hidden_branch, gain_two_grad = norm_back(hidden, gain_b, normed_grad)
        hidden_grad = grad_output + hidden_branch
        branch_low = hidden_grad.astype(bf16)
        out_wgrad = lax.dot_general(attended, branch_low, over_rows, preferred_element_type=f32)
        attended_grad = lax.dot_general(
            branch_low, out_weight, (((1,), (1,)), ((), ())), preferred_element_type=f32
        ).astype(bf16).reshape(count, KEY_VALUE_HEADS, group, HEAD_SIZE)

        attended_grad, expert_grads = lax.optimization_barrier((attended_grad, expert_grads))
        prob_grad = jnp.einsum("qgrd,kgd->grqk", attended_grad, values, preferred_element_type=f32)
        delta = jnp.sum(probs * prob_grad, axis=-1, keepdims=True)
        score_grad = (probs * (prob_grad - delta)).astype(bf16)
        query_grad = (
            jnp.einsum("grqk,kgd->qgrd", score_grad, keys, preferred_element_type=f32) * scale
        ).reshape(count, QUERY_HEADS, HEAD_SIZE)
        key_grad = (
            jnp.einsum("grqk,qgrd->kgd", score_grad, queries, preferred_element_type=f32) * scale
        ).reshape(both, key_columns)
        value_grad = jnp.einsum(
            "grqk,qgrd->kgd", probs_low, attended_grad, preferred_element_type=f32
        ).reshape(both, key_columns)
        kv_grad = jnp.concatenate([key_grad, value_grad], 1)
        kv_back = lax.ppermute(kv_grad[:count].astype(bf16), "seq", back_pair)
        kv_grad = (kv_grad[count:] + kv_back.astype(f32)).astype(bf16).astype(f32)
        query_grad = query_grad.astype(bf16).astype(f32)
        query_back = unrotate(query_grad, cosine, sine).reshape(count, query_columns)
        key_back = unrotate(
            kv_grad[:, :key_columns].reshape(count, KEY_VALUE_HEADS, HEAD_SIZE), cosine, sine
        ).reshape(count, key_columns)
        projected_grad = jnp.concatenate([query_back, key_back, kv_grad[:, key_columns:]], 1).astype(bf16)
        qkv_wgrad = lax.dot_general(normed_one, projected_grad, over_rows, preferred_element_type=f32)
        normed_one_grad = lax.dot_general(
            projected_grad, qkv_weight, (((1,), (1,)), ((), ())), preferred_element_type=f32
        )
        rows_branch, gain_one_grad = norm_back(token_rows, gain_a, normed_one_grad)
        input_grad = (hidden_grad + rows_branch).astype(bf16)[None]

        little = jnp.concatenate(
            [spare(router_wgrad), spare(jnp.stack([gain_one_grad, gain_two_grad], 1))], 1
        )
        qkv_shard, out_shard, little, experts_all = weights_reduce(
            3,
            groups_count,
            (qkv_wgrad.astype(bf16), out_wgrad.astype(bf16), little),
            expert_grads,
        )
        stat_sums = stat_sums + lax.ppermute(stat_sums, "seq", [(0, 1), (1, 0)])
        first = w_gate_up.shape[0]
        stream_rms = jnp.sqrt(stat_sums / (both * MODEL_WIDTH)).reshape(1, 2)
        return (
            output,
            input_grad,
            little[:, 128],
            qkv_shard.astype(f32),
            out_shard.astype(f32),
            little[:, 129],
            little[:, :EXPERTS],
            jnp.swapaxes(experts_all[:, :first], 0, 1).astype(f32),
            jnp.swapaxes(experts_all[:, first:], 0, 1).astype(f32),
            stream_rms,
        )

    return body


def solution(mesh):
    placed = (
        P("dp", "seq", None),
        P("dp", "seq"),
        P("dp", "seq", None),
        P("dp"),
        P("dp", None),
        P("dp", None),
        P("dp"),
        P("dp", None),
        P("dp", None, None),
        P("dp", None, None),
        P("dp", "seq", None),
    )
    return jax.shard_map(
        make_body(mesh.shape["dp"]),
        mesh=mesh,
        in_specs=placed,
        out_specs=(
            P("dp", "seq", None),
            P("dp", "seq", None),
            P("dp"),
            P("dp", None),
            P("dp", None),
            P("dp"),
            P("dp", None),
            P("dp", None, None),
            P("dp", None, None),
            P("dp", None),
        ),
        check_vma=False,
    )
```

```python
import functools

import jax
import jax.numpy as jnp
from jax import lax
from jax.experimental import pallas as pl
from jax.experimental.pallas import tpu as pltpu
from jax.sharding import PartitionSpec as P

MODEL_WIDTH = 1024
QUERY_HEADS = 16
KEY_VALUE_HEADS = 8
HEAD_SIZE = 64
F = 512
EXPERTS = 16
TOPK = 8
RANKS = 8
PLACES = 4
GROUP = 8
OWN = EXPERTS // GROUP

epsilon = 1e-06
rope_base = 10000.0
highest = lax.Precision.HIGHEST
masked_score = -1e30
f32 = jnp.float32
bf16 = jnp.bfloat16
MESH = pl.DeviceIdType.MESH

LINKS = ((8, 4, 2), (4, 2, 8), (2, 8, 4))
TOKEN_LINKS = ((4, 2), (2, 4))


def flip(value, bit):
    return value + bit * (1 - 2 * ((value // bit) % 2))


def flip_mask(value, mask):
    for bit in (1, 2, 4, 8):
        if mask & bit:
            value = flip(value, bit)
    return value


def subsets(bits):
    out = [0]
    for bit in bits:
        out = out + [m | bit for m in out]
    return out


def row_parts(rows):
    first = (rows // 2 + 15) // 16 * 16
    return ((0, first), (first, rows - first))


def my_place(places=RANKS):
    seq = lax.axis_index("seq")
    dp = lax.axis_index("dp")
    rank = seq * places + dp % places

    def peer(mask):
        return {
            "seq": 1 - seq if mask & places else seq,
            "dp": flip_mask(dp, mask & (places - 1)),
        }

    return rank, peer


def meet(devices):
    barrier = pltpu.get_barrier_semaphore()
    for there in devices:
        pl.semaphore_signal(barrier, inc=1, device_id=there, device_id_type=MESH)
    pl.semaphore_wait(barrier, len(devices))


def gather_kernel(count, *refs):
    ins, outs = refs[:count], refs[count : 2 * count]
    send, recv, send_core, recv_core, local = refs[2 * count :]
    rank, peer = my_place(PLACES)
    own = [
        pltpu.make_async_copy(ins[a], outs[a].at[rank], local.at[a]) for a in range(count)
    ]
    for copy in own:
        copy.start()
    meet([peer(bit) for bit in (1, 2, 4)])
    parts = [row_parts(ref.shape[0]) for ref in ins]

    def remote(a, p, mask, bit, sems, index):
        start, size = parts[a][p]
        rows = pl.ds(start, size)
        shard = flip_mask(rank, mask)
        src = ins[a].at[rows] if mask == 0 else outs[a].at[shard, rows]
        return pltpu.make_async_remote_copy(
            src_ref=src,
            dst_ref=outs[a].at[shard, rows],
            send_sem=sems[0].at[a, p, index],
            recv_sem=sems[1].at[a, p, index],
            device_id=peer(bit),
            device_id_type=MESH,
        )

    started = []
    live = {}
    for step in range(3):
        for p in range(2):
            for a in range(count):
                if parts[a][p][1] == 0:
                    continue
                order = TOKEN_LINKS[p]
                if step > 0:
                    for copy in live.pop((a, p)):
                        copy.wait_recv()
                if step < 2:
                    now = []
                    for index, mask in enumerate(subsets(order[:step])):
                        copy = remote(a, p, mask, order[step], (send, recv), 2**step - 1 + index)
                        copy.start()
                        now.append(copy)
                        started.append(copy)
                    live[(a, p)] = now
                fresh = [0] if step == 0 else [m | order[step - 1] for m in subsets(order[: step - 1])]
                base = 0 if step == 0 else 2 ** (step - 1)
                for index, mask in enumerate(fresh):
                    copy = remote(a, p, mask, 1, (send_core, recv_core), base + index)
                    copy.start()
                    live.setdefault("core", []).append(copy)
    for copy in live["core"]:
        copy.wait()
    for copy in started:
        copy.wait_send()
    for copy in own:
        copy.wait()


def group_gather(collective_id, *arrays):
    count = len(arrays)
    return pl.pallas_call(
        functools.partial(gather_kernel, count),
        out_shape=[jax.ShapeDtypeStruct((GROUP,) + a.shape, a.dtype) for a in arrays],
        in_specs=[pl.BlockSpec(memory_space=pltpu.VMEM)] * count,
        out_specs=[pl.BlockSpec(memory_space=pl.ANY)] * count,
        scratch_shapes=[
            pltpu.SemaphoreType.DMA((count, 2, 3)),
            pltpu.SemaphoreType.DMA((count, 2, 3)),
            pltpu.SemaphoreType.DMA((count, 2, 4)),
            pltpu.SemaphoreType.DMA((count, 2, 4)),
            pltpu.SemaphoreType.DMA((count,)),
        ],
        compiler_params=pltpu.CompilerParams(collective_id=collective_id, has_side_effects=True),
        cost_estimate=pl.CostEstimate(flops=60000000000, bytes_accessed=2**24, transcendentals=0),
        name="group_gather",
    )(*arrays)


def add_rows(target, source, start, size):
    def step(i, carry):
        rows = pl.ds(pl.multiple_of(start + i * 16, 16), 16)
        target[rows] = (target[rows].astype(f32) + source[rows].astype(f32)).astype(target.dtype)
        return carry

    lax.fori_loop(0, size // 16, step, 0)


def reduce_kernel(
    mixed_ref, normed_ref, gate_ref, mixed_out, normed_out, gate_out,
    total, got0, got1, got2, sems, gate_sems, local, own_gate,
):
    rank, peer = my_place(PLACES)
    chip = rank // 2
    core = rank % 2
    parts = row_parts(mixed_ref.shape[1])
    ins = (mixed_ref, normed_ref)
    outs = (mixed_out, normed_out)
    loads = []
    for t in range(2):
        for c in range(4):
            copy = pltpu.make_async_copy(ins[t].at[2 * c + core], total.at[t, c], local.at[t, c])
            copy.start()
            loads.append(copy)
    everyone = [peer(mask) for mask in range(1, GROUP)]
    meet(everyone)
    gates = []
    keep = pltpu.make_async_copy(gate_ref.at[rank], gate_out.at[rank], own_gate)
    keep.start()
    for mask, there in zip(range(1, GROUP), everyone):
        copy = pltpu.make_async_remote_copy(
            src_ref=gate_ref.at[flip_mask(rank, mask)],
            dst_ref=gate_out.at[rank],
            send_sem=gate_sems.at[0, mask],
            recv_sem=gate_sems.at[1, mask],
            device_id=there,
            device_id_type=MESH,
        )
        copy.start()
        gates.append(copy)

    started = []
    live = {}

    def send(t, p, stage, index, src, dst, bit):
        copy = pltpu.make_async_remote_copy(
            src_ref=src,
            dst_ref=dst,
            send_sem=sems.at[0, t, p, stage, index],
            recv_sem=sems.at[1, t, p, stage, index],
            device_id=peer(bit),
            device_id_type=MESH,
        )
        copy.start()
        started.append(copy)
        live.setdefault((t, p), []).append(copy)

    def chip_of(mask):
        return flip_mask(rank, mask) // 2

    for p in range(2):
        for t in range(2):
            rows = pl.ds(*parts[p])
            for c in range(4):
                send(
                    t, p, 0, c, ins[t].at[2 * c + 1 - core, rows], got0.at[t, c, rows], 1
                )
    for copy in loads:
        copy.wait()
    got = (got1, got2)
    for stage in range(3):
        for p in range(2):
            for t in range(2):
                order = TOKEN_LINKS[p]
                rows = pl.ds(*parts[p])
                for copy in live.pop((t, p)):
                    copy.wait_recv()
                if stage == 0:

                    def over_chips(c, carry, t=t, p=p):
                        add_rows(total.at[t, c], got0.at[t, c], *parts[p])
                        return carry

                    lax.fori_loop(0, 4, over_chips, 0)
                else:
                    for index, mask in enumerate(subsets(order[stage:])):
                        if stage == 2:
                            outs[t][rows] = total[t, chip, rows].astype(f32) + got2[t, 0, rows].astype(f32)
                        else:
                            add_rows(
                                total.at[t, chip_of(mask)], got[stage - 1].at[t, index], *parts[p]
                            )
                if stage < 2:
                    for index, mask in enumerate(subsets(order[stage + 1 :])):
                        send(
                            t, p, stage + 1, index,
                            total.at[t, chip_of(mask | order[stage]), rows],
                            got[stage].at[t, index, rows],
                            order[stage],
                        )
    for copy in started:
        copy.wait_send()
    for copy in gates:
        copy.wait()
    keep.wait()


def group_reduce(collective_id, mixed, normed, gate_grad):
    rows, width = mixed.shape[1:]
    return pl.pallas_call(
        reduce_kernel,
        out_shape=[
            jax.ShapeDtypeStruct((rows, width), f32),
            jax.ShapeDtypeStruct((rows, width), f32),
            jax.ShapeDtypeStruct(gate_grad.shape, gate_grad.dtype),
        ],
        in_specs=[pl.BlockSpec(memory_space=pl.ANY)] * 3,
        out_specs=[
            pl.BlockSpec(memory_space=pltpu.VMEM),
            pl.BlockSpec(memory_space=pltpu.VMEM),
            pl.BlockSpec(memory_space=pl.ANY),
        ],
        scratch_shapes=[
            pltpu.VMEM((2, 4, rows, width), bf16),
            pltpu.VMEM((2, 4, rows, width), bf16),
            pltpu.VMEM((2, 2, rows, width), bf16),
            pltpu.VMEM((2, 1, rows, width), bf16),
            pltpu.SemaphoreType.DMA((2, 2, 2, 3, 4)),
            pltpu.SemaphoreType.DMA((2, GROUP)),
            pltpu.SemaphoreType.DMA((2, 4)),
            pltpu.SemaphoreType.DMA(()),
        ],
        compiler_params=pltpu.CompilerParams(
            collective_id=collective_id, has_side_effects=True, vmem_limit_bytes=48 * 2**20
        ),
        cost_estimate=pl.CostEstimate(flops=70000000000, bytes_accessed=2**24, transcendentals=0),
        name="group_reduce",
    )(mixed, normed, gate_grad)


def column_parts(half, which):
    tiles = half // 128
    if tiles == 1:
        sizes = (1, 0, 0)
    elif which % 2 == 0:
        big = -(-tiles // 3)
        sizes = (big, big, tiles - 2 * big)
    else:
        small = tiles // 3
        sizes = (small, small, tiles - 2 * small)
    out, start = [], 0
    for size in sizes:
        out.append((start * 128, size * 128))
        start += size
    return out


def shard_view(ref, halves, a, p, rank_value):
    start, size = column_parts(halves[a], a)[p]
    offset = pl.multiple_of((rank_value // RANKS) * halves[a] + start, 128)
    return ref.at[:, rank_value % RANKS, :, pl.ds(offset, size)]


def other_groups(groups_count):
    dp = lax.axis_index("dp")
    seq = lax.axis_index("seq")
    place, home = dp % RANKS, dp // RANKS
    return home, [
        {"seq": seq, "dp": ((home + k) % groups_count) * RANKS + place} for k in range(1, groups_count)
    ]


def weights_gather_kernel(count, groups_count, *refs):
    ins, outs = refs[:count], refs[count : 2 * count]
    send, recv, far_send, far_recv, local = refs[2 * count :]
    rank, peer = my_place()
    home, far = other_groups(groups_count)
    seq = lax.axis_index("seq")
    halves = [ref.shape[1] // 2 for ref in ins]

    def half(ref, a):
        return ref.at[:, pl.ds(pl.multiple_of(seq * halves[a], 128), halves[a])]

    def own_slot(a):
        columns = pl.ds(pl.multiple_of(seq * halves[a], 128), halves[a])
        return outs[a].at[home, rank % RANKS, :, columns]

    own = [pltpu.make_async_copy(half(ins[a], a), own_slot(a), local.at[a]) for a in range(count)]
    for copy in own:
        copy.start()
    meet([peer(bit) for bit in (1, 2, 4, 8)] + far)
    started, waiting = [], []
    for k, there in enumerate(far):
        for a in range(count):
            copy = pltpu.make_async_remote_copy(
                src_ref=half(ins[a], a),
                dst_ref=own_slot(a),
                send_sem=far_send.at[k, a],
                recv_sem=far_recv.at[k, a],
                device_id=there,
                device_id_type=MESH,
            )
            copy.start()
            started.append(copy)
            waiting.append(copy)
    for copy in own:
        copy.wait()
    for copy in waiting:
        copy.wait_recv()

    def remote(a, p, mask, bit, index):
        view = shard_view(outs[a], halves, a, p, flip_mask(rank, mask))
        copy = pltpu.make_async_remote_copy(
            src_ref=view,
            dst_ref=view,
            send_sem=send.at[a, p, index],
            recv_sem=recv.at[a, p, index],
            device_id=peer(bit),
            device_id_type=MESH,
        )
        copy.start()
        started.append(copy)
        return copy

    live = {}
    last = []
    for step in range(4):
        for p in range(3):
            for a in range(count):
                if column_parts(halves[a], a)[p][1] == 0:
                    continue
                order = LINKS[p]
                if step > 0:
                    for copy in live.pop((a, p)):
                        copy.wait_recv()
                if step < 3:
                    live[(a, p)] = [
                        remote(a, p, mask, order[step], 2**step - 1 + index)
                        for index, mask in enumerate(subsets(order[:step]))
                    ]
                fresh = [0] if step == 0 else [m | order[step - 1] for m in subsets(order[: step - 1])]
                base = 0 if step == 0 else 2 ** (step - 1)
                for index, mask in enumerate(fresh):
                    last.append(remote(a, p, mask, 1, 7 + base + index))
    for copy in last:
        copy.wait_recv()
    for copy in started:
        copy.wait_send()


def weights_gather(collective_id, groups_count, *arrays):
    count = len(arrays)
    whole = pl.pallas_call(
        functools.partial(weights_gather_kernel, count, groups_count),
        out_shape=[
            jax.ShapeDtypeStruct((groups_count, RANKS) + a.shape, a.dtype) for a in arrays
        ],
        in_specs=[pl.BlockSpec(memory_space=pltpu.VMEM)] * count,
        out_specs=[pl.BlockSpec(memory_space=pl.ANY)] * count,
        scratch_shapes=[
            pltpu.SemaphoreType.DMA((count, 3, 15)),
            pltpu.SemaphoreType.DMA((count, 3, 15)),
            pltpu.SemaphoreType.DMA((max(groups_count - 1, 1), count)),
            pltpu.SemaphoreType.DMA((max(groups_count - 1, 1), count)),
            pltpu.SemaphoreType.DMA((count,)),
        ],
        compiler_params=pltpu.CompilerParams(collective_id=collective_id, has_side_effects=True),
        cost_estimate=pl.CostEstimate(flops=45000000000, bytes_accessed=2**24, transcendentals=0),
        name="weights_gather",
    )(*arrays)
    return [w.reshape(-1, w.shape[3]) for w in whole]


def add_block(target, source, at, start, size):
    groups, rows = source.shape[0], source.shape[1]
    columns = pl.ds(start, size)
    pieces = rows // 16

    def step(i, carry):
        lines = pl.ds(pl.multiple_of((i % pieces) * 16, 16), 16)
        index = (i // pieces, lines, columns)
        new = target[(at,) + index].astype(f32) + source[index].astype(f32)
        target[(at,) + index] = new.astype(target.dtype)
        return carry

    lax.fori_loop(0, groups * pieces, step, 0)


def weights_reduce_kernel(count, groups_count, *refs):
    ins = refs[:count]
    pieces = refs[count]
    outs = refs[count + 1 : 2 * count + 1]
    whole = refs[2 * count + 1]
    rest = refs[2 * count + 2 :]
    total, got0, got1, got2, got3, far_got = [rest[i * count : (i + 1) * count] for i in range(6)]
    sems, far_sems, seq_sems, piece_sems, local, own_sems = rest[6 * count :]
    rank, peer = my_place()
    chip, core = rank // 2, rank % 2
    home, far = other_groups(groups_count)
    seq = lax.axis_index("seq")
    dp = lax.axis_index("dp")
    halves = [ref.shape[3] // 2 for ref in ins]
    parts = [column_parts(halves[a], a) for a in range(count)]

    def half_view(ref, a, rank_value):
        offset = pl.multiple_of((rank_value // RANKS) * halves[a], 128)
        return ref.at[:, rank_value % RANKS, :, pl.ds(offset, halves[a])]

    loads = []
    for a in range(count):
        for c in range(8):
            copy = pltpu.make_async_copy(
                half_view(ins[a], a, 2 * c + core), total[a].at[c], local.at[a, c]
            )
            copy.start()
            loads.append(copy)
    place = dp % PLACES
    slot = seq * PLACES + place
    keep = pltpu.make_async_copy(pieces.at[place], whole.at[slot], own_sems)
    keep.start()
    masks = (1, 2, 4, 8, 3, 9, 10, 11)
    meet([peer(mask) for mask in masks] + far)

    started = []
    live = {}

    def send(a, p, stage, index, src, dst, bit):
        copy = pltpu.make_async_remote_copy(
            src_ref=src,
            dst_ref=dst,
            send_sem=sems.at[0, a, p, stage, index],
            recv_sem=sems.at[1, a, p, stage, index],
            device_id=peer(bit),
            device_id_type=MESH,
        )
        copy.start()
        started.append(copy)
        live.setdefault((a, p), []).append(copy)

    def chip_of(mask):
        return flip_mask(rank, mask) // 2

    for p in range(3):
        for a in range(count):
            columns = pl.ds(*parts[a][p])
            if parts[a][p][1]:
                for c in range(8):
                    send(
                        a, p, 0, c,
                        shard_view(ins[a], halves, a, p, 2 * c + 1 - core),
                        got0[a].at[c, :, :, columns],
                        1,
                    )
    arrivals = []

    def send_pieces(masks):
        for mask in masks:
            copy = pltpu.make_async_remote_copy(
                src_ref=pieces.at[flip_mask(place, mask & 3)],
                dst_ref=whole.at[slot],
                send_sem=piece_sems.at[0, mask],
                recv_sem=piece_sems.at[1, mask],
                device_id=peer(mask),
                device_id_type=MESH,
            )
            copy.start()
            arrivals.append(copy)

    for copy in loads:
        copy.wait()
    got = (got1, got2, got3)
    for stage in range(4):
        for p in range(3):
            for a in range(count):
                start, size = parts[a][p]
                if size == 0:
                    continue
                order = LINKS[p]
                columns = pl.ds(start, size)
                for copy in live.pop((a, p)):
                    copy.wait_recv()
                if stage == 0:

                    def over_chips(c, carry, a=a, start=start, size=size):
                        add_block(total[a], got0[a].at[c], c, start, size)
                        return carry

                    lax.fori_loop(0, 8, over_chips, 0)
                else:
                    for index, mask in enumerate(subsets(order[stage:])):
                        add_block(total[a], got[stage - 1][a].at[index], chip_of(mask), start, size)
                if stage < 3:
                    for index, mask in enumerate(subsets(order[stage + 1 :])):
                        send(
                            a, p, stage + 1, index,
                            total[a].at[chip_of(mask | order[stage]), :, :, columns],
                            got[stage][a].at[index, :, :, columns],
                            order[stage],
                        )
        send_pieces(((1, 2, 8), (9, 10), (3,), (11,))[stage])
    waiting = []
    for k, there in enumerate(far):
        for a in range(count):
            copy = pltpu.make_async_remote_copy(
                src_ref=total[a].at[chip, there["dp"] // RANKS],
                dst_ref=far_got[a].at[k],
                send_sem=far_sems.at[0, k, a],
                recv_sem=far_sems.at[1, k, a],
                device_id=there,
                device_id_type=MESH,
            )
            copy.start()
            waiting.append(copy)
    for copy in waiting:
        copy.wait()
    last = []
    for a in range(count):
        columns = pl.ds(pl.multiple_of(seq * halves[a], 128), halves[a])
        value = total[a][chip, home].astype(f32)
        for k in range(len(far)):
            value = value + far_got[a][k].astype(f32)
        outs[a][:, columns] = value.astype(outs[a].dtype)
        copy = pltpu.make_async_remote_copy(
            src_ref=outs[a].at[:, columns],
            dst_ref=outs[a].at[:, columns],
            send_sem=seq_sems.at[0, a],
            recv_sem=seq_sems.at[1, a],
            device_id=peer(8),
            device_id_type=MESH,
        )
        copy.start()
        last.append(copy)
    for copy in last + arrivals:
        copy.wait()
    for copy in started:
        copy.wait_send()
    keep.wait()


def weights_reduce(collective_id, groups_count, arrays, pieces):
    count = len(arrays)
    views = [a.reshape(groups_count, RANKS, -1, a.shape[1]) for a in arrays]
    rows = views[0].shape[2]
    halves = [a.shape[1] // 2 for a in arrays]

    def buffers(*lead):
        return [
            pltpu.VMEM(lead + (groups_count, rows, h), a.dtype) for h, a in zip(halves, arrays)
        ]

    far_buffers = [
        pltpu.VMEM((max(groups_count - 1, 1), rows, h), a.dtype) for h, a in zip(halves, arrays)
    ]
    dma = pltpu.SemaphoreType.DMA
    vmem = pl.BlockSpec(memory_space=pltpu.VMEM)
    any_space = pl.BlockSpec(memory_space=pl.ANY)
    return pl.pallas_call(
        functools.partial(weights_reduce_kernel, count, groups_count),
        out_shape=[jax.ShapeDtypeStruct((rows, a.shape[1]), a.dtype) for a in arrays]
        + [jax.ShapeDtypeStruct((GROUP,) + pieces.shape[1:], pieces.dtype)],
        in_specs=[any_space] * count + [vmem],
        out_specs=[vmem] * count + [any_space],
        scratch_shapes=buffers(8) + buffers(8) + buffers(4) + buffers(2) + buffers(1) + far_buffers
        + [
            dma((2, count, 3, 4, 8)),
            dma((2, max(groups_count - 1, 1), count)),
            dma((2, count)),
            dma((2, 16)),
            dma((count, 8)),
            dma(()),
        ],
        compiler_params=pltpu.CompilerParams(
            collective_id=collective_id, has_side_effects=True, vmem_limit_bytes=48 * 2**20
        ),
        cost_estimate=pl.CostEstimate(flops=80000000000, bytes_accessed=2**24, transcendentals=0),
        name="weights_reduce",
    )(*views, pieces)


def expert_kernel(
    first, rows_ref, grad_ref, gate_ref, weights_ref,
    mixed_ref, normed_ref, gate_grad_ref, weights_out,
    gate_up_sum, down_sum, mixed_sum, normed_sum,
):
    step = pl.program_id(0)
    expert = pl.program_id(1)
    shards, each, width = rows_ref.shape
    count = shards * each
    rows = rows_ref[...].reshape(count, width)
    grad = grad_ref[...].reshape(count, width).astype(f32)
    gate = jnp.concatenate(
        [
            jnp.broadcast_to(gate_ref[i, pl.ds(expert, 1)], (128, each)).T[:, :1]
            for i in range(shards)
        ],
        0,
    )
    gate_up_weight = weights_ref[:, expert, :first].reshape(-1, width)
    down = weights_ref[:, expert, first:].reshape(-1, width)
    gate_up = jnp.dot(rows, gate_up_weight, preferred_element_type=f32)
    gate_part, up_part = gate_up[:, :F], gate_up[:, F:]
    sigmoid = 1.0 / (1.0 + jnp.exp(-gate_part))
    silu = gate_part * sigmoid
    act = (silu * up_part).astype(bf16)
    out = jnp.dot(act, down, preferred_element_type=f32)
    inner = jnp.sum(out * grad, axis=-1, keepdims=True)
    for i in range(shards):
        line = jnp.broadcast_to(inner[i * each : (i + 1) * each], (each, 128)).T
        gate_grad_ref[i, pl.ds(expert, 1)] = line[:1]
    mixed = gate * out
    expert_grad = (gate * grad).astype(bf16)
    across = (((1,), (1,)), ((), ()))
    over_rows = (((0,), (0,)), ((), ()))
    act_grad = lax.dot_general(expert_grad, down, across, preferred_element_type=f32)
    gate_up_grad = jnp.concatenate(
        [act_grad * up_part * (sigmoid * (1.0 + gate_part * (1.0 - sigmoid))), act_grad * silu], -1
    ).astype(bf16)
    normed = lax.dot_general(gate_up_grad, gate_up_weight, across, preferred_element_type=f32)

    @pl.when(expert == 0)
    def _():
        mixed_sum[...] = mixed
        normed_sum[...] = normed

    @pl.when(expert > 0)
    def _():
        mixed_sum[...] += mixed
        normed_sum[...] += normed

    @pl.when(expert == OWN - 1)
    def _():
        mixed_ref[...] = mixed_sum[...].astype(bf16).reshape(shards, each, width)
        normed_ref[...] = normed_sum[...].astype(bf16).reshape(shards, each, width)

    @pl.when(step == 0)
    def _():
        gate_up_sum[expert] = jnp.zeros_like(gate_up_sum[0])
        down_sum[expert] = jnp.zeros_like(down_sum[0])

    down_sum[expert] += lax.dot_general(act, expert_grad, over_rows, preferred_element_type=f32)
    gate_up_sum[expert] += lax.dot_general(rows, gate_up_grad, over_rows, preferred_element_type=f32)

    @pl.when(step == pl.num_programs(0) - 1)
    def _():
        owners = weights_out.shape[0]
        weights_out[:, expert, :first] = gate_up_sum[expert].astype(bf16).reshape(owners, first, width)
        weights_out[:, expert, first:] = down_sum[expert].astype(bf16).reshape(owners, -1, width)


def expert_layer(first, rows, grad, gate, weights):
    each, width = rows.shape[1:]
    shards = 2
    owners = weights.shape[0]
    tile = pl.BlockSpec((shards, each, width), lambda i, e: (i, 0, 0))
    whole = pl.BlockSpec(weights.shape, lambda i, e: (0, 0, 0, 0), pipeline_mode=pl.Buffered(1))
    return pl.pallas_call(
        functools.partial(expert_kernel, first),
        grid=(GROUP // shards, OWN),
        out_shape=[
            jax.ShapeDtypeStruct(rows.shape, bf16),
            jax.ShapeDtypeStruct(rows.shape, bf16),
            jax.ShapeDtypeStruct((GROUP, 8, each), f32),
            jax.ShapeDtypeStruct(weights.shape, bf16),
        ],
        in_specs=[
            tile,
            tile,
            pl.BlockSpec((shards, OWN, each), lambda i, e: (i, 0, 0)),
            whole,
        ],
        out_specs=[
            tile,
            tile,
            pl.BlockSpec((shards, 8, each), lambda i, e: (i, 0, 0)),
            whole,
        ],
        scratch_shapes=[
            pltpu.VMEM((OWN, owners * first, width), f32),
            pltpu.VMEM((OWN, owners * (weights.shape[2] - first), width), f32),
            pltpu.VMEM((shards * each, width), f32),
            pltpu.VMEM((shards * each, width), f32),
        ],
        compiler_params=pltpu.CompilerParams(vmem_limit_bytes=62 * 2**20),
        cost_estimate=pl.CostEstimate(flops=45000000000, bytes_accessed=2**24, transcendentals=0),
        name="expert_layer",
    )(rows, grad, gate, weights)


def inverse_rms(rows):
    return lax.rsqrt(jnp.mean(rows * rows, axis=-1, keepdims=True) + epsilon)


def norm_back(rows, gain_row, upstream):
    inverse = inverse_rms(rows)
    gain_grad = jnp.sum(upstream * rows * inverse, axis=0)
    scaled = upstream * gain_row
    rows_grad = inverse * scaled - rows * inverse**3 * jnp.mean(scaled * rows, axis=-1, keepdims=True)
    return rows_grad, gain_grad


def rope_tables(positions):
    half = HEAD_SIZE // 2
    frequency = rope_base ** (-(jnp.arange(half, dtype=f32) * 2.0) / HEAD_SIZE)
    angles = positions.astype(f32)[:, None] * frequency[None, :]
    cosine, sine = jnp.cos(angles), jnp.sin(angles)
    return jnp.concatenate([cosine, cosine], 1), jnp.concatenate([sine, sine], 1)


def rotary_apply(rows, cosine, sine):
    half = HEAD_SIZE // 2
    turned = jnp.concatenate([-rows[..., half:], rows[..., :half]], -1)
    return rows * cosine[:, None, :] + turned * sine[:, None, :]


def unrotate(rows, cosine, sine):
    half = HEAD_SIZE // 2
    scaled = rows * sine[:, None, :]
    back = jnp.concatenate([scaled[..., half:], -scaled[..., :half]], -1)
    return rows * cosine[:, None, :] + back


def make_body(n_dp):
    groups_count = n_dp // RANKS
    expert_groups = n_dp // PLACES
    inside = [[g * PLACES + j for j in range(PLACES)] for g in range(expert_groups)]
    between = [[g * PLACES + j for g in range(expert_groups)] for j in range(PLACES)]
    half_experts = EXPERTS // 2

    def expert_pieces(gate_up_shard, down_shard, seq_rank):
        mine = [
            jnp.swapaxes(lax.dynamic_slice_in_dim(w, seq_rank * half_experts, half_experts, axis=1), 0, 1)
            for w in (gate_up_shard, down_shard)
        ]
        mine = jnp.concatenate(mine, 1)
        mine = mine.reshape((PLACES, OWN) + mine.shape[1:])
        return lax.all_to_all(
            mine, "dp", split_axis=0, concat_axis=0, tiled=True, axis_index_groups=inside
        )

    def body(
        tokens, starts, routes, gain_one, query_key_value_weight, w_out,
        gain_two, w_router, w_gate_up, w_down, cotangent,
    ):
        count = tokens.shape[1]
        seq_rank = lax.axis_index("seq")
        expert = (seq_rank * PLACES + lax.axis_index("dp") % PLACES) * OWN
        query_columns = QUERY_HEADS * HEAD_SIZE
        key_columns = KEY_VALUE_HEADS * HEAD_SIZE
        group = QUERY_HEADS // KEY_VALUE_HEADS
        forward_pair, back_pair = [(0, 1)], [(1, 0)]

        mine = expert_pieces(w_gate_up, w_down, seq_rank)
        tokens_before = lax.ppermute(tokens[0], "seq", forward_pair)
        starts_before = lax.ppermute(starts, "seq", forward_pair)
        spare = lambda value: jnp.pad(value, ((0, 0), (0, 128 - value.shape[1])))
        qkv_weight, out_weight, small = weights_gather(
            0,
            groups_count,
            query_key_value_weight,
            w_out,
            jnp.concatenate(
                [spare(w_router), spare(jnp.stack([gain_one, gain_two], 1))], 1
            ),
        )
        mine, qkv_weight, out_weight, small = lax.optimization_barrier(
            (mine, qkv_weight, out_weight, small)
        )
        weights = lax.all_gather(mine, "dp", axis=0, tiled=True, axis_index_groups=between)
        router_weight = small[:, :EXPERTS]
        gain_a = small[:, 128].astype(f32)
        gain_b = small[:, 129].astype(f32)

        token_rows = tokens[0].astype(f32)
        grad_output = cotangent[0].astype(f32)
        both = 2 * count
        index = jnp.arange(both, dtype=jnp.int32)
        flags = jnp.concatenate([starts_before[0], starts[0]])
        begins = (flags > 0) | (index == jnp.where(seq_rank == 0, count, 0))
        last_begin = jnp.max(
            jnp.where(begins[None, :] & (index[None, :] <= index[:, None]), index[None, :], 0), axis=1
        )
        cosine_all, sine_all = rope_tables(index - last_begin)
        cosine, sine = cosine_all[count:], sine_all[count:]

        rows_all = jnp.concatenate([tokens_before.astype(f32), token_rows], 0)
        normed_all = (rows_all * inverse_rms(rows_all) * gain_a).astype(bf16)
        normed_one = normed_all[count:]
        projected_q = jnp.dot(normed_one, qkv_weight[:, :query_columns], preferred_element_type=f32)
        projected_kv = jnp.dot(normed_all, qkv_weight[:, query_columns:], preferred_element_type=f32)
        queries = rotary_apply(
            projected_q.reshape(count, QUERY_HEADS, HEAD_SIZE), cosine, sine
        ).astype(bf16).reshape(count, KEY_VALUE_HEADS, group, HEAD_SIZE)
        keys = rotary_apply(
            projected_kv[:, :key_columns].reshape(both, KEY_VALUE_HEADS, HEAD_SIZE), cosine_all, sine_all
        ).astype(bf16)
        values = projected_kv[:, key_columns:].astype(bf16).reshape(both, KEY_VALUE_HEADS, HEAD_SIZE)

        scale = HEAD_SIZE ** (-0.5)
        allowed = (index[None, :] <= index[count:, None]) & (index[None, :] >= last_begin[count:, None])
        scores = jnp.einsum("qgrd,kgd->grqk", queries, keys, preferred_element_type=f32) * scale
        scores = jnp.where(allowed[None, None], scores, masked_score)
        top = jnp.max(scores, axis=-1, keepdims=True)
        exps = jnp.exp(scores - top)
        probs = exps / jnp.sum(exps, axis=-1, keepdims=True)
        probs_low = probs.astype(bf16)
        attended = jnp.einsum(
            "grqk,kgd->qgrd", probs_low, values, preferred_element_type=f32
        ).reshape(count, query_columns).astype(bf16)
        hidden = token_rows + jnp.dot(attended, out_weight, preferred_element_type=f32)
        normed_two = (hidden * inverse_rms(hidden) * gain_b).astype(bf16)
        logits = jnp.dot(normed_two, router_weight, preferred_element_type=f32)
        expert_ids = jnp.arange(EXPERTS, dtype=jnp.int32)
        chosen = jnp.any(routes[0][:, :, None] == expert_ids[None, None, :], axis=1)
        gates = jax.nn.softmax(jnp.where(chosen, logits, -jnp.inf), axis=-1)

        rows_in, gates_all, grad_all = group_gather(1, normed_two, gates.T, cotangent[0])
        gate = lax.dynamic_slice_in_dim(gates_all, expert, OWN, axis=1)
        mixed_part, normed_part, gate_grad_part, expert_wgrads = expert_layer(
            w_gate_up.shape[0], rows_in, grad_all, gate, weights
        )
        expert_grads = lax.psum_scatter(
            expert_wgrads, "dp", scatter_dimension=0, tiled=True, axis_index_groups=between
        )
        mixed, normed_grad, gate_grad = group_reduce(2, mixed_part, normed_part, gate_grad_part)
        gate_grad = gate_grad[:, :OWN].reshape(EXPERTS, count).T

        over_rows = (((0,), (0,)), ((), ()))
        output = (hidden + mixed).astype(bf16)[None]
        stat_sums = jnp.stack([jnp.sum(hidden * hidden), jnp.sum(mixed * mixed)])
        weighted = jnp.where(chosen, gates * gate_grad, 0.0)
        logits_grad = weighted - gates * jnp.sum(weighted, axis=-1, keepdims=True)
        router_wide = router_weight.astype(f32)
        normed_grad = normed_grad + jnp.dot(logits_grad, router_wide.T, precision=highest)
        router_wgrad = jnp.dot(normed_two.astype(f32).T, logits_grad, precision=highest)
        hidden_branch, gain_two_grad = norm_back(hidden, gain_b, normed_grad)
        hidden_grad = grad_output + hidden_branch
        branch_low = hidden_grad.astype(bf16)
        out_wgrad = lax.dot_general(attended, branch_low, over_rows, preferred_element_type=f32)
        attended_grad = lax.dot_general(
            branch_low, out_weight, (((1,), (1,)), ((), ())), preferred_element_type=f32
        ).astype(bf16).reshape(count, KEY_VALUE_HEADS, group, HEAD_SIZE)

        prob_grad = jnp.einsum("qgrd,kgd->grqk", attended_grad, values, preferred_element_type=f32)
        delta = jnp.sum(probs * prob_grad, axis=-1, keepdims=True)
        score_grad = (probs * (prob_grad - delta)).astype(bf16)
        query_grad = (
            jnp.einsum("grqk,kgd->qgrd", score_grad, keys, preferred_element_type=f32) * scale
        ).reshape(count, QUERY_HEADS, HEAD_SIZE)
        key_grad = (
            jnp.einsum("grqk,qgrd->kgd", score_grad, queries, preferred_element_type=f32) * scale
        ).reshape(both, key_columns)
        value_grad = jnp.einsum(
            "grqk,qgrd->kgd", probs_low, attended_grad, preferred_element_type=f32
        ).reshape(both, key_columns)
        kv_grad = jnp.concatenate([key_grad, value_grad], 1)
        kv_back = lax.ppermute(kv_grad[:count].astype(bf16), "seq", back_pair)
        kv_grad = (kv_grad[count:] + kv_back.astype(f32)).astype(bf16).astype(f32)
        query_grad = query_grad.astype(bf16).astype(f32)
        query_back = unrotate(query_grad, cosine, sine).reshape(count, query_columns)
        key_back = unrotate(
            kv_grad[:, :key_columns].reshape(count, KEY_VALUE_HEADS, HEAD_SIZE), cosine, sine
        ).reshape(count, key_columns)
        projected_grad = jnp.concatenate([query_back, key_back, kv_grad[:, key_columns:]], 1).astype(bf16)
        qkv_wgrad = lax.dot_general(normed_one, projected_grad, over_rows, preferred_element_type=f32)
        normed_one_grad = lax.dot_general(
            projected_grad, qkv_weight, (((1,), (1,)), ((), ())), preferred_element_type=f32
        )
        rows_branch, gain_one_grad = norm_back(token_rows, gain_a, normed_one_grad)
        input_grad = (hidden_grad + rows_branch).astype(bf16)[None]

        little = jnp.concatenate(
            [spare(router_wgrad), spare(jnp.stack([gain_one_grad, gain_two_grad], 1))], 1
        )
        qkv_shard, out_shard, little, experts_all = weights_reduce(
            3,
            groups_count,
            (qkv_wgrad.astype(bf16), out_wgrad.astype(bf16), little),
            expert_grads,
        )
        experts_all = experts_all.reshape((EXPERTS,) + experts_all.shape[2:])
        stat_sums = stat_sums + lax.ppermute(stat_sums, "seq", [(0, 1), (1, 0)])
        first = w_gate_up.shape[0]
        stream_rms = jnp.sqrt(stat_sums / (both * MODEL_WIDTH)).reshape(1, 2)
        return (
            output,
            input_grad,
            little[:, 128],
            qkv_shard.astype(f32),
            out_shard.astype(f32),
            little[:, 129],
            little[:, :EXPERTS],
            jnp.swapaxes(experts_all[:, :first], 0, 1).astype(f32),
            jnp.swapaxes(experts_all[:, first:], 0, 1).astype(f32),
            stream_rms,
        )

    return body


def solution(mesh):
    placed = (
        P("dp", "seq", None),
        P("dp", "seq"),
        P("dp", "seq", None),
        P("dp"),
        P("dp", None),
        P("dp", None),
        P("dp"),
        P("dp", None),
        P("dp", None, None),
        P("dp", None, None),
        P("dp", "seq", None),
    )
    return jax.shard_map(
        make_body(mesh.shape["dp"]),
        mesh=mesh,
        in_specs=placed,
        out_specs=(
            P("dp", "seq", None),
            P("dp", "seq", None),
            P("dp"),
            P("dp", None),
            P("dp", None),
            P("dp"),
            P("dp", None),
            P("dp", None, None),
            P("dp", None, None),
            P("dp", None),
        ),
        check_vma=False,
    )
```

```python
import functools

import jax
import jax.numpy as jnp
from jax import lax
from jax.experimental import pallas as pl
from jax.experimental.pallas import tpu as pltpu
from jax.sharding import PartitionSpec as P

MODEL_WIDTH = 1024
QUERY_HEADS = 16
KEY_VALUE_HEADS = 8
HEAD_SIZE = 64
F = 512
EXPERTS = 16
TOPK = 8
RANKS = 8
PLACES = 4
GROUP = 8
OWN = EXPERTS // GROUP

epsilon = 1e-06
rope_base = 10000.0
highest = lax.Precision.HIGHEST
masked_score = -1e30
f32 = jnp.float32
bf16 = jnp.bfloat16
MESH = pl.DeviceIdType.MESH

GATHER_LINKS = ((4, 8, 2), (4, 2, 8))
SUM_LINKS = ((8, 2, 4), (2, 8, 4))
TOKEN_LINKS = ((4, 2), (2, 4))


def flip(value, bit):
    return value + bit * (1 - 2 * ((value // bit) % 2))


def flip_mask(value, mask):
    for bit in (1, 2, 4, 8):
        if mask & bit:
            value = flip(value, bit)
    return value


def subsets(bits):
    out = [0]
    for bit in bits:
        out = out + [m | bit for m in out]
    return out


def row_parts(rows):
    first = (rows // 2 + 15) // 16 * 16
    return ((0, first), (first, rows - first))


def my_place(places=RANKS):
    seq = lax.axis_index("seq")
    dp = lax.axis_index("dp")
    rank = seq * places + dp % places

    def peer(mask):
        return {
            "seq": 1 - seq if mask & places else seq,
            "dp": flip_mask(dp, mask & (places - 1)),
        }

    return rank, peer


def meet(devices):
    barrier = pltpu.get_barrier_semaphore()
    for there in devices:
        pl.semaphore_signal(barrier, inc=1, device_id=there, device_id_type=MESH)
    pl.semaphore_wait(barrier, len(devices))


def gather_kernel(count, *refs):
    ins, outs = refs[:count], refs[count : 2 * count]
    send, recv, send_core, recv_core, local = refs[2 * count :]
    rank, peer = my_place(PLACES)
    own = [
        pltpu.make_async_copy(ins[a], outs[a].at[rank], local.at[a]) for a in range(count)
    ]
    for copy in own:
        copy.start()
    meet([peer(bit) for bit in (1, 2, 4)])
    parts = [row_parts(ref.shape[0]) for ref in ins]

    def remote(a, p, mask, bit, sems, index):
        start, size = parts[a][p]
        rows = pl.ds(start, size)
        shard = flip_mask(rank, mask)
        src = ins[a].at[rows] if mask == 0 else outs[a].at[shard, rows]
        return pltpu.make_async_remote_copy(
            src_ref=src,
            dst_ref=outs[a].at[shard, rows],
            send_sem=sems[0].at[a, p, index],
            recv_sem=sems[1].at[a, p, index],
            device_id=peer(bit),
            device_id_type=MESH,
        )

    started = []
    live = {}
    for step in range(3):
        for p in range(2):
            for a in range(count):
                if parts[a][p][1] == 0:
                    continue
                order = TOKEN_LINKS[p]
                if step > 0:
                    for copy in live.pop((a, p)):
                        copy.wait_recv()
                if step < 2:
                    now = []
                    for index, mask in enumerate(subsets(order[:step])):
                        copy = remote(a, p, mask, order[step], (send, recv), 2**step - 1 + index)
                        copy.start()
                        now.append(copy)
                        started.append(copy)
                    live[(a, p)] = now
                fresh = [0] if step == 0 else [m | order[step - 1] for m in subsets(order[: step - 1])]
                base = 0 if step == 0 else 2 ** (step - 1)
                for index, mask in enumerate(fresh):
                    copy = remote(a, p, mask, 1, (send_core, recv_core), base + index)
                    copy.start()
                    live.setdefault("core", []).append(copy)
    for copy in live["core"]:
        copy.wait()
    for copy in started:
        copy.wait_send()
    for copy in own:
        copy.wait()


def group_gather(collective_id, *arrays):
    count = len(arrays)
    return pl.pallas_call(
        functools.partial(gather_kernel, count),
        out_shape=[jax.ShapeDtypeStruct((GROUP,) + a.shape, a.dtype) for a in arrays],
        in_specs=[pl.BlockSpec(memory_space=pltpu.VMEM)] * count,
        out_specs=[pl.BlockSpec(memory_space=pl.ANY)] * count,
        scratch_shapes=[
            pltpu.SemaphoreType.DMA((count, 2, 3)),
            pltpu.SemaphoreType.DMA((count, 2, 3)),
            pltpu.SemaphoreType.DMA((count, 2, 4)),
            pltpu.SemaphoreType.DMA((count, 2, 4)),
            pltpu.SemaphoreType.DMA((count,)),
        ],
        compiler_params=pltpu.CompilerParams(collective_id=collective_id, has_side_effects=True),
        cost_estimate=pl.CostEstimate(flops=1000000000, bytes_accessed=2**24, transcendentals=0),
        name="group_gather",
    )(*arrays)


def add_rows(target, source, start, size):
    def step(i, carry):
        rows = pl.ds(pl.multiple_of(start + i * 16, 16), 16)
        target[rows] = (target[rows].astype(f32) + source[rows].astype(f32)).astype(target.dtype)
        return carry

    lax.fori_loop(0, size // 16, step, 0)


def reduce_kernel(
    mixed_ref, normed_ref, gate_ref, mixed_out, normed_out, gate_out,
    total, got0, got1, got2, sems, gate_sems, local, own_gate,
):
    rank, peer = my_place(PLACES)
    chip = rank // 2
    core = rank % 2
    parts = row_parts(mixed_ref.shape[1])
    ins = (mixed_ref, normed_ref)
    outs = (mixed_out, normed_out)
    loads = []
    for t in range(2):
        for c in range(4):
            copy = pltpu.make_async_copy(ins[t].at[2 * c + core], total.at[t, c], local.at[t, c])
            copy.start()
            loads.append(copy)
    everyone = [peer(mask) for mask in range(1, GROUP)]
    meet(everyone)
    gates = []
    keep = pltpu.make_async_copy(gate_ref.at[rank], gate_out.at[rank], own_gate)
    keep.start()
    for mask, there in zip(range(1, GROUP), everyone):
        copy = pltpu.make_async_remote_copy(
            src_ref=gate_ref.at[flip_mask(rank, mask)],
            dst_ref=gate_out.at[rank],
            send_sem=gate_sems.at[0, mask],
            recv_sem=gate_sems.at[1, mask],
            device_id=there,
            device_id_type=MESH,
        )
        copy.start()
        gates.append(copy)

    started = []
    live = {}

    def send(t, p, stage, index, src, dst, bit):
        copy = pltpu.make_async_remote_copy(
            src_ref=src,
            dst_ref=dst,
            send_sem=sems.at[0, t, p, stage, index],
            recv_sem=sems.at[1, t, p, stage, index],
            device_id=peer(bit),
            device_id_type=MESH,
        )
        copy.start()
        started.append(copy)
        live.setdefault((t, p), []).append(copy)

    def chip_of(mask):
        return flip_mask(rank, mask) // 2

    for p in range(2):
        for t in range(2):
            rows = pl.ds(*parts[p])
            for c in range(4):
                send(
                    t, p, 0, c, ins[t].at[2 * c + 1 - core, rows], got0.at[t, c, rows], 1
                )
    for copy in loads:
        copy.wait()
    got = (got1, got2)
    for stage in range(3):
        for p in range(2):
            for t in range(2):
                order = TOKEN_LINKS[p]
                rows = pl.ds(*parts[p])
                for copy in live.pop((t, p)):
                    copy.wait_recv()
                if stage == 0:

                    def over_chips(c, carry, t=t, p=p):
                        add_rows(total.at[t, c], got0.at[t, c], *parts[p])
                        return carry

                    lax.fori_loop(0, 4, over_chips, 0)
                else:
                    for index, mask in enumerate(subsets(order[stage:])):
                        if stage == 2:
                            outs[t][rows] = total[t, chip, rows].astype(f32) + got2[t, 0, rows].astype(f32)
                        else:
                            add_rows(
                                total.at[t, chip_of(mask)], got[stage - 1].at[t, index], *parts[p]
                            )
                if stage < 2:
                    for index, mask in enumerate(subsets(order[stage + 1 :])):
                        send(
                            t, p, stage + 1, index,
                            total.at[t, chip_of(mask | order[stage]), rows],
                            got[stage].at[t, index, rows],
                            order[stage],
                        )
    for copy in started:
        copy.wait_send()
    for copy in gates:
        copy.wait()
    keep.wait()


def group_reduce(collective_id, mixed, normed, gate_grad):
    rows, width = mixed.shape[1:]
    return pl.pallas_call(
        reduce_kernel,
        out_shape=[
            jax.ShapeDtypeStruct((rows, width), f32),
            jax.ShapeDtypeStruct((rows, width), f32),
            jax.ShapeDtypeStruct(gate_grad.shape, gate_grad.dtype),
        ],
        in_specs=[pl.BlockSpec(memory_space=pl.ANY)] * 3,
        out_specs=[
            pl.BlockSpec(memory_space=pltpu.VMEM),
            pl.BlockSpec(memory_space=pltpu.VMEM),
            pl.BlockSpec(memory_space=pl.ANY),
        ],
        scratch_shapes=[
            pltpu.VMEM((2, 4, rows, width), bf16),
            pltpu.VMEM((2, 4, rows, width), bf16),
            pltpu.VMEM((2, 2, rows, width), bf16),
            pltpu.VMEM((2, 1, rows, width), bf16),
            pltpu.SemaphoreType.DMA((2, 2, 2, 3, 4)),
            pltpu.SemaphoreType.DMA((2, GROUP)),
            pltpu.SemaphoreType.DMA((2, 4)),
            pltpu.SemaphoreType.DMA(()),
        ],
        compiler_params=pltpu.CompilerParams(
            collective_id=collective_id, has_side_effects=True, vmem_limit_bytes=48 * 2**20
        ),
        cost_estimate=pl.CostEstimate(flops=1000000, bytes_accessed=2**24, transcendentals=0),
        name="group_reduce",
    )(mixed, normed, gate_grad)


def column_parts(half):
    first = -(-(half // 128) // 2) * 128
    return ((0, first), (first, half - first))


def shard_view(ref, halves, a, p, rank_value):
    start, size = column_parts(halves[a])[p]
    offset = pl.multiple_of((rank_value // RANKS) * halves[a] + start, 128)
    return ref.at[:, rank_value % RANKS, :, pl.ds(offset, size)]


def other_groups(groups_count):
    dp = lax.axis_index("dp")
    seq = lax.axis_index("seq")
    place, home = dp % RANKS, dp // RANKS
    return home, [
        {"seq": seq, "dp": ((home + k) % groups_count) * RANKS + place} for k in range(1, groups_count)
    ]


def weights_gather_kernel(count, groups_count, *refs):
    ins, outs = refs[:count], refs[count : 2 * count]
    send, recv, far_send, far_recv, local = refs[2 * count :]
    rank, peer = my_place()
    home, far = other_groups(groups_count)
    seq = lax.axis_index("seq")
    halves = [ref.shape[1] // 2 for ref in ins]

    def half(ref, a):
        return ref.at[:, pl.ds(pl.multiple_of(seq * halves[a], 128), halves[a])]

    def own_slot(a):
        columns = pl.ds(pl.multiple_of(seq * halves[a], 128), halves[a])
        return outs[a].at[home, rank % RANKS, :, columns]

    own = [pltpu.make_async_copy(half(ins[a], a), own_slot(a), local.at[a]) for a in range(count)]
    for copy in own:
        copy.start()
    meet([peer(bit) for bit in (1, 2, 4, 8)] + far)
    started, waiting = [], []
    for k, there in enumerate(far):
        for a in range(count):
            copy = pltpu.make_async_remote_copy(
                src_ref=half(ins[a], a),
                dst_ref=own_slot(a),
                send_sem=far_send.at[k, a],
                recv_sem=far_recv.at[k, a],
                device_id=there,
                device_id_type=MESH,
            )
            copy.start()
            started.append(copy)
            waiting.append(copy)
    for copy in own:
        copy.wait()
    for copy in waiting:
        copy.wait_recv()

    def remote(a, p, mask, bit, index):
        view = shard_view(outs[a], halves, a, p, flip_mask(rank, mask))
        copy = pltpu.make_async_remote_copy(
            src_ref=view,
            dst_ref=view,
            send_sem=send.at[a, p, index],
            recv_sem=recv.at[a, p, index],
            device_id=peer(bit),
            device_id_type=MESH,
        )
        copy.start()
        started.append(copy)
        return copy

    live = {}
    last = []
    for step in range(4):
        for p in range(2):
            for a in range(count):
                if column_parts(halves[a])[p][1] == 0:
                    continue
                order = GATHER_LINKS[p]
                if step > 0:
                    for copy in live.pop((a, p)):
                        copy.wait_recv()
                if step < 3:
                    live[(a, p)] = [
                        remote(a, p, mask, order[step], 2**step - 1 + index)
                        for index, mask in enumerate(subsets(order[:step]))
                    ]
                fresh = [0] if step == 0 else [m | order[step - 1] for m in subsets(order[: step - 1])]
                base = 0 if step == 0 else 2 ** (step - 1)
                for index, mask in enumerate(fresh):
                    last.append(remote(a, p, mask, 1, 7 + base + index))
    for copy in last:
        copy.wait_recv()
    for copy in started:
        copy.wait_send()


def weights_gather(collective_id, groups_count, *arrays):
    count = len(arrays)
    whole = pl.pallas_call(
        functools.partial(weights_gather_kernel, count, groups_count),
        out_shape=[
            jax.ShapeDtypeStruct((groups_count, RANKS) + a.shape, a.dtype) for a in arrays
        ],
        in_specs=[pl.BlockSpec(memory_space=pltpu.VMEM)] * count,
        out_specs=[pl.BlockSpec(memory_space=pl.ANY)] * count,
        scratch_shapes=[
            pltpu.SemaphoreType.DMA((count, 2, 15)),
            pltpu.SemaphoreType.DMA((count, 2, 15)),
            pltpu.SemaphoreType.DMA((max(groups_count - 1, 1), count)),
            pltpu.SemaphoreType.DMA((max(groups_count - 1, 1), count)),
            pltpu.SemaphoreType.DMA((count,)),
        ],
        compiler_params=pltpu.CompilerParams(collective_id=collective_id, has_side_effects=True),
        cost_estimate=pl.CostEstimate(flops=45000000000, bytes_accessed=2**24, transcendentals=0),
        name="weights_gather",
    )(*arrays)
    return [w.reshape(-1, w.shape[3]) for w in whole]


def add_block(target, source, at, start, size):
    groups, rows = source.shape[0], source.shape[1]
    columns = pl.ds(start, size)
    pieces = rows // 16

    def step(i, carry):
        lines = pl.ds(pl.multiple_of((i % pieces) * 16, 16), 16)
        index = (i // pieces, lines, columns)
        new = target[(at,) + index].astype(f32) + source[index].astype(f32)
        target[(at,) + index] = new.astype(target.dtype)
        return carry

    lax.fori_loop(0, groups * pieces, step, 0)


def weights_reduce_kernel(count, groups_count, *refs):
    ins = refs[:count]
    outs = refs[count : 2 * count]
    rest = refs[2 * count :]
    total, got0, got1, got2, got3, far_got = [rest[i * count : (i + 1) * count] for i in range(6)]
    sems, far_sems, seq_sems, local = rest[6 * count :]
    rank, peer = my_place()
    chip, core = rank // 2, rank % 2
    home, far = other_groups(groups_count)
    seq = lax.axis_index("seq")
    dp = lax.axis_index("dp")
    halves = [ref.shape[3] // 2 for ref in ins]
    parts = [column_parts(halves[a]) for a in range(count)]

    def half_view(ref, a, rank_value):
        offset = pl.multiple_of((rank_value // RANKS) * halves[a], 128)
        return ref.at[:, rank_value % RANKS, :, pl.ds(offset, halves[a])]

    loads = []
    for a in range(count):
        for c in range(8):
            copy = pltpu.make_async_copy(
                half_view(ins[a], a, 2 * c + core), total[a].at[c], local.at[a, c]
            )
            copy.start()
            loads.append(copy)
    meet([peer(bit) for bit in (1, 2, 4, 8)] + far)

    started = []
    live = {}

    def send(a, p, stage, index, src, dst, bit):
        copy = pltpu.make_async_remote_copy(
            src_ref=src,
            dst_ref=dst,
            send_sem=sems.at[0, a, p, stage, index],
            recv_sem=sems.at[1, a, p, stage, index],
            device_id=peer(bit),
            device_id_type=MESH,
        )
        copy.start()
        started.append(copy)
        live.setdefault((a, p), []).append(copy)

    def chip_of(mask):
        return flip_mask(rank, mask) // 2

    for p in range(2):
        for a in range(count):
            columns = pl.ds(*parts[a][p])
            if parts[a][p][1]:
                for c in range(8):
                    send(
                        a, p, 0, c,
                        shard_view(ins[a], halves, a, p, 2 * c + 1 - core),
                        got0[a].at[c, :, :, columns],
                        1,
                    )
    for copy in loads:
        copy.wait()
    got = (got1, got2, got3)
    for stage in range(4):
        for p in range(2):
            for a in range(count):
                start, size = parts[a][p]
                if size == 0:
                    continue
                order = SUM_LINKS[p]
                columns = pl.ds(start, size)
                for copy in live.pop((a, p)):
                    copy.wait_recv()
                if stage == 0:

                    def over_chips(c, carry, a=a, start=start, size=size):
                        add_block(total[a], got0[a].at[c], c, start, size)
                        return carry

                    lax.fori_loop(0, 8, over_chips, 0)
                else:
                    for index, mask in enumerate(subsets(order[stage:])):
                        add_block(total[a], got[stage - 1][a].at[index], chip_of(mask), start, size)
                if stage < 3:
                    for index, mask in enumerate(subsets(order[stage + 1 :])):
                        send(
                            a, p, stage + 1, index,
                            total[a].at[chip_of(mask | order[stage]), :, :, columns],
                            got[stage][a].at[index, :, :, columns],
                            order[stage],
                        )
    waiting = []
    for k, there in enumerate(far):
        for a in range(count):
            copy = pltpu.make_async_remote_copy(
                src_ref=total[a].at[chip, there["dp"] // RANKS],
                dst_ref=far_got[a].at[k],
                send_sem=far_sems.at[0, k, a],
                recv_sem=far_sems.at[1, k, a],
                device_id=there,
                device_id_type=MESH,
            )
            copy.start()
            waiting.append(copy)
    for copy in waiting:
        copy.wait()
    last = []
    for a in range(count):
        columns = pl.ds(pl.multiple_of(seq * halves[a], 128), halves[a])
        value = total[a][chip, home].astype(f32)
        for k in range(len(far)):
            value = value + far_got[a][k].astype(f32)
        outs[a][:, columns] = value.astype(outs[a].dtype)
        copy = pltpu.make_async_remote_copy(
            src_ref=outs[a].at[:, columns],
            dst_ref=outs[a].at[:, columns],
            send_sem=seq_sems.at[0, a],
            recv_sem=seq_sems.at[1, a],
            device_id=peer(8),
            device_id_type=MESH,
        )
        copy.start()
        last.append(copy)
    for copy in last:
        copy.wait()
    for copy in started:
        copy.wait_send()


def pieces_kernel(pieces, whole, send, recv, local):
    rank, peer = my_place(PLACES)
    place = rank % PLACES
    keep = pltpu.make_async_copy(pieces.at[place], whole.at[rank], local)
    keep.start()
    masks = (6, 7, 2, 4, 3, 5, 1)
    meet([peer(mask) for mask in masks])
    copies = []
    for mask in masks:
        copy = pltpu.make_async_remote_copy(
            src_ref=pieces.at[flip_mask(place, mask & (PLACES - 1))],
            dst_ref=whole.at[rank],
            send_sem=send.at[mask],
            recv_sem=recv.at[mask],
            device_id=peer(mask),
            device_id_type=MESH,
        )
        copy.start()
        copies.append(copy)
    for copy in copies:
        copy.wait()
    keep.wait()


def send_pieces(collective_id, pieces):
    return pl.pallas_call(
        pieces_kernel,
        out_shape=jax.ShapeDtypeStruct((GROUP,) + pieces.shape[1:], pieces.dtype),
        in_specs=[pl.BlockSpec(memory_space=pltpu.VMEM)],
        out_specs=pl.BlockSpec(memory_space=pl.ANY),
        scratch_shapes=[
            pltpu.SemaphoreType.DMA((GROUP,)),
            pltpu.SemaphoreType.DMA((GROUP,)),
            pltpu.SemaphoreType.DMA(()),
        ],
        compiler_params=pltpu.CompilerParams(collective_id=collective_id, has_side_effects=True),
        name="send_pieces",
    )(pieces)


def weights_reduce(collective_id, groups_count, arrays):
    count = len(arrays)
    views = [a.reshape(groups_count, RANKS, -1, a.shape[1]) for a in arrays]
    rows = views[0].shape[2]
    halves = [a.shape[1] // 2 for a in arrays]

    def buffers(*lead):
        return [
            pltpu.VMEM(lead + (groups_count, rows, h), a.dtype) for h, a in zip(halves, arrays)
        ]

    far_buffers = [
        pltpu.VMEM((max(groups_count - 1, 1), rows, h), a.dtype) for h, a in zip(halves, arrays)
    ]
    dma = pltpu.SemaphoreType.DMA
    vmem = pl.BlockSpec(memory_space=pltpu.VMEM)
    any_space = pl.BlockSpec(memory_space=pl.ANY)
    return pl.pallas_call(
        functools.partial(weights_reduce_kernel, count, groups_count),
        out_shape=[jax.ShapeDtypeStruct((rows, a.shape[1]), a.dtype) for a in arrays],
        in_specs=[any_space] * count,
        out_specs=[vmem] * count,
        scratch_shapes=buffers(8) + buffers(8) + buffers(4) + buffers(2) + buffers(1) + far_buffers
        + [
            dma((2, count, 2, 4, 8)),
            dma((2, max(groups_count - 1, 1), count)),
            dma((2, count)),
            dma((count, 8)),
        ],
        compiler_params=pltpu.CompilerParams(
            collective_id=collective_id, has_side_effects=True, vmem_limit_bytes=48 * 2**20
        ),
        cost_estimate=pl.CostEstimate(flops=1000000, bytes_accessed=2**24, transcendentals=0),
        name="weights_reduce",
    )(*views)


def expert_kernel(
    first, rows_ref, grad_ref, gate_ref, weights_ref,
    mixed_ref, normed_ref, gate_grad_ref, weights_out,
    gate_up_sum, down_sum, mixed_sum, normed_sum,
):
    step = pl.program_id(0)
    expert = pl.program_id(1)
    shards, each, width = rows_ref.shape
    count = shards * each
    rows = rows_ref[...].reshape(count, width)
    grad = grad_ref[...].reshape(count, width).astype(f32)
    gate = jnp.concatenate(
        [
            jnp.broadcast_to(gate_ref[i, pl.ds(expert, 1)], (128, each)).T[:, :1]
            for i in range(shards)
        ],
        0,
    )
    gate_up_weight = weights_ref[:, expert, :first].reshape(-1, width)
    down = weights_ref[:, expert, first:].reshape(-1, width)
    gate_up = jnp.dot(rows, gate_up_weight, preferred_element_type=f32)
    gate_part, up_part = gate_up[:, :F], gate_up[:, F:]
    sigmoid = 1.0 / (1.0 + jnp.exp(-gate_part))
    silu = gate_part * sigmoid
    act = (silu * up_part).astype(bf16)
    out = jnp.dot(act, down, preferred_element_type=f32)
    inner = jnp.sum(out * grad, axis=-1, keepdims=True)
    for i in range(shards):
        line = jnp.broadcast_to(inner[i * each : (i + 1) * each], (each, 128)).T
        gate_grad_ref[i, pl.ds(expert, 1)] = line[:1]
    mixed = gate * out
    expert_grad = (gate * grad).astype(bf16)
    across = (((1,), (1,)), ((), ()))
    over_rows = (((0,), (0,)), ((), ()))
    act_grad = lax.dot_general(expert_grad, down, across, preferred_element_type=f32)
    gate_up_grad = jnp.concatenate(
        [act_grad * up_part * (sigmoid * (1.0 + gate_part * (1.0 - sigmoid))), act_grad * silu], -1
    ).astype(bf16)
    normed = lax.dot_general(gate_up_grad, gate_up_weight, across, preferred_element_type=f32)

    @pl.when(expert == 0)
    def _():
        mixed_sum[...] = mixed
        normed_sum[...] = normed

    @pl.when(expert > 0)
    def _():
        mixed_sum[...] += mixed
        normed_sum[...] += normed

    @pl.when(expert == OWN - 1)
    def _():
        mixed_ref[...] = mixed_sum[...].astype(bf16).reshape(shards, each, width)
        normed_ref[...] = normed_sum[...].astype(bf16).reshape(shards, each, width)

    @pl.when(step == 0)
    def _():
        gate_up_sum[expert] = jnp.zeros_like(gate_up_sum[0])
        down_sum[expert] = jnp.zeros_like(down_sum[0])

    down_sum[expert] += lax.dot_general(act, expert_grad, over_rows, preferred_element_type=f32)
    gate_up_sum[expert] += lax.dot_general(rows, gate_up_grad, over_rows, preferred_element_type=f32)

    @pl.when(step == pl.num_programs(0) - 1)
    def _():
        owners = weights_out.shape[0]
        weights_out[:, expert, :first] = gate_up_sum[expert].astype(bf16).reshape(owners, first, width)
        weights_out[:, expert, first:] = down_sum[expert].astype(bf16).reshape(owners, -1, width)


def expert_layer(first, rows, grad, gate, weights):
    each, width = rows.shape[1:]
    shards = 2
    owners = weights.shape[0]
    tile = pl.BlockSpec((shards, each, width), lambda i, e: (i, 0, 0))
    whole = pl.BlockSpec(weights.shape, lambda i, e: (0, 0, 0, 0), pipeline_mode=pl.Buffered(1))
    return pl.pallas_call(
        functools.partial(expert_kernel, first),
        grid=(GROUP // shards, OWN),
        out_shape=[
            jax.ShapeDtypeStruct(rows.shape, bf16),
            jax.ShapeDtypeStruct(rows.shape, bf16),
            jax.ShapeDtypeStruct((GROUP, 8, each), f32),
            jax.ShapeDtypeStruct(weights.shape, bf16),
        ],
        in_specs=[
            tile,
            tile,
            pl.BlockSpec((shards, OWN, each), lambda i, e: (i, 0, 0)),
            whole,
        ],
        out_specs=[
            tile,
            tile,
            pl.BlockSpec((shards, 8, each), lambda i, e: (i, 0, 0)),
            whole,
        ],
        scratch_shapes=[
            pltpu.VMEM((OWN, owners * first, width), f32),
            pltpu.VMEM((OWN, owners * (weights.shape[2] - first), width), f32),
            pltpu.VMEM((shards * each, width), f32),
            pltpu.VMEM((shards * each, width), f32),
        ],
        compiler_params=pltpu.CompilerParams(vmem_limit_bytes=62 * 2**20),
        cost_estimate=pl.CostEstimate(flops=45000000000, bytes_accessed=2**24, transcendentals=0),
        name="expert_layer",
    )(rows, grad, gate, weights)


def inverse_rms(rows):
    return lax.rsqrt(jnp.mean(rows * rows, axis=-1, keepdims=True) + epsilon)


def norm_back(rows, gain_row, upstream):
    inverse = inverse_rms(rows)
    gain_grad = jnp.sum(upstream * rows * inverse, axis=0)
    scaled = upstream * gain_row
    rows_grad = inverse * scaled - rows * inverse**3 * jnp.mean(scaled * rows, axis=-1, keepdims=True)
    return rows_grad, gain_grad


def rope_tables(positions):
    half = HEAD_SIZE // 2
    frequency = rope_base ** (-(jnp.arange(half, dtype=f32) * 2.0) / HEAD_SIZE)
    angles = positions.astype(f32)[:, None] * frequency[None, :]
    cosine, sine = jnp.cos(angles), jnp.sin(angles)
    return jnp.concatenate([cosine, cosine], 1), jnp.concatenate([sine, sine], 1)


def rotary_apply(rows, cosine, sine):
    half = HEAD_SIZE // 2
    turned = jnp.concatenate([-rows[..., half:], rows[..., :half]], -1)
    return rows * cosine[:, None, :] + turned * sine[:, None, :]


def unrotate(rows, cosine, sine):
    half = HEAD_SIZE // 2
    scaled = rows * sine[:, None, :]
    back = jnp.concatenate([scaled[..., half:], -scaled[..., :half]], -1)
    return rows * cosine[:, None, :] + back


def make_body(n_dp):
    groups_count = n_dp // RANKS
    expert_groups = n_dp // PLACES
    inside = [[g * PLACES + j for j in range(PLACES)] for g in range(expert_groups)]
    between = [[g * PLACES + j for g in range(expert_groups)] for j in range(PLACES)]
    half_experts = EXPERTS // 2

    def expert_pieces(gate_up_shard, down_shard, seq_rank):
        mine = [
            jnp.swapaxes(lax.dynamic_slice_in_dim(w, seq_rank * half_experts, half_experts, axis=1), 0, 1)
            for w in (gate_up_shard, down_shard)
        ]
        mine = jnp.concatenate(mine, 1)
        mine = mine.reshape((PLACES, OWN) + mine.shape[1:])
        return lax.all_to_all(
            mine, "dp", split_axis=0, concat_axis=0, tiled=True, axis_index_groups=inside
        )

    def body(
        tokens, starts, routes, gain_one, query_key_value_weight, w_out,
        gain_two, w_router, w_gate_up, w_down, cotangent,
    ):
        count = tokens.shape[1]
        seq_rank = lax.axis_index("seq")
        expert = (seq_rank * PLACES + lax.axis_index("dp") % PLACES) * OWN
        query_columns = QUERY_HEADS * HEAD_SIZE
        key_columns = KEY_VALUE_HEADS * HEAD_SIZE
        group = QUERY_HEADS // KEY_VALUE_HEADS
        forward_pair, back_pair = [(0, 1)], [(1, 0)]

        mine = expert_pieces(w_gate_up, w_down, seq_rank)
        tokens_before = lax.ppermute(tokens[0], "seq", forward_pair)
        starts_before = lax.ppermute(starts, "seq", forward_pair)
        mine, query_key_value_weight = lax.optimization_barrier((mine, query_key_value_weight))
        weights = lax.all_gather(mine, "dp", axis=0, tiled=True, axis_index_groups=between)
        spare = lambda value: jnp.pad(value, ((0, 0), (0, 128 - value.shape[1])))
        qkv_weight, out_weight, small = weights_gather(
            0,
            groups_count,
            query_key_value_weight,
            w_out,
            jnp.concatenate(
                [spare(w_router), spare(jnp.stack([gain_one, gain_two], 1))], 1
            ),
        )
        router_weight = small[:, :EXPERTS]
        gain_a = small[:, 128].astype(f32)
        gain_b = small[:, 129].astype(f32)

        token_rows = tokens[0].astype(f32)
        grad_output = cotangent[0].astype(f32)
        both = 2 * count
        index = jnp.arange(both, dtype=jnp.int32)
        flags = jnp.concatenate([starts_before[0], starts[0]])
        begins = (flags > 0) | (index == jnp.where(seq_rank == 0, count, 0))
        last_begin = jnp.max(
            jnp.where(begins[None, :] & (index[None, :] <= index[:, None]), index[None, :], 0), axis=1
        )
        cosine_all, sine_all = rope_tables(index - last_begin)
        cosine, sine = cosine_all[count:], sine_all[count:]

        rows_all = jnp.concatenate([tokens_before.astype(f32), token_rows], 0)
        normed_all = (rows_all * inverse_rms(rows_all) * gain_a).astype(bf16)
        normed_one = normed_all[count:]
        projected_q = jnp.dot(normed_one, qkv_weight[:, :query_columns], preferred_element_type=f32)
        projected_kv = jnp.dot(normed_all, qkv_weight[:, query_columns:], preferred_element_type=f32)
        queries = rotary_apply(
            projected_q.reshape(count, QUERY_HEADS, HEAD_SIZE), cosine, sine
        ).astype(bf16).reshape(count, KEY_VALUE_HEADS, group, HEAD_SIZE)
        keys = rotary_apply(
            projected_kv[:, :key_columns].reshape(both, KEY_VALUE_HEADS, HEAD_SIZE), cosine_all, sine_all
        ).astype(bf16)
        values = projected_kv[:, key_columns:].astype(bf16).reshape(both, KEY_VALUE_HEADS, HEAD_SIZE)

        scale = HEAD_SIZE ** (-0.5)
        allowed = (index[None, :] <= index[count:, None]) & (index[None, :] >= last_begin[count:, None])
        scores = jnp.einsum("qgrd,kgd->grqk", queries, keys, preferred_element_type=f32) * scale
        scores = jnp.where(allowed[None, None], scores, masked_score)
        top = jnp.max(scores, axis=-1, keepdims=True)
        exps = jnp.exp(scores - top)
        probs = exps / jnp.sum(exps, axis=-1, keepdims=True)
        probs_low = probs.astype(bf16)
        attended = jnp.einsum(
            "grqk,kgd->qgrd", probs_low, values, preferred_element_type=f32
        ).reshape(count, query_columns).astype(bf16)
        hidden = token_rows + jnp.dot(attended, out_weight, preferred_element_type=f32)
        normed_two = (hidden * inverse_rms(hidden) * gain_b).astype(bf16)
        logits = jnp.dot(normed_two, router_weight, preferred_element_type=f32)
        expert_ids = jnp.arange(EXPERTS, dtype=jnp.int32)
        chosen = jnp.any(routes[0][:, :, None] == expert_ids[None, None, :], axis=1)
        gates = jax.nn.softmax(jnp.where(chosen, logits, -jnp.inf), axis=-1)

        rows_in, gates_all, grad_all = group_gather(1, normed_two, gates.T, cotangent[0])
        gate = lax.dynamic_slice_in_dim(gates_all, expert, OWN, axis=1)
        mixed_part, normed_part, gate_grad_part, expert_wgrads = expert_layer(
            w_gate_up.shape[0], rows_in, grad_all, gate, weights
        )
        expert_grads = lax.psum_scatter(
            expert_wgrads, "dp", scatter_dimension=0, tiled=True, axis_index_groups=between
        )
        mixed, normed_grad, gate_grad = group_reduce(2, mixed_part, normed_part, gate_grad_part)
        gate_grad = gate_grad[:, :OWN].reshape(EXPERTS, count).T

        over_rows = (((0,), (0,)), ((), ()))
        output = (hidden + mixed).astype(bf16)[None]
        stat_sums = jnp.stack([jnp.sum(hidden * hidden), jnp.sum(mixed * mixed)])
        weighted = jnp.where(chosen, gates * gate_grad, 0.0)
        logits_grad = weighted - gates * jnp.sum(weighted, axis=-1, keepdims=True)
        router_wide = router_weight.astype(f32)
        normed_grad = normed_grad + jnp.dot(logits_grad, router_wide.T, precision=highest)
        router_wgrad = jnp.dot(normed_two.astype(f32).T, logits_grad, precision=highest)
        hidden_branch, gain_two_grad = norm_back(hidden, gain_b, normed_grad)
        hidden_grad = grad_output + hidden_branch
        branch_low = hidden_grad.astype(bf16)
        out_wgrad = lax.dot_general(attended, branch_low, over_rows, preferred_element_type=f32)
        attended_grad = lax.dot_general(
            branch_low, out_weight, (((1,), (1,)), ((), ())), preferred_element_type=f32
        ).astype(bf16).reshape(count, KEY_VALUE_HEADS, group, HEAD_SIZE)

        prob_grad = jnp.einsum("qgrd,kgd->grqk", attended_grad, values, preferred_element_type=f32)
        delta = jnp.sum(probs * prob_grad, axis=-1, keepdims=True)
        score_grad = (probs * (prob_grad - delta)).astype(bf16)
        query_grad = (
            jnp.einsum("grqk,kgd->qgrd", score_grad, keys, preferred_element_type=f32) * scale
        ).reshape(count, QUERY_HEADS, HEAD_SIZE)
        key_grad = (
            jnp.einsum("grqk,qgrd->kgd", score_grad, queries, preferred_element_type=f32) * scale
        ).reshape(both, key_columns)
        value_grad = jnp.einsum(
            "grqk,qgrd->kgd", probs_low, attended_grad, preferred_element_type=f32
        ).reshape(both, key_columns)
        kv_grad = jnp.concatenate([key_grad, value_grad], 1)
        kv_back = lax.ppermute(kv_grad[:count].astype(bf16), "seq", back_pair)
        kv_grad = (kv_grad[count:] + kv_back.astype(f32)).astype(bf16).astype(f32)
        query_grad = query_grad.astype(bf16).astype(f32)
        query_back = unrotate(query_grad, cosine, sine).reshape(count, query_columns)
        key_back = unrotate(
            kv_grad[:, :key_columns].reshape(count, KEY_VALUE_HEADS, HEAD_SIZE), cosine, sine
        ).reshape(count, key_columns)
        projected_grad = jnp.concatenate([query_back, key_back, kv_grad[:, key_columns:]], 1).astype(bf16)
        qkv_wgrad = lax.dot_general(normed_one, projected_grad, over_rows, preferred_element_type=f32)
        normed_one_grad = lax.dot_general(
            projected_grad, qkv_weight, (((1,), (1,)), ((), ())), preferred_element_type=f32
        )
        rows_branch, gain_one_grad = norm_back(token_rows, gain_a, normed_one_grad)
        input_grad = (hidden_grad + rows_branch).astype(bf16)[None]

        little = jnp.concatenate(
            [spare(router_wgrad), spare(jnp.stack([gain_one_grad, gain_two_grad], 1))], 1
        )
        qkv_shard, out_shard, little = weights_reduce(
            3,
            groups_count,
            (qkv_wgrad.astype(bf16), out_wgrad.astype(bf16), little),
        )
        experts_all = send_pieces(4, expert_grads)
        experts_all = experts_all.reshape((EXPERTS,) + experts_all.shape[2:])
        stat_sums = stat_sums + lax.ppermute(stat_sums, "seq", [(0, 1), (1, 0)])
        first = w_gate_up.shape[0]
        stream_rms = jnp.sqrt(stat_sums / (both * MODEL_WIDTH)).reshape(1, 2)
        return (
            output,
            input_grad,
            little[:, 128],
            qkv_shard.astype(f32),
            out_shard.astype(f32),
            little[:, 129],
            little[:, :EXPERTS],
            jnp.swapaxes(experts_all[:, :first], 0, 1).astype(f32),
            jnp.swapaxes(experts_all[:, first:], 0, 1).astype(f32),
            stream_rms,
        )

    return body


def solution(mesh):
    placed = (
        P("dp", "seq", None),
        P("dp", "seq"),
        P("dp", "seq", None),
        P("dp"),
        P("dp", None),
        P("dp", None),
        P("dp"),
        P("dp", None),
        P("dp", None, None),
        P("dp", None, None),
        P("dp", "seq", None),
    )
    return jax.shard_map(
        make_body(mesh.shape["dp"]),
        mesh=mesh,
        in_specs=placed,
        out_specs=(
            P("dp", "seq", None),
            P("dp", "seq", None),
            P("dp"),
            P("dp", None),
            P("dp", None),
            P("dp"),
            P("dp", None),
            P("dp", None, None),
            P("dp", None, None),
            P("dp", None),
        ),
        check_vma=False,
    )
```

```python
import functools

import jax
import jax.numpy as jnp
from jax import lax
from jax.experimental import pallas as pl
from jax.experimental.pallas import tpu as pltpu
from jax.sharding import PartitionSpec as P

MODEL_WIDTH = 1024
QUERY_HEADS = 16
KEY_VALUE_HEADS = 8
HEAD_SIZE = 64
F = 512
EXPERTS = 16
TOPK = 8
PLACES = 4
GROUP = 8
OWN = EXPERTS // GROUP

epsilon = 1e-06
rope_base = 10000.0
highest = lax.Precision.HIGHEST
masked_score = -1e30
f32 = jnp.float32
bf16 = jnp.bfloat16
MESH = pl.DeviceIdType.MESH

TOKEN_LINKS = ((4, 2), (2, 4))


def flip(value, bit):
    return value + bit * (1 - 2 * ((value // bit) % 2))


def flip_mask(value, mask):
    for bit in (1, 2, 4, 8):
        if mask & bit:
            value = flip(value, bit)
    return value


def subsets(bits):
    out = [0]
    for bit in bits:
        out = out + [m | bit for m in out]
    return out


def row_parts(rows):
    first = (rows // 2 + 15) // 16 * 16
    return ((0, first), (first, rows - first))


def my_place(places=PLACES):
    seq = lax.axis_index("seq")
    dp = lax.axis_index("dp")
    rank = seq * places + dp % places

    def peer(mask):
        return {
            "seq": 1 - seq if mask & places else seq,
            "dp": flip_mask(dp, mask & (places - 1)),
        }

    return rank, peer


def meet(devices):
    barrier = pltpu.get_barrier_semaphore()
    for there in devices:
        pl.semaphore_signal(barrier, inc=1, device_id=there, device_id_type=MESH)
    pl.semaphore_wait(barrier, len(devices))


def gather_kernel(count, *refs):
    ins, outs = refs[:count], refs[count : 2 * count]
    send, recv, send_core, recv_core, local = refs[2 * count :]
    rank, peer = my_place(PLACES)
    own = [
        pltpu.make_async_copy(ins[a], outs[a].at[rank], local.at[a]) for a in range(count)
    ]
    for copy in own:
        copy.start()
    meet([peer(bit) for bit in (1, 2, 4)])
    parts = [row_parts(ref.shape[0]) for ref in ins]

    def remote(a, p, mask, bit, sems, index):
        start, size = parts[a][p]
        rows = pl.ds(start, size)
        shard = flip_mask(rank, mask)
        src = ins[a].at[rows] if mask == 0 else outs[a].at[shard, rows]
        return pltpu.make_async_remote_copy(
            src_ref=src,
            dst_ref=outs[a].at[shard, rows],
            send_sem=sems[0].at[a, p, index],
            recv_sem=sems[1].at[a, p, index],
            device_id=peer(bit),
            device_id_type=MESH,
        )

    started = []
    live = {}
    for step in range(3):
        for p in range(2):
            for a in range(count):
                if parts[a][p][1] == 0:
                    continue
                order = TOKEN_LINKS[p]
                if step > 0:
                    for copy in live.pop((a, p)):
                        copy.wait_recv()
                if step < 2:
                    now = []
                    for index, mask in enumerate(subsets(order[:step])):
                        copy = remote(a, p, mask, order[step], (send, recv), 2**step - 1 + index)
                        copy.start()
                        now.append(copy)
                        started.append(copy)
                    live[(a, p)] = now
                fresh = [0] if step == 0 else [m | order[step - 1] for m in subsets(order[: step - 1])]
                base = 0 if step == 0 else 2 ** (step - 1)
                for index, mask in enumerate(fresh):
                    copy = remote(a, p, mask, 1, (send_core, recv_core), base + index)
                    copy.start()
                    live.setdefault("core", []).append(copy)
    for copy in live["core"]:
        copy.wait()
    for copy in started:
        copy.wait_send()
    for copy in own:
        copy.wait()


def group_gather(collective_id, *arrays):
    count = len(arrays)
    return pl.pallas_call(
        functools.partial(gather_kernel, count),
        out_shape=[jax.ShapeDtypeStruct((GROUP,) + a.shape, a.dtype) for a in arrays],
        in_specs=[pl.BlockSpec(memory_space=pltpu.VMEM)] * count,
        out_specs=[pl.BlockSpec(memory_space=pl.ANY)] * count,
        scratch_shapes=[
            pltpu.SemaphoreType.DMA((count, 2, 3)),
            pltpu.SemaphoreType.DMA((count, 2, 3)),
            pltpu.SemaphoreType.DMA((count, 2, 4)),
            pltpu.SemaphoreType.DMA((count, 2, 4)),
            pltpu.SemaphoreType.DMA((count,)),
        ],
        compiler_params=pltpu.CompilerParams(collective_id=collective_id, has_side_effects=True),
        cost_estimate=pl.CostEstimate(flops=1000000000, bytes_accessed=2**24, transcendentals=0),
        name="group_gather",
    )(*arrays)


def add_rows(target, source, start, size):
    def step(i, carry):
        rows = pl.ds(pl.multiple_of(start + i * 16, 16), 16)
        target[rows] = (target[rows].astype(f32) + source[rows].astype(f32)).astype(target.dtype)
        return carry

    lax.fori_loop(0, size // 16, step, 0)


def reduce_kernel(
    mixed_ref, normed_ref, gate_ref, mixed_out, normed_out, gate_out,
    total, got0, got1, got2, sems, gate_sems, local, own_gate,
):
    rank, peer = my_place(PLACES)
    chip = rank // 2
    core = rank % 2
    parts = row_parts(mixed_ref.shape[1])
    ins = (mixed_ref, normed_ref)
    outs = (mixed_out, normed_out)
    loads = []
    for t in range(2):
        for c in range(4):
            copy = pltpu.make_async_copy(ins[t].at[2 * c + core], total.at[t, c], local.at[t, c])
            copy.start()
            loads.append(copy)
    everyone = [peer(mask) for mask in range(1, GROUP)]
    meet(everyone)
    gates = []
    keep = pltpu.make_async_copy(gate_ref.at[rank], gate_out.at[rank], own_gate)
    keep.start()
    for mask, there in zip(range(1, GROUP), everyone):
        copy = pltpu.make_async_remote_copy(
            src_ref=gate_ref.at[flip_mask(rank, mask)],
            dst_ref=gate_out.at[rank],
            send_sem=gate_sems.at[0, mask],
            recv_sem=gate_sems.at[1, mask],
            device_id=there,
            device_id_type=MESH,
        )
        copy.start()
        gates.append(copy)

    started = []
    live = {}

    def send(t, p, stage, index, src, dst, bit):
        copy = pltpu.make_async_remote_copy(
            src_ref=src,
            dst_ref=dst,
            send_sem=sems.at[0, t, p, stage, index],
            recv_sem=sems.at[1, t, p, stage, index],
            device_id=peer(bit),
            device_id_type=MESH,
        )
        copy.start()
        started.append(copy)
        live.setdefault((t, p), []).append(copy)

    def chip_of(mask):
        return flip_mask(rank, mask) // 2

    for p in range(2):
        for t in range(2):
            rows = pl.ds(*parts[p])
            for c in range(4):
                send(
                    t, p, 0, c, ins[t].at[2 * c + 1 - core, rows], got0.at[t, c, rows], 1
                )
    for copy in loads:
        copy.wait()
    got = (got1, got2)
    for stage in range(3):
        for p in range(2):
            for t in range(2):
                order = TOKEN_LINKS[p]
                rows = pl.ds(*parts[p])
                for copy in live.pop((t, p)):
                    copy.wait_recv()
                if stage == 0:

                    def over_chips(c, carry, t=t, p=p):
                        add_rows(total.at[t, c], got0.at[t, c], *parts[p])
                        return carry

                    lax.fori_loop(0, 4, over_chips, 0)
                else:
                    for index, mask in enumerate(subsets(order[stage:])):
                        if stage == 2:
                            outs[t][rows] = total[t, chip, rows].astype(f32) + got2[t, 0, rows].astype(f32)
                        else:
                            add_rows(
                                total.at[t, chip_of(mask)], got[stage - 1].at[t, index], *parts[p]
                            )
                if stage < 2:
                    for index, mask in enumerate(subsets(order[stage + 1 :])):
                        send(
                            t, p, stage + 1, index,
                            total.at[t, chip_of(mask | order[stage]), rows],
                            got[stage].at[t, index, rows],
                            order[stage],
                        )
    for copy in started:
        copy.wait_send()
    for copy in gates:
        copy.wait()
    keep.wait()


def group_reduce(collective_id, mixed, normed, gate_grad):
    rows, width = mixed.shape[1:]
    return pl.pallas_call(
        reduce_kernel,
        out_shape=[
            jax.ShapeDtypeStruct((rows, width), f32),
            jax.ShapeDtypeStruct((rows, width), f32),
            jax.ShapeDtypeStruct(gate_grad.shape, gate_grad.dtype),
        ],
        in_specs=[pl.BlockSpec(memory_space=pl.ANY)] * 3,
        out_specs=[
            pl.BlockSpec(memory_space=pltpu.VMEM),
            pl.BlockSpec(memory_space=pltpu.VMEM),
            pl.BlockSpec(memory_space=pl.ANY),
        ],
        scratch_shapes=[
            pltpu.VMEM((2, 4, rows, width), bf16),
            pltpu.VMEM((2, 4, rows, width), bf16),
            pltpu.VMEM((2, 2, rows, width), bf16),
            pltpu.VMEM((2, 1, rows, width), bf16),
            pltpu.SemaphoreType.DMA((2, 2, 2, 3, 4)),
            pltpu.SemaphoreType.DMA((2, GROUP)),
            pltpu.SemaphoreType.DMA((2, 4)),
            pltpu.SemaphoreType.DMA(()),
        ],
        compiler_params=pltpu.CompilerParams(
            collective_id=collective_id, has_side_effects=True, vmem_limit_bytes=48 * 2**20
        ),
        cost_estimate=pl.CostEstimate(flops=1000000, bytes_accessed=2**24, transcendentals=0),
        name="group_reduce",
    )(mixed, normed, gate_grad)


def column_parts(half):
    first = -(-(half // 128) // 2) * 128
    return ((0, first), (first, half - first))


def shard_view(ref, halves, a, p, rank_value):
    start, size = column_parts(halves[a])[p]
    offset = pl.multiple_of((rank_value // PLACES) * halves[a] + start, 128)
    return ref.at[:, rank_value % PLACES, :, pl.ds(offset, size)]


def starts_of(sizes):
    return [sum(sizes[:i]) for i in range(len(sizes))]


def weights_gather_kernel(halves, packed, *refs):
    count = len(halves)
    outs = refs[:count]
    send, recv, local = refs[count:]
    rank, peer = my_place()
    firsts = starts_of(halves)
    seq = lax.axis_index("seq")
    own = []
    for a in range(count):
        columns = pl.ds(pl.multiple_of(seq * halves[a], 128), halves[a])
        copy = pltpu.make_async_copy(
            packed.at[:, :, pl.ds(firsts[a], halves[a])],
            outs[a].at[:, rank % PLACES, :, columns],
            local.at[a],
        )
        copy.start()
        own.append(copy)
    meet([peer(bit) for bit in (1, 2, 4)])
    started = []

    def remote(a, p, mask, bit, index):
        view = shard_view(outs[a], halves, a, p, flip_mask(rank, mask))
        start, size = column_parts(halves[a])[p]
        source = packed.at[:, :, pl.ds(firsts[a] + start, size)] if mask == 0 else view
        copy = pltpu.make_async_remote_copy(
            src_ref=source,
            dst_ref=view,
            send_sem=send.at[a, p, index],
            recv_sem=recv.at[a, p, index],
            device_id=peer(bit),
            device_id_type=MESH,
        )
        copy.start()
        started.append(copy)
        return copy

    live = {}
    last = []
    for step in range(3):
        for p in range(2):
            for a in range(count):
                if column_parts(halves[a])[p][1] == 0:
                    continue
                order = TOKEN_LINKS[p]
                if step > 0:
                    for copy in live.pop((a, p)):
                        copy.wait_recv()
                if step < 2:
                    live[(a, p)] = [
                        remote(a, p, mask, order[step], 2**step - 1 + index)
                        for index, mask in enumerate(subsets(order[:step]))
                    ]
                fresh = [0] if step == 0 else [m | order[step - 1] for m in subsets(order[: step - 1])]
                base = 0 if step == 0 else 2 ** (step - 1)
                for index, mask in enumerate(fresh):
                    last.append(remote(a, p, mask, 1, 3 + base + index))
    for copy in last:
        copy.wait_recv()
    for copy in started:
        copy.wait_send()
    for copy in own:
        copy.wait()


def weights_gather(collective_id, halves, packed):
    groups, rows, _ = packed.shape
    count = len(halves)
    whole = pl.pallas_call(
        functools.partial(weights_gather_kernel, halves),
        out_shape=[jax.ShapeDtypeStruct((groups, PLACES, rows, 2 * h), packed.dtype) for h in halves],
        in_specs=[pl.BlockSpec(memory_space=pltpu.VMEM)],
        out_specs=[pl.BlockSpec(memory_space=pl.ANY)] * count,
        scratch_shapes=[
            pltpu.SemaphoreType.DMA((count, 2, 7)),
            pltpu.SemaphoreType.DMA((count, 2, 7)),
            pltpu.SemaphoreType.DMA((count,)),
        ],
        compiler_params=pltpu.CompilerParams(collective_id=collective_id, has_side_effects=True),
        cost_estimate=pl.CostEstimate(flops=1000000, bytes_accessed=2**24, transcendentals=0),
        name="weights_gather",
    )(packed)
    return [w.reshape(-1, w.shape[3]) for w in whole]


def add_block(target, source, at, start, size):
    groups, rows = source.shape[0], source.shape[1]
    columns = pl.ds(start, size)
    pieces = rows // 16

    def step(i, carry):
        lines = pl.ds(pl.multiple_of((i % pieces) * 16, 16), 16)
        index = (i // pieces, lines, columns)
        new = target[(at,) + index].astype(f32) + source[index].astype(f32)
        target[(at,) + index] = new.astype(target.dtype)
        return carry

    lax.fori_loop(0, groups * pieces, step, 0)


def weights_reduce_kernel(count, *refs):
    ins, packed = refs[:count], refs[count]
    rest = refs[count + 1 :]
    total, got0, got1, got2 = [rest[i * count : (i + 1) * count] for i in range(4)]
    sems, local = rest[4 * count :]
    rank, peer = my_place()
    chip, core = rank // 2, rank % 2
    halves = [ref.shape[3] // 2 for ref in ins]
    firsts = starts_of(halves)
    parts = [column_parts(half) for half in halves]
    loads = []
    for a in range(count):
        for c in range(4):
            value = 2 * c + core
            offset = pl.multiple_of((value // PLACES) * halves[a], 128)
            copy = pltpu.make_async_copy(
                ins[a].at[:, value % PLACES, :, pl.ds(offset, halves[a])],
                total[a].at[c],
                local.at[a, c],
            )
            copy.start()
            loads.append(copy)
    meet([peer(bit) for bit in (1, 2, 4)])
    started = []
    live = {}

    def send(a, p, stage, index, src, dst, bit):
        copy = pltpu.make_async_remote_copy(
            src_ref=src,
            dst_ref=dst,
            send_sem=sems.at[0, a, p, stage, index],
            recv_sem=sems.at[1, a, p, stage, index],
            device_id=peer(bit),
            device_id_type=MESH,
        )
        copy.start()
        started.append(copy)
        live.setdefault((a, p), []).append(copy)

    def chip_of(mask):
        return flip_mask(rank, mask) // 2

    for p in range(2):
        for a in range(count):
            columns = pl.ds(*parts[a][p])
            if parts[a][p][1]:
                for c in range(4):
                    send(
                        a, p, 0, c,
                        shard_view(ins[a], halves, a, p, 2 * c + 1 - core),
                        got0[a].at[c, :, :, columns],
                        1,
                    )
    for copy in loads:
        copy.wait()
    got = (got1, got2)
    for stage in range(3):
        for p in range(2):
            for a in range(count):
                start, size = parts[a][p]
                if size == 0:
                    continue
                order = TOKEN_LINKS[p]
                columns = pl.ds(start, size)
                for copy in live.pop((a, p)):
                    copy.wait_recv()
                if stage == 0:

                    def over_chips(c, carry, a=a, start=start, size=size):
                        add_block(total[a], got0[a].at[c], c, start, size)
                        return carry

                    lax.fori_loop(0, 4, over_chips, 0)
                else:
                    for index, mask in enumerate(subsets(order[stage:])):
                        add_block(total[a], got[stage - 1][a].at[index], chip_of(mask), start, size)
                if stage < 2:
                    for index, mask in enumerate(subsets(order[stage + 1 :])):
                        send(
                            a, p, stage + 1, index,
                            total[a].at[chip_of(mask | order[stage]), :, :, columns],
                            got[stage][a].at[index, :, :, columns],
                            order[stage],
                        )
    for a in range(count):
        packed[:, :, pl.ds(firsts[a], halves[a])] = total[a][chip].astype(packed.dtype)
    for copy in started:
        copy.wait_send()


def weights_reduce(collective_id, groups, arrays):
    count = len(arrays)
    views = [a.reshape(groups, PLACES, -1, a.shape[1]) for a in arrays]
    rows = views[0].shape[2]
    halves = [a.shape[1] // 2 for a in arrays]

    def buffers(lead):
        return [pltpu.VMEM((lead, groups, rows, h), a.dtype) for h, a in zip(halves, arrays)]

    dma = pltpu.SemaphoreType.DMA
    return pl.pallas_call(
        functools.partial(weights_reduce_kernel, count),
        out_shape=jax.ShapeDtypeStruct((groups, rows, sum(halves)), bf16),
        in_specs=[pl.BlockSpec(memory_space=pl.ANY)] * count,
        out_specs=pl.BlockSpec(memory_space=pltpu.VMEM),
        scratch_shapes=buffers(4) + buffers(4) + buffers(2) + buffers(1)
        + [dma((2, count, 2, 3, 4)), dma((count, 4))],
        compiler_params=pltpu.CompilerParams(
            collective_id=collective_id, has_side_effects=True, vmem_limit_bytes=48 * 2**20
        ),
        cost_estimate=pl.CostEstimate(flops=1000000, bytes_accessed=2**24, transcendentals=0),
        name="weights_reduce",
    )(*views)


def pieces_kernel(pieces, whole, send, recv, local):
    rank, peer = my_place(PLACES)
    place = rank % PLACES
    keep = pltpu.make_async_copy(pieces.at[place], whole.at[rank], local)
    keep.start()
    masks = (6, 7, 2, 4, 3, 5, 1)
    meet([peer(mask) for mask in masks])
    copies = []
    for mask in masks:
        copy = pltpu.make_async_remote_copy(
            src_ref=pieces.at[flip_mask(place, mask & (PLACES - 1))],
            dst_ref=whole.at[rank],
            send_sem=send.at[mask],
            recv_sem=recv.at[mask],
            device_id=peer(mask),
            device_id_type=MESH,
        )
        copy.start()
        copies.append(copy)
    for copy in copies:
        copy.wait()
    keep.wait()


def send_pieces(collective_id, pieces):
    return pl.pallas_call(
        pieces_kernel,
        out_shape=jax.ShapeDtypeStruct((GROUP,) + pieces.shape[1:], pieces.dtype),
        in_specs=[pl.BlockSpec(memory_space=pltpu.VMEM)],
        out_specs=pl.BlockSpec(memory_space=pl.ANY),
        scratch_shapes=[
            pltpu.SemaphoreType.DMA((GROUP,)),
            pltpu.SemaphoreType.DMA((GROUP,)),
            pltpu.SemaphoreType.DMA(()),
        ],
        compiler_params=pltpu.CompilerParams(collective_id=collective_id, has_side_effects=True),
        name="send_pieces",
    )(pieces)


def expert_kernel(
    first, rows_ref, grad_ref, gate_ref, weights_ref,
    mixed_ref, normed_ref, gate_grad_ref, weights_out,
    gate_up_sum, down_sum, mixed_sum, normed_sum,
):
    step = pl.program_id(0)
    expert = pl.program_id(1)
    shards, each, width = rows_ref.shape
    count = shards * each
    rows = rows_ref[...].reshape(count, width)
    grad = grad_ref[...].reshape(count, width).astype(f32)
    gate = jnp.concatenate(
        [
            jnp.broadcast_to(gate_ref[i, pl.ds(expert, 1)], (128, each)).T[:, :1]
            for i in range(shards)
        ],
        0,
    )
    gate_up_weight = weights_ref[:, expert, :first].reshape(-1, width)
    down = weights_ref[:, expert, first:].reshape(-1, width)
    gate_up = jnp.dot(rows, gate_up_weight, preferred_element_type=f32)
    gate_part, up_part = gate_up[:, :F], gate_up[:, F:]
    sigmoid = 1.0 / (1.0 + jnp.exp(-gate_part))
    silu = gate_part * sigmoid
    act = (silu * up_part).astype(bf16)
    out = jnp.dot(act, down, preferred_element_type=f32)
    inner = jnp.sum(out * grad, axis=-1, keepdims=True)
    for i in range(shards):
        line = jnp.broadcast_to(inner[i * each : (i + 1) * each], (each, 128)).T
        gate_grad_ref[i, pl.ds(expert, 1)] = line[:1]
    mixed = gate * out
    expert_grad = (gate * grad).astype(bf16)
    across = (((1,), (1,)), ((), ()))
    over_rows = (((0,), (0,)), ((), ()))
    act_grad = lax.dot_general(expert_grad, down, across, preferred_element_type=f32)
    gate_up_grad = jnp.concatenate(
        [act_grad * up_part * (sigmoid * (1.0 + gate_part * (1.0 - sigmoid))), act_grad * silu], -1
    ).astype(bf16)
    normed = lax.dot_general(gate_up_grad, gate_up_weight, across, preferred_element_type=f32)

    @pl.when(expert == 0)
    def _():
        mixed_sum[...] = mixed
        normed_sum[...] = normed

    @pl.when(expert > 0)
    def _():
        mixed_sum[...] += mixed
        normed_sum[...] += normed

    @pl.when(expert == OWN - 1)
    def _():
        mixed_ref[...] = mixed_sum[...].astype(bf16).reshape(shards, each, width)
        normed_ref[...] = normed_sum[...].astype(bf16).reshape(shards, each, width)

    @pl.when(step == 0)
    def _():
        gate_up_sum[expert] = jnp.zeros_like(gate_up_sum[0])
        down_sum[expert] = jnp.zeros_like(down_sum[0])

    down_sum[expert] += lax.dot_general(act, expert_grad, over_rows, preferred_element_type=f32)
    gate_up_sum[expert] += lax.dot_general(rows, gate_up_grad, over_rows, preferred_element_type=f32)

    @pl.when(step == pl.num_programs(0) - 1)
    def _():
        owners = weights_out.shape[0]
        weights_out[:, expert, :first] = gate_up_sum[expert].astype(bf16).reshape(owners, first, width)
        weights_out[:, expert, first:] = down_sum[expert].astype(bf16).reshape(owners, -1, width)


def expert_layer(first, rows, grad, gate, weights):
    each, width = rows.shape[1:]
    shards = 2
    owners = weights.shape[0]
    tile = pl.BlockSpec((shards, each, width), lambda i, e: (i, 0, 0))
    whole = pl.BlockSpec(weights.shape, lambda i, e: (0, 0, 0, 0), pipeline_mode=pl.Buffered(1))
    return pl.pallas_call(
        functools.partial(expert_kernel, first),
        grid=(GROUP // shards, OWN),
        out_shape=[
            jax.ShapeDtypeStruct(rows.shape, bf16),
            jax.ShapeDtypeStruct(rows.shape, bf16),
            jax.ShapeDtypeStruct((GROUP, 8, each), f32),
            jax.ShapeDtypeStruct(weights.shape, bf16),
        ],
        in_specs=[
            tile,
            tile,
            pl.BlockSpec((shards, OWN, each), lambda i, e: (i, 0, 0)),
            whole,
        ],
        out_specs=[
            tile,
            tile,
            pl.BlockSpec((shards, 8, each), lambda i, e: (i, 0, 0)),
            whole,
        ],
        scratch_shapes=[
            pltpu.VMEM((OWN, owners * first, width), f32),
            pltpu.VMEM((OWN, owners * (weights.shape[2] - first), width), f32),
            pltpu.VMEM((shards * each, width), f32),
            pltpu.VMEM((shards * each, width), f32),
        ],
        compiler_params=pltpu.CompilerParams(vmem_limit_bytes=62 * 2**20),
        cost_estimate=pl.CostEstimate(flops=45000000000, bytes_accessed=2**24, transcendentals=0),
        name="expert_layer",
    )(rows, grad, gate, weights)


def inverse_rms(rows):
    return lax.rsqrt(jnp.mean(rows * rows, axis=-1, keepdims=True) + epsilon)


def norm_back(rows, gain_row, upstream):
    inverse = inverse_rms(rows)
    gain_grad = jnp.sum(upstream * rows * inverse, axis=0)
    scaled = upstream * gain_row
    rows_grad = inverse * scaled - rows * inverse**3 * jnp.mean(scaled * rows, axis=-1, keepdims=True)
    return rows_grad, gain_grad


def rope_tables(positions):
    half = HEAD_SIZE // 2
    frequency = rope_base ** (-(jnp.arange(half, dtype=f32) * 2.0) / HEAD_SIZE)
    angles = positions.astype(f32)[:, None] * frequency[None, :]
    cosine, sine = jnp.cos(angles), jnp.sin(angles)
    return jnp.concatenate([cosine, cosine], 1), jnp.concatenate([sine, sine], 1)


def rotary_apply(rows, cosine, sine):
    half = HEAD_SIZE // 2
    turned = jnp.concatenate([-rows[..., half:], rows[..., :half]], -1)
    return rows * cosine[:, None, :] + turned * sine[:, None, :]


def unrotate(rows, cosine, sine):
    half = HEAD_SIZE // 2
    scaled = rows * sine[:, None, :]
    back = jnp.concatenate([scaled[..., half:], -scaled[..., :half]], -1)
    return rows * cosine[:, None, :] + back


def make_body(n_dp):
    expert_groups = n_dp // PLACES
    inside = [[g * PLACES + j for j in range(PLACES)] for g in range(expert_groups)]
    between = [[g * PLACES + j for g in range(expert_groups)] for j in range(PLACES)]
    half_experts = EXPERTS // 2

    def expert_pieces(gate_up_shard, down_shard, seq_rank):
        mine = [
            jnp.swapaxes(lax.dynamic_slice_in_dim(w, seq_rank * half_experts, half_experts, axis=1), 0, 1)
            for w in (gate_up_shard, down_shard)
        ]
        mine = jnp.concatenate(mine, 1)
        mine = mine.reshape((PLACES, OWN) + mine.shape[1:])
        return lax.all_to_all(
            mine, "dp", split_axis=0, concat_axis=0, tiled=True, axis_index_groups=inside
        )

    def body(
        tokens, starts, routes, gain_one, query_key_value_weight, w_out,
        gain_two, w_router, w_gate_up, w_down, cotangent,
    ):
        count = tokens.shape[1]
        seq_rank = lax.axis_index("seq")
        expert = (seq_rank * PLACES + lax.axis_index("dp") % PLACES) * OWN
        query_columns = QUERY_HEADS * HEAD_SIZE
        key_columns = KEY_VALUE_HEADS * HEAD_SIZE
        group = QUERY_HEADS // KEY_VALUE_HEADS
        forward_pair, back_pair = [(0, 1)], [(1, 0)]

        mine = expert_pieces(w_gate_up, w_down, seq_rank)
        tokens_before = lax.ppermute(tokens[0], "seq", forward_pair)
        starts_before = lax.ppermute(starts, "seq", forward_pair)
        spare = lambda value: jnp.pad(value, ((0, 0), (0, 128 - value.shape[1])))
        little = jnp.concatenate([spare(w_router), spare(jnp.stack([gain_one, gain_two], 1))], 1)
        shards = (query_key_value_weight, w_out, little)
        halves = [w.shape[1] // 2 for w in shards]
        packed = lax.all_gather(
            jnp.concatenate(
                [
                    lax.dynamic_slice_in_dim(w, seq_rank * h, h, axis=1)
                    for w, h in zip(shards, halves)
                ],
                1,
            ),
            "dp", axis=0, axis_index_groups=between,
        )
        mine, packed = lax.optimization_barrier((mine, packed))
        weights = lax.all_gather(mine, "dp", axis=0, tiled=True, axis_index_groups=between)
        qkv_weight, out_weight, small = weights_gather(0, halves, packed)
        router_weight = small[:, :EXPERTS]
        gain_a = small[:, 128].astype(f32)
        gain_b = small[:, 129].astype(f32)

        token_rows = tokens[0].astype(f32)
        grad_output = cotangent[0].astype(f32)
        both = 2 * count
        index = jnp.arange(both, dtype=jnp.int32)
        flags = jnp.concatenate([starts_before[0], starts[0]])
        begins = (flags > 0) | (index == jnp.where(seq_rank == 0, count, 0))
        last_begin = jnp.max(
            jnp.where(begins[None, :] & (index[None, :] <= index[:, None]), index[None, :], 0), axis=1
        )
        cosine_all, sine_all = rope_tables(index - last_begin)
        cosine, sine = cosine_all[count:], sine_all[count:]

        rows_all = jnp.concatenate([tokens_before.astype(f32), token_rows], 0)
        normed_all = (rows_all * inverse_rms(rows_all) * gain_a).astype(bf16)
        normed_one = normed_all[count:]
        projected_q = jnp.dot(normed_one, qkv_weight[:, :query_columns], preferred_element_type=f32)
        projected_kv = jnp.dot(normed_all, qkv_weight[:, query_columns:], preferred_element_type=f32)
        queries = rotary_apply(
            projected_q.reshape(count, QUERY_HEADS, HEAD_SIZE), cosine, sine
        ).astype(bf16).reshape(count, KEY_VALUE_HEADS, group, HEAD_SIZE)
        keys = rotary_apply(
            projected_kv[:, :key_columns].reshape(both, KEY_VALUE_HEADS, HEAD_SIZE), cosine_all, sine_all
        ).astype(bf16)
        values = projected_kv[:, key_columns:].astype(bf16).reshape(both, KEY_VALUE_HEADS, HEAD_SIZE)

        scale = HEAD_SIZE ** (-0.5)
        allowed = (index[None, :] <= index[count:, None]) & (index[None, :] >= last_begin[count:, None])
        scores = jnp.einsum("qgrd,kgd->grqk", queries, keys, preferred_element_type=f32) * scale
        scores = jnp.where(allowed[None, None], scores, masked_score)
        top = jnp.max(scores, axis=-1, keepdims=True)
        exps = jnp.exp(scores - top)
        probs = exps / jnp.sum(exps, axis=-1, keepdims=True)
        probs_low = probs.astype(bf16)
        attended = jnp.einsum(
            "grqk,kgd->qgrd", probs_low, values, preferred_element_type=f32
        ).reshape(count, query_columns).astype(bf16)
        hidden = token_rows + jnp.dot(attended, out_weight, preferred_element_type=f32)
        normed_two = (hidden * inverse_rms(hidden) * gain_b).astype(bf16)
        logits = jnp.dot(normed_two, router_weight, preferred_element_type=f32)
        expert_ids = jnp.arange(EXPERTS, dtype=jnp.int32)
        chosen = jnp.any(routes[0][:, :, None] == expert_ids[None, None, :], axis=1)
        gates = jax.nn.softmax(jnp.where(chosen, logits, -jnp.inf), axis=-1)

        rows_in, gates_all, grad_all = group_gather(1, normed_two, gates.T, cotangent[0])
        gate = lax.dynamic_slice_in_dim(gates_all, expert, OWN, axis=1)
        mixed_part, normed_part, gate_grad_part, expert_wgrads = expert_layer(
            w_gate_up.shape[0], rows_in, grad_all, gate, weights
        )
        expert_grads = lax.psum_scatter(
            expert_wgrads, "dp", scatter_dimension=0, tiled=True, axis_index_groups=between
        )
        mixed, normed_grad, gate_grad = group_reduce(2, mixed_part, normed_part, gate_grad_part)
        gate_grad = gate_grad[:, :OWN].reshape(EXPERTS, count).T

        over_rows = (((0,), (0,)), ((), ()))
        output = (hidden + mixed).astype(bf16)[None]
        stat_sums = jnp.stack([jnp.sum(hidden * hidden), jnp.sum(mixed * mixed)])
        weighted = jnp.where(chosen, gates * gate_grad, 0.0)
        logits_grad = weighted - gates * jnp.sum(weighted, axis=-1, keepdims=True)
        router_wide = router_weight.astype(f32)
        normed_grad = normed_grad + jnp.dot(logits_grad, router_wide.T, precision=highest)
        router_wgrad = jnp.dot(normed_two.astype(f32).T, logits_grad, precision=highest)
        hidden_branch, gain_two_grad = norm_back(hidden, gain_b, normed_grad)
        hidden_grad = grad_output + hidden_branch
        branch_low = hidden_grad.astype(bf16)
        out_wgrad = lax.dot_general(attended, branch_low, over_rows, preferred_element_type=f32)
        attended_grad = lax.dot_general(
            branch_low, out_weight, (((1,), (1,)), ((), ())), preferred_element_type=f32
        ).astype(bf16).reshape(count, KEY_VALUE_HEADS, group, HEAD_SIZE)

        prob_grad = jnp.einsum("qgrd,kgd->grqk", attended_grad, values, preferred_element_type=f32)
        delta = jnp.sum(probs * prob_grad, axis=-1, keepdims=True)
        score_grad = (probs * (prob_grad - delta)).astype(bf16)
        query_grad = (
            jnp.einsum("grqk,kgd->qgrd", score_grad, keys, preferred_element_type=f32) * scale
        ).reshape(count, QUERY_HEADS, HEAD_SIZE)
        key_grad = (
            jnp.einsum("grqk,qgrd->kgd", score_grad, queries, preferred_element_type=f32) * scale
        ).reshape(both, key_columns)
        value_grad = jnp.einsum(
            "grqk,qgrd->kgd", probs_low, attended_grad, preferred_element_type=f32
        ).reshape(both, key_columns)
        kv_grad = jnp.concatenate([key_grad, value_grad], 1)
        kv_back = lax.ppermute(kv_grad[:count].astype(bf16), "seq", back_pair)
        kv_grad = (kv_grad[count:] + kv_back.astype(f32)).astype(bf16).astype(f32)
        query_grad = query_grad.astype(bf16).astype(f32)
        query_back = unrotate(query_grad, cosine, sine).reshape(count, query_columns)
        key_back = unrotate(
            kv_grad[:, :key_columns].reshape(count, KEY_VALUE_HEADS, HEAD_SIZE), cosine, sine
        ).reshape(count, key_columns)
        projected_grad = jnp.concatenate([query_back, key_back, kv_grad[:, key_columns:]], 1).astype(bf16)
        qkv_wgrad = lax.dot_general(normed_one, projected_grad, over_rows, preferred_element_type=f32)
        normed_one_grad = lax.dot_general(
            projected_grad, qkv_weight, (((1,), (1,)), ((), ())), preferred_element_type=f32
        )
        rows_branch, gain_one_grad = norm_back(token_rows, gain_a, normed_one_grad)
        input_grad = (hidden_grad + rows_branch).astype(bf16)[None]

        little = jnp.concatenate(
            [spare(router_wgrad), spare(jnp.stack([gain_one_grad, gain_two_grad], 1))], 1
        )
        packed = weights_reduce(
            3, expert_groups, (qkv_wgrad.astype(bf16), out_wgrad.astype(bf16), little)
        )
        packed, expert_grads = lax.optimization_barrier((packed, expert_grads))
        packed = lax.psum_scatter(
            packed, "dp", scatter_dimension=0, tiled=True, axis_index_groups=between
        )[0]
        across = lax.ppermute(packed, "seq", [(0, 1), (1, 0)])
        ends = jnp.where(seq_rank == 0, jnp.stack([packed, across]), jnp.stack([across, packed]))
        qkv_shard, out_shard, little = [
            jnp.concatenate([ends[0, :, f : f + h], ends[1, :, f : f + h]], 1).astype(f32)
            for f, h in zip(starts_of(halves), halves)
        ]
        experts_all = send_pieces(4, expert_grads)
        experts_all = experts_all.reshape((EXPERTS,) + experts_all.shape[2:])
        stat_sums = stat_sums + lax.ppermute(stat_sums, "seq", [(0, 1), (1, 0)])
        first = w_gate_up.shape[0]
        stream_rms = jnp.sqrt(stat_sums / (both * MODEL_WIDTH)).reshape(1, 2)
        return (
            output,
            input_grad,
            little[:, 128],
            qkv_shard,
            out_shard,
            little[:, 129],
            little[:, :EXPERTS],
            jnp.swapaxes(experts_all[:, :first], 0, 1).astype(f32),
            jnp.swapaxes(experts_all[:, first:], 0, 1).astype(f32),
            stream_rms,
        )

    return body


def solution(mesh):
    placed = (
        P("dp", "seq", None),
        P("dp", "seq"),
        P("dp", "seq", None),
        P("dp"),
        P("dp", None),
        P("dp", None),
        P("dp"),
        P("dp", None),
        P("dp", None, None),
        P("dp", None, None),
        P("dp", "seq", None),
    )
    return jax.shard_map(
        make_body(mesh.shape["dp"]),
        mesh=mesh,
        in_specs=placed,
        out_specs=(
            P("dp", "seq", None),
            P("dp", "seq", None),
            P("dp"),
            P("dp", None),
            P("dp", None),
            P("dp"),
            P("dp", None),
            P("dp", None, None),
            P("dp", None, None),
            P("dp", None),
        ),
        check_vma=False,
    )
```

```python
import functools

import jax
import jax.numpy as jnp
from jax import lax
from jax.experimental import pallas as pl
from jax.experimental.pallas import tpu as pltpu
from jax.sharding import PartitionSpec as P

MODEL_WIDTH = 1024
QUERY_HEADS = 16
KEY_VALUE_HEADS = 8
HEAD_SIZE = 64
F = 512
EXPERTS = 16
TOPK = 8
PLACES = 4
GROUP = 8
OWN = EXPERTS // GROUP

epsilon = 1e-06
rope_base = 10000.0
highest = lax.Precision.HIGHEST
masked_score = -1e30
f32 = jnp.float32
bf16 = jnp.bfloat16
MESH = pl.DeviceIdType.MESH

TOKEN_LINKS = ((4, 2), (2, 4))


def flip(value, bit):
    return value + bit * (1 - 2 * ((value // bit) % 2))


def flip_mask(value, mask):
    for bit in (1, 2, 4, 8):
        if mask & bit:
            value = flip(value, bit)
    return value


def subsets(bits):
    out = [0]
    for bit in bits:
        out = out + [m | bit for m in out]
    return out


def row_parts(rows):
    first = (rows // 2 + 15) // 16 * 16
    return ((0, first), (first, rows - first))


def my_place(places=PLACES):
    seq = lax.axis_index("seq")
    dp = lax.axis_index("dp")
    rank = seq * places + dp % places

    def peer(mask):
        return {
            "seq": 1 - seq if mask & places else seq,
            "dp": flip_mask(dp, mask & (places - 1)),
        }

    return rank, peer


def meet(devices):
    barrier = pltpu.get_barrier_semaphore()
    for there in devices:
        pl.semaphore_signal(barrier, inc=1, device_id=there, device_id_type=MESH)
    pl.semaphore_wait(barrier, len(devices))


def gather_kernel(count, *refs):
    ins, outs = refs[:count], refs[count : 2 * count]
    send, recv, send_core, recv_core, local = refs[2 * count :]
    rank, peer = my_place(PLACES)
    own = [
        pltpu.make_async_copy(ins[a], outs[a].at[rank], local.at[a]) for a in range(count)
    ]
    for copy in own:
        copy.start()
    meet([peer(bit) for bit in (1, 2, 4)])
    parts = [row_parts(ref.shape[0]) for ref in ins]

    def remote(a, p, mask, bit, sems, index):
        start, size = parts[a][p]
        rows = pl.ds(start, size)
        shard = flip_mask(rank, mask)
        src = ins[a].at[rows] if mask == 0 else outs[a].at[shard, rows]
        return pltpu.make_async_remote_copy(
            src_ref=src,
            dst_ref=outs[a].at[shard, rows],
            send_sem=sems[0].at[a, p, index],
            recv_sem=sems[1].at[a, p, index],
            device_id=peer(bit),
            device_id_type=MESH,
        )

    started = []
    live = {}
    for step in range(3):
        for p in range(2):
            for a in range(count):
                if parts[a][p][1] == 0:
                    continue
                order = TOKEN_LINKS[p]
                if step > 0:
                    for copy in live.pop((a, p)):
                        copy.wait_recv()
                if step < 2:
                    now = []
                    for index, mask in enumerate(subsets(order[:step])):
                        copy = remote(a, p, mask, order[step], (send, recv), 2**step - 1 + index)
                        copy.start()
                        now.append(copy)
                        started.append(copy)
                    live[(a, p)] = now
                fresh = [0] if step == 0 else [m | order[step - 1] for m in subsets(order[: step - 1])]
                base = 0 if step == 0 else 2 ** (step - 1)
                for index, mask in enumerate(fresh):
                    copy = remote(a, p, mask, 1, (send_core, recv_core), base + index)
                    copy.start()
                    live.setdefault("core", []).append(copy)
    for copy in live["core"]:
        copy.wait()
    for copy in started:
        copy.wait_send()
    for copy in own:
        copy.wait()


def group_gather(collective_id, *arrays):
    count = len(arrays)
    return pl.pallas_call(
        functools.partial(gather_kernel, count),
        out_shape=[jax.ShapeDtypeStruct((GROUP,) + a.shape, a.dtype) for a in arrays],
        in_specs=[pl.BlockSpec(memory_space=pltpu.VMEM)] * count,
        out_specs=[pl.BlockSpec(memory_space=pl.ANY)] * count,
        scratch_shapes=[
            pltpu.SemaphoreType.DMA((count, 2, 3)),
            pltpu.SemaphoreType.DMA((count, 2, 3)),
            pltpu.SemaphoreType.DMA((count, 2, 4)),
            pltpu.SemaphoreType.DMA((count, 2, 4)),
            pltpu.SemaphoreType.DMA((count,)),
        ],
        compiler_params=pltpu.CompilerParams(collective_id=collective_id, has_side_effects=True),
        cost_estimate=pl.CostEstimate(flops=1000000000, bytes_accessed=2**24, transcendentals=0),
        name="group_gather",
    )(*arrays)


def add_rows(target, source, start, size):
    def step(i, carry):
        rows = pl.ds(pl.multiple_of(start + i * 16, 16), 16)
        target[rows] = (target[rows].astype(f32) + source[rows].astype(f32)).astype(target.dtype)
        return carry

    lax.fori_loop(0, size // 16, step, 0)


def reduce_kernel(
    mixed_ref, normed_ref, gate_ref, mixed_out, normed_out, gate_out,
    total, got0, got1, got2, sems, gate_sems, local, own_gate,
):
    rank, peer = my_place(PLACES)
    chip = rank // 2
    core = rank % 2
    parts = row_parts(mixed_ref.shape[1])
    ins = (mixed_ref, normed_ref)
    outs = (mixed_out, normed_out)
    loads = []
    for t in range(2):
        for c in range(4):
            copy = pltpu.make_async_copy(ins[t].at[2 * c + core], total.at[t, c], local.at[t, c])
            copy.start()
            loads.append(copy)
    everyone = [peer(mask) for mask in range(1, GROUP)]
    meet(everyone)
    gates = []
    keep = pltpu.make_async_copy(gate_ref.at[rank], gate_out.at[rank], own_gate)
    keep.start()
    for mask, there in zip(range(1, GROUP), everyone):
        copy = pltpu.make_async_remote_copy(
            src_ref=gate_ref.at[flip_mask(rank, mask)],
            dst_ref=gate_out.at[rank],
            send_sem=gate_sems.at[0, mask],
            recv_sem=gate_sems.at[1, mask],
            device_id=there,
            device_id_type=MESH,
        )
        copy.start()
        gates.append(copy)

    started = []
    live = {}

    def send(t, p, stage, index, src, dst, bit):
        copy = pltpu.make_async_remote_copy(
            src_ref=src,
            dst_ref=dst,
            send_sem=sems.at[0, t, p, stage, index],
            recv_sem=sems.at[1, t, p, stage, index],
            device_id=peer(bit),
            device_id_type=MESH,
        )
        copy.start()
        started.append(copy)
        live.setdefault((t, p), []).append(copy)

    def chip_of(mask):
        return flip_mask(rank, mask) // 2

    for p in range(2):
        for t in range(2):
            rows = pl.ds(*parts[p])
            for c in range(4):
                send(
                    t, p, 0, c, ins[t].at[2 * c + 1 - core, rows], got0.at[t, c, rows], 1
                )
    for copy in loads:
        copy.wait()
    got = (got1, got2)
    for stage in range(3):
        for p in range(2):
            for t in range(2):
                order = TOKEN_LINKS[p]
                rows = pl.ds(*parts[p])
                for copy in live.pop((t, p)):
                    copy.wait_recv()
                if stage == 0:

                    def over_chips(c, carry, t=t, p=p):
                        add_rows(total.at[t, c], got0.at[t, c], *parts[p])
                        return carry

                    lax.fori_loop(0, 4, over_chips, 0)
                else:
                    for index, mask in enumerate(subsets(order[stage:])):
                        if stage == 2:
                            outs[t][rows] = total[t, chip, rows].astype(f32) + got2[t, 0, rows].astype(f32)
                        else:
                            add_rows(
                                total.at[t, chip_of(mask)], got[stage - 1].at[t, index], *parts[p]
                            )
                if stage < 2:
                    for index, mask in enumerate(subsets(order[stage + 1 :])):
                        send(
                            t, p, stage + 1, index,
                            total.at[t, chip_of(mask | order[stage]), rows],
                            got[stage].at[t, index, rows],
                            order[stage],
                        )
    for copy in started:
        copy.wait_send()
    for copy in gates:
        copy.wait()
    keep.wait()


def group_reduce(collective_id, mixed, normed, gate_grad):
    rows, width = mixed.shape[1:]
    return pl.pallas_call(
        reduce_kernel,
        out_shape=[
            jax.ShapeDtypeStruct((rows, width), f32),
            jax.ShapeDtypeStruct((rows, width), f32),
            jax.ShapeDtypeStruct(gate_grad.shape, gate_grad.dtype),
        ],
        in_specs=[pl.BlockSpec(memory_space=pl.ANY)] * 3,
        out_specs=[
            pl.BlockSpec(memory_space=pltpu.VMEM),
            pl.BlockSpec(memory_space=pltpu.VMEM),
            pl.BlockSpec(memory_space=pl.ANY),
        ],
        scratch_shapes=[
            pltpu.VMEM((2, 4, rows, width), bf16),
            pltpu.VMEM((2, 4, rows, width), bf16),
            pltpu.VMEM((2, 2, rows, width), bf16),
            pltpu.VMEM((2, 1, rows, width), bf16),
            pltpu.SemaphoreType.DMA((2, 2, 2, 3, 4)),
            pltpu.SemaphoreType.DMA((2, GROUP)),
            pltpu.SemaphoreType.DMA((2, 4)),
            pltpu.SemaphoreType.DMA(()),
        ],
        compiler_params=pltpu.CompilerParams(
            collective_id=collective_id, has_side_effects=True, vmem_limit_bytes=48 * 2**20
        ),
        cost_estimate=pl.CostEstimate(flops=1000000, bytes_accessed=2**24, transcendentals=0),
        name="group_reduce",
    )(mixed, normed, gate_grad)


def column_parts(half):
    first = -(-(half // 128) // 2) * 128
    return ((0, first), (first, half - first))


def shard_view(ref, halves, a, p, rank_value):
    start, size = column_parts(halves[a])[p]
    offset = pl.multiple_of((rank_value // PLACES) * halves[a] + start, 128)
    return ref.at[:, rank_value % PLACES, :, pl.ds(offset, size)]


def starts_of(sizes):
    return [sum(sizes[:i]) for i in range(len(sizes))]


def weights_gather_kernel(halves, packed, *refs):
    count = len(halves)
    outs = refs[:count]
    send, recv, local = refs[count:]
    rank, peer = my_place()
    firsts = starts_of(halves)
    seq = lax.axis_index("seq")
    own = []
    for a in range(count):
        columns = pl.ds(pl.multiple_of(seq * halves[a], 128), halves[a])
        copy = pltpu.make_async_copy(
            packed.at[:, :, pl.ds(firsts[a], halves[a])],
            outs[a].at[:, rank % PLACES, :, columns],
            local.at[a],
        )
        copy.start()
        own.append(copy)
    meet([peer(bit) for bit in (1, 2, 4)])
    started = []

    def remote(a, p, mask, bit, index):
        view = shard_view(outs[a], halves, a, p, flip_mask(rank, mask))
        start, size = column_parts(halves[a])[p]
        source = packed.at[:, :, pl.ds(firsts[a] + start, size)] if mask == 0 else view
        copy = pltpu.make_async_remote_copy(
            src_ref=source,
            dst_ref=view,
            send_sem=send.at[a, p, index],
            recv_sem=recv.at[a, p, index],
            device_id=peer(bit),
            device_id_type=MESH,
        )
        copy.start()
        started.append(copy)
        return copy

    live = {}
    last = []
    for step in range(3):
        for p in range(2):
            for a in range(count):
                if column_parts(halves[a])[p][1] == 0:
                    continue
                order = TOKEN_LINKS[p]
                if step > 0:
                    for copy in live.pop((a, p)):
                        copy.wait_recv()
                if step < 2:
                    live[(a, p)] = [
                        remote(a, p, mask, order[step], 2**step - 1 + index)
                        for index, mask in enumerate(subsets(order[:step]))
                    ]
                fresh = [0] if step == 0 else [m | order[step - 1] for m in subsets(order[: step - 1])]
                base = 0 if step == 0 else 2 ** (step - 1)
                for index, mask in enumerate(fresh):
                    last.append(remote(a, p, mask, 1, 3 + base + index))
    for copy in last:
        copy.wait_recv()
    for copy in started:
        copy.wait_send()
    for copy in own:
        copy.wait()


def weights_gather(collective_id, halves, packed):
    groups, rows, _ = packed.shape
    count = len(halves)
    whole = pl.pallas_call(
        functools.partial(weights_gather_kernel, halves),
        out_shape=[jax.ShapeDtypeStruct((groups, PLACES, rows, 2 * h), packed.dtype) for h in halves],
        in_specs=[pl.BlockSpec(memory_space=pltpu.VMEM)],
        out_specs=[pl.BlockSpec(memory_space=pl.ANY)] * count,
        scratch_shapes=[
            pltpu.SemaphoreType.DMA((count, 2, 7)),
            pltpu.SemaphoreType.DMA((count, 2, 7)),
            pltpu.SemaphoreType.DMA((count,)),
        ],
        compiler_params=pltpu.CompilerParams(collective_id=collective_id, has_side_effects=True),
        cost_estimate=pl.CostEstimate(flops=1000000, bytes_accessed=2**24, transcendentals=0),
        name="weights_gather",
    )(packed)
    return [w.reshape(-1, w.shape[3]) for w in whole]


def add_block(target, source, at, start, size):
    groups, rows = source.shape[0], source.shape[1]
    columns = pl.ds(start, size)
    pieces = rows // 16

    def step(i, carry):
        lines = pl.ds(pl.multiple_of((i % pieces) * 16, 16), 16)
        index = (i // pieces, lines, columns)
        new = target[(at,) + index].astype(f32) + source[index].astype(f32)
        target[(at,) + index] = new.astype(target.dtype)
        return carry

    lax.fori_loop(0, groups * pieces, step, 0)


def weights_reduce_kernel(count, *refs):
    ins, packed = refs[:count], refs[count]
    rest = refs[count + 1 :]
    total, got0, got1, got2 = [rest[i * count : (i + 1) * count] for i in range(4)]
    sems, local = rest[4 * count :]
    rank, peer = my_place()
    chip, core = rank // 2, rank % 2
    halves = [ref.shape[3] // 2 for ref in ins]
    firsts = starts_of(halves)
    parts = [column_parts(half) for half in halves]
    loads = []
    for a in range(count):
        for c in range(4):
            value = 2 * c + core
            offset = pl.multiple_of((value // PLACES) * halves[a], 128)
            copy = pltpu.make_async_copy(
                ins[a].at[:, value % PLACES, :, pl.ds(offset, halves[a])],
                total[a].at[c],
                local.at[a, c],
            )
            copy.start()
            loads.append(copy)
    meet([peer(bit) for bit in (1, 2, 4)])
    started = []
    live = {}

    def send(a, p, stage, index, src, dst, bit):
        copy = pltpu.make_async_remote_copy(
            src_ref=src,
            dst_ref=dst,
            send_sem=sems.at[0, a, p, stage, index],
            recv_sem=sems.at[1, a, p, stage, index],
            device_id=peer(bit),
            device_id_type=MESH,
        )
        copy.start()
        started.append(copy)
        live.setdefault((a, p), []).append(copy)

    def chip_of(mask):
        return flip_mask(rank, mask) // 2

    for p in range(2):
        for a in range(count):
            columns = pl.ds(*parts[a][p])
            if parts[a][p][1]:
                for c in range(4):
                    send(
                        a, p, 0, c,
                        shard_view(ins[a], halves, a, p, 2 * c + 1 - core),
                        got0[a].at[c, :, :, columns],
                        1,
                    )
    for copy in loads:
        copy.wait()
    got = (got1, got2)
    for stage in range(3):
        for p in range(2):
            for a in range(count):
                start, size = parts[a][p]
                if size == 0:
                    continue
                order = TOKEN_LINKS[p]
                columns = pl.ds(start, size)
                for copy in live.pop((a, p)):
                    copy.wait_recv()
                if stage == 0:

                    def over_chips(c, carry, a=a, start=start, size=size):
                        add_block(total[a], got0[a].at[c], c, start, size)
                        return carry

                    lax.fori_loop(0, 4, over_chips, 0)
                else:
                    for index, mask in enumerate(subsets(order[stage:])):
                        add_block(total[a], got[stage - 1][a].at[index], chip_of(mask), start, size)
                if stage < 2:
                    for index, mask in enumerate(subsets(order[stage + 1 :])):
                        send(
                            a, p, stage + 1, index,
                            total[a].at[chip_of(mask | order[stage]), :, :, columns],
                            got[stage][a].at[index, :, :, columns],
                            order[stage],
                        )
    for a in range(count):
        packed[:, :, pl.ds(firsts[a], halves[a])] = total[a][chip].astype(packed.dtype)
    for copy in started:
        copy.wait_send()


def weights_reduce(collective_id, groups, arrays):
    count = len(arrays)
    views = [a.reshape(groups, PLACES, -1, a.shape[1]) for a in arrays]
    rows = views[0].shape[2]
    halves = [a.shape[1] // 2 for a in arrays]

    def buffers(lead):
        return [pltpu.VMEM((lead, groups, rows, h), a.dtype) for h, a in zip(halves, arrays)]

    dma = pltpu.SemaphoreType.DMA
    return pl.pallas_call(
        functools.partial(weights_reduce_kernel, count),
        out_shape=jax.ShapeDtypeStruct((groups, rows, sum(halves)), bf16),
        in_specs=[pl.BlockSpec(memory_space=pl.ANY)] * count,
        out_specs=pl.BlockSpec(memory_space=pltpu.VMEM),
        scratch_shapes=buffers(4) + buffers(4) + buffers(2) + buffers(1)
        + [dma((2, count, 2, 3, 4)), dma((count, 4))],
        compiler_params=pltpu.CompilerParams(
            collective_id=collective_id, has_side_effects=True, vmem_limit_bytes=48 * 2**20
        ),
        cost_estimate=pl.CostEstimate(flops=1000000, bytes_accessed=2**24, transcendentals=0),
        name="weights_reduce",
    )(*views)


def pieces_kernel(pieces, packed, whole, ends, far_got, send, recv, far_send, far_recv, last, local):
    rank, peer = my_place()
    place = rank % PLACES
    groups = packed.shape[0]
    seq = lax.axis_index("seq")
    home = lax.axis_index("dp") // PLACES
    keep = pltpu.make_async_copy(pieces.at[place], whole.at[rank], local)
    keep.start()
    masks = (6, 7, 2, 4, 3, 5, 1)
    others = [(home + k) % groups for k in range(1, groups)]
    far = [{"seq": seq, "dp": g * PLACES + place} for g in others]
    meet([peer(mask) for mask in masks] + far)
    sums = []
    for k, there in enumerate(far):
        copy = pltpu.make_async_remote_copy(
            src_ref=packed.at[others[k]],
            dst_ref=far_got.at[k],
            send_sem=far_send.at[k],
            recv_sem=far_recv.at[k],
            device_id=there,
            device_id_type=MESH,
        )
        copy.start()
        sums.append(copy)
    copies = []
    for mask in masks:
        copy = pltpu.make_async_remote_copy(
            src_ref=pieces.at[flip_mask(place, mask & (PLACES - 1))],
            dst_ref=whole.at[rank],
            send_sem=send.at[mask],
            recv_sem=recv.at[mask],
            device_id=peer(mask),
            device_id_type=MESH,
        )
        copy.start()
        copies.append(copy)
    for copy in sums:
        copy.wait()
    value = packed[home].astype(f32)
    for k in range(groups - 1):
        value = value + far_got[k].astype(f32)
    ends[seq] = value.astype(ends.dtype)
    copy = pltpu.make_async_remote_copy(
        src_ref=ends.at[seq],
        dst_ref=ends.at[seq],
        send_sem=last.at[0],
        recv_sem=last.at[1],
        device_id=peer(4),
        device_id_type=MESH,
    )
    copy.start()
    copies.append(copy)
    for copy in copies:
        copy.wait()
    keep.wait()


def send_pieces(collective_id, pieces, packed):
    groups = packed.shape[0]
    others = max(groups - 1, 1)
    dma = pltpu.SemaphoreType.DMA
    vmem = pl.BlockSpec(memory_space=pltpu.VMEM)
    return pl.pallas_call(
        pieces_kernel,
        out_shape=[
            jax.ShapeDtypeStruct((GROUP,) + pieces.shape[1:], pieces.dtype),
            jax.ShapeDtypeStruct((2,) + packed.shape[1:], packed.dtype),
        ],
        in_specs=[vmem, vmem],
        out_specs=[pl.BlockSpec(memory_space=pl.ANY), vmem],
        scratch_shapes=[
            pltpu.VMEM((others,) + packed.shape[1:], packed.dtype),
            dma((GROUP,)),
            dma((GROUP,)),
            dma((others,)),
            dma((others,)),
            dma((2,)),
            dma(()),
        ],
        compiler_params=pltpu.CompilerParams(collective_id=collective_id, has_side_effects=True),
        name="send_pieces",
    )(pieces, packed)


def expert_kernel(
    first, rows_ref, grad_ref, gate_ref, weights_ref,
    mixed_ref, normed_ref, gate_grad_ref, weights_out,
    gate_up_sum, down_sum, mixed_sum, normed_sum,
):
    step = pl.program_id(0)
    expert = pl.program_id(1)
    shards, each, width = rows_ref.shape
    count = shards * each
    rows = rows_ref[...].reshape(count, width)
    grad = grad_ref[...].reshape(count, width).astype(f32)
    gate = jnp.concatenate(
        [
            jnp.broadcast_to(gate_ref[i, pl.ds(expert, 1)], (128, each)).T[:, :1]
            for i in range(shards)
        ],
        0,
    )
    gate_up_weight = weights_ref[:, expert, :first].reshape(-1, width)
    down = weights_ref[:, expert, first:].reshape(-1, width)
    gate_up = jnp.dot(rows, gate_up_weight, preferred_element_type=f32)
    gate_part, up_part = gate_up[:, :F], gate_up[:, F:]
    sigmoid = 1.0 / (1.0 + jnp.exp(-gate_part))
    silu = gate_part * sigmoid
    act = (silu * up_part).astype(bf16)
    out = jnp.dot(act, down, preferred_element_type=f32)
    inner = jnp.sum(out * grad, axis=-1, keepdims=True)
    for i in range(shards):
        line = jnp.broadcast_to(inner[i * each : (i + 1) * each], (each, 128)).T
        gate_grad_ref[i, pl.ds(expert, 1)] = line[:1]
    mixed = gate * out
    expert_grad = (gate * grad).astype(bf16)
    across = (((1,), (1,)), ((), ()))
    over_rows = (((0,), (0,)), ((), ()))
    act_grad = lax.dot_general(expert_grad, down, across, preferred_element_type=f32)
    gate_up_grad = jnp.concatenate(
        [act_grad * up_part * (sigmoid * (1.0 + gate_part * (1.0 - sigmoid))), act_grad * silu], -1
    ).astype(bf16)
    normed = lax.dot_general(gate_up_grad, gate_up_weight, across, preferred_element_type=f32)

    @pl.when(expert == 0)
    def _():
        mixed_sum[...] = mixed
        normed_sum[...] = normed

    @pl.when(expert > 0)
    def _():
        mixed_sum[...] += mixed
        normed_sum[...] += normed

    @pl.when(expert == OWN - 1)
    def _():
        mixed_ref[...] = mixed_sum[...].astype(bf16).reshape(shards, each, width)
        normed_ref[...] = normed_sum[...].astype(bf16).reshape(shards, each, width)

    @pl.when(step == 0)
    def _():
        gate_up_sum[expert] = jnp.zeros_like(gate_up_sum[0])
        down_sum[expert] = jnp.zeros_like(down_sum[0])

    down_sum[expert] += lax.dot_general(act, expert_grad, over_rows, preferred_element_type=f32)
    gate_up_sum[expert] += lax.dot_general(rows, gate_up_grad, over_rows, preferred_element_type=f32)

    @pl.when(step == pl.num_programs(0) - 1)
    def _():
        owners = weights_out.shape[0]
        weights_out[:, expert, :first] = gate_up_sum[expert].astype(bf16).reshape(owners, first, width)
        weights_out[:, expert, first:] = down_sum[expert].astype(bf16).reshape(owners, -1, width)


def expert_layer(first, rows, grad, gate, weights):
    each, width = rows.shape[1:]
    shards = 2
    owners = weights.shape[0]
    tile = pl.BlockSpec((shards, each, width), lambda i, e: (i, 0, 0))
    whole = pl.BlockSpec(weights.shape, lambda i, e: (0, 0, 0, 0), pipeline_mode=pl.Buffered(1))
    return pl.pallas_call(
        functools.partial(expert_kernel, first),
        grid=(GROUP // shards, OWN),
        out_shape=[
            jax.ShapeDtypeStruct(rows.shape, bf16),
            jax.ShapeDtypeStruct(rows.shape, bf16),
            jax.ShapeDtypeStruct((GROUP, 8, each), f32),
            jax.ShapeDtypeStruct(weights.shape, bf16),
        ],
        in_specs=[
            tile,
            tile,
            pl.BlockSpec((shards, OWN, each), lambda i, e: (i, 0, 0)),
            whole,
        ],
        out_specs=[
            tile,
            tile,
            pl.BlockSpec((shards, 8, each), lambda i, e: (i, 0, 0)),
            whole,
        ],
        scratch_shapes=[
            pltpu.VMEM((OWN, owners * first, width), f32),
            pltpu.VMEM((OWN, owners * (weights.shape[2] - first), width), f32),
            pltpu.VMEM((shards * each, width), f32),
            pltpu.VMEM((shards * each, width), f32),
        ],
        compiler_params=pltpu.CompilerParams(vmem_limit_bytes=62 * 2**20),
        cost_estimate=pl.CostEstimate(flops=45000000000, bytes_accessed=2**24, transcendentals=0),
        name="expert_layer",
    )(rows, grad, gate, weights)


def inverse_rms(rows):
    return lax.rsqrt(jnp.mean(rows * rows, axis=-1, keepdims=True) + epsilon)


def norm_back(rows, gain_row, upstream):
    inverse = inverse_rms(rows)
    gain_grad = jnp.sum(upstream * rows * inverse, axis=0)
    scaled = upstream * gain_row
    rows_grad = inverse * scaled - rows * inverse**3 * jnp.mean(scaled * rows, axis=-1, keepdims=True)
    return rows_grad, gain_grad


def rope_tables(positions):
    half = HEAD_SIZE // 2
    frequency = rope_base ** (-(jnp.arange(half, dtype=f32) * 2.0) / HEAD_SIZE)
    angles = positions.astype(f32)[:, None] * frequency[None, :]
    cosine, sine = jnp.cos(angles), jnp.sin(angles)
    return jnp.concatenate([cosine, cosine], 1), jnp.concatenate([sine, sine], 1)


def rotary_apply(rows, cosine, sine):
    half = HEAD_SIZE // 2
    turned = jnp.concatenate([-rows[..., half:], rows[..., :half]], -1)
    return rows * cosine[:, None, :] + turned * sine[:, None, :]


def unrotate(rows, cosine, sine):
    half = HEAD_SIZE // 2
    scaled = rows * sine[:, None, :]
    back = jnp.concatenate([scaled[..., half:], -scaled[..., :half]], -1)
    return rows * cosine[:, None, :] + back


def make_body(n_dp):
    expert_groups = n_dp // PLACES
    inside = [[g * PLACES + j for j in range(PLACES)] for g in range(expert_groups)]
    between = [[g * PLACES + j for g in range(expert_groups)] for j in range(PLACES)]
    half_experts = EXPERTS // 2

    def over_groups(value):
        home = lax.axis_index("dp") // PLACES

        def turned(k):
            return lax.ppermute(value, "dp", [(d, (d + k * PLACES) % n_dp) for d in range(n_dp)])

        parts = [turned(k) for k in range(expert_groups - 1, 0, -1)] + [value]
        ring = jnp.stack(parts + parts[:-1])
        start = (expert_groups - 1 - home) % expert_groups
        return lax.dynamic_slice_in_dim(ring, start, expert_groups, axis=0)

    def expert_pieces(gate_up_shard, down_shard, seq_rank):
        mine = [
            jnp.swapaxes(lax.dynamic_slice_in_dim(w, seq_rank * half_experts, half_experts, axis=1), 0, 1)
            for w in (gate_up_shard, down_shard)
        ]
        mine = jnp.concatenate(mine, 1)
        mine = mine.reshape((PLACES, OWN) + mine.shape[1:])
        return lax.all_to_all(
            mine, "dp", split_axis=0, concat_axis=0, tiled=True, axis_index_groups=inside
        )

    def body(
        tokens, starts, routes, gain_one, query_key_value_weight, w_out,
        gain_two, w_router, w_gate_up, w_down, cotangent,
    ):
        count = tokens.shape[1]
        seq_rank = lax.axis_index("seq")
        expert = (seq_rank * PLACES + lax.axis_index("dp") % PLACES) * OWN
        query_columns = QUERY_HEADS * HEAD_SIZE
        key_columns = KEY_VALUE_HEADS * HEAD_SIZE
        group = QUERY_HEADS // KEY_VALUE_HEADS
        forward_pair, back_pair = [(0, 1)], [(1, 0)]

        mine = expert_pieces(w_gate_up, w_down, seq_rank)
        tokens_before = lax.ppermute(tokens[0], "seq", forward_pair)
        starts_before = lax.ppermute(starts, "seq", forward_pair)
        spare = lambda value: jnp.pad(value, ((0, 0), (0, 128 - value.shape[1])))
        little = jnp.concatenate([spare(w_router), spare(jnp.stack([gain_one, gain_two], 1))], 1)
        shards = (query_key_value_weight, w_out, little)
        halves = [w.shape[1] // 2 for w in shards]
        packed = over_groups(
            jnp.concatenate(
                [
                    lax.dynamic_slice_in_dim(w, seq_rank * h, h, axis=1)
                    for w, h in zip(shards, halves)
                ],
                1,
            )
        )
        mine, packed, tokens_before, starts_before = lax.optimization_barrier(
            (mine, packed, tokens_before, starts_before)
        )
        weights = lax.all_gather(mine, "dp", axis=0, tiled=True, axis_index_groups=between)
        qkv_weight, out_weight, small = weights_gather(0, halves, packed)
        router_weight = small[:, :EXPERTS]
        gain_a = small[:, 128].astype(f32)
        gain_b = small[:, 129].astype(f32)

        token_rows = tokens[0].astype(f32)
        grad_output = cotangent[0].astype(f32)
        both = 2 * count
        index = jnp.arange(both, dtype=jnp.int32)
        flags = jnp.concatenate([starts_before[0], starts[0]])
        begins = (flags > 0) | (index == jnp.where(seq_rank == 0, count, 0))
        last_begin = jnp.max(
            jnp.where(begins[None, :] & (index[None, :] <= index[:, None]), index[None, :], 0), axis=1
        )
        cosine_all, sine_all = rope_tables(index - last_begin)
        cosine, sine = cosine_all[count:], sine_all[count:]

        rows_all = jnp.concatenate([tokens_before.astype(f32), token_rows], 0)
        normed_all = (rows_all * inverse_rms(rows_all) * gain_a).astype(bf16)
        normed_one = normed_all[count:]
        projected_q = jnp.dot(normed_one, qkv_weight[:, :query_columns], preferred_element_type=f32)
        projected_kv = jnp.dot(normed_all, qkv_weight[:, query_columns:], preferred_element_type=f32)
        queries = rotary_apply(
            projected_q.reshape(count, QUERY_HEADS, HEAD_SIZE), cosine, sine
        ).astype(bf16).reshape(count, KEY_VALUE_HEADS, group, HEAD_SIZE)
        keys = rotary_apply(
            projected_kv[:, :key_columns].reshape(both, KEY_VALUE_HEADS, HEAD_SIZE), cosine_all, sine_all
        ).astype(bf16)
        values = projected_kv[:, key_columns:].astype(bf16).reshape(both, KEY_VALUE_HEADS, HEAD_SIZE)

        scale = HEAD_SIZE ** (-0.5)
        allowed = (index[None, :] <= index[count:, None]) & (index[None, :] >= last_begin[count:, None])
        scores = jnp.einsum("qgrd,kgd->grqk", queries, keys, preferred_element_type=f32) * scale
        scores = jnp.where(allowed[None, None], scores, masked_score)
        top = jnp.max(scores, axis=-1, keepdims=True)
        exps = jnp.exp(scores - top)
        probs = exps / jnp.sum(exps, axis=-1, keepdims=True)
        probs_low = probs.astype(bf16)
        attended = jnp.einsum(
            "grqk,kgd->qgrd", probs_low, values, preferred_element_type=f32
        ).reshape(count, query_columns).astype(bf16)
        hidden = token_rows + jnp.dot(attended, out_weight, preferred_element_type=f32)
        normed_two = (hidden * inverse_rms(hidden) * gain_b).astype(bf16)
        logits = jnp.dot(normed_two, router_weight, preferred_element_type=f32)
        expert_ids = jnp.arange(EXPERTS, dtype=jnp.int32)
        chosen = jnp.any(routes[0][:, :, None] == expert_ids[None, None, :], axis=1)
        gates = jax.nn.softmax(jnp.where(chosen, logits, -jnp.inf), axis=-1)

        rows_in, gates_all, grad_all = group_gather(1, normed_two, gates.T, cotangent[0])
        gate = lax.dynamic_slice_in_dim(gates_all, expert, OWN, axis=1)
        mixed_part, normed_part, gate_grad_part, expert_wgrads = expert_layer(
            w_gate_up.shape[0], rows_in, grad_all, gate, weights
        )
        expert_grads = lax.psum_scatter(
            expert_wgrads, "dp", scatter_dimension=0, tiled=True, axis_index_groups=between
        )
        mixed, normed_grad, gate_grad = group_reduce(2, mixed_part, normed_part, gate_grad_part)
        gate_grad = gate_grad[:, :OWN].reshape(EXPERTS, count).T

        over_rows = (((0,), (0,)), ((), ()))
        output = (hidden + mixed).astype(bf16)[None]
        stat_sums = jnp.stack([jnp.sum(hidden * hidden), jnp.sum(mixed * mixed)])
        weighted = jnp.where(chosen, gates * gate_grad, 0.0)
        logits_grad = weighted - gates * jnp.sum(weighted, axis=-1, keepdims=True)
        router_wide = router_weight.astype(f32)
        normed_grad = normed_grad + jnp.dot(logits_grad, router_wide.T, precision=highest)
        router_wgrad = jnp.dot(normed_two.astype(f32).T, logits_grad, precision=highest)
        hidden_branch, gain_two_grad = norm_back(hidden, gain_b, normed_grad)
        hidden_grad = grad_output + hidden_branch
        branch_low = hidden_grad.astype(bf16)
        out_wgrad = lax.dot_general(attended, branch_low, over_rows, preferred_element_type=f32)
        attended_grad = lax.dot_general(
            branch_low, out_weight, (((1,), (1,)), ((), ())), preferred_element_type=f32
        ).astype(bf16).reshape(count, KEY_VALUE_HEADS, group, HEAD_SIZE)

        stat_sums = stat_sums + lax.ppermute(stat_sums, "seq", [(0, 1), (1, 0)])
        attended_grad, stat_sums = lax.optimization_barrier((attended_grad, stat_sums))
        prob_grad = jnp.einsum("qgrd,kgd->grqk", attended_grad, values, preferred_element_type=f32)
        delta = jnp.sum(probs * prob_grad, axis=-1, keepdims=True)
        score_grad = (probs * (prob_grad - delta)).astype(bf16)
        query_grad = (
            jnp.einsum("grqk,kgd->qgrd", score_grad, keys, preferred_element_type=f32) * scale
        ).reshape(count, QUERY_HEADS, HEAD_SIZE)
        key_grad = (
            jnp.einsum("grqk,qgrd->kgd", score_grad, queries, preferred_element_type=f32) * scale
        ).reshape(both, key_columns)
        value_grad = jnp.einsum(
            "grqk,qgrd->kgd", probs_low, attended_grad, preferred_element_type=f32
        ).reshape(both, key_columns)
        kv_grad = jnp.concatenate([key_grad, value_grad], 1)
        kv_back = lax.ppermute(kv_grad[:count].astype(bf16), "seq", back_pair)
        kv_grad = (kv_grad[count:] + kv_back.astype(f32)).astype(bf16).astype(f32)
        query_grad = query_grad.astype(bf16).astype(f32)
        query_back = unrotate(query_grad, cosine, sine).reshape(count, query_columns)
        key_back = unrotate(
            kv_grad[:, :key_columns].reshape(count, KEY_VALUE_HEADS, HEAD_SIZE), cosine, sine
        ).reshape(count, key_columns)
        projected_grad = jnp.concatenate([query_back, key_back, kv_grad[:, key_columns:]], 1).astype(bf16)
        qkv_wgrad = lax.dot_general(normed_one, projected_grad, over_rows, preferred_element_type=f32)
        normed_one_grad = lax.dot_general(
            projected_grad, qkv_weight, (((1,), (1,)), ((), ())), preferred_element_type=f32
        )
        rows_branch, gain_one_grad = norm_back(token_rows, gain_a, normed_one_grad)
        input_grad = (hidden_grad + rows_branch).astype(bf16)[None]

        little = jnp.concatenate(
            [spare(router_wgrad), spare(jnp.stack([gain_one_grad, gain_two_grad], 1))], 1
        )
        packed = weights_reduce(
            3, expert_groups, (qkv_wgrad.astype(bf16), out_wgrad.astype(bf16), little)
        )
        experts_all, ends = send_pieces(4, expert_grads, packed)
        qkv_shard, out_shard, little = [
            jnp.concatenate([ends[0, :, f : f + h], ends[1, :, f : f + h]], 1).astype(f32)
            for f, h in zip(starts_of(halves), halves)
        ]
        experts_all = experts_all.reshape((EXPERTS,) + experts_all.shape[2:])
        first = w_gate_up.shape[0]
        stream_rms = jnp.sqrt(stat_sums / (both * MODEL_WIDTH)).reshape(1, 2)
        return (
            output,
            input_grad,
            little[:, 128],
            qkv_shard,
            out_shard,
            little[:, 129],
            little[:, :EXPERTS],
            jnp.swapaxes(experts_all[:, :first], 0, 1).astype(f32),
            jnp.swapaxes(experts_all[:, first:], 0, 1).astype(f32),
            stream_rms,
        )

    return body


def solution(mesh):
    placed = (
        P("dp", "seq", None),
        P("dp", "seq"),
        P("dp", "seq", None),
        P("dp"),
        P("dp", None),
        P("dp", None),
        P("dp"),
        P("dp", None),
        P("dp", None, None),
        P("dp", None, None),
        P("dp", "seq", None),
    )
    return jax.shard_map(
        make_body(mesh.shape["dp"]),
        mesh=mesh,
        in_specs=placed,
        out_specs=(
            P("dp", "seq", None),
            P("dp", "seq", None),
            P("dp"),
            P("dp", None),
            P("dp", None),
            P("dp"),
            P("dp", None),
            P("dp", None, None),
            P("dp", None, None),
            P("dp", None),
        ),
        check_vma=False,
    )
```

```python
import functools

import jax
import jax.numpy as jnp
from jax import lax
from jax.experimental import pallas as pl
from jax.experimental.pallas import tpu as pltpu
from jax.sharding import PartitionSpec as P

MODEL_WIDTH = 1024
QUERY_HEADS = 16
KEY_VALUE_HEADS = 8
HEAD_SIZE = 64
F = 512
EXPERTS = 16
TOPK = 8
PLACES = 4
GROUP = 8
OWN = EXPERTS // GROUP

epsilon = 1e-06
rope_base = 10000.0
highest = lax.Precision.HIGHEST
masked_score = -1e30
f32 = jnp.float32
bf16 = jnp.bfloat16
MESH = pl.DeviceIdType.MESH

TOKEN_LINKS = ((4, 2), (2, 4))


def flip(value, bit):
    return value + bit * (1 - 2 * ((value // bit) % 2))


def flip_mask(value, mask):
    for bit in (1, 2, 4, 8):
        if mask & bit:
            value = flip(value, bit)
    return value


def subsets(bits):
    out = [0]
    for bit in bits:
        out = out + [m | bit for m in out]
    return out


def row_parts(rows):
    first = (rows // 2 + 15) // 16 * 16
    return ((0, first), (first, rows - first))


def my_place(places=PLACES):
    seq = lax.axis_index("seq")
    dp = lax.axis_index("dp")
    rank = seq * places + dp % places

    def peer(mask):
        return {
            "seq": 1 - seq if mask & places else seq,
            "dp": flip_mask(dp, mask & (places - 1)),
        }

    return rank, peer


def meet(devices):
    barrier = pltpu.get_barrier_semaphore()
    for there in devices:
        pl.semaphore_signal(barrier, inc=1, device_id=there, device_id_type=MESH)
    pl.semaphore_wait(barrier, len(devices))


def gather_kernel(count, *refs):
    ins, outs = refs[:count], refs[count : 2 * count]
    send, recv, send_core, recv_core, local = refs[2 * count :]
    rank, peer = my_place(PLACES)
    own = [
        pltpu.make_async_copy(ins[a], outs[a].at[rank], local.at[a]) for a in range(count)
    ]
    for copy in own:
        copy.start()
    meet([peer(bit) for bit in (1, 2, 4)])
    parts = [row_parts(ref.shape[0]) for ref in ins]

    def remote(a, p, mask, bit, sems, index):
        start, size = parts[a][p]
        rows = pl.ds(start, size)
        shard = flip_mask(rank, mask)
        src = ins[a].at[rows] if mask == 0 else outs[a].at[shard, rows]
        return pltpu.make_async_remote_copy(
            src_ref=src,
            dst_ref=outs[a].at[shard, rows],
            send_sem=sems[0].at[a, p, index],
            recv_sem=sems[1].at[a, p, index],
            device_id=peer(bit),
            device_id_type=MESH,
        )

    started = []
    live = {}
    for step in range(3):
        for p in range(2):
            for a in range(count):
                if parts[a][p][1] == 0:
                    continue
                order = TOKEN_LINKS[p]
                if step > 0:
                    for copy in live.pop((a, p)):
                        copy.wait_recv()
                if step < 2:
                    now = []
                    for index, mask in enumerate(subsets(order[:step])):
                        copy = remote(a, p, mask, order[step], (send, recv), 2**step - 1 + index)
                        copy.start()
                        now.append(copy)
                        started.append(copy)
                    live[(a, p)] = now
                fresh = [0] if step == 0 else [m | order[step - 1] for m in subsets(order[: step - 1])]
                base = 0 if step == 0 else 2 ** (step - 1)
                for index, mask in enumerate(fresh):
                    copy = remote(a, p, mask, 1, (send_core, recv_core), base + index)
                    copy.start()
                    live.setdefault("core", []).append(copy)
    for copy in live["core"]:
        copy.wait()
    for copy in started:
        copy.wait_send()
    for copy in own:
        copy.wait()


def group_gather(collective_id, *arrays):
    count = len(arrays)
    return pl.pallas_call(
        functools.partial(gather_kernel, count),
        out_shape=[jax.ShapeDtypeStruct((GROUP,) + a.shape, a.dtype) for a in arrays],
        in_specs=[pl.BlockSpec(memory_space=pltpu.VMEM)] * count,
        out_specs=[pl.BlockSpec(memory_space=pl.ANY)] * count,
        scratch_shapes=[
            pltpu.SemaphoreType.DMA((count, 2, 3)),
            pltpu.SemaphoreType.DMA((count, 2, 3)),
            pltpu.SemaphoreType.DMA((count, 2, 4)),
            pltpu.SemaphoreType.DMA((count, 2, 4)),
            pltpu.SemaphoreType.DMA((count,)),
        ],
        compiler_params=pltpu.CompilerParams(collective_id=collective_id, has_side_effects=True),
        cost_estimate=pl.CostEstimate(flops=1000000000, bytes_accessed=2**24, transcendentals=0),
        name="group_gather",
    )(*arrays)


def add_rows(target, source, start, size):
    def step(i, carry):
        rows = pl.ds(pl.multiple_of(start + i * 16, 16), 16)
        target[rows] = (target[rows].astype(f32) + source[rows].astype(f32)).astype(target.dtype)
        return carry

    lax.fori_loop(0, size // 16, step, 0)


def reduce_kernel(
    normed_ref, gate_ref, normed_out, gate_out,
    total, got0, got1, got2, sems, gate_sems, local, own_gate,
):
    rank, peer = my_place(PLACES)
    chip = rank // 2
    core = rank % 2
    parts = row_parts(normed_ref.shape[1])
    ins = (normed_ref,)
    outs = (normed_out,)
    loads = []
    for t in range(1):
        for c in range(4):
            copy = pltpu.make_async_copy(ins[t].at[2 * c + core], total.at[t, c], local.at[t, c])
            copy.start()
            loads.append(copy)
    everyone = [peer(mask) for mask in range(1, GROUP)]
    meet(everyone)
    gates = []
    keep = pltpu.make_async_copy(gate_ref.at[rank], gate_out.at[rank], own_gate)
    keep.start()
    for mask, there in zip(range(1, GROUP), everyone):
        copy = pltpu.make_async_remote_copy(
            src_ref=gate_ref.at[flip_mask(rank, mask)],
            dst_ref=gate_out.at[rank],
            send_sem=gate_sems.at[0, mask],
            recv_sem=gate_sems.at[1, mask],
            device_id=there,
            device_id_type=MESH,
        )
        copy.start()
        gates.append(copy)

    started = []
    live = {}

    def send(t, p, stage, index, src, dst, bit):
        copy = pltpu.make_async_remote_copy(
            src_ref=src,
            dst_ref=dst,
            send_sem=sems.at[0, t, p, stage, index],
            recv_sem=sems.at[1, t, p, stage, index],
            device_id=peer(bit),
            device_id_type=MESH,
        )
        copy.start()
        started.append(copy)
        live.setdefault((t, p), []).append(copy)

    def chip_of(mask):
        return flip_mask(rank, mask) // 2

    for p in range(2):
        for t in range(1):
            rows = pl.ds(*parts[p])
            for c in range(4):
                send(
                    t, p, 0, c, ins[t].at[2 * c + 1 - core, rows], got0.at[t, c, rows], 1
                )
    for copy in loads:
        copy.wait()
    got = (got1, got2)
    for stage in range(3):
        for p in range(2):
            for t in range(1):
                order = TOKEN_LINKS[p]
                rows = pl.ds(*parts[p])
                for copy in live.pop((t, p)):
                    copy.wait_recv()
                if stage == 0:

                    def over_chips(c, carry, t=t, p=p):
                        add_rows(total.at[t, c], got0.at[t, c], *parts[p])
                        return carry

                    lax.fori_loop(0, 4, over_chips, 0)
                else:
                    for index, mask in enumerate(subsets(order[stage:])):
                        if stage == 2:
                            outs[t][rows] = total[t, chip, rows].astype(f32) + got2[t, 0, rows].astype(f32)
                        else:
                            add_rows(
                                total.at[t, chip_of(mask)], got[stage - 1].at[t, index], *parts[p]
                            )
                if stage < 2:
                    for index, mask in enumerate(subsets(order[stage + 1 :])):
                        send(
                            t, p, stage + 1, index,
                            total.at[t, chip_of(mask | order[stage]), rows],
                            got[stage].at[t, index, rows],
                            order[stage],
                        )
    for copy in started:
        copy.wait_send()
    for copy in gates:
        copy.wait()
    keep.wait()


def group_reduce(collective_id, normed, gate_grad):
    rows, width = normed.shape[1:]
    return pl.pallas_call(
        reduce_kernel,
        out_shape=[
            jax.ShapeDtypeStruct((rows, width), f32),
            jax.ShapeDtypeStruct(gate_grad.shape, gate_grad.dtype),
        ],
        in_specs=[pl.BlockSpec(memory_space=pl.ANY)] * 2,
        out_specs=[
            pl.BlockSpec(memory_space=pltpu.VMEM),
            pl.BlockSpec(memory_space=pl.ANY),
        ],
        scratch_shapes=[
            pltpu.VMEM((1, 4, rows, width), bf16),
            pltpu.VMEM((1, 4, rows, width), bf16),
            pltpu.VMEM((1, 2, rows, width), bf16),
            pltpu.VMEM((1, 1, rows, width), bf16),
            pltpu.SemaphoreType.DMA((2, 1, 2, 3, 4)),
            pltpu.SemaphoreType.DMA((2, GROUP)),
            pltpu.SemaphoreType.DMA((1, 4)),
            pltpu.SemaphoreType.DMA(()),
        ],
        compiler_params=pltpu.CompilerParams(
            collective_id=collective_id, has_side_effects=True, vmem_limit_bytes=48 * 2**20
        ),
        cost_estimate=pl.CostEstimate(flops=1000000, bytes_accessed=2**24, transcendentals=0),
        name="group_reduce",
    )(normed, gate_grad)


def column_parts(half):
    first = -(-(half // 128) // 2) * 128
    return ((0, first), (first, half - first))


def shard_view(ref, halves, a, p, rank_value):
    start, size = column_parts(halves[a])[p]
    offset = pl.multiple_of((rank_value // PLACES) * halves[a] + start, 128)
    return ref.at[:, rank_value % PLACES, :, pl.ds(offset, size)]


def starts_of(sizes):
    return [sum(sizes[:i]) for i in range(len(sizes))]


def weights_gather_kernel(halves, packed, *refs):
    count = len(halves)
    outs = refs[:count]
    send, recv, local = refs[count:]
    rank, peer = my_place()
    firsts = starts_of(halves)
    seq = lax.axis_index("seq")
    own = []
    for a in range(count):
        columns = pl.ds(pl.multiple_of(seq * halves[a], 128), halves[a])
        copy = pltpu.make_async_copy(
            packed.at[:, :, pl.ds(firsts[a], halves[a])],
            outs[a].at[:, rank % PLACES, :, columns],
            local.at[a],
        )
        copy.start()
        own.append(copy)
    meet([peer(bit) for bit in (1, 2, 4)])
    started = []

    def remote(a, p, mask, bit, index):
        view = shard_view(outs[a], halves, a, p, flip_mask(rank, mask))
        start, size = column_parts(halves[a])[p]
        source = packed.at[:, :, pl.ds(firsts[a] + start, size)] if mask == 0 else view
        copy = pltpu.make_async_remote_copy(
            src_ref=source,
            dst_ref=view,
            send_sem=send.at[a, p, index],
            recv_sem=recv.at[a, p, index],
            device_id=peer(bit),
            device_id_type=MESH,
        )
        copy.start()
        started.append(copy)
        return copy

    live = {}
    last = []
    for step in range(3):
        for p in range(2):
            for a in range(count):
                if column_parts(halves[a])[p][1] == 0:
                    continue
                order = TOKEN_LINKS[p]
                if step > 0:
                    for copy in live.pop((a, p)):
                        copy.wait_recv()
                if step < 2:
                    live[(a, p)] = [
                        remote(a, p, mask, order[step], 2**step - 1 + index)
                        for index, mask in enumerate(subsets(order[:step]))
                    ]
                fresh = [0] if step == 0 else [m | order[step - 1] for m in subsets(order[: step - 1])]
                base = 0 if step == 0 else 2 ** (step - 1)
                for index, mask in enumerate(fresh):
                    last.append(remote(a, p, mask, 1, 3 + base + index))
    for copy in last:
        copy.wait_recv()
    for copy in started:
        copy.wait_send()
    for copy in own:
        copy.wait()


def weights_gather(collective_id, halves, packed):
    groups, rows, _ = packed.shape
    count = len(halves)
    whole = pl.pallas_call(
        functools.partial(weights_gather_kernel, halves),
        out_shape=[jax.ShapeDtypeStruct((groups, PLACES, rows, 2 * h), packed.dtype) for h in halves],
        in_specs=[pl.BlockSpec(memory_space=pltpu.VMEM)],
        out_specs=[pl.BlockSpec(memory_space=pl.ANY)] * count,
        scratch_shapes=[
            pltpu.SemaphoreType.DMA((count, 2, 7)),
            pltpu.SemaphoreType.DMA((count, 2, 7)),
            pltpu.SemaphoreType.DMA((count,)),
        ],
        compiler_params=pltpu.CompilerParams(collective_id=collective_id, has_side_effects=True),
        cost_estimate=pl.CostEstimate(flops=1000000, bytes_accessed=2**24, transcendentals=0),
        name="weights_gather",
    )(packed)
    return [w.reshape(-1, w.shape[3]) for w in whole]


def add_block(target, source, at, start, size):
    groups, rows = source.shape[0], source.shape[1]
    columns = pl.ds(start, size)
    pieces = rows // 16

    def step(i, carry):
        lines = pl.ds(pl.multiple_of((i % pieces) * 16, 16), 16)
        index = (i // pieces, lines, columns)
        new = target[(at,) + index].astype(f32) + source[index].astype(f32)
        target[(at,) + index] = new.astype(target.dtype)
        return carry

    lax.fori_loop(0, groups * pieces, step, 0)


def weights_reduce_kernel(count, *refs):
    ins, packed, rows_out = refs[:count], refs[count], refs[count + 1]
    rest = refs[count + 2 :]
    total, got0, got1, got2 = [rest[i * count : (i + 1) * count] for i in range(4)]
    sems, local = rest[4 * count :]
    rank, peer = my_place()
    chip, core = rank // 2, rank % 2
    halves = [ref.shape[3] // 2 for ref in ins[:-1]]
    firsts = starts_of(halves)
    halves = halves + [ins[-1].shape[3]]
    parts = [column_parts(half) for half in halves]

    def source(a, value, start, size):
        if a == count - 1:
            return ins[a].at[value, :, :, pl.ds(start, size)]
        offset = pl.multiple_of((value // PLACES) * halves[a] + start, 128)
        return ins[a].at[:, value % PLACES, :, pl.ds(offset, size)]

    loads = []
    for a in range(count):
        for c in range(4):
            copy = pltpu.make_async_copy(
                source(a, 2 * c + core, 0, halves[a]), total[a].at[c], local.at[a, c]
            )
            copy.start()
            loads.append(copy)
    meet([peer(bit) for bit in (1, 2, 4)])
    started = []
    live = {}

    def send(a, p, stage, index, src, dst, bit):
        copy = pltpu.make_async_remote_copy(
            src_ref=src,
            dst_ref=dst,
            send_sem=sems.at[0, a, p, stage, index],
            recv_sem=sems.at[1, a, p, stage, index],
            device_id=peer(bit),
            device_id_type=MESH,
        )
        copy.start()
        started.append(copy)
        live.setdefault((a, p), []).append(copy)

    def chip_of(mask):
        return flip_mask(rank, mask) // 2

    for p in range(2):
        for a in range(count):
            columns = pl.ds(*parts[a][p])
            if parts[a][p][1]:
                for c in range(4):
                    send(
                        a, p, 0, c,
                        source(a, 2 * c + 1 - core, *parts[a][p]),
                        got0[a].at[c, :, :, columns],
                        1,
                    )
    for copy in loads:
        copy.wait()
    got = (got1, got2)
    for stage in range(3):
        for p in range(2):
            for a in range(count):
                start, size = parts[a][p]
                if size == 0:
                    continue
                order = TOKEN_LINKS[p]
                columns = pl.ds(start, size)
                for copy in live.pop((a, p)):
                    copy.wait_recv()
                if stage == 0:

                    def over_chips(c, carry, a=a, start=start, size=size):
                        add_block(total[a], got0[a].at[c], c, start, size)
                        return carry

                    lax.fori_loop(0, 4, over_chips, 0)
                else:
                    for index, mask in enumerate(subsets(order[stage:])):
                        add_block(total[a], got[stage - 1][a].at[index], chip_of(mask), start, size)
                if stage < 2:
                    for index, mask in enumerate(subsets(order[stage + 1 :])):
                        send(
                            a, p, stage + 1, index,
                            total[a].at[chip_of(mask | order[stage]), :, :, columns],
                            got[stage][a].at[index, :, :, columns],
                            order[stage],
                        )
    for a in range(count - 1):
        packed[:, :, pl.ds(firsts[a], halves[a])] = total[a][chip].astype(packed.dtype)
    rows_out[...] = total[-1][chip]
    for copy in started:
        copy.wait_send()


def weights_reduce(collective_id, groups, arrays, token_rows):
    count = len(arrays) + 1
    views = [a.reshape(groups, PLACES, -1, a.shape[1]) for a in arrays]
    rows = views[0].shape[2]
    halves = [a.shape[1] // 2 for a in arrays]

    each, width = token_rows.shape[1:]
    token_shape = (groups, each // groups, width)

    def buffers(lead):
        return [pltpu.VMEM((lead, groups, rows, h), a.dtype) for h, a in zip(halves, arrays)] + [
            pltpu.VMEM((lead,) + token_shape, bf16)
        ]

    dma = pltpu.SemaphoreType.DMA
    return pl.pallas_call(
        functools.partial(weights_reduce_kernel, count),
        out_shape=[
            jax.ShapeDtypeStruct((groups, rows, sum(halves)), bf16),
            jax.ShapeDtypeStruct(token_shape, bf16),
        ],
        in_specs=[pl.BlockSpec(memory_space=pl.ANY)] * count,
        out_specs=[pl.BlockSpec(memory_space=pltpu.VMEM)] * 2,
        scratch_shapes=buffers(4) + buffers(4) + buffers(2) + buffers(1)
        + [dma((2, count, 2, 3, 4)), dma((count, 4))],
        compiler_params=pltpu.CompilerParams(
            collective_id=collective_id, has_side_effects=True, vmem_limit_bytes=48 * 2**20
        ),
        cost_estimate=pl.CostEstimate(flops=1000000, bytes_accessed=2**24, transcendentals=0),
        name="weights_reduce",
    )(*views, token_rows.reshape((GROUP,) + token_shape))


def pieces_kernel(pieces, packed, whole, ends, far_got, send, recv, far_send, far_recv, last, local):
    rank, peer = my_place()
    place = rank % PLACES
    groups = packed.shape[0]
    seq = lax.axis_index("seq")
    home = lax.axis_index("dp") // PLACES
    keep = pltpu.make_async_copy(pieces.at[place], whole.at[rank], local)
    keep.start()
    masks = (6, 7, 2, 4, 3, 5, 1)
    others = [(home + k) % groups for k in range(1, groups)]
    far = [{"seq": seq, "dp": g * PLACES + place} for g in others]
    meet([peer(mask) for mask in masks] + far)
    sums = []
    for k, there in enumerate(far):
        copy = pltpu.make_async_remote_copy(
            src_ref=packed.at[others[k]],
            dst_ref=far_got.at[k],
            send_sem=far_send.at[k],
            recv_sem=far_recv.at[k],
            device_id=there,
            device_id_type=MESH,
        )
        copy.start()
        sums.append(copy)
    copies = []
    for mask in masks:
        copy = pltpu.make_async_remote_copy(
            src_ref=pieces.at[flip_mask(place, mask & (PLACES - 1))],
            dst_ref=whole.at[rank],
            send_sem=send.at[mask],
            recv_sem=recv.at[mask],
            device_id=peer(mask),
            device_id_type=MESH,
        )
        copy.start()
        copies.append(copy)
    for copy in sums:
        copy.wait()
    value = packed[home].astype(f32)
    for k in range(groups - 1):
        value = value + far_got[k].astype(f32)
    ends[seq] = value.astype(ends.dtype)
    copy = pltpu.make_async_remote_copy(
        src_ref=ends.at[seq],
        dst_ref=ends.at[seq],
        send_sem=last.at[0],
        recv_sem=last.at[1],
        device_id=peer(4),
        device_id_type=MESH,
    )
    copy.start()
    copies.append(copy)
    for copy in copies:
        copy.wait()
    keep.wait()


def send_pieces(collective_id, pieces, packed):
    groups = packed.shape[0]
    others = max(groups - 1, 1)
    dma = pltpu.SemaphoreType.DMA
    vmem = pl.BlockSpec(memory_space=pltpu.VMEM)
    return pl.pallas_call(
        pieces_kernel,
        out_shape=[
            jax.ShapeDtypeStruct((GROUP,) + pieces.shape[1:], pieces.dtype),
            jax.ShapeDtypeStruct((2,) + packed.shape[1:], packed.dtype),
        ],
        in_specs=[vmem, vmem],
        out_specs=[pl.BlockSpec(memory_space=pl.ANY), vmem],
        scratch_shapes=[
            pltpu.VMEM((others,) + packed.shape[1:], packed.dtype),
            dma((GROUP,)),
            dma((GROUP,)),
            dma((others,)),
            dma((others,)),
            dma((2,)),
            dma(()),
        ],
        compiler_params=pltpu.CompilerParams(collective_id=collective_id, has_side_effects=True),
        name="send_pieces",
    )(pieces, packed)


def expert_kernel(
    first, rows_ref, grad_ref, gate_ref, weights_ref,
    mixed_ref, normed_ref, gate_grad_ref, weights_out,
    gate_up_sum, down_sum, mixed_sum, normed_sum,
):
    step = pl.program_id(0)
    expert = pl.program_id(1)
    shards, each, width = rows_ref.shape
    count = shards * each
    rows = rows_ref[...].reshape(count, width)
    grad = grad_ref[...].reshape(count, width).astype(f32)
    gate = jnp.concatenate(
        [
            jnp.broadcast_to(gate_ref[i, pl.ds(expert, 1)], (128, each)).T[:, :1]
            for i in range(shards)
        ],
        0,
    )
    gate_up_weight = weights_ref[:, expert, :first].reshape(-1, width)
    down = weights_ref[:, expert, first:].reshape(-1, width)
    gate_up = jnp.dot(rows, gate_up_weight, preferred_element_type=f32)
    gate_part, up_part = gate_up[:, :F], gate_up[:, F:]
    sigmoid = 1.0 / (1.0 + jnp.exp(-gate_part))
    silu = gate_part * sigmoid
    act = (silu * up_part).astype(bf16)
    out = jnp.dot(act, down, preferred_element_type=f32)
    inner = jnp.sum(out * grad, axis=-1, keepdims=True)
    for i in range(shards):
        line = jnp.broadcast_to(inner[i * each : (i + 1) * each], (each, 128)).T
        gate_grad_ref[i, pl.ds(expert, 1)] = line[:1]
    mixed = gate * out
    expert_grad = (gate * grad).astype(bf16)
    across = (((1,), (1,)), ((), ()))
    over_rows = (((0,), (0,)), ((), ()))
    act_grad = lax.dot_general(expert_grad, down, across, preferred_element_type=f32)
    gate_up_grad = jnp.concatenate(
        [act_grad * up_part * (sigmoid * (1.0 + gate_part * (1.0 - sigmoid))), act_grad * silu], -1
    ).astype(bf16)
    normed = lax.dot_general(gate_up_grad, gate_up_weight, across, preferred_element_type=f32)

    @pl.when(expert == 0)
    def _():
        mixed_sum[...] = mixed
        normed_sum[...] = normed

    @pl.when(expert > 0)
    def _():
        mixed_sum[...] += mixed
        normed_sum[...] += normed

    @pl.when(expert == OWN - 1)
    def _():
        mixed_ref[...] = mixed_sum[...].astype(bf16).reshape(shards, each, width)
        normed_ref[...] = normed_sum[...].astype(bf16).reshape(shards, each, width)

    @pl.when(step == 0)
    def _():
        gate_up_sum[expert] = jnp.zeros_like(gate_up_sum[0])
        down_sum[expert] = jnp.zeros_like(down_sum[0])

    down_sum[expert] += lax.dot_general(act, expert_grad, over_rows, preferred_element_type=f32)
    gate_up_sum[expert] += lax.dot_general(rows, gate_up_grad, over_rows, preferred_element_type=f32)

    @pl.when(step == pl.num_programs(0) - 1)
    def _():
        owners = weights_out.shape[0]
        weights_out[:, expert, :first] = gate_up_sum[expert].astype(bf16).reshape(owners, first, width)
        weights_out[:, expert, first:] = down_sum[expert].astype(bf16).reshape(owners, -1, width)


def expert_layer(first, rows, grad, gate, weights):
    each, width = rows.shape[1:]
    shards = 2
    owners = weights.shape[0]
    tile = pl.BlockSpec((shards, each, width), lambda i, e: (i, 0, 0))
    whole = pl.BlockSpec(weights.shape, lambda i, e: (0, 0, 0, 0), pipeline_mode=pl.Buffered(1))
    return pl.pallas_call(
        functools.partial(expert_kernel, first),
        grid=(GROUP // shards, OWN),
        out_shape=[
            jax.ShapeDtypeStruct(rows.shape, bf16),
            jax.ShapeDtypeStruct(rows.shape, bf16),
            jax.ShapeDtypeStruct((GROUP, 8, each), f32),
            jax.ShapeDtypeStruct(weights.shape, bf16),
        ],
        in_specs=[
            tile,
            tile,
            pl.BlockSpec((shards, OWN, each), lambda i, e: (i, 0, 0)),
            whole,
        ],
        out_specs=[
            tile,
            tile,
            pl.BlockSpec((shards, 8, each), lambda i, e: (i, 0, 0)),
            whole,
        ],
        scratch_shapes=[
            pltpu.VMEM((OWN, owners * first, width), f32),
            pltpu.VMEM((OWN, owners * (weights.shape[2] - first), width), f32),
            pltpu.VMEM((shards * each, width), f32),
            pltpu.VMEM((shards * each, width), f32),
        ],
        compiler_params=pltpu.CompilerParams(vmem_limit_bytes=62 * 2**20),
        cost_estimate=pl.CostEstimate(flops=45000000000, bytes_accessed=2**24, transcendentals=0),
        name="expert_layer",
    )(rows, grad, gate, weights)


def inverse_rms(rows):
    return lax.rsqrt(jnp.mean(rows * rows, axis=-1, keepdims=True) + epsilon)


def norm_back(rows, gain_row, upstream):
    inverse = inverse_rms(rows)
    gain_grad = jnp.sum(upstream * rows * inverse, axis=0)
    scaled = upstream * gain_row
    rows_grad = inverse * scaled - rows * inverse**3 * jnp.mean(scaled * rows, axis=-1, keepdims=True)
    return rows_grad, gain_grad


def rope_tables(positions):
    half = HEAD_SIZE // 2
    frequency = rope_base ** (-(jnp.arange(half, dtype=f32) * 2.0) / HEAD_SIZE)
    angles = positions.astype(f32)[:, None] * frequency[None, :]
    cosine, sine = jnp.cos(angles), jnp.sin(angles)
    return jnp.concatenate([cosine, cosine], 1), jnp.concatenate([sine, sine], 1)


def rotary_apply(rows, cosine, sine):
    half = HEAD_SIZE // 2
    turned = jnp.concatenate([-rows[..., half:], rows[..., :half]], -1)
    return rows * cosine[:, None, :] + turned * sine[:, None, :]


def unrotate(rows, cosine, sine):
    half = HEAD_SIZE // 2
    scaled = rows * sine[:, None, :]
    back = jnp.concatenate([scaled[..., half:], -scaled[..., :half]], -1)
    return rows * cosine[:, None, :] + back


def make_body(n_dp):
    expert_groups = n_dp // PLACES
    inside = [[g * PLACES + j for j in range(PLACES)] for g in range(expert_groups)]
    between = [[g * PLACES + j for g in range(expert_groups)] for j in range(PLACES)]
    half_experts = EXPERTS // 2

    def over_groups(value):
        home = lax.axis_index("dp") // PLACES

        def turned(k):
            return lax.ppermute(value, "dp", [(d, (d + k * PLACES) % n_dp) for d in range(n_dp)])

        parts = [turned(k) for k in range(expert_groups - 1, 0, -1)] + [value]
        ring = jnp.stack(parts + parts[:-1])
        start = (expert_groups - 1 - home) % expert_groups
        return lax.dynamic_slice_in_dim(ring, start, expert_groups, axis=0)

    def expert_pieces(gate_up_shard, down_shard, seq_rank):
        mine = [
            jnp.swapaxes(lax.dynamic_slice_in_dim(w, seq_rank * half_experts, half_experts, axis=1), 0, 1)
            for w in (gate_up_shard, down_shard)
        ]
        mine = jnp.concatenate(mine, 1)
        return mine.reshape((PLACES, OWN) + mine.shape[1:])

    def body(
        tokens, starts, routes, gain_one, query_key_value_weight, w_out,
        gain_two, w_router, w_gate_up, w_down, cotangent,
    ):
        count = tokens.shape[1]
        seq_rank = lax.axis_index("seq")
        expert = (seq_rank * PLACES + lax.axis_index("dp") % PLACES) * OWN
        query_columns = QUERY_HEADS * HEAD_SIZE
        key_columns = KEY_VALUE_HEADS * HEAD_SIZE
        group = QUERY_HEADS // KEY_VALUE_HEADS
        forward_pair, back_pair = [(0, 1)], [(1, 0)]

        mine = expert_pieces(w_gate_up, w_down, seq_rank)
        mine, query_key_value_weight, tokens, starts = lax.optimization_barrier(
            (mine, query_key_value_weight, tokens, starts)
        )
        mine = lax.all_to_all(
            mine, "dp", split_axis=0, concat_axis=0, tiled=True, axis_index_groups=inside
        )
        tokens_before = lax.ppermute(tokens[0], "seq", forward_pair)
        starts_before = lax.ppermute(starts, "seq", forward_pair)
        spare = lambda value: jnp.pad(value, ((0, 0), (0, 128 - value.shape[1])))
        little = jnp.concatenate([spare(w_router), spare(jnp.stack([gain_one, gain_two], 1))], 1)
        shards = (query_key_value_weight, w_out, little)
        halves = [w.shape[1] // 2 for w in shards]
        packed = over_groups(
            jnp.concatenate(
                [
                    lax.dynamic_slice_in_dim(w, seq_rank * h, h, axis=1)
                    for w, h in zip(shards, halves)
                ],
                1,
            )
        )
        mine, packed, tokens_before, starts_before = lax.optimization_barrier(
            (mine, packed, tokens_before, starts_before)
        )
        weights = lax.all_gather(mine, "dp", axis=0, tiled=True, axis_index_groups=between)
        qkv_weight, out_weight, small = weights_gather(0, halves, packed)
        router_weight = small[:, :EXPERTS]
        gain_a = small[:, 128].astype(f32)
        gain_b = small[:, 129].astype(f32)

        token_rows = tokens[0].astype(f32)
        grad_output = cotangent[0].astype(f32)
        both = 2 * count
        index = jnp.arange(both, dtype=jnp.int32)
        flags = jnp.concatenate([starts_before[0], starts[0]])
        begins = (flags > 0) | (index == jnp.where(seq_rank == 0, count, 0))
        last_begin = jnp.max(
            jnp.where(begins[None, :] & (index[None, :] <= index[:, None]), index[None, :], 0), axis=1
        )
        cosine_all, sine_all = rope_tables(index - last_begin)
        cosine, sine = cosine_all[count:], sine_all[count:]

        rows_all = jnp.concatenate([tokens_before.astype(f32), token_rows], 0)
        normed_all = (rows_all * inverse_rms(rows_all) * gain_a).astype(bf16)
        normed_one = normed_all[count:]
        projected_q = jnp.dot(normed_one, qkv_weight[:, :query_columns], preferred_element_type=f32)
        projected_kv = jnp.dot(normed_all, qkv_weight[:, query_columns:], preferred_element_type=f32)
        queries = rotary_apply(
            projected_q.reshape(count, QUERY_HEADS, HEAD_SIZE), cosine, sine
        ).astype(bf16).reshape(count, KEY_VALUE_HEADS, group, HEAD_SIZE)
        keys = rotary_apply(
            projected_kv[:, :key_columns].reshape(both, KEY_VALUE_HEADS, HEAD_SIZE), cosine_all, sine_all
        ).astype(bf16)
        values = projected_kv[:, key_columns:].astype(bf16).reshape(both, KEY_VALUE_HEADS, HEAD_SIZE)

        scale = HEAD_SIZE ** (-0.5)
        allowed = (index[None, :] <= index[count:, None]) & (index[None, :] >= last_begin[count:, None])
        scores = jnp.einsum("qgrd,kgd->grqk", queries, keys, preferred_element_type=f32) * scale
        scores = jnp.where(allowed[None, None], scores, masked_score)
        top = jnp.max(scores, axis=-1, keepdims=True)
        exps = jnp.exp(scores - top)
        probs = exps / jnp.sum(exps, axis=-1, keepdims=True)
        probs_low = probs.astype(bf16)
        attended = jnp.einsum(
            "grqk,kgd->qgrd", probs_low, values, preferred_element_type=f32
        ).reshape(count, query_columns).astype(bf16)
        hidden = token_rows + jnp.dot(attended, out_weight, preferred_element_type=f32)
        normed_two = (hidden * inverse_rms(hidden) * gain_b).astype(bf16)
        logits = jnp.dot(normed_two, router_weight, preferred_element_type=f32)
        expert_ids = jnp.arange(EXPERTS, dtype=jnp.int32)
        chosen = jnp.any(routes[0][:, :, None] == expert_ids[None, None, :], axis=1)
        gates = jax.nn.softmax(jnp.where(chosen, logits, -jnp.inf), axis=-1)

        rows_in, gates_all, grad_all = group_gather(1, normed_two, gates.T, cotangent[0])
        gate = lax.dynamic_slice_in_dim(gates_all, expert, OWN, axis=1)
        mixed_part, normed_part, gate_grad_part, expert_wgrads = expert_layer(
            w_gate_up.shape[0], rows_in, grad_all, gate, weights
        )
        expert_grads = lax.psum_scatter(
            expert_wgrads, "dp", scatter_dimension=0, tiled=True, axis_index_groups=between
        )
        normed_grad, gate_grad = group_reduce(2, normed_part, gate_grad_part)
        gate_grad = gate_grad[:, :OWN].reshape(EXPERTS, count).T

        over_rows = (((0,), (0,)), ((), ()))
        weighted = jnp.where(chosen, gates * gate_grad, 0.0)
        logits_grad = weighted - gates * jnp.sum(weighted, axis=-1, keepdims=True)
        router_wide = router_weight.astype(f32)
        normed_grad = normed_grad + jnp.dot(logits_grad, router_wide.T, precision=highest)
        router_wgrad = jnp.dot(normed_two.astype(f32).T, logits_grad, precision=highest)
        hidden_branch, gain_two_grad = norm_back(hidden, gain_b, normed_grad)
        hidden_grad = grad_output + hidden_branch
        branch_low = hidden_grad.astype(bf16)
        out_wgrad = lax.dot_general(attended, branch_low, over_rows, preferred_element_type=f32)
        attended_grad = lax.dot_general(
            branch_low, out_weight, (((1,), (1,)), ((), ())), preferred_element_type=f32
        ).astype(bf16).reshape(count, KEY_VALUE_HEADS, group, HEAD_SIZE)

        prob_grad = jnp.einsum("qgrd,kgd->grqk", attended_grad, values, preferred_element_type=f32)
        delta = jnp.sum(probs * prob_grad, axis=-1, keepdims=True)
        score_grad = (probs * (prob_grad - delta)).astype(bf16)
        query_grad = (
            jnp.einsum("grqk,kgd->qgrd", score_grad, keys, preferred_element_type=f32) * scale
        ).reshape(count, QUERY_HEADS, HEAD_SIZE)
        key_grad = (
            jnp.einsum("grqk,qgrd->kgd", score_grad, queries, preferred_element_type=f32) * scale
        ).reshape(both, key_columns)
        value_grad = jnp.einsum(
            "grqk,qgrd->kgd", probs_low, attended_grad, preferred_element_type=f32
        ).reshape(both, key_columns)
        kv_grad = jnp.concatenate([key_grad, value_grad], 1)
        kv_back = lax.ppermute(kv_grad[:count].astype(bf16), "seq", back_pair)
        kv_grad = (kv_grad[count:] + kv_back.astype(f32)).astype(bf16).astype(f32)
        query_grad = query_grad.astype(bf16).astype(f32)
        query_back = unrotate(query_grad, cosine, sine).reshape(count, query_columns)
        key_back = unrotate(
            kv_grad[:, :key_columns].reshape(count, KEY_VALUE_HEADS, HEAD_SIZE), cosine, sine
        ).reshape(count, key_columns)
        projected_grad = jnp.concatenate([query_back, key_back, kv_grad[:, key_columns:]], 1).astype(bf16)
        qkv_wgrad = lax.dot_general(normed_one, projected_grad, over_rows, preferred_element_type=f32)
        normed_one_grad = lax.dot_general(
            projected_grad, qkv_weight, (((1,), (1,)), ((), ())), preferred_element_type=f32
        )
        rows_branch, gain_one_grad = norm_back(token_rows, gain_a, normed_one_grad)
        input_grad = (hidden_grad + rows_branch).astype(bf16)[None]

        little = jnp.concatenate(
            [spare(router_wgrad), spare(jnp.stack([gain_one_grad, gain_two_grad], 1))], 1
        )
        packed, mixed = weights_reduce(
            3, expert_groups, (qkv_wgrad.astype(bf16), out_wgrad.astype(bf16), little), mixed_part
        )
        mixed = mixed.reshape(count, MODEL_WIDTH).astype(f32)
        output = (hidden + mixed).astype(bf16)[None]
        stat_sums = jnp.stack([jnp.sum(hidden * hidden), jnp.sum(mixed * mixed)])
        stat_sums = stat_sums + lax.ppermute(stat_sums, "seq", [(0, 1), (1, 0)])
        experts_all, ends = send_pieces(4, expert_grads, packed)
        qkv_shard, out_shard, little = [
            jnp.concatenate([ends[0, :, f : f + h], ends[1, :, f : f + h]], 1).astype(f32)
            for f, h in zip(starts_of(halves), halves)
        ]
        experts_all = experts_all.reshape((EXPERTS,) + experts_all.shape[2:])
        first = w_gate_up.shape[0]
        stream_rms = jnp.sqrt(stat_sums / (both * MODEL_WIDTH)).reshape(1, 2)
        return (
            output,
            input_grad,
            little[:, 128],
            qkv_shard,
            out_shard,
            little[:, 129],
            little[:, :EXPERTS],
            jnp.swapaxes(experts_all[:, :first], 0, 1).astype(f32),
            jnp.swapaxes(experts_all[:, first:], 0, 1).astype(f32),
            stream_rms,
        )

    return body


def solution(mesh):
    placed = (
        P("dp", "seq", None),
        P("dp", "seq"),
        P("dp", "seq", None),
        P("dp"),
        P("dp", None),
        P("dp", None),
        P("dp"),
        P("dp", None),
        P("dp", None, None),
        P("dp", None, None),
        P("dp", "seq", None),
    )
    return jax.shard_map(
        make_body(mesh.shape["dp"]),
        mesh=mesh,
        in_specs=placed,
        out_specs=(
            P("dp", "seq", None),
            P("dp", "seq", None),
            P("dp"),
            P("dp", None),
            P("dp", None),
            P("dp"),
            P("dp", None),
            P("dp", None, None),
            P("dp", None, None),
            P("dp", None),
        ),
        check_vma=False,
    )
```

```python
import functools

import jax
import jax.numpy as jnp
from jax import lax
from jax.experimental import pallas as pl
from jax.experimental.pallas import tpu as pltpu
from jax.sharding import PartitionSpec as P

MODEL_WIDTH = 1024
QUERY_HEADS = 16
KEY_VALUE_HEADS = 8
HEAD_SIZE = 64
F = 512
EXPERTS = 16
TOPK = 8
PLACES = 4
GROUP = 8
OWN = EXPERTS // GROUP

epsilon = 1e-06
rope_base = 10000.0
highest = lax.Precision.HIGHEST
masked_score = -1e30
f32 = jnp.float32
bf16 = jnp.bfloat16
MESH = pl.DeviceIdType.MESH

TOKEN_LINKS = ((4, 2), (2, 4))


def flip(value, bit):
    return value + bit * (1 - 2 * ((value // bit) % 2))


def flip_mask(value, mask):
    for bit in (1, 2, 4, 8):
        if mask & bit:
            value = flip(value, bit)
    return value


def subsets(bits):
    out = [0]
    for bit in bits:
        out = out + [m | bit for m in out]
    return out


def row_parts(rows):
    first = (rows // 2 + 15) // 16 * 16
    return ((0, first), (first, rows - first))


def my_place(places=PLACES):
    seq = lax.axis_index("seq")
    dp = lax.axis_index("dp")
    rank = seq * places + dp % places

    def peer(mask):
        return {
            "seq": 1 - seq if mask & places else seq,
            "dp": flip_mask(dp, mask & (places - 1)),
        }

    return rank, peer


def meet(devices):
    barrier = pltpu.get_barrier_semaphore()
    for there in devices:
        pl.semaphore_signal(barrier, inc=1, device_id=there, device_id_type=MESH)
    pl.semaphore_wait(barrier, len(devices))


def gather_kernel(count, *refs):
    ins, outs = refs[:count], refs[count : 2 * count]
    send, recv, send_core, recv_core, local = refs[2 * count :]
    rank, peer = my_place(PLACES)
    own = [
        pltpu.make_async_copy(ins[a], outs[a].at[rank], local.at[a]) for a in range(count)
    ]
    for copy in own:
        copy.start()
    meet([peer(bit) for bit in (1, 2, 4)])
    parts = [row_parts(ref.shape[0]) for ref in ins]

    def remote(a, p, mask, bit, sems, index):
        start, size = parts[a][p]
        rows = pl.ds(start, size)
        shard = flip_mask(rank, mask)
        src = ins[a].at[rows] if mask == 0 else outs[a].at[shard, rows]
        return pltpu.make_async_remote_copy(
            src_ref=src,
            dst_ref=outs[a].at[shard, rows],
            send_sem=sems[0].at[a, p, index],
            recv_sem=sems[1].at[a, p, index],
            device_id=peer(bit),
            device_id_type=MESH,
        )

    started = []
    live = {}
    for step in range(3):
        for p in range(2):
            for a in range(count):
                if parts[a][p][1] == 0:
                    continue
                order = TOKEN_LINKS[p]
                if step > 0:
                    for copy in live.pop((a, p)):
                        copy.wait_recv()
                if step < 2:
                    now = []
                    for index, mask in enumerate(subsets(order[:step])):
                        copy = remote(a, p, mask, order[step], (send, recv), 2**step - 1 + index)
                        copy.start()
                        now.append(copy)
                        started.append(copy)
                    live[(a, p)] = now
                fresh = [0] if step == 0 else [m | order[step - 1] for m in subsets(order[: step - 1])]
                base = 0 if step == 0 else 2 ** (step - 1)
                for index, mask in enumerate(fresh):
                    copy = remote(a, p, mask, 1, (send_core, recv_core), base + index)
                    copy.start()
                    live.setdefault("core", []).append(copy)
    for copy in live["core"]:
        copy.wait()
    for copy in started:
        copy.wait_send()
    for copy in own:
        copy.wait()


def group_gather(collective_id, *arrays):
    count = len(arrays)
    return pl.pallas_call(
        functools.partial(gather_kernel, count),
        out_shape=[jax.ShapeDtypeStruct((GROUP,) + a.shape, a.dtype) for a in arrays],
        in_specs=[pl.BlockSpec(memory_space=pltpu.VMEM)] * count,
        out_specs=[pl.BlockSpec(memory_space=pl.ANY)] * count,
        scratch_shapes=[
            pltpu.SemaphoreType.DMA((count, 2, 3)),
            pltpu.SemaphoreType.DMA((count, 2, 3)),
            pltpu.SemaphoreType.DMA((count, 2, 4)),
            pltpu.SemaphoreType.DMA((count, 2, 4)),
            pltpu.SemaphoreType.DMA((count,)),
        ],
        compiler_params=pltpu.CompilerParams(collective_id=collective_id, has_side_effects=True),
        cost_estimate=pl.CostEstimate(flops=1000000000, bytes_accessed=2**24, transcendentals=0),
        name="group_gather",
    )(*arrays)


def add_rows(target, source, start, size):
    chunk = 32 if size % 32 == 0 else 16

    def step(i, carry):
        rows = pl.ds(pl.multiple_of(start + i * chunk, chunk), chunk)
        target[rows] = (target[rows].astype(f32) + source[rows].astype(f32)).astype(target.dtype)
        return carry

    lax.fori_loop(0, size // chunk, step, 0)


def reduce_kernel(
    normed_ref, gate_ref, normed_out, gate_out,
    total, got0, got1, got2, sems, gate_sems, local, own_gate,
):
    rank, peer = my_place(PLACES)
    chip = rank // 2
    core = rank % 2
    parts = row_parts(normed_ref.shape[1])
    ins = (normed_ref,)
    outs = (normed_out,)
    loads = []
    for t in range(1):
        for c in range(4):
            copy = pltpu.make_async_copy(ins[t].at[2 * c + core], total.at[t, c], local.at[t, c])
            copy.start()
            loads.append(copy)
    everyone = [peer(mask) for mask in range(1, GROUP)]
    meet(everyone)
    gates = []
    keep = pltpu.make_async_copy(gate_ref.at[rank], gate_out.at[rank], own_gate)
    keep.start()
    for mask, there in zip(range(1, GROUP), everyone):
        copy = pltpu.make_async_remote_copy(
            src_ref=gate_ref.at[flip_mask(rank, mask)],
            dst_ref=gate_out.at[rank],
            send_sem=gate_sems.at[0, mask],
            recv_sem=gate_sems.at[1, mask],
            device_id=there,
            device_id_type=MESH,
        )
        copy.start()
        gates.append(copy)

    started = []
    live = {}

    def send(t, p, stage, index, src, dst, bit):
        copy = pltpu.make_async_remote_copy(
            src_ref=src,
            dst_ref=dst,
            send_sem=sems.at[0, t, p, stage, index],
            recv_sem=sems.at[1, t, p, stage, index],
            device_id=peer(bit),
            device_id_type=MESH,
        )
        copy.start()
        started.append(copy)
        live.setdefault((t, p), []).append(copy)

    def chip_of(mask):
        return flip_mask(rank, mask) // 2

    for p in range(2):
        for t in range(1):
            rows = pl.ds(*parts[p])
            for c in range(4):
                send(
                    t, p, 0, c, ins[t].at[2 * c + 1 - core, rows], got0.at[t, c, rows], 1
                )
    for copy in loads:
        copy.wait()
    got = (got1, got2)
    for stage in range(3):
        for p in range(2):
            for t in range(1):
                order = TOKEN_LINKS[p]
                rows = pl.ds(*parts[p])
                for copy in live.pop((t, p)):
                    copy.wait_recv()
                if stage == 0:

                    def over_chips(c, carry, t=t, p=p):
                        add_rows(total.at[t, c], got0.at[t, c], *parts[p])
                        return carry

                    lax.fori_loop(0, 4, over_chips, 0)
                else:
                    for index, mask in enumerate(subsets(order[stage:])):
                        if stage == 2:
                            outs[t][rows] = total[t, chip, rows].astype(f32) + got2[t, 0, rows].astype(f32)
                        else:
                            add_rows(
                                total.at[t, chip_of(mask)], got[stage - 1].at[t, index], *parts[p]
                            )
                if stage < 2:
                    for index, mask in enumerate(subsets(order[stage + 1 :])):
                        send(
                            t, p, stage + 1, index,
                            total.at[t, chip_of(mask | order[stage]), rows],
                            got[stage].at[t, index, rows],
                            order[stage],
                        )
    for copy in started:
        copy.wait_send()
    for copy in gates:
        copy.wait()
    keep.wait()


def group_reduce(collective_id, normed, gate_grad):
    rows, width = normed.shape[1:]
    return pl.pallas_call(
        reduce_kernel,
        out_shape=[
            jax.ShapeDtypeStruct((rows, width), f32),
            jax.ShapeDtypeStruct(gate_grad.shape, gate_grad.dtype),
        ],
        in_specs=[pl.BlockSpec(memory_space=pl.ANY)] * 2,
        out_specs=[
            pl.BlockSpec(memory_space=pltpu.VMEM),
            pl.BlockSpec(memory_space=pl.ANY),
        ],
        scratch_shapes=[
            pltpu.VMEM((1, 4, rows, width), bf16),
            pltpu.VMEM((1, 4, rows, width), bf16),
            pltpu.VMEM((1, 2, rows, width), bf16),
            pltpu.VMEM((1, 1, rows, width), bf16),
            pltpu.SemaphoreType.DMA((2, 1, 2, 3, 4)),
            pltpu.SemaphoreType.DMA((2, GROUP)),
            pltpu.SemaphoreType.DMA((1, 4)),
            pltpu.SemaphoreType.DMA(()),
        ],
        compiler_params=pltpu.CompilerParams(
            collective_id=collective_id, has_side_effects=True, vmem_limit_bytes=48 * 2**20
        ),
        cost_estimate=pl.CostEstimate(flops=1000000, bytes_accessed=2**24, transcendentals=0),
        name="group_reduce",
    )(normed, gate_grad)


def column_parts(half):
    first = -(-(half // 128) // 2) * 128
    return ((0, first), (first, half - first))


def shard_view(ref, halves, a, p, rank_value):
    start, size = column_parts(halves[a])[p]
    offset = pl.multiple_of((rank_value // PLACES) * halves[a] + start, 128)
    return ref.at[:, rank_value % PLACES, :, pl.ds(offset, size)]


def starts_of(sizes):
    return [sum(sizes[:i]) for i in range(len(sizes))]


def weights_gather_kernel(halves, packed, *refs):
    count = len(halves)
    outs = refs[:count]
    send, recv, local = refs[count:]
    rank, peer = my_place()
    firsts = starts_of(halves)
    seq = lax.axis_index("seq")
    own = []
    for a in range(count):
        columns = pl.ds(pl.multiple_of(seq * halves[a], 128), halves[a])
        copy = pltpu.make_async_copy(
            packed.at[:, :, pl.ds(firsts[a], halves[a])],
            outs[a].at[:, rank % PLACES, :, columns],
            local.at[a],
        )
        copy.start()
        own.append(copy)
    meet([peer(bit) for bit in (1, 2, 4)])
    started = []

    def remote(a, p, mask, bit, index):
        view = shard_view(outs[a], halves, a, p, flip_mask(rank, mask))
        start, size = column_parts(halves[a])[p]
        source = packed.at[:, :, pl.ds(firsts[a] + start, size)] if mask == 0 else view
        copy = pltpu.make_async_remote_copy(
            src_ref=source,
            dst_ref=view,
            send_sem=send.at[a, p, index],
            recv_sem=recv.at[a, p, index],
            device_id=peer(bit),
            device_id_type=MESH,
        )
        copy.start()
        started.append(copy)
        return copy

    live = {}
    last = []
    for step in range(3):
        for p in range(2):
            for a in range(count):
                if column_parts(halves[a])[p][1] == 0:
                    continue
                order = TOKEN_LINKS[p]
                if step > 0:
                    for copy in live.pop((a, p)):
                        copy.wait_recv()
                if step < 2:
                    live[(a, p)] = [
                        remote(a, p, mask, order[step], 2**step - 1 + index)
                        for index, mask in enumerate(subsets(order[:step]))
                    ]
                fresh = [0] if step == 0 else [m | order[step - 1] for m in subsets(order[: step - 1])]
                base = 0 if step == 0 else 2 ** (step - 1)
                for index, mask in enumerate(fresh):
                    last.append(remote(a, p, mask, 1, 3 + base + index))
    for copy in last:
        copy.wait_recv()
    for copy in started:
        copy.wait_send()
    for copy in own:
        copy.wait()


def weights_gather(collective_id, halves, packed):
    groups, rows, _ = packed.shape
    count = len(halves)
    whole = pl.pallas_call(
        functools.partial(weights_gather_kernel, halves),
        out_shape=[jax.ShapeDtypeStruct((groups, PLACES, rows, 2 * h), packed.dtype) for h in halves],
        in_specs=[pl.BlockSpec(memory_space=pltpu.VMEM)],
        out_specs=[pl.BlockSpec(memory_space=pl.ANY)] * count,
        scratch_shapes=[
            pltpu.SemaphoreType.DMA((count, 2, 7)),
            pltpu.SemaphoreType.DMA((count, 2, 7)),
            pltpu.SemaphoreType.DMA((count,)),
        ],
        compiler_params=pltpu.CompilerParams(collective_id=collective_id, has_side_effects=True),
        cost_estimate=pl.CostEstimate(flops=1000000, bytes_accessed=2**24, transcendentals=0),
        name="weights_gather",
    )(packed)
    return [w.reshape(-1, w.shape[3]) for w in whole]


def add_block(target, source, at, start, size):
    groups, rows = source.shape[0], source.shape[1]
    columns = pl.ds(start, size)
    chunk = 64 if rows % 64 == 0 else 16
    pieces = rows // chunk

    def step(i, carry):
        lines = pl.ds(pl.multiple_of((i % pieces) * chunk, chunk), chunk)
        index = (i // pieces, lines, columns)
        new = target[(at,) + index].astype(f32) + source[index].astype(f32)
        target[(at,) + index] = new.astype(target.dtype)
        return carry

    lax.fori_loop(0, groups * pieces, step, 0)


def weights_reduce_kernel(count, *refs):
    ins, packed, rows_out = refs[:count], refs[count], refs[count + 1]
    rest = refs[count + 2 :]
    total, got0, got1, got2 = [rest[i * count : (i + 1) * count] for i in range(4)]
    sems, local = rest[4 * count :]
    rank, peer = my_place()
    chip, core = rank // 2, rank % 2
    halves = [ref.shape[3] // 2 for ref in ins[:-1]]
    firsts = starts_of(halves)
    halves = halves + [ins[-1].shape[3]]
    parts = [column_parts(half) for half in halves]

    def source(a, value, start, size):
        if a == count - 1:
            return ins[a].at[value, :, :, pl.ds(start, size)]
        offset = pl.multiple_of((value // PLACES) * halves[a] + start, 128)
        return ins[a].at[:, value % PLACES, :, pl.ds(offset, size)]

    loads = []
    for a in range(count):
        for c in range(4):
            copy = pltpu.make_async_copy(
                source(a, 2 * c + core, 0, halves[a]), total[a].at[c], local.at[a, c]
            )
            copy.start()
            loads.append(copy)
    meet([peer(bit) for bit in (1, 2, 4)])
    started = []
    live = {}

    def send(a, p, stage, index, src, dst, bit):
        copy = pltpu.make_async_remote_copy(
            src_ref=src,
            dst_ref=dst,
            send_sem=sems.at[0, a, p, stage, index],
            recv_sem=sems.at[1, a, p, stage, index],
            device_id=peer(bit),
            device_id_type=MESH,
        )
        copy.start()
        started.append(copy)
        live.setdefault((a, p), []).append(copy)

    def chip_of(mask):
        return flip_mask(rank, mask) // 2

    for p in range(2):
        for a in range(count):
            columns = pl.ds(*parts[a][p])
            if parts[a][p][1]:
                for c in range(4):
                    send(
                        a, p, 0, c,
                        source(a, 2 * c + 1 - core, *parts[a][p]),
                        got0[a].at[c, :, :, columns],
                        1,
                    )
    for copy in loads:
        copy.wait()
    got = (got1, got2)
    for stage in range(3):
        for p in range(2):
            for a in range(count):
                start, size = parts[a][p]
                if size == 0:
                    continue
                order = TOKEN_LINKS[p]
                columns = pl.ds(start, size)
                for copy in live.pop((a, p)):
                    copy.wait_recv()
                if stage == 0:

                    def over_chips(c, carry, a=a, start=start, size=size):
                        add_block(total[a], got0[a].at[c], c, start, size)
                        return carry

                    lax.fori_loop(0, 4, over_chips, 0)
                else:
                    for index, mask in enumerate(subsets(order[stage:])):
                        add_block(total[a], got[stage - 1][a].at[index], chip_of(mask), start, size)
                if stage < 2:
                    for index, mask in enumerate(subsets(order[stage + 1 :])):
                        send(
                            a, p, stage + 1, index,
                            total[a].at[chip_of(mask | order[stage]), :, :, columns],
                            got[stage][a].at[index, :, :, columns],
                            order[stage],
                        )
    for a in range(count - 1):
        packed[:, :, pl.ds(firsts[a], halves[a])] = total[a][chip].astype(packed.dtype)
    rows_out[...] = total[-1][chip]
    for copy in started:
        copy.wait_send()


def weights_reduce(collective_id, groups, arrays, token_rows):
    count = len(arrays) + 1
    views = [a.reshape(groups, PLACES, -1, a.shape[1]) for a in arrays]
    rows = views[0].shape[2]
    halves = [a.shape[1] // 2 for a in arrays]

    each, width = token_rows.shape[1:]
    token_shape = (groups, each // groups, width)

    def buffers(lead):
        return [pltpu.VMEM((lead, groups, rows, h), a.dtype) for h, a in zip(halves, arrays)] + [
            pltpu.VMEM((lead,) + token_shape, bf16)
        ]

    dma = pltpu.SemaphoreType.DMA
    return pl.pallas_call(
        functools.partial(weights_reduce_kernel, count),
        out_shape=[
            jax.ShapeDtypeStruct((groups, rows, sum(halves)), bf16),
            jax.ShapeDtypeStruct(token_shape, bf16),
        ],
        in_specs=[pl.BlockSpec(memory_space=pl.ANY)] * count,
        out_specs=[pl.BlockSpec(memory_space=pltpu.VMEM)] * 2,
        scratch_shapes=buffers(4) + buffers(4) + buffers(2) + buffers(1)
        + [dma((2, count, 2, 3, 4)), dma((count, 4))],
        compiler_params=pltpu.CompilerParams(
            collective_id=collective_id, has_side_effects=True, vmem_limit_bytes=48 * 2**20
        ),
        cost_estimate=pl.CostEstimate(flops=1000000, bytes_accessed=2**24, transcendentals=0),
        name="weights_reduce",
    )(*views, token_rows.reshape((GROUP,) + token_shape))


def pieces_kernel(pieces, packed, whole, ends, far_got, send, recv, far_send, far_recv, last, local):
    rank, peer = my_place()
    place = rank % PLACES
    groups = packed.shape[0]
    seq = lax.axis_index("seq")
    home = lax.axis_index("dp") // PLACES
    keep = pltpu.make_async_copy(pieces.at[place], whole.at[rank], local)
    keep.start()
    masks = (6, 7, 2, 4, 3, 5, 1)
    others = [(home + k) % groups for k in range(1, groups)]
    far = [{"seq": seq, "dp": g * PLACES + place} for g in others]
    meet([peer(mask) for mask in masks] + far)
    sums = []
    for k, there in enumerate(far):
        copy = pltpu.make_async_remote_copy(
            src_ref=packed.at[others[k]],
            dst_ref=far_got.at[k],
            send_sem=far_send.at[k],
            recv_sem=far_recv.at[k],
            device_id=there,
            device_id_type=MESH,
        )
        copy.start()
        sums.append(copy)
    copies = []
    for mask in masks:
        copy = pltpu.make_async_remote_copy(
            src_ref=pieces.at[flip_mask(place, mask & (PLACES - 1))],
            dst_ref=whole.at[rank],
            send_sem=send.at[mask],
            recv_sem=recv.at[mask],
            device_id=peer(mask),
            device_id_type=MESH,
        )
        copy.start()
        copies.append(copy)
    for copy in sums:
        copy.wait()
    value = packed[home].astype(f32)
    for k in range(groups - 1):
        value = value + far_got[k].astype(f32)
    ends[seq] = value.astype(ends.dtype)
    copy = pltpu.make_async_remote_copy(
        src_ref=ends.at[seq],
        dst_ref=ends.at[seq],
        send_sem=last.at[0],
        recv_sem=last.at[1],
        device_id=peer(4),
        device_id_type=MESH,
    )
    copy.start()
    copies.append(copy)
    for copy in copies:
        copy.wait()
    keep.wait()


def send_pieces(collective_id, pieces, packed):
    groups = packed.shape[0]
    others = max(groups - 1, 1)
    dma = pltpu.SemaphoreType.DMA
    vmem = pl.BlockSpec(memory_space=pltpu.VMEM)
    return pl.pallas_call(
        pieces_kernel,
        out_shape=[
            jax.ShapeDtypeStruct((GROUP,) + pieces.shape[1:], pieces.dtype),
            jax.ShapeDtypeStruct((2,) + packed.shape[1:], packed.dtype),
        ],
        in_specs=[vmem, vmem],
        out_specs=[pl.BlockSpec(memory_space=pl.ANY), vmem],
        scratch_shapes=[
            pltpu.VMEM((others,) + packed.shape[1:], packed.dtype),
            dma((GROUP,)),
            dma((GROUP,)),
            dma((others,)),
            dma((others,)),
            dma((2,)),
            dma(()),
        ],
        compiler_params=pltpu.CompilerParams(collective_id=collective_id, has_side_effects=True),
        name="send_pieces",
    )(pieces, packed)


def expert_kernel(
    first, rows_ref, grad_ref, gate_ref, weights_ref,
    mixed_ref, normed_ref, gate_grad_ref, weights_out,
    gate_up_sum, down_sum, mixed_sum, normed_sum,
):
    step = pl.program_id(0)
    expert = pl.program_id(1)
    shards, each, width = rows_ref.shape
    count = shards * each
    rows = rows_ref[...].reshape(count, width)
    grad = grad_ref[...].reshape(count, width).astype(f32)
    gate = jnp.concatenate(
        [
            jnp.broadcast_to(gate_ref[i, pl.ds(expert, 1)], (128, each)).T[:, :1]
            for i in range(shards)
        ],
        0,
    )
    gate_up_weight = weights_ref[:, expert, :first].reshape(-1, width)
    down = weights_ref[:, expert, first:].reshape(-1, width)
    gate_up = jnp.dot(rows, gate_up_weight, preferred_element_type=f32)
    gate_part, up_part = gate_up[:, :F], gate_up[:, F:]
    sigmoid = 1.0 / (1.0 + jnp.exp(-gate_part))
    silu = gate_part * sigmoid
    act = (silu * up_part).astype(bf16)
    out = jnp.dot(act, down, preferred_element_type=f32)
    inner = jnp.sum(out * grad, axis=-1, keepdims=True)
    for i in range(shards):
        line = jnp.broadcast_to(inner[i * each : (i + 1) * each], (each, 128)).T
        gate_grad_ref[i, pl.ds(expert, 1)] = line[:1]
    mixed = gate * out
    expert_grad = (gate * grad).astype(bf16)
    across = (((1,), (1,)), ((), ()))
    over_rows = (((0,), (0,)), ((), ()))
    act_grad = lax.dot_general(expert_grad, down, across, preferred_element_type=f32)
    gate_up_grad = jnp.concatenate(
        [act_grad * up_part * (sigmoid * (1.0 + gate_part * (1.0 - sigmoid))), act_grad * silu], -1
    ).astype(bf16)
    normed = lax.dot_general(gate_up_grad, gate_up_weight, across, preferred_element_type=f32)

    @pl.when(expert == 0)
    def _():
        mixed_sum[...] = mixed
        normed_sum[...] = normed

    @pl.when(expert > 0)
    def _():
        mixed_sum[...] += mixed
        normed_sum[...] += normed

    @pl.when(expert == OWN - 1)
    def _():
        mixed_ref[...] = mixed_sum[...].astype(bf16).reshape(shards, each, width)
        normed_ref[...] = normed_sum[...].astype(bf16).reshape(shards, each, width)

    @pl.when(step == 0)
    def _():
        gate_up_sum[expert] = jnp.zeros_like(gate_up_sum[0])
        down_sum[expert] = jnp.zeros_like(down_sum[0])

    down_sum[expert] += lax.dot_general(act, expert_grad, over_rows, preferred_element_type=f32)
    gate_up_sum[expert] += lax.dot_general(rows, gate_up_grad, over_rows, preferred_element_type=f32)

    @pl.when(step == pl.num_programs(0) - 1)
    def _():
        owners = weights_out.shape[0]
        weights_out[:, expert, :first] = gate_up_sum[expert].astype(bf16).reshape(owners, first, width)
        weights_out[:, expert, first:] = down_sum[expert].astype(bf16).reshape(owners, -1, width)


def expert_layer(first, rows, grad, gate, weights):
    each, width = rows.shape[1:]
    shards = 2
    owners = weights.shape[0]
    tile = pl.BlockSpec((shards, each, width), lambda i, e: (i, 0, 0))
    whole = pl.BlockSpec(weights.shape, lambda i, e: (0, 0, 0, 0), pipeline_mode=pl.Buffered(1))
    return pl.pallas_call(
        functools.partial(expert_kernel, first),
        grid=(GROUP // shards, OWN),
        out_shape=[
            jax.ShapeDtypeStruct(rows.shape, bf16),
            jax.ShapeDtypeStruct(rows.shape, bf16),
            jax.ShapeDtypeStruct((GROUP, 8, each), f32),
            jax.ShapeDtypeStruct(weights.shape, bf16),
        ],
        in_specs=[
            tile,
            tile,
            pl.BlockSpec((shards, OWN, each), lambda i, e: (i, 0, 0)),
            whole,
        ],
        out_specs=[
            tile,
            tile,
            pl.BlockSpec((shards, 8, each), lambda i, e: (i, 0, 0)),
            whole,
        ],
        scratch_shapes=[
            pltpu.VMEM((OWN, owners * first, width), f32),
            pltpu.VMEM((OWN, owners * (weights.shape[2] - first), width), f32),
            pltpu.VMEM((shards * each, width), f32),
            pltpu.VMEM((shards * each, width), f32),
        ],
        compiler_params=pltpu.CompilerParams(vmem_limit_bytes=62 * 2**20),
        cost_estimate=pl.CostEstimate(flops=45000000000, bytes_accessed=2**24, transcendentals=0),
        name="expert_layer",
    )(rows, grad, gate, weights)


def inverse_rms(rows):
    return lax.rsqrt(jnp.mean(rows * rows, axis=-1, keepdims=True) + epsilon)


def norm_back(rows, gain_row, upstream):
    inverse = inverse_rms(rows)
    gain_grad = jnp.sum(upstream * rows * inverse, axis=0)
    scaled = upstream * gain_row
    rows_grad = inverse * scaled - rows * inverse**3 * jnp.mean(scaled * rows, axis=-1, keepdims=True)
    return rows_grad, gain_grad


def rope_tables(positions):
    half = HEAD_SIZE // 2
    frequency = rope_base ** (-(jnp.arange(half, dtype=f32) * 2.0) / HEAD_SIZE)
    angles = positions.astype(f32)[:, None] * frequency[None, :]
    cosine, sine = jnp.cos(angles), jnp.sin(angles)
    return jnp.concatenate([cosine, cosine], 1), jnp.concatenate([sine, sine], 1)


def rotary_apply(rows, cosine, sine):
    half = HEAD_SIZE // 2
    turned = jnp.concatenate([-rows[..., half:], rows[..., :half]], -1)
    return rows * cosine[:, None, :] + turned * sine[:, None, :]


def unrotate(rows, cosine, sine):
    half = HEAD_SIZE // 2
    scaled = rows * sine[:, None, :]
    back = jnp.concatenate([scaled[..., half:], -scaled[..., :half]], -1)
    return rows * cosine[:, None, :] + back


def make_body(n_dp):
    expert_groups = n_dp // PLACES
    inside = [[g * PLACES + j for j in range(PLACES)] for g in range(expert_groups)]
    between = [[g * PLACES + j for g in range(expert_groups)] for j in range(PLACES)]
    half_experts = EXPERTS // 2

    def over_groups(value):
        home = lax.axis_index("dp") // PLACES

        def turned(k):
            return lax.ppermute(value, "dp", [(d, (d + k * PLACES) % n_dp) for d in range(n_dp)])

        parts = [turned(k) for k in range(expert_groups - 1, 0, -1)] + [value]
        ring = jnp.stack(parts + parts[:-1])
        start = (expert_groups - 1 - home) % expert_groups
        return lax.dynamic_slice_in_dim(ring, start, expert_groups, axis=0)

    def expert_pieces(gate_up_shard, down_shard, seq_rank):
        mine = [
            jnp.swapaxes(lax.dynamic_slice_in_dim(w, seq_rank * half_experts, half_experts, axis=1), 0, 1)
            for w in (gate_up_shard, down_shard)
        ]
        mine = jnp.concatenate(mine, 1)
        return mine.reshape((PLACES, OWN) + mine.shape[1:])

    def body(
        tokens, starts, routes, gain_one, query_key_value_weight, w_out,
        gain_two, w_router, w_gate_up, w_down, cotangent,
    ):
        count = tokens.shape[1]
        seq_rank = lax.axis_index("seq")
        expert = (seq_rank * PLACES + lax.axis_index("dp") % PLACES) * OWN
        query_columns = QUERY_HEADS * HEAD_SIZE
        key_columns = KEY_VALUE_HEADS * HEAD_SIZE
        group = QUERY_HEADS // KEY_VALUE_HEADS
        forward_pair, back_pair = [(0, 1)], [(1, 0)]

        mine = expert_pieces(w_gate_up, w_down, seq_rank)
        mine, query_key_value_weight, tokens, starts = lax.optimization_barrier(
            (mine, query_key_value_weight, tokens, starts)
        )
        mine = lax.all_to_all(
            mine, "dp", split_axis=0, concat_axis=0, tiled=True, axis_index_groups=inside
        )
        tokens_before = lax.ppermute(tokens[0], "seq", forward_pair)
        starts_before = lax.ppermute(starts, "seq", forward_pair)
        spare = lambda value: jnp.pad(value, ((0, 0), (0, 128 - value.shape[1])))
        little = jnp.concatenate([spare(w_router), spare(jnp.stack([gain_one, gain_two], 1))], 1)
        shards = (query_key_value_weight, w_out, little)
        halves = [w.shape[1] // 2 for w in shards]
        packed = over_groups(
            jnp.concatenate(
                [
                    lax.dynamic_slice_in_dim(w, seq_rank * h, h, axis=1)
                    for w, h in zip(shards, halves)
                ],
                1,
            )
        )
        mine, packed, tokens_before, starts_before = lax.optimization_barrier(
            (mine, packed, tokens_before, starts_before)
        )
        weights = lax.all_gather(mine, "dp", axis=0, tiled=True, axis_index_groups=between)
        qkv_weight, out_weight, small = weights_gather(0, halves, packed)
        router_weight = small[:, :EXPERTS]
        gain_a = small[:, 128].astype(f32)
        gain_b = small[:, 129].astype(f32)

        token_rows = tokens[0].astype(f32)
        grad_output = cotangent[0].astype(f32)
        both = 2 * count
        index = jnp.arange(both, dtype=jnp.int32)
        flags = jnp.concatenate([starts_before[0], starts[0]])
        begins = (flags > 0) | (index == jnp.where(seq_rank == 0, count, 0))
        last_begin = jnp.max(
            jnp.where(begins[None, :] & (index[None, :] <= index[:, None]), index[None, :], 0), axis=1
        )
        cosine_all, sine_all = rope_tables(index - last_begin)
        cosine, sine = cosine_all[count:], sine_all[count:]

        rows_all = jnp.concatenate([tokens_before.astype(f32), token_rows], 0)
        normed_all = (rows_all * inverse_rms(rows_all) * gain_a).astype(bf16)
        normed_one = normed_all[count:]
        projected_q = jnp.dot(normed_one, qkv_weight[:, :query_columns], preferred_element_type=f32)
        projected_kv = jnp.dot(normed_all, qkv_weight[:, query_columns:], preferred_element_type=f32)
        queries = rotary_apply(
            projected_q.reshape(count, QUERY_HEADS, HEAD_SIZE), cosine, sine
        ).astype(bf16).reshape(count, KEY_VALUE_HEADS, group, HEAD_SIZE)
        keys = rotary_apply(
            projected_kv[:, :key_columns].reshape(both, KEY_VALUE_HEADS, HEAD_SIZE), cosine_all, sine_all
        ).astype(bf16)
        values = projected_kv[:, key_columns:].astype(bf16).reshape(both, KEY_VALUE_HEADS, HEAD_SIZE)

        scale = HEAD_SIZE ** (-0.5)
        allowed = (index[None, :] <= index[count:, None]) & (index[None, :] >= last_begin[count:, None])
        scores = jnp.einsum("qgrd,kgd->grqk", queries, keys, preferred_element_type=f32) * scale
        scores = jnp.where(allowed[None, None], scores, masked_score)
        top = jnp.max(scores, axis=-1, keepdims=True)
        exps = jnp.exp(scores - top)
        probs = exps / jnp.sum(exps, axis=-1, keepdims=True)
        probs_low = probs.astype(bf16)
        attended = jnp.einsum(
            "grqk,kgd->qgrd", probs_low, values, preferred_element_type=f32
        ).reshape(count, query_columns).astype(bf16)
        hidden = token_rows + jnp.dot(attended, out_weight, preferred_element_type=f32)
        normed_two = (hidden * inverse_rms(hidden) * gain_b).astype(bf16)
        logits = jnp.dot(normed_two, router_weight, preferred_element_type=f32)
        expert_ids = jnp.arange(EXPERTS, dtype=jnp.int32)
        chosen = jnp.any(routes[0][:, :, None] == expert_ids[None, None, :], axis=1)
        gates = jax.nn.softmax(jnp.where(chosen, logits, -jnp.inf), axis=-1)

        rows_in, gates_all, grad_all = group_gather(1, normed_two, gates.T, cotangent[0])
        gate = lax.dynamic_slice_in_dim(gates_all, expert, OWN, axis=1)
        mixed_part, normed_part, gate_grad_part, expert_wgrads = expert_layer(
            w_gate_up.shape[0], rows_in, grad_all, gate, weights
        )
        expert_grads = lax.psum_scatter(
            expert_wgrads, "dp", scatter_dimension=0, tiled=True, axis_index_groups=between
        )
        normed_grad, gate_grad = group_reduce(2, normed_part, gate_grad_part)
        gate_grad = gate_grad[:, :OWN].reshape(EXPERTS, count).T

        over_rows = (((0,), (0,)), ((), ()))
        weighted = jnp.where(chosen, gates * gate_grad, 0.0)
        logits_grad = weighted - gates * jnp.sum(weighted, axis=-1, keepdims=True)
        router_wide = router_weight.astype(f32)
        normed_grad = normed_grad + jnp.dot(logits_grad, router_wide.T, precision=highest)
        router_wgrad = jnp.dot(normed_two.astype(f32).T, logits_grad, precision=highest)
        hidden_branch, gain_two_grad = norm_back(hidden, gain_b, normed_grad)
        hidden_grad = grad_output + hidden_branch
        branch_low = hidden_grad.astype(bf16)
        out_wgrad = lax.dot_general(attended, branch_low, over_rows, preferred_element_type=f32)
        attended_grad = lax.dot_general(
            branch_low, out_weight, (((1,), (1,)), ((), ())), preferred_element_type=f32
        ).astype(bf16).reshape(count, KEY_VALUE_HEADS, group, HEAD_SIZE)

        prob_grad = jnp.einsum("qgrd,kgd->grqk", attended_grad, values, preferred_element_type=f32)
        delta = jnp.sum(probs * prob_grad, axis=-1, keepdims=True)
        score_grad = (probs * (prob_grad - delta)).astype(bf16)
        query_grad = (
            jnp.einsum("grqk,kgd->qgrd", score_grad, keys, preferred_element_type=f32) * scale
        ).reshape(count, QUERY_HEADS, HEAD_SIZE)
        key_grad = (
            jnp.einsum("grqk,qgrd->kgd", score_grad, queries, preferred_element_type=f32) * scale
        ).reshape(both, key_columns)
        value_grad = jnp.einsum(
            "grqk,qgrd->kgd", probs_low, attended_grad, preferred_element_type=f32
        ).reshape(both, key_columns)
        kv_grad = jnp.concatenate([key_grad, value_grad], 1)
        kv_back = lax.ppermute(kv_grad[:count].astype(bf16), "seq", back_pair)
        kv_grad = (kv_grad[count:] + kv_back.astype(f32)).astype(bf16).astype(f32)
        query_grad = query_grad.astype(bf16).astype(f32)
        query_back = unrotate(query_grad, cosine, sine).reshape(count, query_columns)
        key_back = unrotate(
            kv_grad[:, :key_columns].reshape(count, KEY_VALUE_HEADS, HEAD_SIZE), cosine, sine
        ).reshape(count, key_columns)
        projected_grad = jnp.concatenate([query_back, key_back, kv_grad[:, key_columns:]], 1).astype(bf16)
        qkv_wgrad = lax.dot_general(normed_one, projected_grad, over_rows, preferred_element_type=f32)
        normed_one_grad = lax.dot_general(
            projected_grad, qkv_weight, (((1,), (1,)), ((), ())), preferred_element_type=f32
        )
        rows_branch, gain_one_grad = norm_back(token_rows, gain_a, normed_one_grad)
        input_grad = (hidden_grad + rows_branch).astype(bf16)[None]

        little = jnp.concatenate(
            [spare(router_wgrad), spare(jnp.stack([gain_one_grad, gain_two_grad], 1))], 1
        )
        packed, mixed = weights_reduce(
            3, expert_groups, (qkv_wgrad.astype(bf16), out_wgrad.astype(bf16), little), mixed_part
        )
        mixed = mixed.reshape(count, MODEL_WIDTH).astype(f32)
        output = (hidden + mixed).astype(bf16)[None]
        stat_sums = jnp.stack([jnp.sum(hidden * hidden), jnp.sum(mixed * mixed)])
        stat_sums = stat_sums + lax.ppermute(stat_sums, "seq", [(0, 1), (1, 0)])
        experts_all, ends = send_pieces(4, expert_grads, packed)
        qkv_shard, out_shard, little = [
            jnp.concatenate([ends[0, :, f : f + h], ends[1, :, f : f + h]], 1).astype(f32)
            for f, h in zip(starts_of(halves), halves)
        ]
        experts_all = experts_all.reshape((EXPERTS,) + experts_all.shape[2:])
        first = w_gate_up.shape[0]
        stream_rms = jnp.sqrt(stat_sums / (both * MODEL_WIDTH)).reshape(1, 2)
        return (
            output,
            input_grad,
            little[:, 128],
            qkv_shard,
            out_shard,
            little[:, 129],
            little[:, :EXPERTS],
            jnp.swapaxes(experts_all[:, :first], 0, 1).astype(f32),
            jnp.swapaxes(experts_all[:, first:], 0, 1).astype(f32),
            stream_rms,
        )

    return body


def solution(mesh):
    placed = (
        P("dp", "seq", None),
        P("dp", "seq"),
        P("dp", "seq", None),
        P("dp"),
        P("dp", None),
        P("dp", None),
        P("dp"),
        P("dp", None),
        P("dp", None, None),
        P("dp", None, None),
        P("dp", "seq", None),
    )
    return jax.shard_map(
        make_body(mesh.shape["dp"]),
        mesh=mesh,
        in_specs=placed,
        out_specs=(
            P("dp", "seq", None),
            P("dp", "seq", None),
            P("dp"),
            P("dp", None),
            P("dp", None),
            P("dp"),
            P("dp", None),
            P("dp", None, None),
            P("dp", None, None),
            P("dp", None),
        ),
        check_vma=False,
    )
```

```python
import functools

import jax
import jax.numpy as jnp
from jax import lax
from jax.experimental import pallas as pl
from jax.experimental.pallas import tpu as pltpu
from jax.sharding import PartitionSpec as P

MODEL_WIDTH = 1024
QUERY_HEADS = 16
KEY_VALUE_HEADS = 8
HEAD_SIZE = 64
F = 512
EXPERTS = 16
TOPK = 8
PLACES = 4
GROUP = 8
OWN = EXPERTS // GROUP

epsilon = 1e-06
rope_base = 10000.0
highest = lax.Precision.HIGHEST
masked_score = -1e30
f32 = jnp.float32
bf16 = jnp.bfloat16
MESH = pl.DeviceIdType.MESH

TOKEN_LINKS = ((4, 2), (2, 4))


def flip(value, bit):
    return value + bit * (1 - 2 * ((value // bit) % 2))


def flip_mask(value, mask):
    for bit in (1, 2, 4, 8):
        if mask & bit:
            value = flip(value, bit)
    return value


def subsets(bits):
    out = [0]
    for bit in bits:
        out = out + [m | bit for m in out]
    return out


def row_parts(rows):
    first = (rows // 2 + 15) // 16 * 16
    return ((0, first), (first, rows - first))


def my_place(places=PLACES):
    seq = lax.axis_index("seq")
    dp = lax.axis_index("dp")
    rank = seq * places + dp % places

    def peer(mask):
        return {
            "seq": 1 - seq if mask & places else seq,
            "dp": flip_mask(dp, mask & (places - 1)),
        }

    return rank, peer


def meet(devices):
    barrier = pltpu.get_barrier_semaphore()
    for there in devices:
        pl.semaphore_signal(barrier, inc=1, device_id=there, device_id_type=MESH)
    pl.semaphore_wait(barrier, len(devices))


def gather_kernel(count, *refs):
    ins, outs = refs[:count], refs[count : 2 * count]
    send, recv, send_core, recv_core, local = refs[2 * count :]
    rank, peer = my_place(PLACES)
    own = [
        pltpu.make_async_copy(ins[a], outs[a].at[rank], local.at[a]) for a in range(count)
    ]
    for copy in own:
        copy.start()
    meet([peer(bit) for bit in (1, 2, 4)])
    parts = [row_parts(ref.shape[0]) for ref in ins]

    def remote(a, p, mask, bit, sems, index):
        start, size = parts[a][p]
        rows = pl.ds(start, size)
        shard = flip_mask(rank, mask)
        src = ins[a].at[rows] if mask == 0 else outs[a].at[shard, rows]
        return pltpu.make_async_remote_copy(
            src_ref=src,
            dst_ref=outs[a].at[shard, rows],
            send_sem=sems[0].at[a, p, index],
            recv_sem=sems[1].at[a, p, index],
            device_id=peer(bit),
            device_id_type=MESH,
        )

    started = []
    live = {}
    for step in range(3):
        for p in range(2):
            for a in range(count):
                if parts[a][p][1] == 0:
                    continue
                order = TOKEN_LINKS[p]
                if step > 0:
                    for copy in live.pop((a, p)):
                        copy.wait_recv()
                if step < 2:
                    now = []
                    for index, mask in enumerate(subsets(order[:step])):
                        copy = remote(a, p, mask, order[step], (send, recv), 2**step - 1 + index)
                        copy.start()
                        now.append(copy)
                        started.append(copy)
                    live[(a, p)] = now
                fresh = [0] if step == 0 else [m | order[step - 1] for m in subsets(order[: step - 1])]
                base = 0 if step == 0 else 2 ** (step - 1)
                for index, mask in enumerate(fresh):
                    copy = remote(a, p, mask, 1, (send_core, recv_core), base + index)
                    copy.start()
                    live.setdefault("core", []).append(copy)
    for copy in live["core"]:
        copy.wait()
    for copy in started:
        copy.wait_send()
    for copy in own:
        copy.wait()


def group_gather(collective_id, *arrays):
    count = len(arrays)
    return pl.pallas_call(
        functools.partial(gather_kernel, count),
        out_shape=[jax.ShapeDtypeStruct((GROUP,) + a.shape, a.dtype) for a in arrays],
        in_specs=[pl.BlockSpec(memory_space=pltpu.VMEM)] * count,
        out_specs=[pl.BlockSpec(memory_space=pl.ANY)] * count,
        scratch_shapes=[
            pltpu.SemaphoreType.DMA((count, 2, 3)),
            pltpu.SemaphoreType.DMA((count, 2, 3)),
            pltpu.SemaphoreType.DMA((count, 2, 4)),
            pltpu.SemaphoreType.DMA((count, 2, 4)),
            pltpu.SemaphoreType.DMA((count,)),
        ],
        compiler_params=pltpu.CompilerParams(collective_id=collective_id, has_side_effects=True),
        cost_estimate=pl.CostEstimate(flops=1000000000, bytes_accessed=2**24, transcendentals=0),
        name="group_gather",
    )(*arrays)


def add_rows(target, source, start, size):
    chunk = 32 if size % 32 == 0 else 16

    def step(i, carry):
        rows = pl.ds(pl.multiple_of(start + i * chunk, chunk), chunk)
        target[rows] = (target[rows].astype(f32) + source[rows].astype(f32)).astype(target.dtype)
        return carry

    lax.fori_loop(0, size // chunk, step, 0)


def reduce_kernel(
    normed_ref, gate_ref, normed_out, gate_out,
    total, got0, got1, got2, sems, gate_sems, local, own_gate,
):
    rank, peer = my_place(PLACES)
    chip = rank // 2
    core = rank % 2
    parts = row_parts(normed_ref.shape[1])
    ins = (normed_ref,)
    outs = (normed_out,)
    loads = []
    for t in range(1):
        for c in range(4):
            copy = pltpu.make_async_copy(ins[t].at[2 * c + core], total.at[t, c], local.at[t, c])
            copy.start()
            loads.append(copy)
    everyone = [peer(mask) for mask in range(1, GROUP)]
    meet(everyone)
    gates = []
    keep = pltpu.make_async_copy(gate_ref.at[rank], gate_out.at[rank], own_gate)
    keep.start()
    for mask, there in zip(range(1, GROUP), everyone):
        copy = pltpu.make_async_remote_copy(
            src_ref=gate_ref.at[flip_mask(rank, mask)],
            dst_ref=gate_out.at[rank],
            send_sem=gate_sems.at[0, mask],
            recv_sem=gate_sems.at[1, mask],
            device_id=there,
            device_id_type=MESH,
        )
        copy.start()
        gates.append(copy)

    started = []
    live = {}

    def send(t, p, stage, index, src, dst, bit):
        copy = pltpu.make_async_remote_copy(
            src_ref=src,
            dst_ref=dst,
            send_sem=sems.at[0, t, p, stage, index],
            recv_sem=sems.at[1, t, p, stage, index],
            device_id=peer(bit),
            device_id_type=MESH,
        )
        copy.start()
        started.append(copy)
        live.setdefault((t, p), []).append(copy)

    def chip_of(mask):
        return flip_mask(rank, mask) // 2

    for p in range(2):
        for t in range(1):
            rows = pl.ds(*parts[p])
            for c in range(4):
                send(
                    t, p, 0, c, ins[t].at[2 * c + 1 - core, rows], got0.at[t, c, rows], 1
                )
    for copy in loads:
        copy.wait()
    got = (got1, got2)
    for stage in range(3):
        for p in range(2):
            for t in range(1):
                order = TOKEN_LINKS[p]
                rows = pl.ds(*parts[p])
                for copy in live.pop((t, p)):
                    copy.wait_recv()
                if stage == 0:

                    def over_chips(c, carry, t=t, p=p):
                        add_rows(total.at[t, c], got0.at[t, c], *parts[p])
                        return carry

                    lax.fori_loop(0, 4, over_chips, 0)
                else:
                    for index, mask in enumerate(subsets(order[stage:])):
                        if stage == 2:
                            outs[t][rows] = total[t, chip, rows].astype(f32) + got2[t, 0, rows].astype(f32)
                        else:
                            add_rows(
                                total.at[t, chip_of(mask)], got[stage - 1].at[t, index], *parts[p]
                            )
                if stage < 2:
                    for index, mask in enumerate(subsets(order[stage + 1 :])):
                        send(
                            t, p, stage + 1, index,
                            total.at[t, chip_of(mask | order[stage]), rows],
                            got[stage].at[t, index, rows],
                            order[stage],
                        )
    for copy in started:
        copy.wait_send()
    for copy in gates:
        copy.wait()
    keep.wait()


def group_reduce(collective_id, normed, gate_grad):
    rows, width = normed.shape[1:]
    return pl.pallas_call(
        reduce_kernel,
        out_shape=[
            jax.ShapeDtypeStruct((rows, width), f32),
            jax.ShapeDtypeStruct(gate_grad.shape, gate_grad.dtype),
        ],
        in_specs=[pl.BlockSpec(memory_space=pl.ANY)] * 2,
        out_specs=[
            pl.BlockSpec(memory_space=pltpu.VMEM),
            pl.BlockSpec(memory_space=pl.ANY),
        ],
        scratch_shapes=[
            pltpu.VMEM((1, 4, rows, width), bf16),
            pltpu.VMEM((1, 4, rows, width), bf16),
            pltpu.VMEM((1, 2, rows, width), bf16),
            pltpu.VMEM((1, 1, rows, width), bf16),
            pltpu.SemaphoreType.DMA((2, 1, 2, 3, 4)),
            pltpu.SemaphoreType.DMA((2, GROUP)),
            pltpu.SemaphoreType.DMA((1, 4)),
            pltpu.SemaphoreType.DMA(()),
        ],
        compiler_params=pltpu.CompilerParams(
            collective_id=collective_id, has_side_effects=True, vmem_limit_bytes=48 * 2**20
        ),
        cost_estimate=pl.CostEstimate(flops=1000000, bytes_accessed=2**24, transcendentals=0),
        name="group_reduce",
    )(normed, gate_grad)


def column_parts(half):
    first = -(-(half // 128) // 2) * 128
    return ((0, first), (first, half - first))


def shard_view(ref, halves, a, p, rank_value):
    start, size = column_parts(halves[a])[p]
    offset = pl.multiple_of((rank_value // PLACES) * halves[a] + start, 128)
    return ref.at[:, rank_value % PLACES, :, pl.ds(offset, size)]


def starts_of(sizes):
    return [sum(sizes[:i]) for i in range(len(sizes))]


def weights_gather_kernel(halves, packed, *refs):
    count = len(halves)
    outs = refs[:count]
    send, recv, local = refs[count:]
    rank, peer = my_place()
    firsts = starts_of(halves)
    seq = lax.axis_index("seq")
    own = []
    for a in range(count):
        columns = pl.ds(pl.multiple_of(seq * halves[a], 128), halves[a])
        copy = pltpu.make_async_copy(
            packed.at[:, :, pl.ds(firsts[a], halves[a])],
            outs[a].at[:, rank % PLACES, :, columns],
            local.at[a],
        )
        copy.start()
        own.append(copy)
    meet([peer(bit) for bit in (1, 2, 4)])
    started = []

    def remote(a, p, mask, bit, index):
        view = shard_view(outs[a], halves, a, p, flip_mask(rank, mask))
        start, size = column_parts(halves[a])[p]
        source = packed.at[:, :, pl.ds(firsts[a] + start, size)] if mask == 0 else view
        copy = pltpu.make_async_remote_copy(
            src_ref=source,
            dst_ref=view,
            send_sem=send.at[a, p, index],
            recv_sem=recv.at[a, p, index],
            device_id=peer(bit),
            device_id_type=MESH,
        )
        copy.start()
        started.append(copy)
        return copy

    live = {}
    last = []
    for step in range(3):
        for p in range(2):
            for a in range(count):
                if column_parts(halves[a])[p][1] == 0:
                    continue
                order = TOKEN_LINKS[p]
                if step > 0:
                    for copy in live.pop((a, p)):
                        copy.wait_recv()
                if step < 2:
                    live[(a, p)] = [
                        remote(a, p, mask, order[step], 2**step - 1 + index)
                        for index, mask in enumerate(subsets(order[:step]))
                    ]
                fresh = [0] if step == 0 else [m | order[step - 1] for m in subsets(order[: step - 1])]
                base = 0 if step == 0 else 2 ** (step - 1)
                for index, mask in enumerate(fresh):
                    last.append(remote(a, p, mask, 1, 3 + base + index))
    for copy in last:
        copy.wait_recv()
    for copy in started:
        copy.wait_send()
    for copy in own:
        copy.wait()


def weights_gather(collective_id, halves, packed):
    groups, rows, _ = packed.shape
    count = len(halves)
    whole = pl.pallas_call(
        functools.partial(weights_gather_kernel, halves),
        out_shape=[jax.ShapeDtypeStruct((groups, PLACES, rows, 2 * h), packed.dtype) for h in halves],
        in_specs=[pl.BlockSpec(memory_space=pltpu.VMEM)],
        out_specs=[pl.BlockSpec(memory_space=pl.ANY)] * count,
        scratch_shapes=[
            pltpu.SemaphoreType.DMA((count, 2, 7)),
            pltpu.SemaphoreType.DMA((count, 2, 7)),
            pltpu.SemaphoreType.DMA((count,)),
        ],
        compiler_params=pltpu.CompilerParams(collective_id=collective_id, has_side_effects=True),
        cost_estimate=pl.CostEstimate(flops=1000000, bytes_accessed=2**24, transcendentals=0),
        name="weights_gather",
    )(packed)
    return [w.reshape(-1, w.shape[3]) for w in whole]


def add_block(target, source, at, start, size):
    groups, rows = source.shape[0], source.shape[1]
    columns = pl.ds(start, size)
    chunk = 64 if rows % 64 == 0 else 16
    pieces = rows // chunk

    def step(i, carry):
        lines = pl.ds(pl.multiple_of((i % pieces) * chunk, chunk), chunk)
        index = (i // pieces, lines, columns)
        new = target[(at,) + index].astype(f32) + source[index].astype(f32)
        target[(at,) + index] = new.astype(target.dtype)
        return carry

    lax.fori_loop(0, groups * pieces, step, 0)


def weights_reduce_kernel(count, *refs):
    ins, packed, rows_out = refs[:count], refs[count], refs[count + 1]
    rest = refs[count + 2 :]
    total, got0, got1, got2 = [rest[i * count : (i + 1) * count] for i in range(4)]
    sems, local = rest[4 * count :]
    rank, peer = my_place()
    chip, core = rank // 2, rank % 2
    halves = [ref.shape[3] // 2 for ref in ins[:-1]]
    firsts = starts_of(halves)
    halves = halves + [ins[-1].shape[3]]
    parts = [column_parts(half) for half in halves]

    def source(a, value, start, size):
        if a == count - 1:
            return ins[a].at[value, :, :, pl.ds(start, size)]
        offset = pl.multiple_of((value // PLACES) * halves[a] + start, 128)
        return ins[a].at[:, value % PLACES, :, pl.ds(offset, size)]

    loads = []
    for a in range(count):
        for c in range(4):
            copy = pltpu.make_async_copy(
                source(a, 2 * c + core, 0, halves[a]), total[a].at[c], local.at[a, c]
            )
            copy.start()
            loads.append(copy)
    meet([peer(bit) for bit in (1, 2, 4)])
    started = []
    live = {}

    def send(a, p, stage, index, src, dst, bit):
        copy = pltpu.make_async_remote_copy(
            src_ref=src,
            dst_ref=dst,
            send_sem=sems.at[0, a, p, stage, index],
            recv_sem=sems.at[1, a, p, stage, index],
            device_id=peer(bit),
            device_id_type=MESH,
        )
        copy.start()
        started.append(copy)
        live.setdefault((a, p), []).append(copy)

    def chip_of(mask):
        return flip_mask(rank, mask) // 2

    for p in range(2):
        for a in range(count):
            columns = pl.ds(*parts[a][p])
            if parts[a][p][1]:
                for c in range(4):
                    send(
                        a, p, 0, c,
                        source(a, 2 * c + 1 - core, *parts[a][p]),
                        got0[a].at[c, :, :, columns],
                        1,
                    )
    for copy in loads:
        copy.wait()
    got = (got1, got2)
    for stage in range(3):
        for p in range(2):
            for a in range(count):
                start, size = parts[a][p]
                if size == 0:
                    continue
                order = TOKEN_LINKS[p]
                columns = pl.ds(start, size)
                for copy in live.pop((a, p)):
                    copy.wait_recv()
                if stage == 0:

                    def over_chips(c, carry, a=a, start=start, size=size):
                        add_block(total[a], got0[a].at[c], c, start, size)
                        return carry

                    lax.fori_loop(0, 4, over_chips, 0)
                else:
                    for index, mask in enumerate(subsets(order[stage:])):
                        add_block(total[a], got[stage - 1][a].at[index], chip_of(mask), start, size)
                if stage < 2:
                    for index, mask in enumerate(subsets(order[stage + 1 :])):
                        send(
                            a, p, stage + 1, index,
                            total[a].at[chip_of(mask | order[stage]), :, :, columns],
                            got[stage][a].at[index, :, :, columns],
                            order[stage],
                        )
    for a in range(count - 1):
        packed[:, :, pl.ds(firsts[a], halves[a])] = total[a][chip].astype(packed.dtype)
    rows_out[...] = total[-1][chip]
    for copy in started:
        copy.wait_send()


def weights_reduce(collective_id, groups, arrays, token_rows):
    count = len(arrays) + 1
    views = [a.reshape(groups, PLACES, -1, a.shape[1]) for a in arrays]
    rows = views[0].shape[2]
    halves = [a.shape[1] // 2 for a in arrays]

    each, width = token_rows.shape[1:]
    token_shape = (groups, each // groups, width)

    def buffers(lead):
        return [pltpu.VMEM((lead, groups, rows, h), a.dtype) for h, a in zip(halves, arrays)] + [
            pltpu.VMEM((lead,) + token_shape, bf16)
        ]

    dma = pltpu.SemaphoreType.DMA
    return pl.pallas_call(
        functools.partial(weights_reduce_kernel, count),
        out_shape=[
            jax.ShapeDtypeStruct((groups, rows, sum(halves)), bf16),
            jax.ShapeDtypeStruct(token_shape, bf16),
        ],
        in_specs=[pl.BlockSpec(memory_space=pl.ANY)] * count,
        out_specs=[pl.BlockSpec(memory_space=pltpu.VMEM)] * 2,
        scratch_shapes=buffers(4) + buffers(4) + buffers(2) + buffers(1)
        + [dma((2, count, 2, 3, 4)), dma((count, 4))],
        compiler_params=pltpu.CompilerParams(
            collective_id=collective_id, has_side_effects=True, vmem_limit_bytes=48 * 2**20
        ),
        cost_estimate=pl.CostEstimate(flops=1000000, bytes_accessed=2**24, transcendentals=0),
        name="weights_reduce",
    )(*views, token_rows.reshape((GROUP,) + token_shape))


def pieces_kernel(pieces, packed, whole, ends, far_got, send, recv, far_send, far_recv, last, local):
    rank, peer = my_place()
    place = rank % PLACES
    groups = packed.shape[0]
    seq = lax.axis_index("seq")
    home = lax.axis_index("dp") // PLACES
    keep = pltpu.make_async_copy(pieces.at[place], whole.at[rank], local)
    keep.start()
    masks = (6, 7, 2, 4, 3, 5, 1)
    others = [(home + k) % groups for k in range(1, groups)]
    far = [{"seq": seq, "dp": g * PLACES + place} for g in others]
    meet([peer(mask) for mask in masks] + far)
    sums = []
    for k, there in enumerate(far):
        copy = pltpu.make_async_remote_copy(
            src_ref=packed.at[others[k]],
            dst_ref=far_got.at[k],
            send_sem=far_send.at[k],
            recv_sem=far_recv.at[k],
            device_id=there,
            device_id_type=MESH,
        )
        copy.start()
        sums.append(copy)
    copies = []
    for mask in masks:
        copy = pltpu.make_async_remote_copy(
            src_ref=pieces.at[flip_mask(place, mask & (PLACES - 1))],
            dst_ref=whole.at[rank],
            send_sem=send.at[mask],
            recv_sem=recv.at[mask],
            device_id=peer(mask),
            device_id_type=MESH,
        )
        copy.start()
        copies.append(copy)
    for copy in sums:
        copy.wait()
    value = packed[home].astype(f32)
    for k in range(groups - 1):
        value = value + far_got[k].astype(f32)
    ends[seq] = value.astype(ends.dtype)
    copy = pltpu.make_async_remote_copy(
        src_ref=ends.at[seq],
        dst_ref=ends.at[seq],
        send_sem=last.at[0],
        recv_sem=last.at[1],
        device_id=peer(4),
        device_id_type=MESH,
    )
    copy.start()
    copies.append(copy)
    for copy in copies:
        copy.wait()
    keep.wait()


def send_pieces(collective_id, pieces, packed):
    groups = packed.shape[0]
    others = max(groups - 1, 1)
    dma = pltpu.SemaphoreType.DMA
    vmem = pl.BlockSpec(memory_space=pltpu.VMEM)
    return pl.pallas_call(
        pieces_kernel,
        out_shape=[
            jax.ShapeDtypeStruct((GROUP,) + pieces.shape[1:], pieces.dtype),
            jax.ShapeDtypeStruct((2,) + packed.shape[1:], packed.dtype),
        ],
        in_specs=[vmem, vmem],
        out_specs=[pl.BlockSpec(memory_space=pl.ANY), vmem],
        scratch_shapes=[
            pltpu.VMEM((others,) + packed.shape[1:], packed.dtype),
            dma((GROUP,)),
            dma((GROUP,)),
            dma((others,)),
            dma((others,)),
            dma((2,)),
            dma(()),
        ],
        compiler_params=pltpu.CompilerParams(collective_id=collective_id, has_side_effects=True),
        name="send_pieces",
    )(pieces, packed)


def expert_kernel(
    first, rows_ref, grad_ref, gate_ref, weights_ref,
    mixed_ref, normed_ref, gate_grad_ref, weights_out,
    gate_up_sum, down_sum, mixed_sum, normed_sum,
):
    step = pl.program_id(0)
    expert = pl.program_id(1)
    shards, each, width = rows_ref.shape
    count = shards * each
    rows = rows_ref[...].reshape(count, width)
    grad = grad_ref[...].reshape(count, width).astype(f32)
    gate = jnp.concatenate(
        [
            jnp.broadcast_to(gate_ref[i, pl.ds(expert, 1)], (128, each)).T[:, :1]
            for i in range(shards)
        ],
        0,
    )
    gate_up_weight = weights_ref[:, expert, :first].reshape(-1, width)
    down = weights_ref[:, expert, first:].reshape(-1, width)
    gate_up = jnp.dot(rows, gate_up_weight, preferred_element_type=f32)
    gate_part, up_part = gate_up[:, :F], gate_up[:, F:]
    sigmoid = 1.0 / (1.0 + jnp.exp(-gate_part))
    silu = gate_part * sigmoid
    act = (silu * up_part).astype(bf16)
    out = jnp.dot(act, down, preferred_element_type=f32)
    inner = jnp.sum(out * grad, axis=-1, keepdims=True)
    for i in range(shards):
        line = jnp.broadcast_to(inner[i * each : (i + 1) * each], (each, 128)).T
        gate_grad_ref[i, pl.ds(expert, 1)] = line[:1]
    mixed = gate * out
    expert_grad = (gate * grad).astype(bf16)
    across = (((1,), (1,)), ((), ()))
    over_rows = (((0,), (0,)), ((), ()))
    act_grad = lax.dot_general(expert_grad, down, across, preferred_element_type=f32)
    gate_up_grad = jnp.concatenate(
        [act_grad * up_part * (sigmoid * (1.0 + gate_part * (1.0 - sigmoid))), act_grad * silu], -1
    ).astype(bf16)
    normed = lax.dot_general(gate_up_grad, gate_up_weight, across, preferred_element_type=f32)

    @pl.when(expert == 0)
    def _():
        mixed_sum[...] = mixed
        normed_sum[...] = normed

    @pl.when(expert > 0)
    def _():
        mixed_sum[...] += mixed
        normed_sum[...] += normed

    @pl.when(expert == OWN - 1)
    def _():
        mixed_ref[...] = mixed_sum[...].astype(bf16).reshape(shards, each, width)
        normed_ref[...] = normed_sum[...].astype(bf16).reshape(shards, each, width)

    @pl.when(step == 0)
    def _():
        gate_up_sum[expert] = jnp.zeros_like(gate_up_sum[0])
        down_sum[expert] = jnp.zeros_like(down_sum[0])

    down_sum[expert] += lax.dot_general(act, expert_grad, over_rows, preferred_element_type=f32)
    gate_up_sum[expert] += lax.dot_general(rows, gate_up_grad, over_rows, preferred_element_type=f32)

    @pl.when(step == pl.num_programs(0) - 1)
    def _():
        owners = weights_out.shape[0]
        weights_out[:, expert, :first] = gate_up_sum[expert].astype(bf16).reshape(owners, first, width)
        weights_out[:, expert, first:] = down_sum[expert].astype(bf16).reshape(owners, -1, width)


def expert_layer(first, rows, grad, gate, weights):
    each, width = rows.shape[1:]
    shards = 2
    owners = weights.shape[0]
    tile = pl.BlockSpec((shards, each, width), lambda i, e: (i, 0, 0))
    whole = pl.BlockSpec(weights.shape, lambda i, e: (0, 0, 0, 0), pipeline_mode=pl.Buffered(1))
    return pl.pallas_call(
        functools.partial(expert_kernel, first),
        grid=(GROUP // shards, OWN),
        out_shape=[
            jax.ShapeDtypeStruct(rows.shape, bf16),
            jax.ShapeDtypeStruct(rows.shape, bf16),
            jax.ShapeDtypeStruct((GROUP, 8, each), f32),
            jax.ShapeDtypeStruct(weights.shape, bf16),
        ],
        in_specs=[
            tile,
            tile,
            pl.BlockSpec((shards, OWN, each), lambda i, e: (i, 0, 0)),
            whole,
        ],
        out_specs=[
            tile,
            tile,
            pl.BlockSpec((shards, 8, each), lambda i, e: (i, 0, 0)),
            whole,
        ],
        scratch_shapes=[
            pltpu.VMEM((OWN, owners * first, width), f32),
            pltpu.VMEM((OWN, owners * (weights.shape[2] - first), width), f32),
            pltpu.VMEM((shards * each, width), f32),
            pltpu.VMEM((shards * each, width), f32),
        ],
        compiler_params=pltpu.CompilerParams(vmem_limit_bytes=62 * 2**20),
        cost_estimate=pl.CostEstimate(flops=45000000000, bytes_accessed=2**24, transcendentals=0),
        name="expert_layer",
    )(rows, grad, gate, weights)


def inverse_rms(rows):
    return lax.rsqrt(jnp.mean(rows * rows, axis=-1, keepdims=True) + epsilon)


def norm_back(rows, gain_row, upstream):
    inverse = inverse_rms(rows)
    gain_grad = jnp.sum(upstream * rows * inverse, axis=0)
    scaled = upstream * gain_row
    rows_grad = inverse * scaled - rows * inverse**3 * jnp.mean(scaled * rows, axis=-1, keepdims=True)
    return rows_grad, gain_grad


def rope_tables(positions):
    half = HEAD_SIZE // 2
    frequency = rope_base ** (-(jnp.arange(half, dtype=f32) * 2.0) / HEAD_SIZE)
    angles = positions.astype(f32)[:, None] * frequency[None, :]
    cosine, sine = jnp.cos(angles), jnp.sin(angles)
    return jnp.concatenate([cosine, cosine], 1), jnp.concatenate([sine, sine], 1)


def rotary_apply(rows, cosine, sine):
    half = HEAD_SIZE // 2
    turned = jnp.concatenate([-rows[..., half:], rows[..., :half]], -1)
    return rows * cosine[:, None, :] + turned * sine[:, None, :]


def unrotate(rows, cosine, sine):
    half = HEAD_SIZE // 2
    scaled = rows * sine[:, None, :]
    back = jnp.concatenate([scaled[..., half:], -scaled[..., :half]], -1)
    return rows * cosine[:, None, :] + back


def make_body(n_dp):
    expert_groups = n_dp // PLACES
    inside = [[g * PLACES + j for j in range(PLACES)] for g in range(expert_groups)]
    between = [[g * PLACES + j for g in range(expert_groups)] for j in range(PLACES)]
    half_experts = EXPERTS // 2

    def over_groups(value):
        home = lax.axis_index("dp") // PLACES

        def turned(k):
            return lax.ppermute(value, "dp", [(d, (d + k * PLACES) % n_dp) for d in range(n_dp)])

        parts = [turned(k) for k in range(expert_groups - 1, 0, -1)] + [value]
        ring = jnp.stack(parts + parts[:-1])
        start = (expert_groups - 1 - home) % expert_groups
        return lax.dynamic_slice_in_dim(ring, start, expert_groups, axis=0)

    def expert_pieces(gate_up_shard, down_shard, seq_rank):
        mine = [
            jnp.swapaxes(lax.dynamic_slice_in_dim(w, seq_rank * half_experts, half_experts, axis=1), 0, 1)
            for w in (gate_up_shard, down_shard)
        ]
        mine = jnp.concatenate(mine, 1)
        return mine.reshape((PLACES, OWN) + mine.shape[1:])

    def body(
        tokens, starts, routes, gain_one, query_key_value_weight, w_out,
        gain_two, w_router, w_gate_up, w_down, cotangent,
    ):
        count = tokens.shape[1]
        seq_rank = lax.axis_index("seq")
        expert = (seq_rank * PLACES + lax.axis_index("dp") % PLACES) * OWN
        query_columns = QUERY_HEADS * HEAD_SIZE
        key_columns = KEY_VALUE_HEADS * HEAD_SIZE
        group = QUERY_HEADS // KEY_VALUE_HEADS
        forward_pair, back_pair = [(0, 1)], [(1, 0)]

        mine = expert_pieces(w_gate_up, w_down, seq_rank)
        mine, query_key_value_weight, tokens, starts = lax.optimization_barrier(
            (mine, query_key_value_weight, tokens, starts)
        )
        mine = lax.all_to_all(
            mine, "dp", split_axis=0, concat_axis=0, tiled=True, axis_index_groups=inside
        )
        tokens_before = lax.ppermute(tokens[0], "seq", forward_pair)
        starts_before = lax.ppermute(starts, "seq", forward_pair)
        spare = lambda value: jnp.pad(value, ((0, 0), (0, 128 - value.shape[1])))
        little = jnp.concatenate([spare(w_router), spare(jnp.stack([gain_one, gain_two], 1))], 1)
        shards = (query_key_value_weight, w_out, little)
        halves = [w.shape[1] // 2 for w in shards]
        packed = over_groups(
            jnp.concatenate(
                [
                    lax.dynamic_slice_in_dim(w, seq_rank * h, h, axis=1)
                    for w, h in zip(shards, halves)
                ],
                1,
            )
        )
        mine, packed, tokens_before, starts_before = lax.optimization_barrier(
            (mine, packed, tokens_before, starts_before)
        )
        weights = lax.all_gather(mine, "dp", axis=0, tiled=True, axis_index_groups=between)
        qkv_weight, out_weight, small = weights_gather(0, halves, packed)
        router_weight = small[:, :EXPERTS]
        gain_a = small[:, 128].astype(f32)
        gain_b = small[:, 129].astype(f32)

        token_rows = tokens[0].astype(f32)
        grad_output = cotangent[0].astype(f32)
        both = 2 * count
        index = jnp.arange(both, dtype=jnp.int32)
        flags = jnp.concatenate([starts_before[0], starts[0]])
        begins = (flags > 0) | (index == jnp.where(seq_rank == 0, count, 0))
        last_begin = jnp.max(
            jnp.where(begins[None, :] & (index[None, :] <= index[:, None]), index[None, :], 0), axis=1
        )
        cosine_all, sine_all = rope_tables(index - last_begin)
        cosine, sine = cosine_all[count:], sine_all[count:]

        rows_all = jnp.concatenate([tokens_before.astype(f32), token_rows], 0)
        normed_all = (rows_all * inverse_rms(rows_all) * gain_a).astype(bf16)
        normed_one = normed_all[count:]
        projected_q = jnp.dot(normed_one, qkv_weight[:, :query_columns], preferred_element_type=f32)
        projected_kv = jnp.dot(normed_all, qkv_weight[:, query_columns:], preferred_element_type=f32)
        queries = rotary_apply(
            projected_q.reshape(count, QUERY_HEADS, HEAD_SIZE), cosine, sine
        ).astype(bf16).reshape(count, KEY_VALUE_HEADS, group, HEAD_SIZE)
        keys = rotary_apply(
            projected_kv[:, :key_columns].reshape(both, KEY_VALUE_HEADS, HEAD_SIZE), cosine_all, sine_all
        ).astype(bf16)
        values = projected_kv[:, key_columns:].astype(bf16).reshape(both, KEY_VALUE_HEADS, HEAD_SIZE)

        scale = HEAD_SIZE ** (-0.5)
        allowed = (index[None, :] <= index[count:, None]) & (index[None, :] >= last_begin[count:, None])
        scores = jnp.einsum("qgrd,kgd->grqk", queries, keys, preferred_element_type=f32) * scale
        scores = jnp.where(allowed[None, None], scores, masked_score)
        top = jnp.max(scores, axis=-1, keepdims=True)
        exps = jnp.exp(scores - top)
        probs = exps / jnp.sum(exps, axis=-1, keepdims=True)
        probs_low = probs.astype(bf16)
        attended = jnp.einsum(
            "grqk,kgd->qgrd", probs_low, values, preferred_element_type=f32
        ).reshape(count, query_columns).astype(bf16)
        hidden = token_rows + jnp.dot(attended, out_weight, preferred_element_type=f32)
        normed_two = (hidden * inverse_rms(hidden) * gain_b).astype(bf16)
        logits = jnp.dot(normed_two, router_weight, preferred_element_type=f32)
        expert_ids = jnp.arange(EXPERTS, dtype=jnp.int32)
        chosen = jnp.any(routes[0][:, :, None] == expert_ids[None, None, :], axis=1)
        gates = jax.nn.softmax(jnp.where(chosen, logits, -jnp.inf), axis=-1)

        rows_in, gates_all, grad_all = group_gather(1, normed_two, gates.T, cotangent[0])
        gate = lax.dynamic_slice_in_dim(gates_all, expert, OWN, axis=1)
        mixed_part, normed_part, gate_grad_part, expert_wgrads = expert_layer(
            w_gate_up.shape[0], rows_in, grad_all, gate, weights
        )
        expert_grads = lax.psum_scatter(
            expert_wgrads, "dp", scatter_dimension=0, tiled=True, axis_index_groups=between
        )
        normed_grad, gate_grad = group_reduce(2, normed_part, gate_grad_part)
        gate_grad = gate_grad[:, :OWN].reshape(EXPERTS, count).T

        over_rows = (((0,), (0,)), ((), ()))
        weighted = jnp.where(chosen, gates * gate_grad, 0.0)
        logits_grad = weighted - gates * jnp.sum(weighted, axis=-1, keepdims=True)
        router_wide = router_weight.astype(f32)
        normed_grad = normed_grad + jnp.dot(logits_grad, router_wide.T, precision=highest)
        router_wgrad = jnp.dot(normed_two.astype(f32).T, logits_grad, precision=highest)
        hidden_branch, gain_two_grad = norm_back(hidden, gain_b, normed_grad)
        hidden_grad = grad_output + hidden_branch
        branch_low = hidden_grad.astype(bf16)
        out_wgrad = lax.dot_general(attended, branch_low, over_rows, preferred_element_type=f32)
        attended_grad = lax.dot_general(
            branch_low, out_weight, (((1,), (1,)), ((), ())), preferred_element_type=f32
        ).astype(bf16).reshape(count, KEY_VALUE_HEADS, group, HEAD_SIZE)

        prob_grad = jnp.einsum("qgrd,kgd->grqk", attended_grad, values, preferred_element_type=f32)
        delta = jnp.sum(probs * prob_grad, axis=-1, keepdims=True)
        score_grad = (probs * (prob_grad - delta)).astype(bf16)
        query_grad = (
            jnp.einsum("grqk,kgd->qgrd", score_grad, keys, preferred_element_type=f32) * scale
        ).reshape(count, QUERY_HEADS, HEAD_SIZE)
        key_grad = (
            jnp.einsum("grqk,qgrd->kgd", score_grad, queries, preferred_element_type=f32) * scale
        ).reshape(both, key_columns)
        value_grad = jnp.einsum(
            "grqk,qgrd->kgd", probs_low, attended_grad, preferred_element_type=f32
        ).reshape(both, key_columns)
        kv_grad = jnp.concatenate([key_grad, value_grad], 1)
        kv_back = lax.ppermute(kv_grad[:count].astype(bf16), "seq", back_pair)
        kv_grad = (kv_grad[count:] + kv_back.astype(f32)).astype(bf16).astype(f32)
        query_grad = query_grad.astype(bf16).astype(f32)
        query_back = unrotate(query_grad, cosine, sine).reshape(count, query_columns)
        key_back = unrotate(
            kv_grad[:, :key_columns].reshape(count, KEY_VALUE_HEADS, HEAD_SIZE), cosine, sine
        ).reshape(count, key_columns)
        query_projected = query_back.astype(bf16)
        kv_projected = jnp.concatenate([key_back, kv_grad[:, key_columns:]], 1).astype(bf16)
        query_wgrad = lax.dot_general(normed_one, query_projected, over_rows, preferred_element_type=f32)
        kv_wgrad = lax.dot_general(normed_one, kv_projected, over_rows, preferred_element_type=f32)
        over_columns = (((1,), (1,)), ((), ()))
        normed_one_grad = lax.dot_general(
            query_projected, qkv_weight[:, :query_columns], over_columns, preferred_element_type=f32
        ) + lax.dot_general(
            kv_projected, qkv_weight[:, query_columns:], over_columns, preferred_element_type=f32
        )
        rows_branch, gain_one_grad = norm_back(token_rows, gain_a, normed_one_grad)
        input_grad = (hidden_grad + rows_branch).astype(bf16)[None]

        little = jnp.concatenate(
            [spare(router_wgrad), spare(jnp.stack([gain_one_grad, gain_two_grad], 1))], 1
        )
        packed, mixed = weights_reduce(
            3, expert_groups,
            (query_wgrad.astype(bf16), kv_wgrad.astype(bf16), out_wgrad.astype(bf16), little), mixed_part
        )
        mixed = mixed.reshape(count, MODEL_WIDTH).astype(f32)
        output = (hidden + mixed).astype(bf16)[None]
        stat_sums = jnp.stack([jnp.sum(hidden * hidden), jnp.sum(mixed * mixed)])
        stat_sums = stat_sums + lax.ppermute(stat_sums, "seq", [(0, 1), (1, 0)])
        experts_all, ends = send_pieces(4, expert_grads, packed)
        widths = [query_columns // 2, key_columns, MODEL_WIDTH // 2, 128]
        query_shard, kv_shard, out_shard, little = [
            jnp.concatenate([ends[0, :, f : f + h], ends[1, :, f : f + h]], 1).astype(f32)
            for f, h in zip(starts_of(widths), widths)
        ]
        qkv_shard = jnp.concatenate([query_shard, kv_shard], 1)
        experts_all = experts_all.reshape((EXPERTS,) + experts_all.shape[2:])
        first = w_gate_up.shape[0]
        stream_rms = jnp.sqrt(stat_sums / (both * MODEL_WIDTH)).reshape(1, 2)
        return (
            output,
            input_grad,
            little[:, 128],
            qkv_shard,
            out_shard,
            little[:, 129],
            little[:, :EXPERTS],
            jnp.swapaxes(experts_all[:, :first], 0, 1).astype(f32),
            jnp.swapaxes(experts_all[:, first:], 0, 1).astype(f32),
            stream_rms,
        )

    return body


def solution(mesh):
    placed = (
        P("dp", "seq", None),
        P("dp", "seq"),
        P("dp", "seq", None),
        P("dp"),
        P("dp", None),
        P("dp", None),
        P("dp"),
        P("dp", None),
        P("dp", None, None),
        P("dp", None, None),
        P("dp", "seq", None),
    )
    return jax.shard_map(
        make_body(mesh.shape["dp"]),
        mesh=mesh,
        in_specs=placed,
        out_specs=(
            P("dp", "seq", None),
            P("dp", "seq", None),
            P("dp"),
            P("dp", None),
            P("dp", None),
            P("dp"),
            P("dp", None),
            P("dp", None, None),
            P("dp", None, None),
            P("dp", None),
        ),
        check_vma=False,
    )
```

```python
import functools

import jax
import jax.numpy as jnp
from jax import lax
from jax.experimental import pallas as pl
from jax.experimental.pallas import tpu as pltpu
from jax.sharding import PartitionSpec as P

MODEL_WIDTH = 1024
QUERY_HEADS = 16
KEY_VALUE_HEADS = 8
HEAD_SIZE = 64
F = 512
EXPERTS = 16
TOPK = 8
PLACES = 4
GROUP = 8
OWN = EXPERTS // GROUP

epsilon = 1e-06
rope_base = 10000.0
highest = lax.Precision.HIGHEST
masked_score = -1e30
f32 = jnp.float32
bf16 = jnp.bfloat16
MESH = pl.DeviceIdType.MESH

TOKEN_LINKS = ((4, 2), (2, 4))


def flip(value, bit):
    return value + bit * (1 - 2 * ((value // bit) % 2))


def flip_mask(value, mask):
    for bit in (1, 2, 4, 8):
        if mask & bit:
            value = flip(value, bit)
    return value


def subsets(bits):
    out = [0]
    for bit in bits:
        out = out + [m | bit for m in out]
    return out


def row_parts(rows):
    first = (rows // 2 + 15) // 16 * 16
    return ((0, first), (first, rows - first))


def my_place(places=PLACES):
    seq = lax.axis_index("seq")
    dp = lax.axis_index("dp")
    rank = seq * places + dp % places

    def peer(mask):
        return {
            "seq": 1 - seq if mask & places else seq,
            "dp": flip_mask(dp, mask & (places - 1)),
        }

    return rank, peer


def meet(devices):
    barrier = pltpu.get_barrier_semaphore()
    for there in devices:
        pl.semaphore_signal(barrier, inc=1, device_id=there, device_id_type=MESH)
    pl.semaphore_wait(barrier, len(devices))


def gather_kernel(count, *refs):
    ins, outs = refs[:count], refs[count : 2 * count]
    send, recv, send_core, recv_core, local = refs[2 * count :]
    rank, peer = my_place(PLACES)
    own = [
        pltpu.make_async_copy(ins[a], outs[a].at[rank], local.at[a]) for a in range(count)
    ]
    for copy in own:
        copy.start()
    meet([peer(bit) for bit in (1, 2, 4)])
    parts = [row_parts(ref.shape[0]) for ref in ins]

    def remote(a, p, mask, bit, sems, index):
        start, size = parts[a][p]
        rows = pl.ds(start, size)
        shard = flip_mask(rank, mask)
        src = ins[a].at[rows] if mask == 0 else outs[a].at[shard, rows]
        return pltpu.make_async_remote_copy(
            src_ref=src,
            dst_ref=outs[a].at[shard, rows],
            send_sem=sems[0].at[a, p, index],
            recv_sem=sems[1].at[a, p, index],
            device_id=peer(bit),
            device_id_type=MESH,
        )

    started = []
    live = {}
    for step in range(3):
        for p in range(2):
            for a in range(count):
                if parts[a][p][1] == 0:
                    continue
                order = TOKEN_LINKS[p]
                if step > 0:
                    for copy in live.pop((a, p)):
                        copy.wait_recv()
                if step < 2:
                    now = []
                    for index, mask in enumerate(subsets(order[:step])):
                        copy = remote(a, p, mask, order[step], (send, recv), 2**step - 1 + index)
                        copy.start()
                        now.append(copy)
                        started.append(copy)
                    live[(a, p)] = now
                fresh = [0] if step == 0 else [m | order[step - 1] for m in subsets(order[: step - 1])]
                base = 0 if step == 0 else 2 ** (step - 1)
                for index, mask in enumerate(fresh):
                    copy = remote(a, p, mask, 1, (send_core, recv_core), base + index)
                    copy.start()
                    live.setdefault("core", []).append(copy)
    for copy in live["core"]:
        copy.wait()
    for copy in started:
        copy.wait_send()
    for copy in own:
        copy.wait()


def group_gather(collective_id, *arrays):
    count = len(arrays)
    return pl.pallas_call(
        functools.partial(gather_kernel, count),
        out_shape=[jax.ShapeDtypeStruct((GROUP,) + a.shape, a.dtype) for a in arrays],
        in_specs=[pl.BlockSpec(memory_space=pltpu.VMEM)] * count,
        out_specs=[pl.BlockSpec(memory_space=pl.ANY)] * count,
        scratch_shapes=[
            pltpu.SemaphoreType.DMA((count, 2, 3)),
            pltpu.SemaphoreType.DMA((count, 2, 3)),
            pltpu.SemaphoreType.DMA((count, 2, 4)),
            pltpu.SemaphoreType.DMA((count, 2, 4)),
            pltpu.SemaphoreType.DMA((count,)),
        ],
        compiler_params=pltpu.CompilerParams(collective_id=collective_id, has_side_effects=True),
        cost_estimate=pl.CostEstimate(flops=1000000000, bytes_accessed=2**24, transcendentals=0),
        name="group_gather",
    )(*arrays)


def add_rows(target, source, start, size):
    chunk = 32 if size % 32 == 0 else 16

    def step(i, carry):
        rows = pl.ds(pl.multiple_of(start + i * chunk, chunk), chunk)
        target[rows] = (target[rows].astype(f32) + source[rows].astype(f32)).astype(target.dtype)
        return carry

    lax.fori_loop(0, size // chunk, step, 0)


def reduce_kernel(
    normed_ref, gate_ref, normed_out, gate_out,
    total, got0, got1, got2, sems, gate_sems, local, own_gate,
):
    rank, peer = my_place(PLACES)
    chip = rank // 2
    core = rank % 2
    parts = row_parts(normed_ref.shape[1])
    ins = (normed_ref,)
    outs = (normed_out,)
    loads = []
    for t in range(1):
        for c in range(4):
            copy = pltpu.make_async_copy(ins[t].at[2 * c + core], total.at[t, c], local.at[t, c])
            copy.start()
            loads.append(copy)
    everyone = [peer(mask) for mask in range(1, GROUP)]
    meet(everyone)
    gates = []
    keep = pltpu.make_async_copy(gate_ref.at[rank], gate_out.at[rank], own_gate)
    keep.start()
    for mask, there in zip(range(1, GROUP), everyone):
        copy = pltpu.make_async_remote_copy(
            src_ref=gate_ref.at[flip_mask(rank, mask)],
            dst_ref=gate_out.at[rank],
            send_sem=gate_sems.at[0, mask],
            recv_sem=gate_sems.at[1, mask],
            device_id=there,
            device_id_type=MESH,
        )
        copy.start()
        gates.append(copy)

    started = []
    live = {}

    def send(t, p, stage, index, src, dst, bit):
        copy = pltpu.make_async_remote_copy(
            src_ref=src,
            dst_ref=dst,
            send_sem=sems.at[0, t, p, stage, index],
            recv_sem=sems.at[1, t, p, stage, index],
            device_id=peer(bit),
            device_id_type=MESH,
        )
        copy.start()
        started.append(copy)
        live.setdefault((t, p), []).append(copy)

    def chip_of(mask):
        return flip_mask(rank, mask) // 2

    for p in range(2):
        for t in range(1):
            rows = pl.ds(*parts[p])
            for c in range(4):
                send(
                    t, p, 0, c, ins[t].at[2 * c + 1 - core, rows], got0.at[t, c, rows], 1
                )
    for copy in loads:
        copy.wait()
    got = (got1, got2)
    for stage in range(3):
        for p in range(2):
            for t in range(1):
                order = TOKEN_LINKS[p]
                rows = pl.ds(*parts[p])
                for copy in live.pop((t, p)):
                    copy.wait_recv()
                if stage == 0:

                    def over_chips(c, carry, t=t, p=p):
                        add_rows(total.at[t, c], got0.at[t, c], *parts[p])
                        return carry

                    lax.fori_loop(0, 4, over_chips, 0)
                else:
                    for index, mask in enumerate(subsets(order[stage:])):
                        if stage == 2:
                            outs[t][rows] = total[t, chip, rows].astype(f32) + got2[t, 0, rows].astype(f32)
                        else:
                            add_rows(
                                total.at[t, chip_of(mask)], got[stage - 1].at[t, index], *parts[p]
                            )
                if stage < 2:
                    for index, mask in enumerate(subsets(order[stage + 1 :])):
                        send(
                            t, p, stage + 1, index,
                            total.at[t, chip_of(mask | order[stage]), rows],
                            got[stage].at[t, index, rows],
                            order[stage],
                        )
    for copy in started:
        copy.wait_send()
    for copy in gates:
        copy.wait()
    keep.wait()


def group_reduce(collective_id, normed, gate_grad):
    rows, width = normed.shape[1:]
    return pl.pallas_call(
        reduce_kernel,
        out_shape=[
            jax.ShapeDtypeStruct((rows, width), f32),
            jax.ShapeDtypeStruct(gate_grad.shape, gate_grad.dtype),
        ],
        in_specs=[pl.BlockSpec(memory_space=pl.ANY)] * 2,
        out_specs=[
            pl.BlockSpec(memory_space=pltpu.VMEM),
            pl.BlockSpec(memory_space=pl.ANY),
        ],
        scratch_shapes=[
            pltpu.VMEM((1, 4, rows, width), bf16),
            pltpu.VMEM((1, 4, rows, width), bf16),
            pltpu.VMEM((1, 2, rows, width), bf16),
            pltpu.VMEM((1, 1, rows, width), bf16),
            pltpu.SemaphoreType.DMA((2, 1, 2, 3, 4)),
            pltpu.SemaphoreType.DMA((2, GROUP)),
            pltpu.SemaphoreType.DMA((1, 4)),
            pltpu.SemaphoreType.DMA(()),
        ],
        compiler_params=pltpu.CompilerParams(
            collective_id=collective_id, has_side_effects=True, vmem_limit_bytes=48 * 2**20
        ),
        cost_estimate=pl.CostEstimate(flops=1000000, bytes_accessed=2**24, transcendentals=0),
        name="group_reduce",
    )(normed, gate_grad)


def column_parts(half):
    first = -(-(half // 128) // 2) * 128
    return ((0, first), (first, half - first))


def shard_view(ref, halves, a, p, rank_value):
    start, size = column_parts(halves[a])[p]
    offset = pl.multiple_of((rank_value // PLACES) * halves[a] + start, 128)
    return ref.at[:, rank_value % PLACES, :, pl.ds(offset, size)]


def starts_of(sizes):
    return [sum(sizes[:i]) for i in range(len(sizes))]


def weights_gather_kernel(halves, packed, *refs):
    count = len(halves)
    outs = refs[:count]
    send, recv, local = refs[count:]
    rank, peer = my_place()
    firsts = starts_of(halves)
    seq = lax.axis_index("seq")
    own = []
    for a in range(count):
        columns = pl.ds(pl.multiple_of(seq * halves[a], 128), halves[a])
        copy = pltpu.make_async_copy(
            packed.at[:, :, pl.ds(firsts[a], halves[a])],
            outs[a].at[:, rank % PLACES, :, columns],
            local.at[a],
        )
        copy.start()
        own.append(copy)
    meet([peer(bit) for bit in (1, 2, 4)])
    started = []

    def remote(a, p, mask, bit, index):
        view = shard_view(outs[a], halves, a, p, flip_mask(rank, mask))
        start, size = column_parts(halves[a])[p]
        source = packed.at[:, :, pl.ds(firsts[a] + start, size)] if mask == 0 else view
        copy = pltpu.make_async_remote_copy(
            src_ref=source,
            dst_ref=view,
            send_sem=send.at[a, p, index],
            recv_sem=recv.at[a, p, index],
            device_id=peer(bit),
            device_id_type=MESH,
        )
        copy.start()
        started.append(copy)
        return copy

    live = {}
    last = []
    for step in range(3):
        for p in range(2):
            for a in range(count):
                if column_parts(halves[a])[p][1] == 0:
                    continue
                order = TOKEN_LINKS[p]
                if step > 0:
                    for copy in live.pop((a, p)):
                        copy.wait_recv()
                if step < 2:
                    live[(a, p)] = [
                        remote(a, p, mask, order[step], 2**step - 1 + index)
                        for index, mask in enumerate(subsets(order[:step]))
                    ]
                fresh = [0] if step == 0 else [m | order[step - 1] for m in subsets(order[: step - 1])]
                base = 0 if step == 0 else 2 ** (step - 1)
                for index, mask in enumerate(fresh):
                    last.append(remote(a, p, mask, 1, 3 + base + index))
    for copy in last:
        copy.wait_recv()
    for copy in started:
        copy.wait_send()
    for copy in own:
        copy.wait()


def weights_gather(collective_id, halves, packed):
    groups, rows, _ = packed.shape
    count = len(halves)
    whole = pl.pallas_call(
        functools.partial(weights_gather_kernel, halves),
        out_shape=[jax.ShapeDtypeStruct((groups, PLACES, rows, 2 * h), packed.dtype) for h in halves],
        in_specs=[pl.BlockSpec(memory_space=pltpu.VMEM)],
        out_specs=[pl.BlockSpec(memory_space=pl.ANY)] * count,
        scratch_shapes=[
            pltpu.SemaphoreType.DMA((count, 2, 7)),
            pltpu.SemaphoreType.DMA((count, 2, 7)),
            pltpu.SemaphoreType.DMA((count,)),
        ],
        compiler_params=pltpu.CompilerParams(collective_id=collective_id, has_side_effects=True),
        cost_estimate=pl.CostEstimate(flops=1000000, bytes_accessed=2**24, transcendentals=0),
        name="weights_gather",
    )(packed)
    return [w.reshape(-1, w.shape[3]) for w in whole]


def add_block(target, source, at, start, size):
    groups, rows = source.shape[0], source.shape[1]
    columns = pl.ds(start, size)
    chunk = 64 if rows % 64 == 0 else 16
    pieces = rows // chunk

    def step(i, carry):
        lines = pl.ds(pl.multiple_of((i % pieces) * chunk, chunk), chunk)
        index = (i // pieces, lines, columns)
        new = target[(at,) + index].astype(f32) + source[index].astype(f32)
        target[(at,) + index] = new.astype(target.dtype)
        return carry

    lax.fori_loop(0, groups * pieces, step, 0)


def weights_reduce_kernel(count, *refs):
    ins, packed, rows_out = refs[:count], refs[count], refs[count + 1]
    rest = refs[count + 2 :]
    total, got0, got1, got2 = [rest[i * count : (i + 1) * count] for i in range(4)]
    sems, local = rest[4 * count :]
    rank, peer = my_place()
    chip, core = rank // 2, rank % 2
    halves = [ref.shape[3] // 2 for ref in ins[:-1]]
    firsts = starts_of(halves)
    halves = halves + [ins[-1].shape[3]]
    parts = [column_parts(half) for half in halves]

    def source(a, value, start, size):
        if a == count - 1:
            return ins[a].at[value, :, :, pl.ds(start, size)]
        offset = pl.multiple_of((value // PLACES) * halves[a] + start, 128)
        return ins[a].at[:, value % PLACES, :, pl.ds(offset, size)]

    loads = []
    for a in range(count):
        for c in range(4):
            copy = pltpu.make_async_copy(
                source(a, 2 * c + core, 0, halves[a]), total[a].at[c], local.at[a, c]
            )
            copy.start()
            loads.append(copy)
    meet([peer(bit) for bit in (1, 2, 4)])
    started = []
    live = {}

    def send(a, p, stage, index, src, dst, bit):
        copy = pltpu.make_async_remote_copy(
            src_ref=src,
            dst_ref=dst,
            send_sem=sems.at[0, a, p, stage, index],
            recv_sem=sems.at[1, a, p, stage, index],
            device_id=peer(bit),
            device_id_type=MESH,
        )
        copy.start()
        started.append(copy)
        live.setdefault((a, p), []).append(copy)

    def chip_of(mask):
        return flip_mask(rank, mask) // 2

    for p in range(2):
        for a in range(count):
            columns = pl.ds(*parts[a][p])
            if parts[a][p][1]:
                for c in range(4):
                    send(
                        a, p, 0, c,
                        source(a, 2 * c + 1 - core, *parts[a][p]),
                        got0[a].at[c, :, :, columns],
                        1,
                    )
    for copy in loads:
        copy.wait()
    got = (got1, got2)
    for stage in range(3):
        for p in range(2):
            for a in range(count):
                start, size = parts[a][p]
                if size == 0:
                    continue
                order = TOKEN_LINKS[p]
                columns = pl.ds(start, size)
                for copy in live.pop((a, p)):
                    copy.wait_recv()
                if stage == 0:

                    def over_chips(c, carry, a=a, start=start, size=size):
                        add_block(total[a], got0[a].at[c], c, start, size)
                        return carry

                    lax.fori_loop(0, 4, over_chips, 0)
                else:
                    for index, mask in enumerate(subsets(order[stage:])):
                        add_block(total[a], got[stage - 1][a].at[index], chip_of(mask), start, size)
                if stage < 2:
                    for index, mask in enumerate(subsets(order[stage + 1 :])):
                        send(
                            a, p, stage + 1, index,
                            total[a].at[chip_of(mask | order[stage]), :, :, columns],
                            got[stage][a].at[index, :, :, columns],
                            order[stage],
                        )
    for a in range(count - 1):
        packed[:, :, pl.ds(firsts[a], halves[a])] = total[a][chip].astype(packed.dtype)
    rows_out[...] = total[-1][chip]
    for copy in started:
        copy.wait_send()


def weights_reduce(collective_id, groups, arrays, token_rows):
    count = len(arrays) + 1
    views = [a.reshape(groups, PLACES, -1, a.shape[1]) for a in arrays]
    rows = views[0].shape[2]
    halves = [a.shape[1] // 2 for a in arrays]

    each, width = token_rows.shape[1:]
    token_shape = (groups, each // groups, width)

    def buffers(lead):
        return [pltpu.VMEM((lead, groups, rows, h), a.dtype) for h, a in zip(halves, arrays)] + [
            pltpu.VMEM((lead,) + token_shape, bf16)
        ]

    dma = pltpu.SemaphoreType.DMA
    return pl.pallas_call(
        functools.partial(weights_reduce_kernel, count),
        out_shape=[
            jax.ShapeDtypeStruct((groups, rows, sum(halves)), bf16),
            jax.ShapeDtypeStruct(token_shape, bf16),
        ],
        in_specs=[pl.BlockSpec(memory_space=pl.ANY)] * count,
        out_specs=[pl.BlockSpec(memory_space=pltpu.VMEM)] * 2,
        scratch_shapes=buffers(4) + buffers(4) + buffers(2) + buffers(1)
        + [dma((2, count, 2, 3, 4)), dma((count, 4))],
        compiler_params=pltpu.CompilerParams(
            collective_id=collective_id, has_side_effects=True, vmem_limit_bytes=48 * 2**20
        ),
        cost_estimate=pl.CostEstimate(flops=1000000, bytes_accessed=2**24, transcendentals=0),
        name="weights_reduce",
    )(*views, token_rows.reshape((GROUP,) + token_shape))


def pieces_kernel(pieces, packed, whole, ends, far_got, send, recv, far_send, far_recv, last, local):
    rank, peer = my_place()
    place = rank % PLACES
    groups = packed.shape[0]
    seq = lax.axis_index("seq")
    home = lax.axis_index("dp") // PLACES
    keep = pltpu.make_async_copy(pieces.at[place], whole.at[rank], local)
    keep.start()
    masks = (4, 2, 6, 5, 3, 7, 1)
    others = [(home + k) % groups for k in range(1, groups)]
    far = [{"seq": seq, "dp": g * PLACES + place} for g in others]
    meet([peer(mask) for mask in masks] + far)
    sums = []
    for k, there in enumerate(far):
        copy = pltpu.make_async_remote_copy(
            src_ref=packed.at[others[k]],
            dst_ref=far_got.at[k],
            send_sem=far_send.at[k],
            recv_sem=far_recv.at[k],
            device_id=there,
            device_id_type=MESH,
        )
        copy.start()
        sums.append(copy)
    copies = []
    for mask in masks:
        copy = pltpu.make_async_remote_copy(
            src_ref=pieces.at[flip_mask(place, mask & (PLACES - 1))],
            dst_ref=whole.at[rank],
            send_sem=send.at[mask],
            recv_sem=recv.at[mask],
            device_id=peer(mask),
            device_id_type=MESH,
        )
        copy.start()
        copies.append(copy)
    for copy in sums:
        copy.wait()
    value = packed[home].astype(f32)
    for k in range(groups - 1):
        value = value + far_got[k].astype(f32)
    ends[seq] = value.astype(ends.dtype)
    copy = pltpu.make_async_remote_copy(
        src_ref=ends.at[seq],
        dst_ref=ends.at[seq],
        send_sem=last.at[0],
        recv_sem=last.at[1],
        device_id=peer(4),
        device_id_type=MESH,
    )
    copy.start()
    copies.append(copy)
    for copy in copies:
        copy.wait()
    keep.wait()


def send_pieces(collective_id, pieces, packed):
    groups = packed.shape[0]
    others = max(groups - 1, 1)
    dma = pltpu.SemaphoreType.DMA
    vmem = pl.BlockSpec(memory_space=pltpu.VMEM)
    return pl.pallas_call(
        pieces_kernel,
        out_shape=[
            jax.ShapeDtypeStruct((GROUP,) + pieces.shape[1:], pieces.dtype),
            jax.ShapeDtypeStruct((2,) + packed.shape[1:], packed.dtype),
        ],
        in_specs=[vmem, vmem],
        out_specs=[pl.BlockSpec(memory_space=pl.ANY), vmem],
        scratch_shapes=[
            pltpu.VMEM((others,) + packed.shape[1:], packed.dtype),
            dma((GROUP,)),
            dma((GROUP,)),
            dma((others,)),
            dma((others,)),
            dma((2,)),
            dma(()),
        ],
        compiler_params=pltpu.CompilerParams(collective_id=collective_id, has_side_effects=True),
        name="send_pieces",
    )(pieces, packed)


def expert_kernel(
    first, rows_ref, grad_ref, gate_ref, weights_ref,
    mixed_ref, normed_ref, gate_grad_ref, weights_out,
    gate_up_sum, down_sum, mixed_sum, normed_sum,
):
    step = pl.program_id(0)
    expert = pl.program_id(1)
    shards, each, width = rows_ref.shape
    count = shards * each
    rows = rows_ref[...].reshape(count, width)
    grad = grad_ref[...].reshape(count, width).astype(f32)
    gate = jnp.concatenate(
        [
            jnp.broadcast_to(gate_ref[i, pl.ds(expert, 1)], (128, each)).T[:, :1]
            for i in range(shards)
        ],
        0,
    )
    gate_up_weight = weights_ref[:, expert, :first].reshape(-1, width)
    down = weights_ref[:, expert, first:].reshape(-1, width)
    gate_up = jnp.dot(rows, gate_up_weight, preferred_element_type=f32)
    gate_part, up_part = gate_up[:, :F], gate_up[:, F:]
    sigmoid = 1.0 / (1.0 + jnp.exp(-gate_part))
    silu = gate_part * sigmoid
    act = (silu * up_part).astype(bf16)
    out = jnp.dot(act, down, preferred_element_type=f32)
    inner = jnp.sum(out * grad, axis=-1, keepdims=True)
    for i in range(shards):
        line = jnp.broadcast_to(inner[i * each : (i + 1) * each], (each, 128)).T
        gate_grad_ref[i, pl.ds(expert, 1)] = line[:1]
    mixed = gate * out
    expert_grad = (gate * grad).astype(bf16)
    across = (((1,), (1,)), ((), ()))
    over_rows = (((0,), (0,)), ((), ()))
    act_grad = lax.dot_general(expert_grad, down, across, preferred_element_type=f32)
    gate_up_grad = jnp.concatenate(
        [act_grad * up_part * (sigmoid * (1.0 + gate_part * (1.0 - sigmoid))), act_grad * silu], -1
    ).astype(bf16)
    normed = lax.dot_general(gate_up_grad, gate_up_weight, across, preferred_element_type=f32)

    @pl.when(expert == 0)
    def _():
        mixed_sum[...] = mixed
        normed_sum[...] = normed

    @pl.when(expert > 0)
    def _():
        mixed_sum[...] += mixed
        normed_sum[...] += normed

    @pl.when(expert == OWN - 1)
    def _():
        mixed_ref[...] = mixed_sum[...].astype(bf16).reshape(shards, each, width)
        normed_ref[...] = normed_sum[...].astype(bf16).reshape(shards, each, width)

    @pl.when(step == 0)
    def _():
        gate_up_sum[expert] = jnp.zeros_like(gate_up_sum[0])
        down_sum[expert] = jnp.zeros_like(down_sum[0])

    down_sum[expert] += lax.dot_general(act, expert_grad, over_rows, preferred_element_type=f32)
    gate_up_sum[expert] += lax.dot_general(rows, gate_up_grad, over_rows, preferred_element_type=f32)

    @pl.when(step == pl.num_programs(0) - 1)
    def _():
        owners = weights_out.shape[0]
        weights_out[:, expert, :first] = gate_up_sum[expert].astype(bf16).reshape(owners, first, width)
        weights_out[:, expert, first:] = down_sum[expert].astype(bf16).reshape(owners, -1, width)


def expert_layer(first, rows, grad, gate, weights):
    each, width = rows.shape[1:]
    shards = 2
    owners = weights.shape[0]
    tile = pl.BlockSpec((shards, each, width), lambda i, e: (i, 0, 0))
    whole = pl.BlockSpec(weights.shape, lambda i, e: (0, 0, 0, 0), pipeline_mode=pl.Buffered(1))
    return pl.pallas_call(
        functools.partial(expert_kernel, first),
        grid=(GROUP // shards, OWN),
        out_shape=[
            jax.ShapeDtypeStruct(rows.shape, bf16),
            jax.ShapeDtypeStruct(rows.shape, bf16),
            jax.ShapeDtypeStruct((GROUP, 8, each), f32),
            jax.ShapeDtypeStruct(weights.shape, bf16),
        ],
        in_specs=[
            tile,
            tile,
            pl.BlockSpec((shards, OWN, each), lambda i, e: (i, 0, 0)),
            whole,
        ],
        out_specs=[
            tile,
            tile,
            pl.BlockSpec((shards, 8, each), lambda i, e: (i, 0, 0)),
            whole,
        ],
        scratch_shapes=[
            pltpu.VMEM((OWN, owners * first, width), f32),
            pltpu.VMEM((OWN, owners * (weights.shape[2] - first), width), f32),
            pltpu.VMEM((shards * each, width), f32),
            pltpu.VMEM((shards * each, width), f32),
        ],
        compiler_params=pltpu.CompilerParams(vmem_limit_bytes=62 * 2**20),
        cost_estimate=pl.CostEstimate(flops=45000000000, bytes_accessed=2**24, transcendentals=0),
        name="expert_layer",
    )(rows, grad, gate, weights)


def inverse_rms(rows):
    return lax.rsqrt(jnp.mean(rows * rows, axis=-1, keepdims=True) + epsilon)


def norm_back(rows, gain_row, upstream):
    inverse = inverse_rms(rows)
    gain_grad = jnp.sum(upstream * rows * inverse, axis=0)
    scaled = upstream * gain_row
    rows_grad = inverse * scaled - rows * inverse**3 * jnp.mean(scaled * rows, axis=-1, keepdims=True)
    return rows_grad, gain_grad


def rope_tables(positions):
    half = HEAD_SIZE // 2
    frequency = rope_base ** (-(jnp.arange(half, dtype=f32) * 2.0) / HEAD_SIZE)
    angles = positions.astype(f32)[:, None] * frequency[None, :]
    cosine, sine = jnp.cos(angles), jnp.sin(angles)
    return jnp.concatenate([cosine, cosine], 1), jnp.concatenate([sine, sine], 1)


def rotary_apply(rows, cosine, sine):
    half = HEAD_SIZE // 2
    turned = jnp.concatenate([-rows[..., half:], rows[..., :half]], -1)
    return rows * cosine[:, None, :] + turned * sine[:, None, :]


def unrotate(rows, cosine, sine):
    half = HEAD_SIZE // 2
    scaled = rows * sine[:, None, :]
    back = jnp.concatenate([scaled[..., half:], -scaled[..., :half]], -1)
    return rows * cosine[:, None, :] + back


def make_body(n_dp):
    expert_groups = n_dp // PLACES
    inside = [[g * PLACES + j for j in range(PLACES)] for g in range(expert_groups)]
    between = [[g * PLACES + j for g in range(expert_groups)] for j in range(PLACES)]
    half_experts = EXPERTS // 2

    def over_groups(value):
        home = lax.axis_index("dp") // PLACES

        def turned(k):
            return lax.ppermute(value, "dp", [(d, (d + k * PLACES) % n_dp) for d in range(n_dp)])

        parts = [turned(k) for k in range(expert_groups - 1, 0, -1)] + [value]
        ring = jnp.stack(parts + parts[:-1])
        start = (expert_groups - 1 - home) % expert_groups
        return lax.dynamic_slice_in_dim(ring, start, expert_groups, axis=0)

    def expert_pieces(gate_up_shard, down_shard, seq_rank):
        mine = [
            jnp.swapaxes(lax.dynamic_slice_in_dim(w, seq_rank * half_experts, half_experts, axis=1), 0, 1)
            for w in (gate_up_shard, down_shard)
        ]
        mine = jnp.concatenate(mine, 1)
        return mine.reshape((PLACES, OWN) + mine.shape[1:])

    def body(
        tokens, starts, routes, gain_one, query_key_value_weight, w_out,
        gain_two, w_router, w_gate_up, w_down, cotangent,
    ):
        count = tokens.shape[1]
        seq_rank = lax.axis_index("seq")
        expert = (seq_rank * PLACES + lax.axis_index("dp") % PLACES) * OWN
        query_columns = QUERY_HEADS * HEAD_SIZE
        key_columns = KEY_VALUE_HEADS * HEAD_SIZE
        group = QUERY_HEADS // KEY_VALUE_HEADS
        forward_pair, back_pair = [(0, 1)], [(1, 0)]

        mine = expert_pieces(w_gate_up, w_down, seq_rank)
        mine, query_key_value_weight, tokens, starts = lax.optimization_barrier(
            (mine, query_key_value_weight, tokens, starts)
        )
        mine = lax.all_to_all(
            mine, "dp", split_axis=0, concat_axis=0, tiled=True, axis_index_groups=inside
        )
        tokens_before = lax.ppermute(tokens[0], "seq", forward_pair)
        starts_before = lax.ppermute(starts, "seq", forward_pair)
        spare = lambda value: jnp.pad(value, ((0, 0), (0, 128 - value.shape[1])))
        little = jnp.concatenate([spare(w_router), spare(jnp.stack([gain_one, gain_two], 1))], 1)
        shards = (query_key_value_weight, w_out, little)
        halves = [w.shape[1] // 2 for w in shards]
        packed = over_groups(
            jnp.concatenate(
                [
                    lax.dynamic_slice_in_dim(w, seq_rank * h, h, axis=1)
                    for w, h in zip(shards, halves)
                ],
                1,
            )
        )
        mine, packed, tokens_before, starts_before = lax.optimization_barrier(
            (mine, packed, tokens_before, starts_before)
        )
        weights = lax.all_gather(mine, "dp", axis=0, tiled=True, axis_index_groups=between)
        qkv_weight, out_weight, small = weights_gather(0, halves, packed)
        router_weight = small[:, :EXPERTS]
        gain_a = small[:, 128].astype(f32)
        gain_b = small[:, 129].astype(f32)

        token_rows = tokens[0].astype(f32)
        grad_output = cotangent[0].astype(f32)
        both = 2 * count
        index = jnp.arange(both, dtype=jnp.int32)
        flags = jnp.concatenate([starts_before[0], starts[0]])
        begins = (flags > 0) | (index == jnp.where(seq_rank == 0, count, 0))
        last_begin = jnp.max(
            jnp.where(begins[None, :] & (index[None, :] <= index[:, None]), index[None, :], 0), axis=1
        )
        cosine_all, sine_all = rope_tables(index - last_begin)
        cosine, sine = cosine_all[count:], sine_all[count:]

        rows_all = jnp.concatenate([tokens_before.astype(f32), token_rows], 0)
        normed_all = (rows_all * inverse_rms(rows_all) * gain_a).astype(bf16)
        normed_one = normed_all[count:]
        projected_q = jnp.dot(normed_one, qkv_weight[:, :query_columns], preferred_element_type=f32)
        projected_kv = jnp.dot(normed_all, qkv_weight[:, query_columns:], preferred_element_type=f32)
        queries = rotary_apply(
            projected_q.reshape(count, QUERY_HEADS, HEAD_SIZE), cosine, sine
        ).astype(bf16).reshape(count, KEY_VALUE_HEADS, group, HEAD_SIZE)
        keys = rotary_apply(
            projected_kv[:, :key_columns].reshape(both, KEY_VALUE_HEADS, HEAD_SIZE), cosine_all, sine_all
        ).astype(bf16)
        values = projected_kv[:, key_columns:].astype(bf16).reshape(both, KEY_VALUE_HEADS, HEAD_SIZE)

        scale = HEAD_SIZE ** (-0.5)
        allowed = (index[None, :] <= index[count:, None]) & (index[None, :] >= last_begin[count:, None])
        scores = jnp.einsum("qgrd,kgd->grqk", queries, keys, preferred_element_type=f32) * scale
        scores = jnp.where(allowed[None, None], scores, masked_score)
        top = jnp.max(scores, axis=-1, keepdims=True)
        exps = jnp.exp(scores - top)
        probs = exps / jnp.sum(exps, axis=-1, keepdims=True)
        probs_low = probs.astype(bf16)
        attended = jnp.einsum(
            "grqk,kgd->qgrd", probs_low, values, preferred_element_type=f32
        ).reshape(count, query_columns).astype(bf16)
        hidden = token_rows + jnp.dot(attended, out_weight, preferred_element_type=f32)
        normed_two = (hidden * inverse_rms(hidden) * gain_b).astype(bf16)
        logits = jnp.dot(normed_two, router_weight, preferred_element_type=f32)
        expert_ids = jnp.arange(EXPERTS, dtype=jnp.int32)
        chosen = jnp.any(routes[0][:, :, None] == expert_ids[None, None, :], axis=1)
        gates = jax.nn.softmax(jnp.where(chosen, logits, -jnp.inf), axis=-1)

        rows_in, gates_all, grad_all = group_gather(1, normed_two, gates.T, cotangent[0])
        gate = lax.dynamic_slice_in_dim(gates_all, expert, OWN, axis=1)
        mixed_part, normed_part, gate_grad_part, expert_wgrads = expert_layer(
            w_gate_up.shape[0], rows_in, grad_all, gate, weights
        )
        expert_grads = lax.psum_scatter(
            expert_wgrads, "dp", scatter_dimension=0, tiled=True, axis_index_groups=between
        )
        normed_grad, gate_grad = group_reduce(2, normed_part, gate_grad_part)
        gate_grad = gate_grad[:, :OWN].reshape(EXPERTS, count).T

        over_rows = (((0,), (0,)), ((), ()))
        weighted = jnp.where(chosen, gates * gate_grad, 0.0)
        logits_grad = weighted - gates * jnp.sum(weighted, axis=-1, keepdims=True)
        router_wide = router_weight.astype(f32)
        normed_grad = normed_grad + jnp.dot(logits_grad, router_wide.T, precision=highest)
        router_wgrad = jnp.dot(normed_two.astype(f32).T, logits_grad, precision=highest)
        hidden_branch, gain_two_grad = norm_back(hidden, gain_b, normed_grad)
        hidden_grad = grad_output + hidden_branch
        branch_low = hidden_grad.astype(bf16)
        out_wgrad = lax.dot_general(attended, branch_low, over_rows, preferred_element_type=f32)
        attended_grad = lax.dot_general(
            branch_low, out_weight, (((1,), (1,)), ((), ())), preferred_element_type=f32
        ).astype(bf16).reshape(count, KEY_VALUE_HEADS, group, HEAD_SIZE)

        prob_grad = jnp.einsum("qgrd,kgd->grqk", attended_grad, values, preferred_element_type=f32)
        delta = jnp.sum(probs * prob_grad, axis=-1, keepdims=True)
        score_grad = (probs * (prob_grad - delta)).astype(bf16)
        query_grad = (
            jnp.einsum("grqk,kgd->qgrd", score_grad, keys, preferred_element_type=f32) * scale
        ).reshape(count, QUERY_HEADS, HEAD_SIZE)
        key_grad = (
            jnp.einsum("grqk,qgrd->kgd", score_grad, queries, preferred_element_type=f32) * scale
        ).reshape(both, key_columns)
        value_grad = jnp.einsum(
            "grqk,qgrd->kgd", probs_low, attended_grad, preferred_element_type=f32
        ).reshape(both, key_columns)
        kv_grad = jnp.concatenate([key_grad, value_grad], 1)
        kv_back = lax.ppermute(kv_grad[:count].astype(bf16), "seq", back_pair)
        kv_grad = (kv_grad[count:] + kv_back.astype(f32)).astype(bf16).astype(f32)
        query_grad = query_grad.astype(bf16).astype(f32)
        query_back = unrotate(query_grad, cosine, sine).reshape(count, query_columns)
        key_back = unrotate(
            kv_grad[:, :key_columns].reshape(count, KEY_VALUE_HEADS, HEAD_SIZE), cosine, sine
        ).reshape(count, key_columns)
        projected_grad = jnp.concatenate([query_back, key_back, kv_grad[:, key_columns:]], 1).astype(bf16)
        qkv_wgrad = lax.dot_general(normed_one, projected_grad, over_rows, preferred_element_type=f32)
        normed_one_grad = lax.dot_general(
            projected_grad, qkv_weight, (((1,), (1,)), ((), ())), preferred_element_type=f32
        )
        rows_branch, gain_one_grad = norm_back(token_rows, gain_a, normed_one_grad)
        input_grad = (hidden_grad + rows_branch).astype(bf16)[None]

        little = jnp.concatenate(
            [spare(router_wgrad), spare(jnp.stack([gain_one_grad, gain_two_grad], 1))], 1
        )
        packed, mixed = weights_reduce(
            3, expert_groups, (qkv_wgrad.astype(bf16), out_wgrad.astype(bf16), little), mixed_part
        )
        mixed = mixed.reshape(count, MODEL_WIDTH).astype(f32)
        output = (hidden + mixed).astype(bf16)[None]
        stat_sums = jnp.stack([jnp.sum(hidden * hidden), jnp.sum(mixed * mixed)])
        stat_sums = stat_sums + lax.ppermute(stat_sums, "seq", [(0, 1), (1, 0)])
        experts_all, ends = send_pieces(4, expert_grads, packed)
        qkv_shard, out_shard, little = [
            jnp.concatenate([ends[0, :, f : f + h], ends[1, :, f : f + h]], 1).astype(f32)
            for f, h in zip(starts_of(halves), halves)
        ]
        experts_all = experts_all.reshape((EXPERTS,) + experts_all.shape[2:])
        first = w_gate_up.shape[0]
        stream_rms = jnp.sqrt(stat_sums / (both * MODEL_WIDTH)).reshape(1, 2)
        return (
            output,
            input_grad,
            little[:, 128],
            qkv_shard,
            out_shard,
            little[:, 129],
            little[:, :EXPERTS],
            jnp.swapaxes(experts_all[:, :first], 0, 1).astype(f32),
            jnp.swapaxes(experts_all[:, first:], 0, 1).astype(f32),
            stream_rms,
        )

    return body


def solution(mesh):
    placed = (
        P("dp", "seq", None),
        P("dp", "seq"),
        P("dp", "seq", None),
        P("dp"),
        P("dp", None),
        P("dp", None),
        P("dp"),
        P("dp", None),
        P("dp", None, None),
        P("dp", None, None),
        P("dp", "seq", None),
    )
    return jax.shard_map(
        make_body(mesh.shape["dp"]),
        mesh=mesh,
        in_specs=placed,
        out_specs=(
            P("dp", "seq", None),
            P("dp", "seq", None),
            P("dp"),
            P("dp", None),
            P("dp", None),
            P("dp"),
            P("dp", None),
            P("dp", None, None),
            P("dp", None, None),
            P("dp", None),
        ),
        check_vma=False,
    )
```
